32 devices in a mesh: expert: 4 (over z), shard: 8 (over y, x, core).
Axes of the slice: x: 2, y: 2, z: 4, core: 2. Of those that a mesh axis runs over, the one named last changes fastest.
Arguments:
- token_ids: int32 [8192], P('expert'), may hold values from 0 to 49151
- positions: int32 [32, 32], P('expert'), may hold values from 0 to 254, as said below
- pair_index: int32 [16, 2], replicated, may hold values from 0 to 31, as said below
- ref_logps: float32 [32], replicated, may hold values from -64 to 64
- routes: int32 [8192, 8], P(('expert', 'shard')), may hold values from 0 to 31, all different within a row; in each aligned block of 256 rows (0 to 255, 256 to 511, ...) at most 88 rows name the same one
- step_count: int32 [], replicated, may hold values from 2 to 20
- embed_table: float32 [49152, 1536], P('shard', 'expert'), may hold values from -1.75 to 1.75
- embed_first: float32 [49152, 1536], P('shard', 'expert'), may hold values from -0.00015258789 to 0.00015258789
- embed_second: float32 [49152, 1536], P('shard', 'expert'), may hold values from 6.25e-11 to 2.5e-10
- qkv_weight: float32 [1536, 2560], P(('expert', 'shard')), may hold values from -0.21875 to 0.21875
- qkv_first: float32 [1536, 2560], P(('expert', 'shard')), may hold values from -0.00390625 to 0.00390625
- qkv_second: float32 [1536, 2560], P(('expert', 'shard')), may hold values from 1.8e-08 to 2.88e-07
- out_weight: float32 [1536, 1536], P(('expert', 'shard')), may hold values from -0.625 to 0.625
- out_first: float32 [1536, 1536], P(('expert', 'shard')), may hold values from -0.0009765625 to 0.0009765625
- out_second: float32 [1536, 1536], P(('expert', 'shard')), may hold values from 2.25e-09 to 9e-09
- router_weight: float32 [1536, 32], P(('expert', 'shard')), may hold values from -0.078125 to 0.078125
- router_first: float32 [1536, 32], P(('expert', 'shard')), may hold values from -0.00048828125 to 0.00048828125
- router_second: float32 [1536, 32], P(('expert', 'shard')), may hold values from 5.625e-10 to 2.25e-09
- norm_gains: float32 [3, 1536], P(None, ('expert', 'shard')), may hold values from 0.5 to 1.5
- gains_first: float32 [3, 1536], P(None, ('expert', 'shard')), may hold values from -0.0034179688 to 0.0034179688
- gains_second: float32 [3, 1536], P(None, ('expert', 'shard')), may hold values from 2.5e-08 to 1e-07
- in_weight: float32 [32, 1536, 2, 512], P('shard', None, None, 'expert'), may hold values from -0.15625 to 0.15625
- in_first: float32 [32, 1536, 2, 512], P('shard', None, None, 'expert'), may hold values from -0.00048828125 to 0.00048828125
- in_second: float32 [32, 1536, 2, 512], P('shard', None, None, 'expert'), may hold values from 5.625e-10 to 2.25e-09
- down_weight: float32 [32, 512, 1536], P('shard', 'expert'), may hold values from -1 to 1
- down_first: float32 [32, 512, 1536], P('shard', 'expert'), may hold values from -0.00024414062 to 0.00024414062
- down_second: float32 [32, 512, 1536], P('shard', 'expert'), may hold values from 6.125e-11 to 9.8e-10
Outputs:
- loss_value: float32 [], replicated
- new_table: float32 [49152, 1536], P('shard', 'expert')
- new_table_first: float32 [49152, 1536], P('shard', 'expert')
- new_table_second: float32 [49152, 1536], P('shard', 'expert')
- new_qkv: float32 [1536, 2560], P(('expert', 'shard'))
- new_qkv_first: float32 [1536, 2560], P(('expert', 'shard'))
- new_qkv_second: float32 [1536, 2560], P(('expert', 'shard'))
- new_out: float32 [1536, 1536], P(('expert', 'shard'))
- new_out_first: float32 [1536, 1536], P(('expert', 'shard'))
- new_out_second: float32 [1536, 1536], P(('expert', 'shard'))
- new_router: float32 [1536, 32], P(('expert', 'shard'))
- new_router_first: float32 [1536, 32], P(('expert', 'shard'))
- new_router_second: float32 [1536, 32], P(('expert', 'shard'))
- new_gains: float32 [3, 1536], P(None, ('expert', 'shard'))
- new_gains_first: float32 [3, 1536], P(None, ('expert', 'shard'))
- new_gains_second: float32 [3, 1536], P(None, ('expert', 'shard'))
- new_in: float32 [32, 1536, 2, 512], P('shard', None, None, 'expert')
- new_in_first: float32 [32, 1536, 2, 512], P('shard', None, None, 'expert')
- new_in_second: float32 [32, 1536, 2, 512], P('shard', None, None, 'expert')
- new_down: float32 [32, 512, 1536], P('shard', 'expert')
- new_down_first: float32 [32, 512, 1536], P('shard', 'expert')
- new_down_second: float32 [32, 512, 1536], P('shard', 'expert')
- lamb_stats: float32 [7, 3], replicated
The draws below stay inside these ranges and needn't reach their ends.
Inputs may be any that keep to these rules, and one draw needn't show every extreme that they name: Each row holds 32 consecutive positions. `pair_index`: every sequence appears exactly once. `routes`: each token names 8 different experts; within the rows of one device no expert is named by more than 88 tokens.
All inputs are finite; a program needn't handle non-finite values.
Results may differ from the reference program's by a relative error of at most 0.028.
The reference program's roundings to bfloat16 on the way count: a program that leaves them out, or rounds other values in their place, can miss the bound.
Values may be sent and summed in bfloat16 or wider, within the bound.
A program may use at most 384 MiB of HBM per device.

```python
import math
from functools import partial
import jax
import jax.numpy as jnp
import numpy as np
from jax import lax

D = 1536
QUERY_HEADS = 24
KEY_VALUE_HEADS = 8
HEAD_WIDTH = 64
FF = 512
TOP = 8
V = 49152
EXPERTS = 32
SEQUENCE_TOKENS = 256
COMP = 32
CAP = 88
QKV = 2560
SEQS = 32
PAIRS = 16
TOKENS = 8192


def draw_positions(key, part):
    starts = jax.random.randint(key, (SEQS,), 0, SEQUENCE_TOKENS - COMP)
    starts = jnp.where(jnp.arange(SEQS) == 0, SEQUENCE_TOKENS - 1 - COMP, starts)
    return (starts[:, None] + jnp.arange(COMP)[None, :]).astype(jnp.int32)


def draw_pair_index(key, part):
    return jax.random.permutation(key, SEQS).reshape(PAIRS, 2).astype(jnp.int32)


def moment_field(key, shape, base):
    spread = jax.random.uniform(key, shape, jnp.float32, 0.0, jnp.log(4.0))
    return (base * jnp.exp(spread)).astype(jnp.float32)


def draw_qkv_second(key, part):
    base = 0.001 * (0.024 / PAIRS ** 0.5) ** 2
    return moment_field(jax.random.fold_in(key, 11), (D, QKV), base)


def draw_down_second(key, part):
    base = 0.001 * (0.0014 / PAIRS ** 0.5) ** 2
    return moment_field(jax.random.fold_in(key, 23), (EXPERTS, FF, D), base)


def set_ends(result, own_key, low, largest):
    dims = result.shape
    index_at = [jax.random.randint(jax.random.fold_in(own_key, axis), (), 0, dims[axis]) for axis in range(len(dims))]
    result = result.at[tuple(index_at)].set(low)
    longest = dims.index(max(dims))
    index_at[longest] = (index_at[longest] + 1) % dims[longest]
    return result.at[tuple(index_at)].set(largest)


def steps_of(rng, shape, pieces, smallest, high):
    def one(axis_at, shards_of):
        heights = jax.random.uniform(jax.random.fold_in(jax.random.fold_in(rng, 6), axis_at), (shards_of,), jnp.float32, smallest / len(pieces), high / len(pieces))
        return jnp.repeat(jnp.exp(heights), shape[axis_at] // shards_of).reshape((-1,) + (1,) * (len(shape) - axis_at - 1))

    factor_of = one(*pieces[0])
    for cut in pieces[1:]:
        factor_of = factor_of * one(*cut)
    return factor_of


def cumulative_ranks(number_of, skew):
    portions = [(1 << 20) // math.isqrt(grade ** skew) + 1 for grade in range(1, number_of + 1)]
    scale = 1 + sum(portions) // (1 << 30)
    return np.cumsum(np.array([max(1, weight // scale) for weight in portions]))


def ranked(rng, dims, amount, lean):
    listing = cumulative_ranks(amount, lean)
    lot = jax.random.randint(jax.random.fold_in(rng, 1), dims, 0, int(listing[amount - 1]))
    standing = jnp.searchsorted(jnp.asarray(listing, jnp.int32), lot, side="right")
    return jax.random.permutation(jax.random.fold_in(rng, 2), amount)[standing].astype(jnp.int32)


def routed_block(own_key, own, number, rows, count, top, most, slope):
    ranking = jax.random.permutation(own_key, count)
    crowded, common = shares(count, rows * top, most, slope, True), shares(count, rows * top, most, slope, False)
    places = jnp.arange(count)

    def named(tallies, offset_by):
        used = int((tallies > 0).sum())
        fixed = max(1, used // 4)
        moved = fixed + (places - fixed + offset_by * (used - fixed)) % max(1, count - fixed)
        return jnp.zeros((count,), jnp.int32).at[ranking[jnp.where(places < fixed, places, moved)]].set(jnp.asarray(tallies, jnp.int32))

    tallies = jnp.where(number % 4 == 0, named(crowded, number // 4), named(common, number - number // 4 - 1))
    mixed = jax.random.permutation(jax.random.fold_in(own, 3), count)
    source_of, sink = mixed[0:count // 2 * 2:2], mixed[1:count // 2 * 2:2]
    room = jnp.minimum(tallies[source_of] - 1, most - tallies[sink]) // 2
    room = jnp.where((source_of == ranking[0]) | (sink == ranking[0]) | (tallies[sink] == 0), 0, jnp.maximum(room, 0))
    moved = jax.random.randint(jax.random.fold_in(own, 4), (count // 2,), 0, 1 << 20) % (room + 1)
    tallies = tallies.at[source_of].add(-moved).at[sink].add(moved)
    labels = jnp.searchsorted(jnp.cumsum(tallies), jnp.arange(rows * top), side="right").astype(jnp.int32)
    listing = labels.reshape(top, rows).T
    listing = listing[jax.random.permutation(jax.random.fold_in(own, 1), rows)]
    offset_by = jax.random.randint(jax.random.fold_in(own, 2), (rows, 1), 0, top)
    return jnp.take_along_axis(listing, (jnp.arange(top)[None, :] + offset_by) % top, axis=1)


def shares(amount, total, limit, skew, full):
    weights = [(1 << 20) // math.isqrt(standing ** skew) + 1 for standing in range(1, amount + 1)]
    largest = limit if full else min(limit, max(-(-total // amount), total * weights[0] // sum(weights)))
    least = 1 if total - largest >= amount - 1 else 0
    given, surplus = [largest] + [least] * (amount - 1), total - largest - least * (amount - 1)
    while surplus > 0:
        candidates = [i for i in range(1, amount) if given[i] < largest] or [i for i in range(1, amount) if given[i] < limit]
        pool, budget = sum([weights[i] for i in candidates]), surplus
        for i in candidates:
            extra = min(limit - given[i], max(1, budget * weights[i] // pool), surplus)
            given[i] = given[i] + extra
            surplus = surplus - extra
    return np.array(given)


def noise(key, extent, scale, reach, shards=(), held_as=jnp.bfloat16):
    level = steps_of(key, extent, shards, -0.22, 0.18) if shards else 1.0
    array = jax.random.normal(key, extent, jnp.float32) * scale * level
    return jnp.minimum(jnp.maximum(array, -reach), reach).astype(held_as)


def setup_inputs(seed: int = 0) -> dict:
    keys = jax.random.split(jax.random.key(seed), 28)
    token_ids = set_ends(ranked(keys[0], (TOKENS,), V, 2), jax.random.fold_in(keys[0], 3), 0, V - 1).astype(jnp.int32)
    positions = draw_positions(jax.random.fold_in(keys[27], 71), 0)
    pair_index = draw_pair_index(jax.random.fold_in(keys[27], 71), 0)
    ref_logps = noise(keys[3], (SEQS,), (2 * COMP ** 0.5), 64.0, (), jnp.float32)
    routes_keys = jax.random.split(jax.random.fold_in(keys[4], 1), TOKENS // SEQUENCE_TOKENS)
    routes_turns = jax.random.permutation(jax.random.fold_in(keys[4], 3), TOKENS // SEQUENCE_TOKENS)
    routes = jax.vmap(lambda own, number: routed_block(jax.random.fold_in(keys[4], 2), own, number, SEQUENCE_TOKENS, EXPERTS, TOP, CAP, 1))(routes_keys, routes_turns).reshape((TOKENS, TOP))
    step_count = jax.random.randint(keys[5], (), 2, 21).astype(jnp.int32)
    embed_table = noise(keys[6], (V, D), (12 / D ** 0.5), 1.75, ((0, 8), (1, 4)), jnp.float32)
    embed_first = noise(keys[7], (V, D), (0.11 * 0.001 / PAIRS ** 0.5), 0.00015258789, ((0, 8), (1, 4)), jnp.float32)
    embed_second = jnp.clip(jnp.exp(math.log(2.4999999292951713e-10) - 1.3862944 * jax.random.uniform(keys[8], (V, D), jnp.float32) ** steps_of(keys[8], (V, D), ((0, 8), (1, 4)), -0.2, 0.2)), 6.249999823237928e-11, 2.4999999292951713e-10)
    qkv_weight = noise(keys[9], (D, QKV), (D // 2) ** -0.5, 0.21875, ((0, 32),), jnp.float32)
    qkv_first = noise(keys[10], (D, QKV), (0.11 * 0.024 / PAIRS ** 0.5), 0.00390625, ((0, 32),), jnp.float32)
    qkv_second = draw_qkv_second(jax.random.fold_in(keys[27], 71), 0)
    out_weight = noise(keys[12], (QUERY_HEADS * HEAD_WIDTH, D), (QUERY_HEADS * HEAD_WIDTH // 16) ** -0.5, 0.625, ((0, 32),), jnp.float32)
    out_first = noise(keys[13], (QUERY_HEADS * HEAD_WIDTH, D), (0.11 * 0.006 / PAIRS ** 0.5), 0.0009765625, ((0, 32),), jnp.float32)
    out_second = jnp.clip(jnp.exp(math.log(8.99999985648492e-09) - 1.3862944 * jax.random.uniform(keys[14], (QUERY_HEADS * HEAD_WIDTH, D), jnp.float32) ** steps_of(keys[14], (QUERY_HEADS * HEAD_WIDTH, D), ((0, 32),), -0.2, 0.2)), 2.24999996412123e-09, 8.99999985648492e-09)
    router_weight = noise(keys[15], (D, EXPERTS), (4 * D) ** -0.5, 0.078125, ((0, 32),), jnp.float32)
    router_first = noise(keys[16], (D, EXPERTS), (0.11 * 0.003 / PAIRS ** 0.5), 0.00048828125, ((0, 32),), jnp.float32)
    router_second = jnp.clip(jnp.exp(math.log(2.24999996412123e-09) - 1.3862944 * jax.random.uniform(keys[17], (D, EXPERTS), jnp.float32) ** steps_of(keys[17], (D, EXPERTS), ((0, 32),), -0.2, 0.2)), 5.624999910303075e-10, 2.24999996412123e-09)
    norm_gains = jnp.clip(1.0 + 0.1 * jax.random.normal(keys[18], (3, D), jnp.float32), 0.5, 1.5)
    gains_first = noise(keys[19], (3, D), (0.11 * 0.02 / PAIRS ** 0.5), 0.0034179688, ((1, 32),), jnp.float32)
    gains_second = jnp.clip(jnp.exp(math.log(1.0000000116860974e-07) - 1.3862944 * jax.random.uniform(keys[20], (3, D), jnp.float32) ** steps_of(keys[20], (3, D), ((1, 32),), -0.2, 0.2)), 2.5000000292152436e-08, 1.0000000116860974e-07)
    in_weight = noise(keys[21], (EXPERTS, D, 2, FF), D ** -0.5, 0.15625, ((0, 8), (3, 4)), jnp.float32)
    in_first = noise(keys[22], (EXPERTS, D, 2, FF), (0.11 * 0.003 / PAIRS ** 0.5), 0.00048828125, ((0, 8), (3, 4)), jnp.float32)
    in_second = jnp.clip(jnp.exp(math.log(2.24999996412123e-09) - 1.3862944 * jax.random.uniform(keys[23], (EXPERTS, D, 2, FF), jnp.float32) ** steps_of(keys[23], (EXPERTS, D, 2, FF), ((0, 8), (3, 4)), -0.2, 0.2)), 5.624999910303075e-10, 2.24999996412123e-09)
    down_weight = noise(keys[24], (EXPERTS, FF, D), (FF // 16) ** -0.5, 1.0, ((0, 8), (1, 4)), jnp.float32)
    down_first = noise(keys[25], (EXPERTS, FF, D), (0.11 * 0.0014 / PAIRS ** 0.5), 0.00024414062, ((0, 8), (1, 4)), jnp.float32)
    down_second = draw_down_second(jax.random.fold_in(keys[27], 71), 0)
    return {"token_ids": token_ids, "positions": positions, "pair_index": pair_index, "ref_logps": ref_logps, "routes": routes, "step_count": step_count, "embed_table": embed_table, "embed_first": embed_first, "embed_second": embed_second, "qkv_weight": qkv_weight, "qkv_first": qkv_first, "qkv_second": qkv_second, "out_weight": out_weight, "out_first": out_first, "out_second": out_second, "router_weight": router_weight, "router_first": router_first, "router_second": router_second, "norm_gains": norm_gains, "gains_first": gains_first, "gains_second": gains_second, "in_weight": in_weight, "in_first": in_first, "in_second": in_second, "down_weight": down_weight, "down_first": down_first, "down_second": down_second}


@jax.custom_vjp
def lower_precision(v):
    return lax.optimization_barrier(v.astype(jnp.bfloat16)).astype(jnp.float32)

@jax.custom_vjp
def low_back(v):
    return v

def low_keep(v):
    return (lower_precision(v), None)

def low_pass(kept, grad):
    return (grad,)

def back_keep(v):
    return (v, None)

def back_low(kept, grad):
    return (lower_precision(grad),)
lower_precision.defvjp(low_keep, low_pass)
low_back.defvjp(back_keep, back_low)
HIGH = lax.Precision.HIGHEST
BETA = 0.1
LOGIT_SCALE = 6.0
RATE_ONE = 0.9
RATE_TWO = 0.999
EPSILON = 1e-06
DECAY = 0.01
STEP_RATE = 0.3

def norm_apply(values, gain):
    return values * lax.rsqrt(lax.optimization_barrier(jnp.mean(values * values, axis=-1, keepdims=True)) + 1e-06) * gain

def rotary_apply(values):
    half = values.shape[-1] // 2
    places = jnp.arange(values.shape[0], dtype=jnp.float32)
    freqs = jnp.exp(-jnp.log(10000.0) * jnp.arange(half, dtype=jnp.float32) / half)
    angles = places[:, None] * freqs[None, :]
    cosine = jnp.cos(angles)[:, None, :]
    sine = jnp.sin(angles)[:, None, :]
    first_half = values[..., :half]
    second_half = values[..., half:]
    return jnp.concatenate([first_half * cosine - second_half * sine, second_half * cosine + first_half * sine], axis=-1)

def slot_places(route_flat, expert_count, capacity):
    onehot = (route_flat[:, None] == jnp.arange(expert_count, dtype=jnp.int32)[None, :]).astype(jnp.int32)
    before = jnp.cumsum(onehot, axis=0, dtype=jnp.int32) - onehot
    return route_flat * capacity + lax.optimization_barrier(jnp.sum(before * onehot, axis=1, dtype=jnp.int32))

def gate_soft(router_logits, route):
    chosen = jnp.take_along_axis(router_logits, route, axis=1)
    return jax.nn.softmax(chosen, axis=-1)

def pair_loss(seq_sums, ref_logps, pair_index):
    margin = seq_sums - ref_logps
    scaled = BETA * (margin[pair_index[:, 0]] - margin[pair_index[:, 1]])
    return -jnp.mean(jax.nn.log_sigmoid(scaled))

def lamb_parts(weight, moment_one, moment_two, gradient, step_value):
    moment_one = RATE_ONE * moment_one + (1.0 - RATE_ONE) * gradient
    moment_two = RATE_TWO * moment_two + (1.0 - RATE_TWO) * gradient * gradient
    fixed_one = moment_one / (1.0 - RATE_ONE ** step_value)
    fixed_two = moment_two / (1.0 - RATE_TWO ** step_value)
    update = fixed_one / (jnp.sqrt(fixed_two) + EPSILON) + DECAY * weight
    return (moment_one, moment_two, update)

def sequence(weights, item):
    table_w, qkv_w, out_w, router_w, gains, in_w, down_w = weights
    tok_ids, places, route = item
    query_group_width = QUERY_HEADS // KEY_VALUE_HEADS
    embedded = low_back(table_w[tok_ids])
    normed = lower_precision(norm_apply(embedded, gains[0]))
    projected_rows = low_back(jnp.dot(normed, qkv_w, precision=HIGH))
    query_matrix_rows = lower_precision(rotary_apply(projected_rows[:, :QUERY_HEADS * HEAD_WIDTH].reshape(SEQUENCE_TOKENS, QUERY_HEADS, HEAD_WIDTH))).reshape(SEQUENCE_TOKENS, KEY_VALUE_HEADS, query_group_width, HEAD_WIDTH)
    key_matrix_rows = lower_precision(rotary_apply(projected_rows[:, QUERY_HEADS * HEAD_WIDTH:(QUERY_HEADS + KEY_VALUE_HEADS) * HEAD_WIDTH].reshape(SEQUENCE_TOKENS, KEY_VALUE_HEADS, HEAD_WIDTH)))
    value_matrix_rows = lower_precision(projected_rows[:, (QUERY_HEADS + KEY_VALUE_HEADS) * HEAD_WIDTH:].reshape(SEQUENCE_TOKENS, KEY_VALUE_HEADS, HEAD_WIDTH))
    scores = jnp.einsum('qhgd,khd->hgqk', query_matrix_rows, key_matrix_rows, precision=HIGH) * HEAD_WIDTH ** (-0.5)
    causal = jnp.arange(SEQUENCE_TOKENS)[:, None] >= jnp.arange(SEQUENCE_TOKENS)[None, :]
    scores = low_back(jnp.where(causal, scores, -1000000000.0))
    attn_probs = low_back(lower_precision(jax.nn.softmax(scores, axis=-1)))
    attended = jnp.einsum('hgqk,khd->qhgd', attn_probs, value_matrix_rows, precision=HIGH).reshape(SEQUENCE_TOKENS, QUERY_HEADS * HEAD_WIDTH)
    attended = low_back(lower_precision(attended))
    branch = low_back(jnp.dot(attended, out_w, precision=HIGH))
    resid = embedded + branch
    normed_two = lower_precision(norm_apply(resid, gains[1]))
    gate_probs = gate_soft(jnp.dot(normed_two, router_w, precision=HIGH), route)
    slot_index = slot_places(route.reshape(-1), EXPERTS, CAP)
    copies = low_back(jnp.repeat(normed_two, TOP, axis=0))
    buffer = jnp.zeros((EXPERTS * CAP, D), jnp.float32).at[slot_index].set(copies).reshape(EXPERTS, CAP, D)
    gate_up = low_back(jnp.einsum('ecd,edjf->ecjf', buffer, in_w, precision=HIGH))
    hidden = low_back(lower_precision(jax.nn.silu(gate_up[:, :, 0]) * gate_up[:, :, 1]))
    produced = low_back(lower_precision(jnp.einsum('ecf,efd->ecd', hidden, down_w, precision=HIGH)))
    routed = produced.reshape(EXPERTS * CAP, D)[slot_index].reshape(SEQUENCE_TOKENS, TOP, D)
    resid = resid + lax.optimization_barrier(jnp.sum(gate_probs[:, :, None] * routed, axis=1))
    final_rows = lower_precision(norm_apply(resid[places], gains[2]))
    logits = low_back(jnp.dot(final_rows, table_w.T, precision=HIGH) / LOGIT_SCALE)
    targets = tok_ids[places + 1]
    log_probs = jax.nn.log_softmax(logits, axis=-1)
    return jnp.sum(jnp.take_along_axis(log_probs, targets[:, None], axis=1))

def total_loss(weights, token_ids, positions, routes, pair_index, ref_logps):
    rounded = tuple((lower_precision(weight) for weight in weights))
    items = (token_ids.reshape(-1, SEQUENCE_TOKENS), positions, routes.reshape(-1, SEQUENCE_TOKENS, TOP))
    seq_sums = lax.map(jax.checkpoint(partial(sequence, rounded)), items)
    return pair_loss(seq_sums, ref_logps, pair_index)

def reference(token_ids, positions, pair_index, ref_logps, routes, step_count, embed_table, embed_first, embed_second, qkv_weight, qkv_first, qkv_second, out_weight, out_first, out_second, router_weight, router_first, router_second, norm_gains, gains_first, gains_second, in_weight, in_first, in_second, down_weight, down_first, down_second):
    weights = (embed_table, qkv_weight, out_weight, router_weight, norm_gains, in_weight, down_weight)
    firsts = (embed_first, qkv_first, out_first, router_first, gains_first, in_first, down_first)
    seconds = (embed_second, qkv_second, out_second, router_second, gains_second, in_second, down_second)
    loss_value, pullback = jax.vjp(lambda packed: total_loss(packed, token_ids, positions, routes, pair_index, ref_logps), weights)
    gradients = pullback(jnp.ones_like(loss_value))[0]
    step_value = step_count.astype(jnp.float32)
    results = [loss_value]
    stat_rows = []
    for weight, moment_one, moment_two, gradient in zip(weights, firsts, seconds, gradients):
        moment_one, moment_two, update = lamb_parts(weight, moment_one, moment_two, gradient, step_value)
        weight_norm = jnp.sqrt(jnp.sum(weight * weight))
        update_norm = jnp.sqrt(jnp.sum(update * update))
        trust_ratio = weight_norm / update_norm
        results.extend([weight - STEP_RATE * trust_ratio * update, moment_one, moment_two])
        stat_rows.append(jnp.stack([weight_norm, update_norm, trust_ratio]))
    results.append(jnp.stack(stat_rows))
    return tuple(results)
```

```python
import jax
import jax.numpy as jnp
from jax import lax
from jax.experimental import pallas as pl
from jax.experimental.pallas import tpu as pltpu
from jax.sharding import PartitionSpec as P

D = 1536
QUERY_HEADS = 24
KEY_VALUE_HEADS = 8
GROUP = QUERY_HEADS // KEY_VALUE_HEADS
HEAD_WIDTH = 64
TOP = 8
EXPERTS = 32
SEQUENCE_TOKENS = 256
COMP = 32

BETA = 0.1
LOGIT_SCALE = 6.0
RATE_ONE = 0.9
RATE_TWO = 0.999
EPSILON = 1e-06
DECAY = 0.01
STEP_RATE = 0.3

BOTH = ("expert", "shard")
bf16 = jnp.bfloat16
f32 = jnp.float32


def norm_apply(values, gain):
    return values * lax.rsqrt(jnp.mean(values * values, axis=-1, keepdims=True) + 1e-06) * gain


def rotary_apply(values, places):
    half = values.shape[-1] // 2
    freqs = jnp.exp(-jnp.log(10000.0) * jnp.arange(half, dtype=f32) / half)
    angles = places[:, None] * freqs[None, :]
    cosine = jnp.cos(angles)[:, None, :]
    sine = jnp.sin(angles)[:, None, :]
    first_half = values[..., :half]
    second_half = values[..., half:]
    return jnp.concatenate(
        [first_half * cosine - second_half * sine, second_half * cosine + first_half * sine],
        axis=-1,
    )


def lamb_parts(weight, moment_one, moment_two, gradient, step_value):
    moment_one = RATE_ONE * moment_one + (1.0 - RATE_ONE) * gradient
    moment_two = RATE_TWO * moment_two + (1.0 - RATE_TWO) * gradient * gradient
    fixed_one = moment_one / (1.0 - RATE_ONE**step_value)
    fixed_two = moment_two / (1.0 - RATE_TWO**step_value)
    update = fixed_one / (jnp.sqrt(fixed_two) + EPSILON) + DECAY * weight
    return (moment_one, moment_two, update)


STEPS = 4


def row_lists(tokens, base, rows):
    inside = (tokens >= base) & (tokens < base + rows)
    count = jnp.sum(inside.astype(jnp.int32), axis=1)
    place = jnp.arange(SEQUENCE_TOKENS, dtype=jnp.int32)
    before = (place[:, None] < place[None, :]).astype(bf16)
    rank = jnp.dot(inside.astype(bf16), before, preferred_element_type=f32).astype(jnp.int32)
    packed = place[None, :] * 65536 + (tokens - base)
    hit = inside[:, :, None] & (rank[:, :, None] == place[None, None, :])
    entry = jnp.sum(jnp.where(hit, packed[:, :, None], 0), axis=1)
    empty = SEQUENCE_TOKENS * 65536
    return jnp.where(place[None, :] < count[:, None], entry, empty), count


def gather_kernel(list_ref, count_ref, table_ref, out_ref, rows_ref):
    b = pl.program_id(0)
    rows_ref[...] = jnp.zeros_like(rows_ref)

    def step(k, carry):
        for j in range(STEPS):
            entry = list_ref[b, k * STEPS + j]
            rows_ref[pl.ds(entry >> 16, 1), :] = table_ref[pl.ds(entry & 65535, 1), :]
        return carry

    lax.fori_loop(0, (count_ref[b] + STEPS - 1) // STEPS, step, 0)
    out_ref[0] = rows_ref[:SEQUENCE_TOKENS].astype(bf16)


def gather_rows(lists, counts, table):
    blocks = lists.shape[0]
    rows, columns = table.shape
    return pl.pallas_call(
        gather_kernel,
        grid_spec=pltpu.PrefetchScalarGridSpec(
            num_scalar_prefetch=2,
            grid=(blocks,),
            in_specs=[pl.BlockSpec((rows, columns), lambda b, *_: (0, 0))],
            out_specs=pl.BlockSpec((1, SEQUENCE_TOKENS, columns), lambda b, *_: (b, 0, 0)),
            scratch_shapes=[pltpu.VMEM((SEQUENCE_TOKENS + 8, columns), f32)],
        ),
        out_shape=jax.ShapeDtypeStruct((blocks, SEQUENCE_TOKENS, columns), bf16),
        compiler_params=pltpu.CompilerParams(vmem_limit_bytes=40 << 20),
        name="gather_rows",
    )(lists, counts, table)


def scatter_kernel(list_ref, count_ref, grad_ref, head_ref, out_ref, rows_ref):
    b = pl.program_id(0)

    @pl.when(b == 0)
    def _():
        out_ref[...] = head_ref[...].astype(f32)

    rows_ref[:SEQUENCE_TOKENS] = grad_ref[0].astype(f32)
    rows_ref[SEQUENCE_TOKENS:] = jnp.zeros((8, rows_ref.shape[1]), f32)

    def step(k, carry):
        for j in range(STEPS):
            entry = list_ref[b, k * STEPS + j]
            out_ref[pl.ds(entry & 65535, 1), :] += rows_ref[pl.ds(entry >> 16, 1), :]
        return carry

    lax.fori_loop(0, (count_ref[b] + STEPS - 1) // STEPS, step, 0)


def scatter_rows(lists, counts, grads, head):
    blocks = lists.shape[0]
    rows, columns = head.shape
    return pl.pallas_call(
        scatter_kernel,
        grid_spec=pltpu.PrefetchScalarGridSpec(
            num_scalar_prefetch=2,
            grid=(blocks,),
            in_specs=[
                pl.BlockSpec((1, SEQUENCE_TOKENS, columns), lambda b, *_: (b, 0, 0)),
                pl.BlockSpec((rows, columns), lambda b, *_: (0, 0)),
            ],
            out_specs=pl.BlockSpec((rows, columns), lambda b, *_: (0, 0)),
            scratch_shapes=[pltpu.VMEM((SEQUENCE_TOKENS + 8, columns), f32)],
        ),
        out_shape=jax.ShapeDtypeStruct((rows, columns), f32),
        compiler_params=pltpu.CompilerParams(vmem_limit_bytes=50 << 20),
        name="scatter_rows",
    )(lists, counts, grads, head)


def on_device(
    token_ids,
    positions,
    pair_index,
    ref_logps,
    routes,
    step_count,
    embed_table,
    embed_first,
    embed_second,
    qkv_weight,
    qkv_first,
    qkv_second,
    out_weight,
    out_first,
    out_second,
    router_weight,
    router_first,
    router_second,
    norm_gains,
    gains_first,
    gains_second,
    in_weight,
    in_first,
    in_second,
    down_weight,
    down_first,
    down_second,
):
    shard_id = lax.axis_index("shard")
    expert_id = lax.axis_index("expert")
    shards = lax.axis_size("shard")
    planes = lax.axis_size("expert")
    devices = shards * planes
    vocab_rows, columns = embed_table.shape
    vocab_base = shard_id * vocab_rows
    own_rows = vocab_rows // planes
    local_experts = in_weight.shape[0]
    hidden_units = in_weight.shape[3]
    head_cols = QUERY_HEADS * HEAD_WIDTH
    key_cols = KEY_VALUE_HEADS * HEAD_WIDTH
    rows_all = devices * COMP

    tokens_all = lax.all_gather(token_ids, "expert", axis=0, tiled=True).reshape(
        devices, SEQUENCE_TOKENS
    )
    places_all = lax.all_gather(positions, "expert", axis=0, tiled=True)
    own_places = lax.dynamic_index_in_dim(positions, shard_id, 0, keepdims=False)
    start = own_places[0]
    routes_all = lax.all_gather(
        lax.dynamic_slice_in_dim(routes, start, COMP, 0), BOTH, axis=0, tiled=True
    )
    spots = jnp.arange(SEQUENCE_TOKENS, dtype=jnp.int32)
    targets = jnp.sum(
        jnp.where(
            places_all[:, :, None] + 1 == spots[None, None, :], tokens_all[:, None, :], 0
        ),
        axis=2,
    ).reshape(-1)

    lists, counts = row_lists(tokens_all, vocab_base, vocab_rows)
    picked = gather_rows(lists, counts, embed_table).reshape(
        planes, shards, SEQUENCE_TOKENS, columns
    )
    picked = lax.psum_scatter(picked, "shard", scatter_dimension=1, tiled=True)
    picked = lax.all_to_all(picked[:, 0], "expert", split_axis=0, concat_axis=0, tiled=True)
    embedded = jnp.concatenate([picked[p] for p in range(planes)], axis=1).astype(f32)

    qkv_full, out_full, router_full, gains_full = (
        lax.all_gather(qkv_weight.astype(bf16), BOTH, axis=0, tiled=True),
        lax.all_gather(out_weight.astype(bf16), BOTH, axis=0, tiled=True),
        lax.all_gather(router_weight.astype(bf16), BOTH, axis=0, tiled=True),
        lax.all_gather(norm_gains.astype(bf16), BOTH, axis=1, tiled=True),
    )
    gains_value = gains_full.astype(f32)
    table_own = lax.all_to_all(
        embed_table.astype(bf16).reshape(planes, own_rows, columns),
        "expert",
        split_axis=0,
        concat_axis=0,
        tiled=True,
    )
    table_own = jnp.concatenate([table_own[p] for p in range(planes)], axis=1)

    normed, norm_back_one = jax.vjp(norm_apply, embedded, gains_value[0])
    normed_b = normed.astype(bf16)
    normed_rows = lax.dynamic_slice_in_dim(normed_b, start, COMP, 0)
    query_weight, pair_weight = qkv_full[:, :head_cols], qkv_full[:, head_cols:]
    places_f = own_places.astype(f32)
    spots_f = spots.astype(f32)

    def make_query(projected):
        return rotary_apply(projected.reshape(COMP, QUERY_HEADS, HEAD_WIDTH), places_f)

    def make_key(projected):
        return rotary_apply(
            projected.reshape(SEQUENCE_TOKENS, KEY_VALUE_HEADS, HEAD_WIDTH), spots_f
        )

    query_f, query_back = jax.vjp(
        make_query, jnp.dot(normed_rows, query_weight, preferred_element_type=f32)
    )
    projected_pair = jnp.dot(normed_b, pair_weight, preferred_element_type=f32)
    key_f, key_back = jax.vjp(make_key, projected_pair[:, :key_cols])
    query = query_f.astype(bf16).reshape(COMP, KEY_VALUE_HEADS, GROUP, HEAD_WIDTH)
    key = key_f.astype(bf16)
    value = (
        projected_pair[:, key_cols:]
        .reshape(SEQUENCE_TOKENS, KEY_VALUE_HEADS, HEAD_WIDTH)
        .astype(bf16)
    )
    scores = jnp.einsum("qhgd,khd->hgqk", query, key, preferred_element_type=f32) * HEAD_WIDTH ** (
        -0.5
    )
    scores = jnp.where(own_places[:, None] >= spots[None, :], scores, -1000000000.0)
    expd = jnp.exp(scores - jnp.max(scores, axis=-1, keepdims=True))
    probs = expd / jnp.sum(expd, axis=-1, keepdims=True)
    probs_b = probs.astype(bf16)
    attended = (
        jnp.einsum("hgqk,khd->qhgd", probs_b, value, preferred_element_type=f32)
        .reshape(COMP, head_cols)
        .astype(bf16)
    )
    resid = lax.dynamic_slice_in_dim(embedded, start, COMP, 0) + jnp.dot(
        attended, out_full, preferred_element_type=f32
    )
    normed_two, norm_back_two = jax.vjp(norm_apply, resid, gains_value[1])
    normed_two_b = normed_two.astype(bf16)

    expert_rows = lax.all_gather(normed_two_b, BOTH, axis=0, tiled=True)
    chosen = jnp.any(
        routes_all[:, :, None] == jnp.arange(EXPERTS, dtype=jnp.int32)[None, None, :], axis=1
    )

    def soft_gates(router_logits, mask):
        top = jnp.max(jnp.where(mask, router_logits, -3e38), axis=-1, keepdims=True)
        weight = jnp.where(mask, jnp.exp(jnp.where(mask, router_logits - top, 0.0)), 0.0)
        return weight / jnp.sum(weight, axis=-1, keepdims=True)

    gates = soft_gates(jnp.dot(expert_rows, router_full, preferred_element_type=f32), chosen)
    own_index = expert_id * shards + shard_id
    own_gates = lax.dynamic_slice_in_dim(gates, own_index * COMP, COMP, 0)
    local_gates = lax.dynamic_slice_in_dim(gates, shard_id * local_experts, local_experts, 1)
    in_b = in_weight.astype(bf16)
    down_b = down_weight.astype(bf16)
    gate_up = jnp.einsum("td,edjf->tejf", expert_rows, in_b, preferred_element_type=f32)

    def swiglu(both):
        return jax.nn.silu(both[:, :, 0]) * both[:, :, 1]

    hidden, swiglu_back = jax.vjp(swiglu, gate_up)
    gated_hidden = (hidden.astype(bf16).astype(f32) * local_gates[:, :, None]).astype(bf16)
    produced = jnp.einsum("tef,efd->td", gated_hidden, down_b, preferred_element_type=f32)
    combined = lax.psum_scatter(produced.astype(bf16), BOTH, scatter_dimension=0, tiled=True)
    resid_two = resid + combined.astype(f32)

    final_rows, norm_back_three = jax.vjp(norm_apply, resid_two, gains_value[2])
    head_rows = lax.all_gather(final_rows.astype(bf16), BOTH, axis=0, tiled=True)
    logits = jnp.einsum("rd,vd->rv", head_rows, table_own, preferred_element_type=f32) / LOGIT_SCALE
    own_base = vocab_base + expert_id * own_rows
    target_hot = targets[:, None] == own_base + jnp.arange(own_rows, dtype=jnp.int32)[None, :]
    row_top = jnp.max(logits, axis=1)
    row_total = jnp.sum(jnp.exp(logits - row_top[:, None]), axis=1)
    row_hit = jnp.sum(jnp.where(target_hot, logits, 0.0), axis=1)
    stats = lax.all_gather(jnp.stack([row_top, row_total, row_hit]), BOTH, axis=0, tiled=False)
    top_all = jnp.max(stats[:, 0], axis=0)
    total_all = jnp.sum(stats[:, 1] * jnp.exp(stats[:, 0] - top_all[None]), axis=0)
    row_lse = top_all + jnp.log(total_all)
    seq_sums = jnp.sum((jnp.sum(stats[:, 2], axis=0) - row_lse).reshape(-1, COMP), axis=1)

    sequences = jnp.arange(devices, dtype=jnp.int32)[None, :]
    pair_sign = (pair_index[:, :1] == sequences).astype(f32) - (
        pair_index[:, 1:] == sequences
    ).astype(f32)
    scaled = BETA * jnp.sum(pair_sign * (seq_sums - ref_logps)[None, :], axis=1)
    loss_value = -jnp.mean(jax.nn.log_sigmoid(scaled))
    pair_grad = jax.nn.sigmoid(-scaled) * (-BETA / scaled.shape[0])
    seq_grad = jnp.sum(pair_sign * pair_grad[:, None], axis=0)
    row_grad = jnp.repeat(seq_grad, COMP)
    grad_logits = (
        row_grad[:, None] * (target_hot.astype(f32) - jnp.exp(logits - row_lse[:, None]))
    ).astype(bf16)
    grad_rows = jnp.dot(grad_logits, table_own, preferred_element_type=f32) / LOGIT_SCALE
    head_grad = (
        jnp.einsum("rv,rd->vd", grad_logits, head_rows, preferred_element_type=f32) / LOGIT_SCALE
    ).astype(bf16)
    head_grad = lax.all_to_all(
        jnp.stack([head_grad[:, p * columns : (p + 1) * columns] for p in range(planes)]),
        "expert",
        split_axis=0,
        concat_axis=0,
        tiled=True,
    ).reshape(vocab_rows, columns)
    own_grad_rows = lax.psum_scatter(
        grad_rows.astype(bf16), BOTH, scatter_dimension=0, tiled=True
    ).astype(f32)
    grad_resid_two, grad_gain_three = norm_back_three(own_grad_rows)

    grad_all = lax.all_gather(grad_resid_two.astype(bf16), BOTH, axis=0, tiled=True)
    grad_down = jnp.einsum("tef,td->efd", gated_hidden, grad_all, preferred_element_type=f32)
    pulled = jnp.einsum("td,efd->tef", grad_all, down_b, preferred_element_type=f32)
    grad_gates_local = jnp.sum(hidden.astype(bf16).astype(f32) * pulled, axis=2)
    grad_hidden = (pulled * local_gates[:, :, None]).astype(bf16)
    grad_gate_up = swiglu_back(grad_hidden.astype(f32))[0].astype(bf16)
    grad_in = jnp.einsum("td,tejf->edjf", expert_rows, grad_gate_up, preferred_element_type=f32)
    grad_copies = jnp.einsum("tejf,edjf->td", grad_gate_up, in_b, preferred_element_type=f32)
    grad_gates_all = lax.dynamic_update_slice_in_dim(
        jnp.zeros((rows_all, 128), f32), grad_gates_local, shard_id * local_experts, 1
    )
    back = lax.psum_scatter(
        jnp.concatenate([grad_copies.astype(bf16), grad_gates_all.astype(bf16)], axis=1),
        BOTH,
        scatter_dimension=0,
        tiled=True,
    ).astype(f32)
    grad_gates = back[:, D : D + EXPERTS]
    grad_router_logits = own_gates * (
        grad_gates - jnp.sum(own_gates * grad_gates, axis=1, keepdims=True)
    )
    grad_normed_two = back[:, :D] + jnp.einsum(
        "se,de->sd", grad_router_logits, router_full.astype(f32)
    )
    grad_router = jnp.einsum("sd,se->de", normed_two_b.astype(f32), grad_router_logits)
    grad_resid, grad_gain_two = norm_back_two(grad_normed_two)
    grad_resid = grad_resid + grad_resid_two
    grad_branch = grad_resid.astype(bf16)
    grad_out = jnp.einsum("sk,sd->kd", attended, grad_branch, preferred_element_type=f32)
    grad_attended = (
        jnp.einsum("sd,kd->sk", grad_branch, out_full, preferred_element_type=f32)
        .astype(bf16)
        .reshape(COMP, KEY_VALUE_HEADS, GROUP, HEAD_WIDTH)
    )

    grad_probs = jnp.einsum("qhgd,khd->hgqk", grad_attended, value, preferred_element_type=f32)
    grad_probs = grad_probs.astype(bf16).astype(f32)
    inner = jnp.sum(grad_probs * probs, axis=-1, keepdims=True)
    grad_scores = (probs * (grad_probs - inner)).astype(bf16)
    grad_value = jnp.einsum("hgqk,qhgd->khd", probs_b, grad_attended, preferred_element_type=f32)
    grad_query = jnp.einsum(
        "hgqk,khd->qhgd", grad_scores, key, preferred_element_type=f32
    ) * HEAD_WIDTH ** (-0.5)
    grad_key = jnp.einsum(
        "hgqk,qhgd->khd", grad_scores, query, preferred_element_type=f32
    ) * HEAD_WIDTH ** (-0.5)
    grad_query_rows = query_back(grad_query.reshape(COMP, QUERY_HEADS, HEAD_WIDTH))[0].astype(bf16)
    grad_pair_rows = jnp.concatenate(
        [key_back(grad_key)[0], grad_value.reshape(SEQUENCE_TOKENS, key_cols)], axis=1
    ).astype(bf16)
    grad_qkv = jnp.concatenate(
        [
            jnp.einsum("sd,sk->dk", normed_rows, grad_query_rows, preferred_element_type=f32),
            jnp.einsum("sd,sk->dk", normed_b, grad_pair_rows, preferred_element_type=f32),
        ],
        axis=1,
    )
    grad_normed = jnp.einsum("sk,dk->sd", grad_pair_rows, pair_weight, preferred_element_type=f32)
    grad_normed_rows = jnp.einsum(
        "sk,dk->sd", grad_query_rows, query_weight, preferred_element_type=f32
    )

    def spread(rows):
        return lax.dynamic_update_slice_in_dim(
            jnp.zeros((SEQUENCE_TOKENS, D), f32), rows, start, 0
        )

    grad_embedded, grad_gain_one = norm_back_one(grad_normed + spread(grad_normed_rows))
    grad_embedded = (grad_embedded + spread(grad_resid)).astype(bf16)
    sent = jnp.stack([grad_embedded[:, p * columns : (p + 1) * columns] for p in range(planes)])
    sent = lax.all_to_all(sent, "expert", split_axis=0, concat_axis=0, tiled=True)
    sent = lax.all_gather(sent, "shard", axis=1, tiled=False).reshape(
        devices, SEQUENCE_TOKENS, columns
    )
    table_grad = scatter_rows(lists, counts, sent, head_grad)

    gains_grad = jnp.stack([grad_gain_one, grad_gain_two, grad_gain_three])
    layer_sums = (
        lax.psum_scatter(grad_qkv.astype(bf16), BOTH, scatter_dimension=0, tiled=True).astype(f32),
        lax.psum_scatter(grad_out.astype(bf16), BOTH, scatter_dimension=0, tiled=True).astype(f32),
        lax.psum_scatter(grad_router, BOTH, scatter_dimension=0, tiled=True),
        lax.psum_scatter(gains_grad, BOTH, scatter_dimension=1, tiled=True),
    )
    weights = (
        embed_table,
        qkv_weight,
        out_weight,
        router_weight,
        norm_gains,
        in_weight,
        down_weight,
    )
    firsts = (embed_first, qkv_first, out_first, router_first, gains_first, in_first, down_first)
    seconds = (
        embed_second,
        qkv_second,
        out_second,
        router_second,
        gains_second,
        in_second,
        down_second,
    )
    gradients = (
        table_grad,
        layer_sums[0],
        layer_sums[1],
        layer_sums[2],
        layer_sums[3],
        grad_in,
        grad_down,
    )
    step_value = step_count.astype(f32)
    moved = [
        lamb_parts(weight, moment_one, moment_two, gradient, step_value)
        for weight, moment_one, moment_two, gradient in zip(weights, firsts, seconds, gradients)
    ]
    partial_norms = jnp.stack(
        [
            jnp.stack([jnp.sum(weight * weight), jnp.sum(parts[2] * parts[2])])
            for weight, parts in zip(weights, moved)
        ]
    )
    norm_values = jnp.sqrt(lax.psum(partial_norms, BOTH))
    trust_ratio = norm_values[:, 0] / norm_values[:, 1]
    results = [loss_value]
    for place, (weight, parts) in enumerate(zip(weights, moved)):
        results.extend([weight - STEP_RATE * trust_ratio[place] * parts[2], parts[0], parts[1]])
    results.append(jnp.stack([norm_values[:, 0], norm_values[:, 1], trust_ratio], axis=1))
    return tuple(results)


def solution(mesh):
    rows = P(BOTH, None)
    vocab = P("shard", "expert")
    gains = P(None, BOTH)
    inner = P("shard", None, None, "expert")
    outer = P("shard", "expert", None)
    state = (vocab,) * 3 + (rows,) * 9 + (gains,) * 3 + (inner,) * 3 + (outer,) * 3
    return jax.shard_map(
        on_device,
        mesh=mesh,
        in_specs=(P("expert"), P("expert", None), P(), P(), rows, P()) + state,
        out_specs=(P(),) + state + (P(),),
        check_vma=False,
    )
```

```python
import functools
import math

import jax
import jax.numpy as jnp
from jax import lax
from jax.experimental import pallas as pl
from jax.experimental.pallas import tpu as pltpu
from jax.sharding import PartitionSpec as P

D = 1536
QUERY_HEADS = 24
KEY_VALUE_HEADS = 8
GROUP = QUERY_HEADS // KEY_VALUE_HEADS
HEAD_WIDTH = 64
TOP = 8
EXPERTS = 32
SEQUENCE_TOKENS = 256
COMP = 32
QKV = 2560

BETA = 0.1
LOGIT_SCALE = 6.0
RATE_ONE = 0.9
RATE_TWO = 0.999
EPSILON = 1e-06
DECAY = 0.01
STEP_RATE = 0.3

BOTH = ("expert", "shard")
bf16 = jnp.bfloat16
f32 = jnp.float32


MESH = pl.DeviceIdType.MESH


class Spot:
    def __init__(self, planes, side):
        self.planes, self.side = planes, side
        self.z = lax.axis_index("expert")
        self.shard = lax.axis_index("shard")
        self.core = lax.rem(self.shard, 2)
        self.b = lax.rem(lax.div(self.shard, 2), side)
        self.a = lax.div(self.shard, 2 * side)

    def plane(self, k):
        z = lax.rem(self.z + k, self.planes)
        return z, (z, self.shard)

    def along_a(self, k):
        a = lax.rem(self.a + k, self.side)
        return a, (self.z, (a * self.side + self.b) * 2 + self.core)

    def along_b(self, k):
        b = lax.rem(self.b + k, self.side)
        return b, (self.z, (self.a * self.side + b) * 2 + self.core)

    def along(self, first, k):
        return self.along_a(k) if first else self.along_b(k)

    def mate(self):
        other = 1 - self.core
        return other, (self.z, (self.a * self.side + self.b) * 2 + other)

    def near(self, k):
        return self.z, lax.rem(self.shard + k, 2 * self.side * self.side)

    def greet(self, flat):
        targets = [self.plane(k)[1] for k in range(1, self.planes)]
        if flat:
            targets += [self.near(k) for k in range(1, 2 * self.side * self.side)]
        else:
            targets.append(self.mate()[1])
            for k in range(1, self.side):
                targets += [self.along_a(k)[1], self.along_b(k)[1]]
        barrier = pltpu.get_barrier_semaphore()
        for target in targets:
            pl.semaphore_signal(barrier, inc=1, device_id=target, device_id_type=MESH)
        pl.semaphore_wait(barrier, len(targets))


class Mail:
    def __init__(self, send, recv):
        self.send, self.recv, self.count, self.open = send, recv, 0, []

    def start(self, src, dst, target):
        copy = pltpu.make_async_remote_copy(
            src_ref=src,
            dst_ref=dst,
            send_sem=self.send.at[self.count],
            recv_sem=self.recv.at[self.count],
            device_id=target,
            device_id_type=MESH,
        )
        self.count += 1
        copy.start()
        self.open.append(copy)
        return copy

    def finish(self):
        for copy in self.open:
            copy.wait_send()


def arrive(copies):
    for copy in copies:
        copy.wait_recv()


class Tiny:
    flat = True
    scratch = ()

    def __init__(self, x, planes, side):
        self.planes, self.side, self.inputs = planes, side, [x]
        shape = (planes, 2 * side * side) + x.shape
        self.outputs = [jax.ShapeDtypeStruct(shape, x.dtype)]
        self.copies = planes + 2 * side * side - 2

    def steps(self, spot, mail, x, out):
        out[spot.z, spot.shard] = x[...]
        sent = []
        for k in range(1, self.planes):
            sent.append(mail.start(x, out.at[spot.z, spot.shard], spot.plane(k)[1]))
        yield
        arrive(sent)
        part = out.at[:, spot.shard]
        yield
        arrive([mail.start(part, part, spot.near(k)) for k in range(1, 2 * self.side**2)])


def split(array, rows, columns, row_parts, column_parts):
    r, c = rows // row_parts, columns // column_parts
    cuts = [
        (array, slice(i * r, i * r + r), slice(j * c, j * c + c))
        for j in range(column_parts)
        for i in range(row_parts)
    ]
    cuts = [cut + (n % 2 == 0,) for n, cut in enumerate(cuts)]
    return [cuts[n : n + 2] for n in range(0, len(cuts), 2)]


def pipeline(groups, stage, last):
    sent = [[[] for _ in group] for group in groups]
    for tick in range(len(groups) + last):
        for step in range(last, -1, -1):
            turn = tick - step
            if 0 <= turn < len(groups):
                for n, cut in enumerate(groups[turn]):
                    for copy in sent[turn][n]:
                        copy.wait_recv()
                    sent[turn][n] = stage(step, (turn, n), cut)
        yield


class Gather:
    flat = False
    scratch = ()

    def __init__(self, xs, groups, planes, side, exchange=False):
        self.planes, self.side, self.inputs, self.groups = planes, side, xs, groups
        self.exchange = exchange
        grid = (planes, side, side, 2)
        self.outputs = [jax.ShapeDtypeStruct(grid + x.shape[-2:], x.dtype) for x in xs]
        self.copies = sum(map(len, groups)) * (planes - 1 + 2 * (side - 1) + 1)

    def steps(self, spot, mail, *refs):
        xs, outs = refs[: len(self.inputs)], refs[len(self.inputs) :]
        z, a, b, core = spot.z, spot.a, spot.b, spot.core
        for x, out in zip(xs, outs):
            out[z, a, b, core] = x[z] if self.exchange else x[...]

        def stage(step, key, cut):
            i, rows, columns, first = cut
            x, out = xs[i], outs[i]
            if step == 0:
                place = out.at[z, a, b, core, rows, columns]
                sent = []
                for k in range(1, self.planes):
                    peer, target = spot.plane(k)
                    own = x.at[peer, rows, columns] if self.exchange else x.at[rows, columns]
                    sent.append(mail.start(own, place, target))
                return sent
            if step in (1, 2):
                if step == 1:
                    part = out.at[:, a, b, core, rows, columns]
                elif first:
                    part = out.at[:, :, b, core, rows, columns]
                else:
                    part = out.at[:, a, :, core, rows, columns]
                return [
                    mail.start(part, part, spot.along(first == (step == 1), k)[1])
                    for k in range(1, self.side)
                ]
            if step == 3:
                part = out.at[:, :, :, core, rows, columns]
                return [mail.start(part, part, spot.mate()[1])]
            return []

        return pipeline(self.groups, stage, 4)


class Reduce:
    flat = False

    def __init__(self, xs, groups, planes, side, exchange=False):
        self.planes, self.side, self.inputs, self.groups = planes, side, xs, groups
        self.exchange = exchange
        self.outputs = [
            jax.ShapeDtypeStruct((planes,) + x.shape[-2:], x.dtype)
            if exchange
            else jax.ShapeDtypeStruct(x.shape[-2:], f32)
            for x in xs
        ]
        self.scratch = []
        for i, rows, columns, _ in [cut for group in groups for cut in group]:
            block = (rows.stop - rows.start, columns.stop - columns.start)
            self.scratch += [
                pltpu.VMEM(shape + block, xs[i].dtype)
                for shape in (
                    (planes, side, side),
                    (side - 1, planes, side),
                    (planes, side),
                    (side - 1, planes),
                    (planes,),
                )
                + (() if exchange else ((planes - 1,),))
            ]
        self.copies = sum(map(len, groups)) * (planes - 1 + 2 * (side - 1) + 1)

    def steps(self, spot, mail, *refs):
        planes, side, number = self.planes, self.side, len(self.inputs)
        xs, outs, rest = refs[:number], refs[number : 2 * number], refs[2 * number :]
        each = 5 if self.exchange else 6
        order = [(t, n) for t, group in enumerate(self.groups) for n in range(len(group))]
        held = {key: rest[each * p : each * (p + 1)] for p, key in enumerate(order)}
        core, z = spot.core, spot.z
        other, mate = spot.mate()

        def stage(step, key, cut):
            i, rows, columns, first = cut
            x, out = xs[i], outs[i]
            one, hop_two, two, hop_three, three = held[key][:5]
            if step == 0:
                return [mail.start(x.at[:, :, :, other, rows, columns], one, mate)]
            sent = []
            if step == 1:

                def add(n, carry):
                    ia, ib = lax.rem(lax.div(n, side), side), lax.rem(n, side)
                    iz = lax.div(n, side * side)
                    total = x[iz, ia, ib, core, rows, columns].astype(f32)
                    one[iz, ia, ib] = (total + one[iz, ia, ib].astype(f32)).astype(one.dtype)
                    return carry

                lax.fori_loop(0, planes * side * side, add, 0)
                for k in range(1, side):
                    peer, target = spot.along(first, k)
                    part = one.at[:, peer] if first else one.at[:, :, peer]
                    sent.append(mail.start(part, hop_two.at[k - 1], target))
            elif step == 2:

                def add(n, carry):
                    iz, ir = lax.div(n, side), lax.rem(n, side)
                    total = (one[iz, spot.a, ir] if first else one[iz, ir, spot.b]).astype(f32)
                    for k in range(side - 1):
                        total += hop_two[k, iz, ir].astype(f32)
                    two[iz, ir] = total.astype(two.dtype)
                    return carry

                lax.fori_loop(0, planes * side, add, 0)
                for k in range(1, side):
                    peer, target = spot.along(not first, k)
                    sent.append(mail.start(two.at[:, peer], hop_three.at[k - 1], target))
            elif step == 3:
                mine = spot.b if first else spot.a

                def add(iz, carry):
                    total = two[iz, mine].astype(f32)
                    for k in range(side - 1):
                        total += hop_three[k, iz].astype(f32)
                    three[iz] = total.astype(three.dtype)
                    return carry

                lax.fori_loop(0, planes, add, 0)
                for k in range(1, planes):
                    peer, target = spot.plane(k)
                    if self.exchange:
                        place = out.at[z, rows, columns]
                    else:
                        place = held[key][5].at[k - 1]
                    sent.append(mail.start(three.at[peer], place, target))
                if self.exchange:
                    out[z, rows, columns] = three[z]
            elif not self.exchange:
                total = three[z].astype(f32)
                for k in range(planes - 1):
                    total += held[key][5][k].astype(f32)
                out[rows, columns] = total
            return sent

        return pipeline(self.groups, stage, 4)


def communicate(parts, ident):
    planes, side = parts[0].planes, parts[0].side
    counts = [(len(p.inputs), len(p.outputs), len(p.scratch)) for p in parts]
    n_in, n_out = (sum(c[i] for c in counts) for i in range(2))
    copies = sum(p.copies for p in parts)

    def kernel(*refs):
        ins, outs, rest = refs[:n_in], refs[n_in : n_in + n_out], refs[n_in + n_out :]
        send, recv = rest[-2:]
        spot = Spot(planes, side)
        spot.greet(parts[0].flat)
        mail = Mail(send, recv)
        running, i, o, s = [], 0, 0, 0
        for part, (ci, co, cs) in zip(parts, counts):
            running.append(
                part.steps(spot, mail, *ins[i : i + ci], *outs[o : o + co], *rest[s : s + cs])
            )
            i, o, s = i + ci, o + co, s + cs
        while running:
            running = [steps for steps in running if next(steps, True) is None]
        mail.finish()

    size = sum(x.size * x.dtype.itemsize for p in parts for x in p.inputs + p.outputs)
    return pl.pallas_call(
        kernel,
        out_shape=[x for p in parts for x in p.outputs],
        in_specs=[pl.BlockSpec(memory_space=pltpu.VMEM)] * n_in,
        out_specs=[pl.BlockSpec(memory_space=pltpu.VMEM)] * n_out,
        scratch_shapes=[s for p in parts for s in p.scratch]
        + [pltpu.SemaphoreType.DMA((copies,)), pltpu.SemaphoreType.DMA((copies,))],
        compiler_params=pltpu.CompilerParams(
            collective_id=ident, has_side_effects=True, vmem_limit_bytes=62 << 20
        ),
        cost_estimate=pl.CostEstimate(flops=0, bytes_accessed=20 * size, transcendentals=0),
        name="exchange_" + str(ident),
    )(*[x for p in parts for x in p.inputs])

def expert_weights(in_ref, cat_ref):
    units = in_ref.shape[1]
    for j in range(2):
        cat_ref[:, j * units : (j + 1) * units] = in_ref[pl.ds(j, D, stride=2), :].astype(bf16)


def expert_gate(gates, lane):
    lanes = lax.broadcasted_iota(jnp.int32, gates.shape, 1)
    return jnp.sum(jnp.where(lanes == lane, gates, 0.0), axis=1, keepdims=True)


CHUNK = 256
BLOCK = 1024


def forward_kernel(
    lane_ref, rows_ref, routes_ref, router_ref, in_ref, down_ref, out_ref, mid_ref, gates_ref, sums, cat
):
    e = pl.program_id(1)
    units = in_ref.shape[1]
    expert_weights(in_ref, cat)
    down = down_ref[0].astype(bf16)

    def chunk(i, carry):
        here = pl.ds(pl.multiple_of(i * CHUNK, CHUNK), CHUNK)
        rows = rows_ref[here, :]

        @pl.when(e == 0)
        def _():
            logits = jnp.dot(rows, router_ref[...], preferred_element_type=f32)
            lanes = lax.broadcasted_iota(jnp.int32, logits.shape, 1)
            mask = lanes == routes_ref[here, 0:1]
            for j in range(1, TOP):
                mask |= lanes == routes_ref[here, j : j + 1]
            top = jnp.max(jnp.where(mask, logits, -3e38), axis=1, keepdims=True)
            weight = jnp.where(mask, jnp.exp(jnp.where(mask, logits - top, 0.0)), 0.0)
            gates_ref[here, :] = weight / jnp.sum(weight, axis=1, keepdims=True)

        mid = jnp.dot(rows, cat[...], preferred_element_type=f32)
        mid_ref[here, :] = mid
        gate, up = mid[:, :units], mid[:, units:]
        hidden = (gate * jax.nn.sigmoid(gate) * up).astype(bf16).astype(f32)
        hidden = (hidden * expert_gate(gates_ref[here, :], lane_ref[0] + e)).astype(bf16)
        part = jnp.dot(hidden, down, preferred_element_type=f32)

        @pl.when(e == 0)
        def _():
            sums[here, :] = part

        @pl.when(e > 0)
        def _():
            sums[here, :] += part

        @pl.when(e == pl.num_programs(1) - 1)
        def _():
            out_ref[here, :] = sums[here, :].astype(bf16)

        return carry

    lax.fori_loop(0, rows_ref.shape[0] // CHUNK, chunk, 0)


def experts_forward(lane, rows, routes, router, in_rows, down):
    number, units = down.shape[:2]
    total = rows.shape[0]
    block = min(total, BLOCK)
    return pl.pallas_call(
        forward_kernel,
        grid_spec=pltpu.PrefetchScalarGridSpec(
            num_scalar_prefetch=1,
            grid=(total // block, number),
            in_specs=[
                pl.BlockSpec((block, D), lambda r, e, *_: (r, 0)),
                pl.BlockSpec((block, TOP), lambda r, e, *_: (r, 0)),
                pl.BlockSpec((D, 128), lambda r, e, *_: (0, 0)),
                pl.BlockSpec((2 * D, units), lambda r, e, *_: (e, 0)),
                pl.BlockSpec((1, units, D), lambda r, e, *_: (e, 0, 0)),
            ],
            out_specs=[
                pl.BlockSpec((block, D), lambda r, e, *_: (r, 0)),
                pl.BlockSpec((block, 2 * units), lambda r, e, *_: (r, e)),
                pl.BlockSpec((block, 128), lambda r, e, *_: (r, 0)),
            ],
            scratch_shapes=[pltpu.VMEM((block, D), f32), pltpu.VMEM((D, 2 * units), bf16)],
        ),
        out_shape=[
            jax.ShapeDtypeStruct((total, D), bf16),
            jax.ShapeDtypeStruct((total, 2 * units * number), f32),
            jax.ShapeDtypeStruct((total, 128), f32),
        ],
        compiler_params=pltpu.CompilerParams(vmem_limit_bytes=62 << 20),
        name="experts_forward",
    )(lane, rows, routes, router, in_rows, down)


def backward_kernel(
    lane_ref, grad_ref, mid_ref, gates_ref, in_ref, down_ref, out_ref, mid_grad_ref, hidden_ref, sums, cat, gate_sums
):
    e = pl.program_id(1)
    units = in_ref.shape[1]
    expert_weights(in_ref, cat)
    down = down_ref[0].astype(bf16)
    across = (((1,), (1,)), ((), ()))

    def chunk(i, carry):
        here = pl.ds(pl.multiple_of(i * CHUNK, CHUNK), CHUNK)
        weight = expert_gate(gates_ref[here, :], lane_ref[0] + e)
        mid = mid_ref[here, :]
        gate, up = mid[:, :units], mid[:, units:]
        soft = jax.nn.sigmoid(gate)
        silu = gate * soft
        hidden = (silu * up).astype(bf16).astype(f32)
        hidden_ref[here, :] = (hidden * weight).astype(bf16)
        pulled = lax.dot_general(grad_ref[here, :], down, across, preferred_element_type=f32)
        gate_grad = jnp.sum(hidden * pulled, axis=1, keepdims=True)
        hidden_grad = (pulled * weight).astype(bf16).astype(f32)
        turned = jnp.concatenate(
            [hidden_grad * up * (soft * (1.0 + gate * (1.0 - soft))), hidden_grad * silu], axis=1
        ).astype(bf16)
        mid_grad_ref[here, :] = turned
        part = lax.dot_general(turned, cat[...], across, preferred_element_type=f32)
        lanes = lax.broadcasted_iota(jnp.int32, (CHUNK, 128), 1)
        gate_part = jnp.where(lanes == lane_ref[0] + e, gate_grad, 0.0)

        @pl.when(e == 0)
        def _():
            sums[here, :] = part
            gate_sums[here, :] = gate_part

        @pl.when(e > 0)
        def _():
            sums[here, :] += part
            gate_sums[here, :] += gate_part

        @pl.when(e == pl.num_programs(1) - 1)
        def _():
            out_ref[here, :D] = sums[here, :].astype(bf16)
            out_ref[here, D:] = gate_sums[here, :].astype(bf16)

        return carry

    lax.fori_loop(0, grad_ref.shape[0] // CHUNK, chunk, 0)


def experts_backward(lane, grad, mid, gates, in_rows, down):
    number, units = down.shape[:2]
    total = grad.shape[0]
    block = min(total, BLOCK)
    return pl.pallas_call(
        backward_kernel,
        grid_spec=pltpu.PrefetchScalarGridSpec(
            num_scalar_prefetch=1,
            grid=(total // block, number),
            in_specs=[
                pl.BlockSpec((block, D), lambda r, e, *_: (r, 0)),
                pl.BlockSpec((block, 2 * units), lambda r, e, *_: (r, e)),
                pl.BlockSpec((block, 128), lambda r, e, *_: (r, 0)),
                pl.BlockSpec((2 * D, units), lambda r, e, *_: (e, 0)),
                pl.BlockSpec((1, units, D), lambda r, e, *_: (e, 0, 0)),
            ],
            out_specs=[
                pl.BlockSpec((block, D + 128), lambda r, e, *_: (r, 0)),
                pl.BlockSpec((block, 2 * units), lambda r, e, *_: (r, e)),
                pl.BlockSpec((block, units), lambda r, e, *_: (r, e)),
            ],
            scratch_shapes=[
                pltpu.VMEM((block, D), f32),
                pltpu.VMEM((D, 2 * units), bf16),
                pltpu.VMEM((block, 128), f32),
            ],
        ),
        out_shape=[
            jax.ShapeDtypeStruct((total, D + 128), bf16),
            jax.ShapeDtypeStruct((total, 2 * units * number), bf16),
            jax.ShapeDtypeStruct((total, units * number), bf16),
        ],
        compiler_params=pltpu.CompilerParams(vmem_limit_bytes=62 << 20),
        name="experts_backward",
    )(lane, grad, mid, gates, in_rows, down)


def moments_kernel(scale_ref, grad_ref, w_ref, first_ref, second_ref, new_first, new_second, norms):
    units = w_ref.shape[1]
    part = w_ref.shape[0] // 2

    @pl.when((pl.program_id(0) == 0) & (pl.program_id(1) == 0))
    def _():
        norms[...] = jnp.zeros_like(norms)

    for j in range(2):
        here = pl.ds(j, part, stride=2)
        grad = grad_ref[:, j * units : (j + 1) * units]
        weight = w_ref[here, :]
        one = RATE_ONE * first_ref[here, :] + (1.0 - RATE_ONE) * grad
        two = RATE_TWO * second_ref[here, :] + (1.0 - RATE_TWO) * grad * grad
        update = lamb_update(weight, one, two, scale_ref[0], scale_ref[1])
        new_first[here, :] = one
        new_second[here, :] = two
        norms[0] += jnp.sum((weight * weight).reshape(-1, 8, units), axis=0)
        norms[1] += jnp.sum((update * update).reshape(-1, 8, units), axis=0)


def in_moments(scales, grad, weight, first, second):
    units = weight.shape[1]
    number = grad.shape[1] // (2 * units)
    parts = 2
    row = pl.BlockSpec((2 * D // parts, units), lambda e, p, *_: (e * parts + p, 0))
    return pl.pallas_call(
        moments_kernel,
        grid_spec=pltpu.PrefetchScalarGridSpec(
            num_scalar_prefetch=1,
            grid=(number, parts),
            in_specs=[pl.BlockSpec((D // parts, 2 * units), lambda e, p, *_: (p, e)), row, row, row],
            out_specs=[row, row, pl.BlockSpec((2, 8, units), lambda e, p, *_: (0, 0, 0))],
        ),
        out_shape=[jax.ShapeDtypeStruct(weight.shape, f32)] * 2
        + [jax.ShapeDtypeStruct((2, 8, units), f32)],
        compiler_params=pltpu.CompilerParams(vmem_limit_bytes=40 << 20),
        name="in_moments",
    )(scales, grad, weight, first, second)


def norm_apply(values, gain):
    return values * lax.rsqrt(jnp.mean(values * values, axis=-1, keepdims=True) + 1e-06) * gain


def rotary_apply(values, places):
    half = values.shape[-1] // 2
    freqs = jnp.exp(-jnp.log(10000.0) * jnp.arange(half, dtype=f32) / half)
    angles = places[:, None] * freqs[None, :]
    cosine = jnp.cos(angles)[:, None, :]
    sine = jnp.sin(angles)[:, None, :]
    first_half = values[..., :half]
    second_half = values[..., half:]
    return jnp.concatenate(
        [first_half * cosine - second_half * sine, second_half * cosine + first_half * sine],
        axis=-1,
    )


def lamb_update(weight, moment_one, moment_two, scale_one, scale_two):
    return (moment_one * scale_one) / (jnp.sqrt(moment_two * scale_two) + EPSILON) + DECAY * weight


def lamb_parts(weight, moment_one, moment_two, gradient, scales):
    moment_one = RATE_ONE * moment_one + (1.0 - RATE_ONE) * gradient
    moment_two = RATE_TWO * moment_two + (1.0 - RATE_TWO) * gradient * gradient
    return (moment_one, moment_two, lamb_update(weight, moment_one, moment_two, *scales))


STEPS = 4


def row_lists(tokens, base, rows):
    inside = (tokens >= base) & (tokens < base + rows)
    count = jnp.sum(inside.astype(jnp.int32), axis=1)
    place = jnp.arange(SEQUENCE_TOKENS, dtype=jnp.int32)
    before = (place[:, None] < place[None, :]).astype(bf16)
    rank = jnp.dot(inside.astype(bf16), before, preferred_element_type=f32).astype(jnp.int32)
    packed = place[None, :] * 65536 + (tokens - base)
    hit = inside[:, :, None] & (rank[:, :, None] == place[None, None, :])
    entry = jnp.sum(jnp.where(hit, packed[:, :, None], 0), axis=1)
    empty = SEQUENCE_TOKENS * 65536
    return jnp.where(place[None, :] < count[:, None], entry, empty), count


def gather_kernel(list_ref, count_ref, table_ref, out_ref, rows_ref):
    b = pl.program_id(0)
    rows_ref[...] = jnp.zeros_like(rows_ref)

    def step(k, carry):
        for j in range(STEPS):
            entry = list_ref[b, k * STEPS + j]
            rows_ref[pl.ds(entry >> 16, 1), :] = table_ref[pl.ds(entry & 65535, 1), :]
        return carry

    lax.fori_loop(0, (count_ref[b] + STEPS - 1) // STEPS, step, 0)
    out_ref[0] = rows_ref[:SEQUENCE_TOKENS].astype(bf16)


def gather_rows(lists, counts, table):
    blocks = lists.shape[0]
    rows, columns = table.shape
    return pl.pallas_call(
        gather_kernel,
        grid_spec=pltpu.PrefetchScalarGridSpec(
            num_scalar_prefetch=2,
            grid=(blocks,),
            in_specs=[pl.BlockSpec((rows, columns), lambda b, *_: (0, 0))],
            out_specs=pl.BlockSpec((1, SEQUENCE_TOKENS, columns), lambda b, *_: (b, 0, 0)),
            scratch_shapes=[pltpu.VMEM((SEQUENCE_TOKENS + 8, columns), f32)],
        ),
        out_shape=jax.ShapeDtypeStruct((blocks, SEQUENCE_TOKENS, columns), bf16),
        compiler_params=pltpu.CompilerParams(vmem_limit_bytes=40 << 20),
        name="gather_rows",
    )(lists, counts, table)


def scatter_kernel(list_ref, count_ref, grad_ref, head_ref, out_ref, rows_ref):
    b = pl.program_id(0)

    @pl.when(b == 0)
    def _():
        out_ref[...] = head_ref[...].astype(f32)

    rows_ref[:SEQUENCE_TOKENS] = grad_ref[0].astype(f32)
    rows_ref[SEQUENCE_TOKENS:] = jnp.zeros((8, rows_ref.shape[1]), f32)

    def step(k, carry):
        for j in range(STEPS):
            entry = list_ref[b, k * STEPS + j]
            out_ref[pl.ds(entry & 65535, 1), :] += rows_ref[pl.ds(entry >> 16, 1), :]
        return carry

    lax.fori_loop(0, (count_ref[b] + STEPS - 1) // STEPS, step, 0)


def scatter_rows(lists, counts, grads, head):
    blocks = lists.shape[0]
    rows, columns = head.shape
    return pl.pallas_call(
        scatter_kernel,
        grid_spec=pltpu.PrefetchScalarGridSpec(
            num_scalar_prefetch=2,
            grid=(blocks,),
            in_specs=[
                pl.BlockSpec((1, SEQUENCE_TOKENS, columns), lambda b, *_: (b, 0, 0)),
                pl.BlockSpec((rows, columns), lambda b, *_: (0, 0)),
            ],
            out_specs=pl.BlockSpec((rows, columns), lambda b, *_: (0, 0)),
            scratch_shapes=[pltpu.VMEM((SEQUENCE_TOKENS + 8, columns), f32)],
        ),
        out_shape=jax.ShapeDtypeStruct((rows, columns), f32),
        compiler_params=pltpu.CompilerParams(vmem_limit_bytes=50 << 20),
        name="scatter_rows",
    )(lists, counts, grads, head)


def on_device(
    token_ids,
    positions,
    pair_index,
    ref_logps,
    routes,
    step_count,
    embed_table,
    embed_first,
    embed_second,
    qkv_weight,
    qkv_first,
    qkv_second,
    out_weight,
    out_first,
    out_second,
    router_weight,
    router_first,
    router_second,
    norm_gains,
    gains_first,
    gains_second,
    in_weight,
    in_first,
    in_second,
    down_weight,
    down_first,
    down_second,
):
    shard_id = lax.axis_index("shard")
    expert_id = lax.axis_index("expert")
    shards = lax.axis_size("shard")
    planes = lax.axis_size("expert")
    devices = shards * planes
    vocab_rows, columns = embed_table.shape
    vocab_base = shard_id * vocab_rows
    own_rows = vocab_rows // planes
    local_experts = in_weight.shape[0]
    hidden_units = in_weight.shape[3]
    head_cols = QUERY_HEADS * HEAD_WIDTH
    key_cols = KEY_VALUE_HEADS * HEAD_WIDTH
    rows_all = devices * COMP

    side = math.isqrt(shards // 2)
    grid = (planes, side, side, 2)
    together = devices <= 32

    def send(parts, ident):
        if together:
            return communicate(parts, ident)
        return [
            out for n, part in enumerate(parts) for out in communicate([part], ident + 20 * n)
        ]

    def gather_completion(rows, ident):
        part = Gather([rows], split(0, COMP, rows.shape[1], 2, 2), planes, side)
        return communicate([part], ident)[0].reshape(rows_all, rows.shape[1])

    def reduce_completion(rows, ident, cuts=2):
        rows = rows.reshape(grid + (COMP, rows.shape[1]))
        part = Reduce([rows], split(0, COMP, rows.shape[-1], 2, cuts), planes, side)
        return communicate([part], ident)[0]

    def gather_tiny(block, ident):
        return communicate([Tiny(block, planes, side)], ident)[0].reshape((devices,) + block.shape)

    weight_rows = qkv_weight.shape[0]
    weight_cols = head_cols + key_cols + 128
    cuts = 3 if weight_rows % 48 == 0 else 1
    weight_groups = [
        [
            (i, slice(n * (weight_rows // cuts), (n + 1) * (weight_rows // cuts)), slice(0, weight_cols), i == 0)
            for i in range(2)
        ]
        for n in range(cuts)
    ]
    embed_groups = split(0, SEQUENCE_TOKENS, columns, 8, 1)

    own_places = lax.dynamic_index_in_dim(positions, shard_id, 0, keepdims=False)
    start = own_places[0]
    own_tokens = lax.dynamic_slice_in_dim(token_ids, shard_id * SEQUENCE_TOKENS, SEQUENCE_TOKENS, 0)
    own_routes = lax.dynamic_slice_in_dim(routes, start, COMP, 0)
    sheet = jnp.concatenate(
        [
            own_tokens,
            own_routes.reshape(-1),
            own_places,
            jnp.zeros((1024 - SEQUENCE_TOKENS - COMP * TOP - COMP,), jnp.int32),
        ]
    )
    sheets = gather_tiny(sheet.reshape(8, 128), 0).reshape(devices, 1024)
    tokens_all = sheets[:, :SEQUENCE_TOKENS]
    routes_all = sheets[:, SEQUENCE_TOKENS : SEQUENCE_TOKENS + COMP * TOP].reshape(rows_all, TOP)
    places_all = sheets[:, SEQUENCE_TOKENS + COMP * TOP : SEQUENCE_TOKENS + COMP * TOP + COMP]
    spots = jnp.arange(SEQUENCE_TOKENS, dtype=jnp.int32)
    targets = jnp.sum(
        jnp.where(
            places_all[:, :, None] + 1 == spots[None, None, :], tokens_all[:, None, :], 0
        ),
        axis=2,
    ).reshape(-1)

    lists, counts = row_lists(tokens_all, vocab_base, vocab_rows)
    picked = gather_rows(lists, counts, embed_table).reshape(grid + (SEQUENCE_TOKENS, columns))
    packs = [
        jnp.concatenate(
            [
                qkv_weight[:, : head_cols + key_cols],
                router_weight,
                norm_gains.T,
                jnp.zeros((weight_rows, 128 - EXPERTS - 3), f32),
            ],
            axis=1,
        ).astype(bf16),
        jnp.concatenate(
            [
                qkv_weight[:, head_cols + key_cols :],
                out_weight,
                jnp.zeros((weight_rows, 128), f32),
            ],
            axis=1,
        ).astype(bf16),
    ]
    picked, first_pack, second_pack = send(
        [
            Reduce([picked], embed_groups, planes, side, exchange=True),
            Gather(packs, weight_groups, planes, side),
        ],
        1,
    )
    first_pack = first_pack.reshape(D, weight_cols)
    second_pack = second_pack.reshape(D, weight_cols)
    table_sent, picked = lax.optimization_barrier(
        (embed_table.astype(bf16).reshape(planes, own_rows, columns), picked)
    )
    table_own = lax.all_to_all(table_sent, "expert", split_axis=0, concat_axis=0, tiled=True)
    table_own = jnp.concatenate([table_own[p] for p in range(planes)], axis=1)
    embedded = jnp.concatenate([picked[p] for p in range(planes)], axis=1).astype(f32)
    router_block = first_pack[:, head_cols + key_cols :]
    gains_value = router_block[:, EXPERTS : EXPERTS + 3].T.astype(f32)
    out_full = second_pack[:, key_cols : key_cols + D]

    normed, norm_back_one = jax.vjp(norm_apply, embedded, gains_value[0])
    normed_b = normed.astype(bf16)
    places_f = own_places.astype(f32)
    spots_f = spots.astype(f32)

    def make_query(projected):
        return rotary_apply(projected.reshape(COMP, QUERY_HEADS, HEAD_WIDTH), places_f)

    def make_key(projected):
        return rotary_apply(
            projected.reshape(SEQUENCE_TOKENS, KEY_VALUE_HEADS, HEAD_WIDTH), spots_f
        )

    projected = jnp.dot(normed_b, first_pack, preferred_element_type=f32)
    query_f, query_back = jax.vjp(
        make_query, lax.dynamic_slice(projected, (start, 0), (COMP, head_cols))
    )
    key_f, key_back = jax.vjp(make_key, projected[:, head_cols : head_cols + key_cols])
    query = query_f.astype(bf16).reshape(COMP, KEY_VALUE_HEADS, GROUP, HEAD_WIDTH)
    key = key_f.astype(bf16)
    value = (
        jnp.dot(normed_b, second_pack[:, :key_cols], preferred_element_type=f32)
        .reshape(SEQUENCE_TOKENS, KEY_VALUE_HEADS, HEAD_WIDTH)
        .astype(bf16)
    )
    scores = jnp.einsum("qhgd,khd->hgqk", query, key, preferred_element_type=f32) * HEAD_WIDTH ** (
        -0.5
    )
    scores = jnp.where(own_places[:, None] >= spots[None, :], scores, -1000000000.0)
    expd = jnp.exp(scores - jnp.max(scores, axis=-1, keepdims=True))
    probs = expd / jnp.sum(expd, axis=-1, keepdims=True)
    probs_b = probs.astype(bf16)
    attended = (
        jnp.einsum("hgqk,khd->qhgd", probs_b, value, preferred_element_type=f32)
        .reshape(COMP, head_cols)
        .astype(bf16)
    )
    resid = lax.dynamic_slice_in_dim(embedded, start, COMP, 0) + jnp.dot(
        attended, out_full, preferred_element_type=f32
    )
    normed_two, norm_back_two = jax.vjp(norm_apply, resid, gains_value[1])
    normed_two_b = normed_two.astype(bf16)

    expert_rows = gather_completion(normed_two_b, 2)
    lane = (shard_id * local_experts).astype(jnp.int32).reshape(1)
    in_rows = in_weight.reshape(-1, hidden_units)
    produced, mid, gates = experts_forward(
        lane, expert_rows, routes_all, router_block, in_rows, down_weight
    )
    own_index = expert_id * shards + shard_id
    own_gates = lax.dynamic_slice(gates, (own_index * COMP, 0), (COMP, 128))[:, :EXPERTS]
    resid_two = resid + reduce_completion(produced, 3)

    final_rows, norm_back_three = jax.vjp(norm_apply, resid_two, gains_value[2])
    head_rows = gather_completion(final_rows.astype(bf16), 4)
    logits = jnp.einsum("rd,vd->rv", head_rows, table_own, preferred_element_type=f32) / LOGIT_SCALE
    own_base = vocab_base + expert_id * own_rows
    target_hot = targets[:, None] == own_base + jnp.arange(own_rows, dtype=jnp.int32)[None, :]
    row_top = jnp.max(logits, axis=1)
    row_total = jnp.sum(jnp.exp(logits - row_top[:, None]), axis=1)
    row_hit = jnp.sum(jnp.where(target_hot, logits, 0.0), axis=1)
    stats = jnp.stack([row_top, row_total, row_hit]).reshape(8, 3 * rows_all // 8)
    stats = gather_tiny(stats, 5).reshape(devices, 3, rows_all)
    top_all = jnp.max(stats[:, 0], axis=0)
    total_all = jnp.sum(stats[:, 1] * jnp.exp(stats[:, 0] - top_all[None]), axis=0)
    row_lse = top_all + jnp.log(total_all)
    seq_sums = jnp.sum((jnp.sum(stats[:, 2], axis=0) - row_lse).reshape(-1, COMP), axis=1)

    sequences = jnp.arange(devices, dtype=jnp.int32)[None, :]
    pair_sign = (pair_index[:, :1] == sequences).astype(f32) - (
        pair_index[:, 1:] == sequences
    ).astype(f32)
    scaled = BETA * jnp.sum(pair_sign * (seq_sums - ref_logps)[None, :], axis=1)
    loss_value = -jnp.mean(jax.nn.log_sigmoid(scaled))
    pair_grad = jax.nn.sigmoid(-scaled) * (-BETA / scaled.shape[0])
    seq_grad = jnp.sum(pair_sign * pair_grad[:, None], axis=0)
    row_grad = jnp.repeat(seq_grad, COMP)
    grad_logits = (
        row_grad[:, None] * (target_hot.astype(f32) - jnp.exp(logits - row_lse[:, None]))
    ).astype(bf16)
    grad_rows = jnp.dot(grad_logits, table_own, preferred_element_type=f32) / LOGIT_SCALE
    own_grad_rows = reduce_completion(grad_rows.astype(bf16), 6)
    grad_resid_two, grad_gain_three = norm_back_three(own_grad_rows)

    grad_all = gather_completion(grad_resid_two.astype(bf16), 7)
    head_grad = (
        jnp.einsum("rv,rd->vd", grad_logits, head_rows, preferred_element_type=f32) / LOGIT_SCALE
    ).astype(bf16)
    head_sent = jnp.stack([head_grad[:, p * columns : (p + 1) * columns] for p in range(planes)])
    head_sent, grad_all = lax.optimization_barrier((head_sent, grad_all))
    head_grad = lax.all_to_all(
        head_sent, "expert", split_axis=0, concat_axis=0, tiled=True
    ).reshape(vocab_rows, columns)
    back, mid_grad, gated_hidden = experts_backward(
        lane, grad_all, mid, gates, in_rows, down_weight
    )
    back = reduce_completion(back, 8, 1)
    grad_gates = back[:, D : D + EXPERTS]
    grad_router_logits = own_gates * (
        grad_gates - jnp.sum(own_gates * grad_gates, axis=1, keepdims=True)
    )
    grad_router_logits = jnp.pad(grad_router_logits, ((0, 0), (0, 128 - EXPERTS)))
    grad_normed_two = back[:, :D] + jnp.einsum(
        "se,de->sd", grad_router_logits, router_block.astype(f32)
    )
    grad_resid, grad_gain_two = norm_back_two(grad_normed_two)
    grad_resid = grad_resid + grad_resid_two
    grad_branch = grad_resid.astype(bf16)
    grad_attended = (
        jnp.einsum("sd,kd->sk", grad_branch, out_full, preferred_element_type=f32)
        .astype(bf16)
        .reshape(COMP, KEY_VALUE_HEADS, GROUP, HEAD_WIDTH)
    )

    grad_probs = jnp.einsum("qhgd,khd->hgqk", grad_attended, value, preferred_element_type=f32)
    grad_probs = grad_probs.astype(bf16).astype(f32)
    inner = jnp.sum(grad_probs * probs, axis=-1, keepdims=True)
    grad_scores = (probs * (grad_probs - inner)).astype(bf16)
    grad_value = jnp.einsum("hgqk,qhgd->khd", probs_b, grad_attended, preferred_element_type=f32)
    grad_query = jnp.einsum(
        "hgqk,khd->qhgd", grad_scores, key, preferred_element_type=f32
    ) * HEAD_WIDTH ** (-0.5)
    grad_key = jnp.einsum(
        "hgqk,qhgd->khd", grad_scores, query, preferred_element_type=f32
    ) * HEAD_WIDTH ** (-0.5)

    def spread(rows):
        return lax.dynamic_update_slice_in_dim(
            jnp.zeros((SEQUENCE_TOKENS, rows.shape[1]), rows.dtype), rows, start, 0
        )

    grad_query_rows = query_back(grad_query.reshape(COMP, QUERY_HEADS, HEAD_WIDTH))[0].astype(bf16)
    grad_first = jnp.concatenate(
        [
            spread(grad_query_rows),
            key_back(grad_key)[0].astype(bf16),
            jnp.zeros((SEQUENCE_TOKENS, 128), bf16),
        ],
        axis=1,
    )
    grad_value = grad_value.reshape(SEQUENCE_TOKENS, key_cols).astype(bf16)
    across = "sk,dk->sd"
    grad_normed = jnp.einsum(across, grad_first, first_pack, preferred_element_type=f32)
    grad_normed += jnp.einsum(
        across, grad_value, second_pack[:, :key_cols], preferred_element_type=f32
    )
    grad_embedded, grad_gain_one = norm_back_one(grad_normed)
    grad_embedded = (grad_embedded + spread(grad_resid)).astype(bf16)
    grad_embedded = jnp.stack(
        [grad_embedded[:, p * columns : (p + 1) * columns] for p in range(planes)]
    )

    gains_grad = jnp.pad(
        jnp.stack([grad_gain_one, grad_gain_two, grad_gain_three]), ((0, 13), (0, 0))
    ).astype(bf16)
    gains_lanes = (
        jnp.arange(16)[:, None] + EXPERTS == jnp.arange(128)[None, :]
    ).astype(bf16)
    wide = head_cols + key_cols
    first_left = jnp.concatenate([normed_b, normed_two_b, gains_grad], axis=0)
    first_right = jnp.concatenate(
        [
            grad_first,
            jnp.pad(
                jnp.concatenate([grad_router_logits.astype(bf16), gains_lanes], axis=0),
                ((0, 0), (wide, 0)),
            ),
        ],
        axis=0,
    )
    second_left = jnp.concatenate([normed_b, attended], axis=0)
    second_right = jnp.concatenate(
        [
            jnp.pad(grad_value, ((0, 0), (0, D + 128))),
            jnp.pad(grad_branch, ((0, 0), (key_cols, 128))),
        ],
        axis=0,
    )
    grad_packs = [
        jnp.einsum("sd,sk->dk", left, right, preferred_element_type=f32)
        .astype(bf16)
        .reshape(grid + (weight_rows, weight_cols))
        for left, right in ((first_left, first_right), (second_left, second_right))
    ]
    sent, first_grad, second_grad = send(
        [
            Gather([grad_embedded], embed_groups, planes, side, exchange=True),
            Reduce(grad_packs, weight_groups, planes, side),
        ],
        9,
    )
    table_grad = scatter_rows(
        lists, counts, sent.reshape(devices, SEQUENCE_TOKENS, columns), head_grad
    )

    step_value = step_count.astype(f32)
    scales = (1.0 / (1.0 - RATE_ONE**step_value), 1.0 / (1.0 - RATE_TWO**step_value))
    grad_in = jnp.einsum("td,tk->dk", expert_rows, mid_grad, preferred_element_type=f32)
    grad_down = jnp.einsum(
        "tk,td->kd", gated_hidden, grad_all, preferred_element_type=f32
    ).reshape(down_weight.shape)
    in_first_new, in_second_new, in_norms = in_moments(
        jnp.stack(scales),
        grad_in,
        in_rows,
        in_first.reshape(in_rows.shape),
        in_second.reshape(in_rows.shape),
    )
    weights = (embed_table, qkv_weight, out_weight, router_weight, norm_gains, down_weight)
    firsts = (embed_first, qkv_first, out_first, router_first, gains_first, down_first)
    seconds = (embed_second, qkv_second, out_second, router_second, gains_second, down_second)
    gradients = (
        table_grad,
        jnp.concatenate([first_grad[:, :wide], second_grad[:, :key_cols]], axis=1),
        second_grad[:, key_cols : key_cols + D],
        first_grad[:, wide : wide + EXPERTS],
        first_grad[:, wide + EXPERTS : wide + EXPERTS + 3].T,
        grad_down,
    )
    moved = [
        lamb_parts(weight, moment_one, moment_two, gradient, scales)
        for weight, moment_one, moment_two, gradient in zip(weights, firsts, seconds, gradients)
    ]
    partial_norms = [
        jnp.stack([jnp.sum(weight * weight), jnp.sum(parts[2] * parts[2])])
        for weight, parts in zip(weights, moved)
    ]
    partial_norms.insert(5, jnp.sum(in_norms, axis=(1, 2)))
    partial_norms = jnp.pad(jnp.stack(partial_norms), ((0, 1), (0, 126)))
    norm_values = jnp.sqrt(jnp.sum(gather_tiny(partial_norms, 10), axis=0))[:7, :2]
    trust_ratio = norm_values[:, 0] / norm_values[:, 1]
    moved.insert(
        5, (in_first_new, in_second_new, lamb_update(in_rows, in_first_new, in_second_new, *scales))
    )
    weights = weights[:5] + (in_rows,) + weights[5:]
    results = [loss_value]
    for place, (weight, parts) in enumerate(zip(weights, moved)):
        made = [weight - STEP_RATE * trust_ratio[place] * parts[2], parts[0], parts[1]]
        if place == 5:
            made = [x.reshape(in_weight.shape) for x in made]
        results.extend(made)
    results.append(jnp.stack([norm_values[:, 0], norm_values[:, 1], trust_ratio], axis=1))
    return tuple(results)


def solution(mesh):
    rows = P(BOTH, None)
    vocab = P("shard", "expert")
    gains = P(None, BOTH)
    inner = P("shard", None, None, "expert")
    outer = P("shard", "expert", None)
    state = (vocab,) * 3 + (rows,) * 9 + (gains,) * 3 + (inner,) * 3 + (outer,) * 3
    return jax.shard_map(
        on_device,
        mesh=mesh,
        in_specs=(P("expert"), P("expert", None), P(), P(), rows, P()) + state,
        out_specs=(P(),) + state + (P(),),
        check_vma=False,
    )
```

```python
import functools
import math

import jax
import jax.numpy as jnp
from jax import lax
from jax.experimental import pallas as pl
from jax.experimental.pallas import tpu as pltpu
from jax.sharding import PartitionSpec as P

D = 1536
QUERY_HEADS = 24
KEY_VALUE_HEADS = 8
GROUP = QUERY_HEADS // KEY_VALUE_HEADS
HEAD_WIDTH = 64
TOP = 8
EXPERTS = 32
SEQUENCE_TOKENS = 256
COMP = 32
QKV = 2560

BETA = 0.1
LOGIT_SCALE = 6.0
RATE_ONE = 0.9
RATE_TWO = 0.999
EPSILON = 1e-06
DECAY = 0.01
STEP_RATE = 0.3

BOTH = ("expert", "shard")
bf16 = jnp.bfloat16
f32 = jnp.float32


MESH = pl.DeviceIdType.MESH


class Spot:
    def __init__(self, planes, side):
        self.planes, self.side = planes, side
        self.z = lax.axis_index("expert")
        self.shard = lax.axis_index("shard")
        self.core = lax.rem(self.shard, 2)
        self.b = lax.rem(lax.div(self.shard, 2), side)
        self.a = lax.div(self.shard, 2 * side)

    def plane(self, k):
        z = lax.rem(self.z + k, self.planes)
        return z, (z, self.shard)

    def along_a(self, k):
        a = lax.rem(self.a + k, self.side)
        return a, (self.z, (a * self.side + self.b) * 2 + self.core)

    def along_b(self, k):
        b = lax.rem(self.b + k, self.side)
        return b, (self.z, (self.a * self.side + b) * 2 + self.core)

    def along(self, first, k):
        return self.along_a(k) if first else self.along_b(k)

    def mate(self):
        other = 1 - self.core
        return other, (self.z, (self.a * self.side + self.b) * 2 + other)

    def near(self, k):
        return self.z, lax.rem(self.shard + k, 2 * self.side * self.side)

    def greet(self, flat):
        targets = [self.plane(k)[1] for k in range(1, self.planes)]
        if flat:
            targets += [self.near(k) for k in range(1, 2 * self.side * self.side)]
        else:
            targets.append(self.mate()[1])
            for k in range(1, self.side):
                targets += [self.along_a(k)[1], self.along_b(k)[1]]
        barrier = pltpu.get_barrier_semaphore()
        for target in targets:
            pl.semaphore_signal(barrier, inc=1, device_id=target, device_id_type=MESH)
        pl.semaphore_wait(barrier, len(targets))


class Mail:
    def __init__(self, send, recv):
        self.send, self.recv, self.count, self.open = send, recv, 0, []

    def start(self, src, dst, target):
        copy = pltpu.make_async_remote_copy(
            src_ref=src,
            dst_ref=dst,
            send_sem=self.send.at[self.count],
            recv_sem=self.recv.at[self.count],
            device_id=target,
            device_id_type=MESH,
        )
        self.count += 1
        copy.start()
        self.open.append(copy)
        return copy

    def finish(self):
        for copy in self.open:
            copy.wait_send()


def arrive(copies):
    for copy in copies:
        copy.wait_recv()


class Tiny:
    flat = True
    scratch = ()

    def __init__(self, x, planes, side):
        self.planes, self.side, self.inputs = planes, side, [x]
        shape = (planes, 2 * side * side) + x.shape
        self.outputs = [jax.ShapeDtypeStruct(shape, x.dtype)]
        self.copies = planes + 2 * side * side - 2

    def steps(self, spot, mail, x, out):
        out[spot.z, spot.shard] = x[...]
        sent = []
        for k in range(1, self.planes):
            sent.append(mail.start(x, out.at[spot.z, spot.shard], spot.plane(k)[1]))
        yield
        arrive(sent)
        part = out.at[:, spot.shard]
        yield
        arrive([mail.start(part, part, spot.near(k)) for k in range(1, 2 * self.side**2)])


def split(array, rows, columns, row_parts, column_parts):
    r, c = rows // row_parts, columns // column_parts
    cuts = [
        (array, slice(i * r, i * r + r), slice(j * c, j * c + c))
        for j in range(column_parts)
        for i in range(row_parts)
    ]
    cuts = [cut + (n % 2 == 0,) for n, cut in enumerate(cuts)]
    return [cuts[n : n + 2] for n in range(0, len(cuts), 2)]


def pipeline(groups, stage, last):
    sent = [[[] for _ in group] for group in groups]
    for tick in range(len(groups) + last):
        for step in range(last, -1, -1):
            turn = tick - step
            if 0 <= turn < len(groups):
                for n, cut in enumerate(groups[turn]):
                    for copy in sent[turn][n]:
                        copy.wait_recv()
                    sent[turn][n] = stage(step, (turn, n), cut)
        yield


class Gather:
    flat = False
    scratch = ()

    def __init__(self, xs, groups, planes, side, exchange=False):
        self.planes, self.side, self.inputs, self.groups = planes, side, xs, groups
        self.exchange = exchange
        grid = (planes, side, side, 2)
        self.outputs = [jax.ShapeDtypeStruct(grid + x.shape[-2:], x.dtype) for x in xs]
        self.copies = sum(map(len, groups)) * (planes - 1 + 2 * (side - 1) + 1)

    def steps(self, spot, mail, *refs):
        xs, outs = refs[: len(self.inputs)], refs[len(self.inputs) :]
        z, a, b, core = spot.z, spot.a, spot.b, spot.core
        for x, out in zip(xs, outs):
            out[z, a, b, core] = x[z] if self.exchange else x[...]

        def stage(step, key, cut):
            i, rows, columns, first = cut
            x, out = xs[i], outs[i]
            if step == 0:
                place = out.at[z, a, b, core, rows, columns]
                sent = []
                for k in range(1, self.planes):
                    peer, target = spot.plane(k)
                    own = x.at[peer, rows, columns] if self.exchange else x.at[rows, columns]
                    sent.append(mail.start(own, place, target))
                return sent
            if step in (1, 2):
                if step == 1:
                    part = out.at[:, a, b, core, rows, columns]
                elif first:
                    part = out.at[:, :, b, core, rows, columns]
                else:
                    part = out.at[:, a, :, core, rows, columns]
                return [
                    mail.start(part, part, spot.along(first == (step == 1), k)[1])
                    for k in range(1, self.side)
                ]
            if step == 3:
                part = out.at[:, :, :, core, rows, columns]
                return [mail.start(part, part, spot.mate()[1])]
            return []

        return pipeline(self.groups, stage, 4)


class Reduce:
    flat = False

    def __init__(self, xs, groups, planes, side, exchange=False):
        self.planes, self.side, self.inputs, self.groups = planes, side, xs, groups
        self.exchange = exchange
        self.outputs = [
            jax.ShapeDtypeStruct((planes,) + x.shape[-2:], x.dtype)
            if exchange
            else jax.ShapeDtypeStruct(x.shape[-2:], f32)
            for x in xs
        ]
        self.scratch = []
        for i, rows, columns, _ in [cut for group in groups for cut in group]:
            block = (rows.stop - rows.start, columns.stop - columns.start)
            self.scratch += [
                pltpu.VMEM(shape + block, xs[i].dtype)
                for shape in (
                    (planes, side, side),
                    (side - 1, planes, side),
                    (planes, side),
                    (side - 1, planes),
                    (planes,),
                )
                + (() if exchange else ((planes - 1,),))
            ]
        self.copies = sum(map(len, groups)) * (planes - 1 + 2 * (side - 1) + 1)

    def steps(self, spot, mail, *refs):
        planes, side, number = self.planes, self.side, len(self.inputs)
        xs, outs, rest = refs[:number], refs[number : 2 * number], refs[2 * number :]
        each = 5 if self.exchange else 6
        order = [(t, n) for t, group in enumerate(self.groups) for n in range(len(group))]
        held = {key: rest[each * p : each * (p + 1)] for p, key in enumerate(order)}
        core, z = spot.core, spot.z
        other, mate = spot.mate()

        def stage(step, key, cut):
            i, rows, columns, first = cut
            x, out = xs[i], outs[i]
            one, hop_two, two, hop_three, three = held[key][:5]
            if step == 0:
                return [mail.start(x.at[:, :, :, other, rows, columns], one, mate)]
            sent = []
            if step == 1:

                def add(n, carry):
                    ia, ib = lax.rem(lax.div(n, side), side), lax.rem(n, side)
                    iz = lax.div(n, side * side)
                    total = x[iz, ia, ib, core, rows, columns].astype(f32)
                    one[iz, ia, ib] = (total + one[iz, ia, ib].astype(f32)).astype(one.dtype)
                    return carry

                lax.fori_loop(0, planes * side * side, add, 0)
                for k in range(1, side):
                    peer, target = spot.along(first, k)
                    part = one.at[:, peer] if first else one.at[:, :, peer]
                    sent.append(mail.start(part, hop_two.at[k - 1], target))
            elif step == 2:

                def add(n, carry):
                    iz, ir = lax.div(n, side), lax.rem(n, side)
                    total = (one[iz, spot.a, ir] if first else one[iz, ir, spot.b]).astype(f32)
                    for k in range(side - 1):
                        total += hop_two[k, iz, ir].astype(f32)
                    two[iz, ir] = total.astype(two.dtype)
                    return carry

                lax.fori_loop(0, planes * side, add, 0)
                for k in range(1, side):
                    peer, target = spot.along(not first, k)
                    sent.append(mail.start(two.at[:, peer], hop_three.at[k - 1], target))
            elif step == 3:
                mine = spot.b if first else spot.a

                def add(iz, carry):
                    total = two[iz, mine].astype(f32)
                    for k in range(side - 1):
                        total += hop_three[k, iz].astype(f32)
                    three[iz] = total.astype(three.dtype)
                    return carry

                lax.fori_loop(0, planes, add, 0)
                for k in range(1, planes):
                    peer, target = spot.plane(k)
                    if self.exchange:
                        place = out.at[z, rows, columns]
                    else:
                        place = held[key][5].at[k - 1]
                    sent.append(mail.start(three.at[peer], place, target))
                if self.exchange:
                    out[z, rows, columns] = three[z]
            elif not self.exchange:
                total = three[z].astype(f32)
                for k in range(planes - 1):
                    total += held[key][5][k].astype(f32)
                out[rows, columns] = total
            return sent

        return pipeline(self.groups, stage, 4)


class Swap:
    flat = False
    scratch = (pltpu.SemaphoreType.DMA(()),)
    spaces = (pl.ANY,)

    def __init__(self, x, start, size, planes, side, rounds, back=False):
        self.planes, self.side, self.inputs = planes, side, [x]
        self.begin, self.size, self.rounds, self.back = start, size, rounds, back
        self.columns = x.shape[1] // planes if back else x.shape[1]
        shape = (planes, size, self.columns) if back else (size, planes * self.columns)
        self.outputs = [jax.ShapeDtypeStruct(shape, x.dtype)]
        self.copies = planes - 1

    def steps(self, spot, mail, x, out, own_sem):
        def block(z):
            return pl.ds(pl.multiple_of(z * self.columns, 128), self.columns)

        def source(z):
            if self.back:
                return x.at[pl.ds(self.begin, self.size), block(z)]
            first = z * (x.shape[0] // self.planes) + self.begin
            return x.at[pl.ds(pl.multiple_of(first, 16), self.size), :]

        for _ in range(self.rounds):
            yield
        place = out.at[spot.z] if self.back else out.at[:, block(spot.z)]
        sent = []
        for k in range(1, self.planes):
            peer, target = spot.plane(k)
            sent.append(mail.start(source(peer), place, target))
        own = pltpu.make_async_copy(source(spot.z), place, own_sem)
        own.start()
        for _ in range(20):
            yield
        own.wait()
        for copy in sent:
            copy.wait_recv()


def communicate(parts, ident):
    planes, side = parts[0].planes, parts[0].side
    counts = [(len(p.inputs), len(p.outputs), len(p.scratch)) for p in parts]
    n_in, n_out = (sum(c[i] for c in counts) for i in range(2))
    copies = sum(p.copies for p in parts)

    def kernel(*refs):
        ins, outs, rest = refs[:n_in], refs[n_in : n_in + n_out], refs[n_in + n_out :]
        send, recv = rest[-2:]
        spot = Spot(planes, side)
        spot.greet(parts[0].flat)
        mail = Mail(send, recv)
        running, i, o, s = [], 0, 0, 0
        for part, (ci, co, cs) in zip(parts, counts):
            running.append(
                part.steps(spot, mail, *ins[i : i + ci], *outs[o : o + co], *rest[s : s + cs])
            )
            i, o, s = i + ci, o + co, s + cs
        while running:
            running = [steps for steps in running if next(steps, True) is None]
        mail.finish()

    size = sum(x.size * x.dtype.itemsize for p in parts for x in p.inputs + p.outputs)
    out = pl.pallas_call(
        kernel,
        out_shape=[x for p in parts for x in p.outputs],
        in_specs=[
            pl.BlockSpec(memory_space=space)
            for p in parts
            for space in getattr(p, "spaces", (pltpu.VMEM,) * len(p.inputs))
        ],
        out_specs=[pl.BlockSpec(memory_space=pltpu.VMEM)] * n_out,
        scratch_shapes=[s for p in parts for s in p.scratch]
        + [pltpu.SemaphoreType.DMA((copies,)), pltpu.SemaphoreType.DMA((copies,))],
        compiler_params=pltpu.CompilerParams(
            collective_id=ident, has_side_effects=True, vmem_limit_bytes=62 << 20
        ),
        cost_estimate=pl.CostEstimate(flops=0, bytes_accessed=20 * size, transcendentals=0),
        name="exchange_" + str(ident),
    )(*[x for p in parts for x in p.inputs])
    return list(out)

def expert_gate(gates, lane):
    lanes = lax.broadcasted_iota(jnp.int32, gates.shape, 1)
    return jnp.sum(jnp.where(lanes == lane, gates, 0.0), axis=1, keepdims=True)


CHUNK = 512
BLOCK = 1024
ACROSS = (((1,), (1,)), ((), ()))


def forward_kernel(
    lane_ref, rows_ref, routes_ref, router_ref, in_ref, down_ref, out_ref, mid_ref, gates_ref, cat_ref, down_out, hidden_ref
):
    e, number = pl.program_id(1), pl.num_programs(1)
    units = in_ref.shape[1]
    for j in range(2):
        cat_ref[:, j * units : (j + 1) * units] = in_ref[pl.ds(j, D, stride=2), :].astype(bf16)
    down_out[pl.ds(pl.multiple_of(e * units, units), units), :] = down_ref[0].astype(bf16)

    def chunk(i, carry):
        here = pl.ds(pl.multiple_of(i * CHUNK, CHUNK), CHUNK)
        rows = rows_ref[here, :]

        @pl.when(e == 0)
        def _():
            logits = jnp.dot(rows, router_ref[...], preferred_element_type=f32)
            lanes = lax.broadcasted_iota(jnp.int32, logits.shape, 1)
            mask = lanes == routes_ref[here, 0:1]
            for j in range(1, TOP):
                mask |= lanes == routes_ref[here, j : j + 1]
            top = jnp.max(jnp.where(mask, logits, -3e38), axis=1, keepdims=True)
            weight = jnp.where(mask, jnp.exp(jnp.where(mask, logits - top, 0.0)), 0.0)
            gates_ref[here, :] = weight / jnp.sum(weight, axis=1, keepdims=True)

        mid = jnp.dot(rows, cat_ref[...], preferred_element_type=f32)
        mid_ref[here, :] = mid
        gate, up = mid[:, :units], mid[:, units:]
        hidden = (gate * jax.nn.sigmoid(gate) * up).astype(bf16).astype(f32)
        hidden = (hidden * expert_gate(gates_ref[here, :], lane_ref[0] + e)).astype(bf16)
        hidden_ref[here, pl.ds(pl.multiple_of(e * units, units), units)] = hidden

        @pl.when(e == number - 1)
        def _():
            out_ref[here, :] = jnp.dot(
                hidden_ref[here, :], down_out[...], preferred_element_type=f32
            ).astype(bf16)

        return carry

    lax.fori_loop(0, rows_ref.shape[0] // CHUNK, chunk, 0)


def experts_forward(lane, rows, routes, router, in_rows, down):
    number, units = down.shape[:2]
    total = rows.shape[0]
    block = min(total, BLOCK)
    row = lambda r, e, *_: (r, 0)
    still = lambda r, e, *_: (0, 0)
    return pl.pallas_call(
        forward_kernel,
        grid_spec=pltpu.PrefetchScalarGridSpec(
            num_scalar_prefetch=1,
            grid=(total // block, number),
            in_specs=[
                pl.BlockSpec((block, D), row),
                pl.BlockSpec((block, TOP), row),
                pl.BlockSpec((D, 128), still),
                pl.BlockSpec((2 * D, units), lambda r, e, *_: (e, 0)),
                pl.BlockSpec((1, units, D), lambda r, e, *_: (e, 0, 0)),
            ],
            out_specs=[
                pl.BlockSpec((block, D), row),
                pl.BlockSpec((block, 2 * units), lambda r, e, *_: (r, e)),
                pl.BlockSpec((block, 128), row),
                pl.BlockSpec((D, 2 * units), lambda r, e, *_: (0, e)),
                pl.BlockSpec((number * units, D), still),
                pl.BlockSpec((block, number * units), row),
            ],
        ),
        out_shape=[
            jax.ShapeDtypeStruct((total, D), bf16),
            jax.ShapeDtypeStruct((total, 2 * units * number), f32),
            jax.ShapeDtypeStruct((total, 128), f32),
            jax.ShapeDtypeStruct((D, 2 * units * number), bf16),
            jax.ShapeDtypeStruct((number * units, D), bf16),
            jax.ShapeDtypeStruct((total, number * units), bf16),
        ],
        compiler_params=pltpu.CompilerParams(vmem_limit_bytes=60 << 20),
        name="experts_forward",
    )(lane, rows, routes, router, in_rows, down)


def backward_kernel(
    lane_ref, grad_ref, mid_ref, gates_ref, cat_ref, down_ref, out_ref, mid_grad_ref, pulled_ref
):
    number = lane_ref.shape[0]
    units = pulled_ref.shape[1] // number

    def chunk(i, carry):
        here = pl.ds(pl.multiple_of(i * CHUNK, CHUNK), CHUNK)
        pulled_ref[...] = lax.dot_general(
            grad_ref[here, :], down_ref[...], ACROSS, preferred_element_type=f32
        )
        lanes = lax.broadcasted_iota(jnp.int32, (CHUNK, 128), 1)
        gate_part = jnp.zeros((CHUNK, 128), f32)
        for e in range(number):
            lane = lane_ref[e]
            weight = expert_gate(gates_ref[here, :], lane)
            gate = mid_ref[here, 2 * e * units : (2 * e + 1) * units]
            up = mid_ref[here, (2 * e + 1) * units : (2 * e + 2) * units]
            pulled = pulled_ref[:, e * units : (e + 1) * units]
            soft = jax.nn.sigmoid(gate)
            silu = gate * soft
            hidden = (silu * up).astype(bf16).astype(f32)
            gate_grad = jnp.sum(hidden * pulled, axis=1, keepdims=True)
            gate_part = jnp.where(lanes == lane, gate_grad, gate_part)
            hidden_grad = (pulled * weight).astype(bf16).astype(f32)
            turned = hidden_grad * up * (soft * (1.0 + gate * (1.0 - soft)))
            mid_grad_ref[here, 2 * e * units : (2 * e + 1) * units] = turned.astype(bf16)
            mid_grad_ref[here, (2 * e + 1) * units : (2 * e + 2) * units] = (
                hidden_grad * silu
            ).astype(bf16)
        out_ref[here, D:] = gate_part.astype(bf16)
        out_ref[here, :D] = lax.dot_general(
            mid_grad_ref[here, :], cat_ref[...], ACROSS, preferred_element_type=f32
        ).astype(bf16)
        return carry

    lax.fori_loop(0, grad_ref.shape[0] // CHUNK, chunk, 0)


def experts_backward(lanes, grad, mid, gates, cat, down):
    number = lanes.shape[0]
    total = grad.shape[0]
    block = min(total, BLOCK)
    row = lambda r, *_: (r, 0)
    still = lambda r, *_: (0, 0)
    return pl.pallas_call(
        backward_kernel,
        grid_spec=pltpu.PrefetchScalarGridSpec(
            num_scalar_prefetch=1,
            grid=(total // block,),
            in_specs=[
                pl.BlockSpec((block, D), row),
                pl.BlockSpec((block, mid.shape[1]), row),
                pl.BlockSpec((block, 128), row),
                pl.BlockSpec(cat.shape, still),
                pl.BlockSpec(down.shape, still),
            ],
            out_specs=[
                pl.BlockSpec((block, D + 128), row),
                pl.BlockSpec((block, mid.shape[1]), row),
            ],
            scratch_shapes=[pltpu.VMEM((CHUNK, down.shape[0]), f32)],
        ),
        out_shape=[
            jax.ShapeDtypeStruct((total, D + 128), bf16),
            jax.ShapeDtypeStruct(mid.shape, bf16),
        ],
        compiler_params=pltpu.CompilerParams(vmem_limit_bytes=60 << 20),
        name="experts_backward",
    )(lanes, grad, mid, gates, cat, down)


def moments_kernel(scale_ref, grad_ref, w_ref, first_ref, second_ref, new_first, new_second, norms):
    units = w_ref.shape[1]
    part = w_ref.shape[0] // 2

    @pl.when((pl.program_id(0) == 0) & (pl.program_id(1) == 0))
    def _():
        norms[...] = jnp.zeros_like(norms)

    for j in range(2):
        here = pl.ds(j, part, stride=2)
        grad = grad_ref[:, j * units : (j + 1) * units]
        weight = w_ref[here, :]
        one = RATE_ONE * first_ref[here, :] + (1.0 - RATE_ONE) * grad
        two = RATE_TWO * second_ref[here, :] + (1.0 - RATE_TWO) * grad * grad
        update = lamb_update(weight, one, two, scale_ref[0], scale_ref[1])
        new_first[here, :] = one
        new_second[here, :] = two
        norms[0] += jnp.sum((weight * weight).reshape(-1, 8, units), axis=0)
        norms[1] += jnp.sum((update * update).reshape(-1, 8, units), axis=0)


def in_moments(scales, grad, weight, first, second):
    units = weight.shape[1]
    number = grad.shape[1] // (2 * units)
    parts = 2
    row = pl.BlockSpec((2 * D // parts, units), lambda e, p, *_: (e * parts + p, 0))
    return pl.pallas_call(
        moments_kernel,
        grid_spec=pltpu.PrefetchScalarGridSpec(
            num_scalar_prefetch=1,
            grid=(number, parts),
            in_specs=[pl.BlockSpec((D // parts, 2 * units), lambda e, p, *_: (p, e)), row, row, row],
            out_specs=[row, row, pl.BlockSpec((2, 8, units), lambda e, p, *_: (0, 0, 0))],
        ),
        out_shape=[jax.ShapeDtypeStruct(weight.shape, f32)] * 2
        + [jax.ShapeDtypeStruct((2, 8, units), f32)],
        compiler_params=pltpu.CompilerParams(vmem_limit_bytes=40 << 20),
        name="in_moments",
    )(scales, grad, weight, first, second)


def norm_apply(values, gain):
    return values * lax.rsqrt(jnp.mean(values * values, axis=-1, keepdims=True) + 1e-06) * gain


def rotary_apply(values, places):
    half = values.shape[-1] // 2
    freqs = jnp.exp(-jnp.log(10000.0) * jnp.arange(half, dtype=f32) / half)
    angles = places[:, None] * freqs[None, :]
    cosine = jnp.cos(angles)[:, None, :]
    sine = jnp.sin(angles)[:, None, :]
    first_half = values[..., :half]
    second_half = values[..., half:]
    return jnp.concatenate(
        [first_half * cosine - second_half * sine, second_half * cosine + first_half * sine],
        axis=-1,
    )


def lamb_update(weight, moment_one, moment_two, scale_one, scale_two):
    return (moment_one * scale_one) / (jnp.sqrt(moment_two * scale_two) + EPSILON) + DECAY * weight


def lamb_parts(weight, moment_one, moment_two, gradient, scales):
    moment_one = RATE_ONE * moment_one + (1.0 - RATE_ONE) * gradient
    moment_two = RATE_TWO * moment_two + (1.0 - RATE_TWO) * gradient * gradient
    return (moment_one, moment_two, lamb_update(weight, moment_one, moment_two, *scales))


STEPS = 4


def row_lists(tokens, base, rows):
    inside = (tokens >= base) & (tokens < base + rows)
    count = jnp.sum(inside.astype(jnp.int32), axis=1)
    place = jnp.arange(SEQUENCE_TOKENS, dtype=jnp.int32)
    before = (place[:, None] < place[None, :]).astype(bf16)
    rank = jnp.dot(inside.astype(bf16), before, preferred_element_type=f32).astype(jnp.int32)
    packed = place[None, :] * 65536 + (tokens - base)
    hit = inside[:, :, None] & (rank[:, :, None] == place[None, None, :])
    entry = jnp.sum(jnp.where(hit, packed[:, :, None], 0), axis=1)
    empty = SEQUENCE_TOKENS * 65536
    return jnp.where(place[None, :] < count[:, None], entry, empty), count


def gather_kernel(list_ref, count_ref, table_ref, out_ref, rows_ref):
    b = pl.program_id(0)
    rows_ref[...] = jnp.zeros_like(rows_ref)

    def step(k, carry):
        for j in range(STEPS):
            entry = list_ref[b, k * STEPS + j]
            rows_ref[pl.ds(entry >> 16, 1), :] = table_ref[pl.ds(entry & 65535, 1), :]
        return carry

    lax.fori_loop(0, (count_ref[b] + STEPS - 1) // STEPS, step, 0)
    out_ref[0] = rows_ref[:SEQUENCE_TOKENS].astype(bf16)


def gather_rows(lists, counts, table):
    blocks = lists.shape[0]
    rows, columns = table.shape
    return pl.pallas_call(
        gather_kernel,
        grid_spec=pltpu.PrefetchScalarGridSpec(
            num_scalar_prefetch=2,
            grid=(blocks,),
            in_specs=[pl.BlockSpec((rows, columns), lambda b, *_: (0, 0))],
            out_specs=pl.BlockSpec((1, SEQUENCE_TOKENS, columns), lambda b, *_: (b, 0, 0)),
            scratch_shapes=[pltpu.VMEM((SEQUENCE_TOKENS + 8, columns), f32)],
        ),
        out_shape=jax.ShapeDtypeStruct((blocks, SEQUENCE_TOKENS, columns), bf16),
        compiler_params=pltpu.CompilerParams(vmem_limit_bytes=40 << 20),
        name="gather_rows",
    )(lists, counts, table)


def scatter_kernel(list_ref, count_ref, grad_ref, head_ref, out_ref, rows_ref):
    b = pl.program_id(0)

    @pl.when(b == 0)
    def _():
        out_ref[...] = head_ref[...].astype(f32)

    rows_ref[:SEQUENCE_TOKENS] = grad_ref[0].astype(f32)
    rows_ref[SEQUENCE_TOKENS:] = jnp.zeros((8, rows_ref.shape[1]), f32)

    def step(k, carry):
        for j in range(STEPS):
            entry = list_ref[b, k * STEPS + j]
            out_ref[pl.ds(entry & 65535, 1), :] += rows_ref[pl.ds(entry >> 16, 1), :]
        return carry

    lax.fori_loop(0, (count_ref[b] + STEPS - 1) // STEPS, step, 0)


def scatter_rows(lists, counts, grads, head):
    blocks = lists.shape[0]
    rows, columns = head.shape
    return pl.pallas_call(
        scatter_kernel,
        grid_spec=pltpu.PrefetchScalarGridSpec(
            num_scalar_prefetch=2,
            grid=(blocks,),
            in_specs=[
                pl.BlockSpec((1, SEQUENCE_TOKENS, columns), lambda b, *_: (b, 0, 0)),
                pl.BlockSpec((rows, columns), lambda b, *_: (0, 0)),
            ],
            out_specs=pl.BlockSpec((rows, columns), lambda b, *_: (0, 0)),
            scratch_shapes=[pltpu.VMEM((SEQUENCE_TOKENS + 8, columns), f32)],
        ),
        out_shape=jax.ShapeDtypeStruct((rows, columns), f32),
        compiler_params=pltpu.CompilerParams(vmem_limit_bytes=50 << 20),
        name="scatter_rows",
    )(lists, counts, grads, head)


def on_device(
    token_ids,
    positions,
    pair_index,
    ref_logps,
    routes,
    step_count,
    embed_table,
    embed_first,
    embed_second,
    qkv_weight,
    qkv_first,
    qkv_second,
    out_weight,
    out_first,
    out_second,
    router_weight,
    router_first,
    router_second,
    norm_gains,
    gains_first,
    gains_second,
    in_weight,
    in_first,
    in_second,
    down_weight,
    down_first,
    down_second,
):
    shard_id = lax.axis_index("shard")
    expert_id = lax.axis_index("expert")
    shards = lax.axis_size("shard")
    planes = lax.axis_size("expert")
    devices = shards * planes
    vocab_rows, columns = embed_table.shape
    vocab_base = shard_id * vocab_rows
    own_rows = vocab_rows // planes
    local_experts = in_weight.shape[0]
    hidden_units = in_weight.shape[3]
    head_cols = QUERY_HEADS * HEAD_WIDTH
    key_cols = KEY_VALUE_HEADS * HEAD_WIDTH
    rows_all = devices * COMP

    side = math.isqrt(shards // 2)
    grid = (planes, side, side, 2)
    together = devices <= 32

    def send(parts, ident):
        if together:
            return communicate(parts, ident)
        return [
            out for n, part in enumerate(parts) for out in communicate([part], ident + 20 * n)
        ]

    unit = own_rows // 24

    def swap(x, start, size, rounds, back=False):
        return Swap(x, start * unit, size * unit, planes, side, rounds, back)

    def gather_completion(rows, ident, *beside):
        part = Gather([rows], split(0, COMP, rows.shape[1], 2, 2), planes, side)
        out = communicate([part, *beside], ident)
        return (out[0].reshape(rows_all, rows.shape[1]), *out[1:])

    def reduce_completion(rows, ident, cuts, *beside):
        rows = rows.reshape(grid + (COMP, rows.shape[1]))
        part = Reduce([rows], split(0, COMP, rows.shape[-1], 2, cuts), planes, side)
        return communicate([part, *beside], ident)

    def gather_tiny(block, ident):
        return communicate([Tiny(block, planes, side)], ident)[0].reshape((devices,) + block.shape)

    weight_rows = qkv_weight.shape[0]
    weight_cols = head_cols + key_cols + 128
    cuts = 3 if weight_rows % 48 == 0 else 1
    weight_groups = [
        [
            (i, slice(n * (weight_rows // cuts), (n + 1) * (weight_rows // cuts)), slice(0, weight_cols), i == 0)
            for i in range(2)
        ]
        for n in range(cuts)
    ]
    embed_groups = split(0, SEQUENCE_TOKENS, columns, 8, 1)

    own_places = lax.dynamic_index_in_dim(positions, shard_id, 0, keepdims=False)
    start = own_places[0]
    own_tokens = lax.dynamic_slice_in_dim(token_ids, shard_id * SEQUENCE_TOKENS, SEQUENCE_TOKENS, 0)
    own_routes = lax.dynamic_slice_in_dim(routes, start, COMP, 0)
    sheet = jnp.concatenate(
        [
            own_tokens,
            own_routes.reshape(-1),
            own_places,
            jnp.zeros((1024 - SEQUENCE_TOKENS - COMP * TOP - COMP,), jnp.int32),
        ]
    )
    sheets = gather_tiny(sheet.reshape(8, 128), 0).reshape(devices, 1024)
    tokens_all = sheets[:, :SEQUENCE_TOKENS]
    routes_all = sheets[:, SEQUENCE_TOKENS : SEQUENCE_TOKENS + COMP * TOP].reshape(rows_all, TOP)
    places_all = sheets[:, SEQUENCE_TOKENS + COMP * TOP : SEQUENCE_TOKENS + COMP * TOP + COMP]
    spots = jnp.arange(SEQUENCE_TOKENS, dtype=jnp.int32)
    targets = jnp.sum(
        jnp.where(
            places_all[:, :, None] + 1 == spots[None, None, :], tokens_all[:, None, :], 0
        ),
        axis=2,
    ).reshape(-1)

    lists, counts = row_lists(tokens_all, vocab_base, vocab_rows)
    picked = gather_rows(lists, counts, embed_table).reshape(grid + (SEQUENCE_TOKENS, columns))
    packs = [
        jnp.concatenate(
            [
                qkv_weight[:, : head_cols + key_cols],
                router_weight,
                norm_gains.T,
                jnp.zeros((weight_rows, 128 - EXPERTS - 3), f32),
            ],
            axis=1,
        ).astype(bf16),
        jnp.concatenate(
            [
                qkv_weight[:, head_cols + key_cols :],
                out_weight,
                jnp.zeros((weight_rows, 128), f32),
            ],
            axis=1,
        ).astype(bf16),
    ]
    table_b = embed_table.astype(bf16)
    picked, first_pack, second_pack, table_one = send(
        [
            Reduce([picked], embed_groups, planes, side, exchange=True),
            Gather(packs, weight_groups, planes, side),
            swap(table_b, 0, 12, 3),
        ],
        1,
    )
    first_pack = first_pack.reshape(D, weight_cols)
    second_pack = second_pack.reshape(D, weight_cols)
    embedded = jnp.concatenate([picked[p] for p in range(planes)], axis=1).astype(f32)
    router_block = first_pack[:, head_cols + key_cols :]
    gains_value = router_block[:, EXPERTS : EXPERTS + 3].T.astype(f32)
    out_full = second_pack[:, key_cols : key_cols + D]

    normed, norm_back_one = jax.vjp(norm_apply, embedded, gains_value[0])
    normed_b = normed.astype(bf16)
    places_f = own_places.astype(f32)
    spots_f = spots.astype(f32)

    def make_query(projected):
        return rotary_apply(projected.reshape(COMP, QUERY_HEADS, HEAD_WIDTH), places_f)

    def make_key(projected):
        return rotary_apply(
            projected.reshape(SEQUENCE_TOKENS, KEY_VALUE_HEADS, HEAD_WIDTH), spots_f
        )

    projected = jnp.dot(normed_b, first_pack, preferred_element_type=f32)
    query_f, query_back = jax.vjp(
        make_query, lax.dynamic_slice(projected, (start, 0), (COMP, head_cols))
    )
    key_f, key_back = jax.vjp(make_key, projected[:, head_cols : head_cols + key_cols])
    query = query_f.astype(bf16).reshape(COMP, KEY_VALUE_HEADS, GROUP, HEAD_WIDTH)
    key = key_f.astype(bf16)
    value = (
        jnp.dot(normed_b, second_pack[:, :key_cols], preferred_element_type=f32)
        .reshape(SEQUENCE_TOKENS, KEY_VALUE_HEADS, HEAD_WIDTH)
        .astype(bf16)
    )
    scores = jnp.einsum("qhgd,khd->hgqk", query, key, preferred_element_type=f32) * HEAD_WIDTH ** (
        -0.5
    )
    scores = jnp.where(own_places[:, None] >= spots[None, :], scores, -1000000000.0)
    expd = jnp.exp(scores - jnp.max(scores, axis=-1, keepdims=True))
    probs = expd / jnp.sum(expd, axis=-1, keepdims=True)
    probs_b = probs.astype(bf16)
    attended = (
        jnp.einsum("hgqk,khd->qhgd", probs_b, value, preferred_element_type=f32)
        .reshape(COMP, head_cols)
        .astype(bf16)
    )
    resid = lax.dynamic_slice_in_dim(embedded, start, COMP, 0) + jnp.dot(
        attended, out_full, preferred_element_type=f32
    )
    normed_two, norm_back_two = jax.vjp(norm_apply, resid, gains_value[1])
    normed_two_b = normed_two.astype(bf16)

    expert_rows, table_two = gather_completion(normed_two_b, 2, swap(table_b, 12, 4, 2))
    lanes = shard_id * local_experts + jnp.arange(local_experts, dtype=jnp.int32)
    in_rows = in_weight.reshape(-1, hidden_units)
    produced, mid, gates, in_cat, down_b, gated_hidden = experts_forward(
        lanes, expert_rows, routes_all, router_block, in_rows, down_weight
    )
    own_index = expert_id * shards + shard_id
    own_gates = lax.dynamic_slice(gates, (own_index * COMP, 0), (COMP, 128))[:, :EXPERTS]
    combined, table_three = reduce_completion(produced, 3, 2, swap(table_b, 16, 4, 0))
    resid_two = resid + combined

    final_rows, norm_back_three = jax.vjp(norm_apply, resid_two, gains_value[2])
    head_rows, table_four = gather_completion(
        final_rows.astype(bf16), 4, swap(table_b, 20, 4, 2)
    )
    table_own = jnp.concatenate([table_one, table_two, table_three, table_four], axis=0)
    logits = jnp.einsum("rd,vd->rv", head_rows, table_own, preferred_element_type=f32) / LOGIT_SCALE
    own_base = vocab_base + expert_id * own_rows
    target_hot = targets[:, None] == own_base + jnp.arange(own_rows, dtype=jnp.int32)[None, :]
    row_top = jnp.max(logits, axis=1)
    row_total = jnp.sum(jnp.exp(logits - row_top[:, None]), axis=1)
    row_hit = jnp.sum(jnp.where(target_hot, logits, 0.0), axis=1)
    stats = jnp.stack([row_top, row_total, row_hit]).reshape(8, 3 * rows_all // 8)
    stats = gather_tiny(stats, 5).reshape(devices, 3, rows_all)
    top_all = jnp.max(stats[:, 0], axis=0)
    total_all = jnp.sum(stats[:, 1] * jnp.exp(stats[:, 0] - top_all[None]), axis=0)
    row_lse = top_all + jnp.log(total_all)
    seq_sums = jnp.sum((jnp.sum(stats[:, 2], axis=0) - row_lse).reshape(-1, COMP), axis=1)

    sequences = jnp.arange(devices, dtype=jnp.int32)[None, :]
    pair_sign = (pair_index[:, :1] == sequences).astype(f32) - (
        pair_index[:, 1:] == sequences
    ).astype(f32)
    scaled = BETA * jnp.sum(pair_sign * (seq_sums - ref_logps)[None, :], axis=1)
    loss_value = -jnp.mean(jax.nn.log_sigmoid(scaled))
    pair_grad = jax.nn.sigmoid(-scaled) * (-BETA / scaled.shape[0])
    seq_grad = jnp.sum(pair_sign * pair_grad[:, None], axis=0)
    row_grad = jnp.repeat(seq_grad, COMP)
    grad_logits = (
        row_grad[:, None] * (target_hot.astype(f32) - jnp.exp(logits - row_lse[:, None]))
    ).astype(bf16)
    grad_rows = jnp.dot(grad_logits, table_own, preferred_element_type=f32) / LOGIT_SCALE
    head_grad = (
        jnp.einsum("rv,rd->vd", grad_logits, head_rows, preferred_element_type=f32) / LOGIT_SCALE
    ).astype(bf16)
    own_grad_rows, head_one = reduce_completion(
        grad_rows.astype(bf16), 6, 2, swap(head_grad, 0, 5, 0, back=True)
    )
    grad_resid_two, grad_gain_three = norm_back_three(own_grad_rows)

    grad_all, head_two = gather_completion(
        grad_resid_two.astype(bf16), 7, swap(head_grad, 5, 5, 2, back=True)
    )
    back, mid_grad = experts_backward(lanes, grad_all, mid, gates, in_cat, down_b)
    back, head_three = reduce_completion(back, 8, 1, swap(head_grad, 10, 5, 0, back=True))
    grad_gates = back[:, D : D + EXPERTS]
    grad_router_logits = own_gates * (
        grad_gates - jnp.sum(own_gates * grad_gates, axis=1, keepdims=True)
    )
    grad_router_logits = jnp.pad(grad_router_logits, ((0, 0), (0, 128 - EXPERTS)))
    grad_normed_two = back[:, :D] + jnp.einsum(
        "se,de->sd", grad_router_logits, router_block.astype(f32)
    )
    grad_resid, grad_gain_two = norm_back_two(grad_normed_two)
    grad_resid = grad_resid + grad_resid_two
    grad_branch = grad_resid.astype(bf16)
    grad_attended = (
        jnp.einsum("sd,kd->sk", grad_branch, out_full, preferred_element_type=f32)
        .astype(bf16)
        .reshape(COMP, KEY_VALUE_HEADS, GROUP, HEAD_WIDTH)
    )

    grad_probs = jnp.einsum("qhgd,khd->hgqk", grad_attended, value, preferred_element_type=f32)
    grad_probs = grad_probs.astype(bf16).astype(f32)
    inner = jnp.sum(grad_probs * probs, axis=-1, keepdims=True)
    grad_scores = (probs * (grad_probs - inner)).astype(bf16)
    grad_value = jnp.einsum("hgqk,qhgd->khd", probs_b, grad_attended, preferred_element_type=f32)
    grad_query = jnp.einsum(
        "hgqk,khd->qhgd", grad_scores, key, preferred_element_type=f32
    ) * HEAD_WIDTH ** (-0.5)
    grad_key = jnp.einsum(
        "hgqk,qhgd->khd", grad_scores, query, preferred_element_type=f32
    ) * HEAD_WIDTH ** (-0.5)

    def spread(rows):
        return lax.dynamic_update_slice_in_dim(
            jnp.zeros((SEQUENCE_TOKENS, rows.shape[1]), rows.dtype), rows, start, 0
        )

    grad_query_rows = query_back(grad_query.reshape(COMP, QUERY_HEADS, HEAD_WIDTH))[0].astype(bf16)
    grad_first = jnp.concatenate(
        [
            spread(grad_query_rows),
            key_back(grad_key)[0].astype(bf16),
            jnp.zeros((SEQUENCE_TOKENS, 128), bf16),
        ],
        axis=1,
    )
    grad_value = grad_value.reshape(SEQUENCE_TOKENS, key_cols).astype(bf16)
    across = "sk,dk->sd"
    grad_normed = jnp.einsum(across, grad_first, first_pack, preferred_element_type=f32)
    grad_normed += jnp.einsum(
        across, grad_value, second_pack[:, :key_cols], preferred_element_type=f32
    )
    grad_embedded, grad_gain_one = norm_back_one(grad_normed)
    grad_embedded = (grad_embedded + spread(grad_resid)).astype(bf16)
    grad_embedded = jnp.stack(
        [grad_embedded[:, p * columns : (p + 1) * columns] for p in range(planes)]
    )

    gains_grad = jnp.pad(
        jnp.stack([grad_gain_one, grad_gain_two, grad_gain_three]), ((0, 13), (0, 0))
    ).astype(bf16)
    gains_lanes = (
        jnp.arange(16)[:, None] + EXPERTS == jnp.arange(128)[None, :]
    ).astype(bf16)
    wide = head_cols + key_cols
    first_left = jnp.concatenate([normed_b, normed_two_b, gains_grad], axis=0)
    first_right = jnp.concatenate(
        [
            grad_first,
            jnp.pad(
                jnp.concatenate([grad_router_logits.astype(bf16), gains_lanes], axis=0),
                ((0, 0), (wide, 0)),
            ),
        ],
        axis=0,
    )
    second_left = jnp.concatenate([normed_b, attended], axis=0)
    second_right = jnp.concatenate(
        [
            jnp.pad(grad_value, ((0, 0), (0, D + 128))),
            jnp.pad(grad_branch, ((0, 0), (key_cols, 128))),
        ],
        axis=0,
    )
    grad_packs = [
        jnp.einsum("sd,sk->dk", left, right, preferred_element_type=f32)
        .astype(bf16)
        .reshape(grid + (weight_rows, weight_cols))
        for left, right in ((first_left, first_right), (second_left, second_right))
    ]
    sent, first_grad, second_grad, head_four = send(
        [
            Gather([grad_embedded], embed_groups, planes, side, exchange=True),
            Reduce(grad_packs, weight_groups, planes, side),
            swap(head_grad, 15, 9, 3, back=True),
        ],
        9,
    )
    head_grad = jnp.concatenate([head_one, head_two, head_three, head_four], axis=1)
    table_grad = scatter_rows(
        lists,
        counts,
        sent.reshape(devices, SEQUENCE_TOKENS, columns),
        head_grad.reshape(vocab_rows, columns),
    )

    step_value = step_count.astype(f32)
    scales = (1.0 / (1.0 - RATE_ONE**step_value), 1.0 / (1.0 - RATE_TWO**step_value))
    grad_in = jnp.einsum("td,tk->dk", expert_rows, mid_grad, preferred_element_type=f32)
    grad_down = jnp.einsum(
        "tk,td->kd", gated_hidden, grad_all, preferred_element_type=f32
    ).reshape(down_weight.shape)
    in_first_new, in_second_new, in_norms = in_moments(
        jnp.stack(scales),
        grad_in,
        in_rows,
        in_first.reshape(in_rows.shape),
        in_second.reshape(in_rows.shape),
    )
    weights = (embed_table, qkv_weight, out_weight, router_weight, norm_gains, down_weight)
    firsts = (embed_first, qkv_first, out_first, router_first, gains_first, down_first)
    seconds = (embed_second, qkv_second, out_second, router_second, gains_second, down_second)
    gradients = (
        table_grad,
        jnp.concatenate([first_grad[:, :wide], second_grad[:, :key_cols]], axis=1),
        second_grad[:, key_cols : key_cols + D],
        first_grad[:, wide : wide + EXPERTS],
        first_grad[:, wide + EXPERTS : wide + EXPERTS + 3].T,
        grad_down,
    )
    moved = [
        lamb_parts(weight, moment_one, moment_two, gradient, scales)
        for weight, moment_one, moment_two, gradient in zip(weights, firsts, seconds, gradients)
    ]
    partial_norms = [
        (jnp.sum(weight * weight), jnp.sum(parts[2] * parts[2]))
        for weight, parts in zip(weights, moved)
    ]
    partial_norms.insert(5, (jnp.sum(in_norms[0]), jnp.sum(in_norms[1])))
    norm_row = lax.broadcasted_iota(jnp.int32, (8, 128), 0)
    norm_lane = lax.broadcasted_iota(jnp.int32, (8, 128), 1)
    norm_block = jnp.zeros((8, 128), f32)
    for n, pair in enumerate(partial_norms):
        for lane, part in enumerate(pair):
            norm_block = jnp.where((norm_row == n) & (norm_lane == lane), part, norm_block)
    norm_values = jnp.sqrt(jnp.sum(gather_tiny(norm_block, 10), axis=0))[:7, :2]
    trust_ratio = norm_values[:, 0] / norm_values[:, 1]
    moved.insert(
        5, (in_first_new, in_second_new, lamb_update(in_rows, in_first_new, in_second_new, *scales))
    )
    weights = weights[:5] + (in_rows,) + weights[5:]
    results = [loss_value]
    for place, (weight, parts) in enumerate(zip(weights, moved)):
        made = [weight - STEP_RATE * trust_ratio[place] * parts[2], parts[0], parts[1]]
        if place == 5:
            made = [x.reshape(in_weight.shape) for x in made]
        results.extend(made)
    results.append(jnp.stack([norm_values[:, 0], norm_values[:, 1], trust_ratio], axis=1))
    return tuple(results)


def solution(mesh):
    rows = P(BOTH, None)
    vocab = P("shard", "expert")
    gains = P(None, BOTH)
    inner = P("shard", None, None, "expert")
    outer = P("shard", "expert", None)
    state = (vocab,) * 3 + (rows,) * 9 + (gains,) * 3 + (inner,) * 3 + (outer,) * 3
    return jax.shard_map(
        on_device,
        mesh=mesh,
        in_specs=(P("expert"), P("expert", None), P(), P(), rows, P()) + state,
        out_specs=(P(),) + state + (P(),),
        check_vma=False,
    )
```

```python
import functools
import math

import jax
import jax.numpy as jnp
from jax import lax
from jax.experimental import pallas as pl
from jax.experimental.pallas import tpu as pltpu
from jax.sharding import PartitionSpec as P

D = 1536
QUERY_HEADS = 24
KEY_VALUE_HEADS = 8
GROUP = QUERY_HEADS // KEY_VALUE_HEADS
HEAD_WIDTH = 64
TOP = 8
EXPERTS = 32
SEQUENCE_TOKENS = 256
COMP = 32
QKV = 2560

BETA = 0.1
LOGIT_SCALE = 6.0
RATE_ONE = 0.9
RATE_TWO = 0.999
EPSILON = 1e-06
DECAY = 0.01
STEP_RATE = 0.3

BOTH = ("expert", "shard")
bf16 = jnp.bfloat16
f32 = jnp.float32


MESH = pl.DeviceIdType.MESH


class Spot:
    def __init__(self, planes, side):
        self.planes, self.side = planes, side
        self.z = lax.axis_index("expert")
        self.shard = lax.axis_index("shard")
        self.core = lax.rem(self.shard, 2)
        self.b = lax.rem(lax.div(self.shard, 2), side)
        self.a = lax.div(self.shard, 2 * side)

    def plane(self, k):
        z = lax.rem(self.z + k, self.planes)
        return z, (z, self.shard)

    def along_a(self, k):
        a = lax.rem(self.a + k, self.side)
        return a, (self.z, (a * self.side + self.b) * 2 + self.core)

    def along_b(self, k):
        b = lax.rem(self.b + k, self.side)
        return b, (self.z, (self.a * self.side + b) * 2 + self.core)

    def along(self, first, k):
        return self.along_a(k) if first else self.along_b(k)

    def mate(self):
        other = 1 - self.core
        return other, (self.z, (self.a * self.side + self.b) * 2 + other)

    def near(self, k):
        return self.z, lax.rem(self.shard + k, 2 * self.side * self.side)

    def greet(self, flat):
        targets = [self.plane(k)[1] for k in range(1, self.planes)]
        if flat:
            targets += [self.near(k) for k in range(1, 2 * self.side * self.side)]
        else:
            targets.append(self.mate()[1])
            for k in range(1, self.side):
                targets += [self.along_a(k)[1], self.along_b(k)[1]]
        barrier = pltpu.get_barrier_semaphore()
        for target in targets:
            pl.semaphore_signal(barrier, inc=1, device_id=target, device_id_type=MESH)
        pl.semaphore_wait(barrier, len(targets))


class Mail:
    def __init__(self, send, recv):
        self.send, self.recv, self.count, self.open = send, recv, 0, []

    def start(self, src, dst, target):
        copy = pltpu.make_async_remote_copy(
            src_ref=src,
            dst_ref=dst,
            send_sem=self.send.at[self.count],
            recv_sem=self.recv.at[self.count],
            device_id=target,
            device_id_type=MESH,
        )
        self.count += 1
        copy.start()
        self.open.append(copy)
        return copy

    def finish(self):
        for copy in self.open:
            copy.wait_send()


def arrive(copies):
    for copy in copies:
        copy.wait_recv()


class Tiny:
    flat = True
    scratch = ()

    def __init__(self, x, planes, side):
        self.planes, self.side, self.inputs = planes, side, [x]
        shape = (planes, 2 * side * side) + x.shape
        self.outputs = [jax.ShapeDtypeStruct(shape, x.dtype)]
        self.copies = planes + 2 * side * side - 2

    def steps(self, spot, mail, x, out):
        out[spot.z, spot.shard] = x[...]
        sent = []
        for k in range(1, self.planes):
            sent.append(mail.start(x, out.at[spot.z, spot.shard], spot.plane(k)[1]))
        yield
        arrive(sent)
        part = out.at[:, spot.shard]
        yield
        arrive([mail.start(part, part, spot.near(k)) for k in range(1, 2 * self.side**2)])


def split(array, rows, columns, row_parts, column_parts):
    r, c = rows // row_parts, columns // column_parts
    cuts = [
        (array, slice(i * r, i * r + r), slice(j * c, j * c + c))
        for j in range(column_parts)
        for i in range(row_parts)
    ]
    cuts = [cut + (n % 2 == 0,) for n, cut in enumerate(cuts)]
    return [cuts[n : n + 2] for n in range(0, len(cuts), 2)]


def pipeline(groups, stage, last):
    sent = [[[] for _ in group] for group in groups]
    for tick in range(len(groups) + last):
        for step in range(last, -1, -1):
            turn = tick - step
            if 0 <= turn < len(groups):
                for n, cut in enumerate(groups[turn]):
                    for copy in sent[turn][n]:
                        copy.wait_recv()
                    sent[turn][n] = stage(step, (turn, n), cut)
        yield


class Gather:
    flat = False
    scratch = ()

    def __init__(self, xs, groups, planes, side, exchange=False):
        self.planes, self.side, self.inputs, self.groups = planes, side, xs, groups
        self.exchange = exchange
        grid = (planes, side, side, 2)
        self.outputs = [jax.ShapeDtypeStruct(grid + x.shape[-2:], x.dtype) for x in xs]
        self.copies = sum(map(len, groups)) * (planes - 1 + 2 * (side - 1) + 1)

    def steps(self, spot, mail, *refs):
        xs, outs = refs[: len(self.inputs)], refs[len(self.inputs) :]
        z, a, b, core = spot.z, spot.a, spot.b, spot.core
        for x, out in zip(xs, outs):
            out[z, a, b, core] = x[z] if self.exchange else x[...]

        def stage(step, key, cut):
            i, rows, columns, first = cut
            x, out = xs[i], outs[i]
            if step == 0:
                place = out.at[z, a, b, core, rows, columns]
                sent = []
                for k in range(1, self.planes):
                    peer, target = spot.plane(k)
                    own = x.at[peer, rows, columns] if self.exchange else x.at[rows, columns]
                    sent.append(mail.start(own, place, target))
                return sent
            if step in (1, 2):
                if step == 1:
                    part = out.at[:, a, b, core, rows, columns]
                elif first:
                    part = out.at[:, :, b, core, rows, columns]
                else:
                    part = out.at[:, a, :, core, rows, columns]
                return [
                    mail.start(part, part, spot.along(first == (step == 1), k)[1])
                    for k in range(1, self.side)
                ]
            if step == 3:
                part = out.at[:, :, :, core, rows, columns]
                return [mail.start(part, part, spot.mate()[1])]
            return []

        return pipeline(self.groups, stage, 4)


class Reduce:
    flat = False

    def __init__(self, xs, groups, planes, side, exchange=False):
        self.planes, self.side, self.inputs, self.groups = planes, side, xs, groups
        self.exchange = exchange
        self.outputs = [
            jax.ShapeDtypeStruct((planes,) + x.shape[-2:], x.dtype)
            if exchange
            else jax.ShapeDtypeStruct(x.shape[-2:], f32)
            for x in xs
        ]
        self.scratch = []
        for i, rows, columns, _ in [cut for group in groups for cut in group]:
            block = (rows.stop - rows.start, columns.stop - columns.start)
            self.scratch += [
                pltpu.VMEM(shape + block, xs[i].dtype)
                for shape in (
                    (planes, side, side),
                    (side - 1, planes, side),
                    (planes, side),
                    (side - 1, planes),
                    (planes,),
                )
                + (() if exchange else ((planes - 1,),))
            ]
        self.copies = sum(map(len, groups)) * (planes - 1 + 2 * (side - 1) + 1)

    def steps(self, spot, mail, *refs):
        planes, side, number = self.planes, self.side, len(self.inputs)
        xs, outs, rest = refs[:number], refs[number : 2 * number], refs[2 * number :]
        each = 5 if self.exchange else 6
        order = [(t, n) for t, group in enumerate(self.groups) for n in range(len(group))]
        held = {key: rest[each * p : each * (p + 1)] for p, key in enumerate(order)}
        core, z = spot.core, spot.z
        other, mate = spot.mate()

        def stage(step, key, cut):
            i, rows, columns, first = cut
            x, out = xs[i], outs[i]
            one, hop_two, two, hop_three, three = held[key][:5]
            if step == 0:
                return [mail.start(x.at[:, :, :, other, rows, columns], one, mate)]
            sent = []
            if step == 1:

                def add(n, carry):
                    ia, ib = lax.rem(lax.div(n, side), side), lax.rem(n, side)
                    iz = lax.div(n, side * side)
                    total = x[iz, ia, ib, core, rows, columns].astype(f32)
                    one[iz, ia, ib] = (total + one[iz, ia, ib].astype(f32)).astype(one.dtype)
                    return carry

                lax.fori_loop(0, planes * side * side, add, 0)
                for k in range(1, side):
                    peer, target = spot.along(first, k)
                    part = one.at[:, peer] if first else one.at[:, :, peer]
                    sent.append(mail.start(part, hop_two.at[k - 1], target))
            elif step == 2:

                def add(n, carry):
                    iz, ir = lax.div(n, side), lax.rem(n, side)
                    total = (one[iz, spot.a, ir] if first else one[iz, ir, spot.b]).astype(f32)
                    for k in range(side - 1):
                        total += hop_two[k, iz, ir].astype(f32)
                    two[iz, ir] = total.astype(two.dtype)
                    return carry

                lax.fori_loop(0, planes * side, add, 0)
                for k in range(1, side):
                    peer, target = spot.along(not first, k)
                    sent.append(mail.start(two.at[:, peer], hop_three.at[k - 1], target))
            elif step == 3:
                mine = spot.b if first else spot.a

                def add(iz, carry):
                    total = two[iz, mine].astype(f32)
                    for k in range(side - 1):
                        total += hop_three[k, iz].astype(f32)
                    three[iz] = total.astype(three.dtype)
                    return carry

                lax.fori_loop(0, planes, add, 0)
                for k in range(1, planes):
                    peer, target = spot.plane(k)
                    if self.exchange:
                        place = out.at[z, rows, columns]
                    else:
                        place = held[key][5].at[k - 1]
                    sent.append(mail.start(three.at[peer], place, target))
                if self.exchange:
                    out[z, rows, columns] = three[z]
            elif not self.exchange:
                total = three[z].astype(f32)
                for k in range(planes - 1):
                    total += held[key][5][k].astype(f32)
                out[rows, columns] = total
            return sent

        return pipeline(self.groups, stage, 4)


class Swap:
    flat = False
    scratch = (pltpu.SemaphoreType.DMA(()),)

    def __init__(self, x, start, size, planes, side, rounds, back=False, held=None):
        self.planes, self.side = planes, side
        self.inputs = [x] if held is None else [x, held]
        self.in_spaces, self.out_spaces = (pl.ANY,) * len(self.inputs), (pl.ANY,)
        self.aliases = {} if held is None else {1: 0}
        self.begin, self.size, self.rounds, self.back = start, size, rounds, back
        self.columns = x.shape[1] // planes if back else x.shape[1]
        self.rows = x.shape[0] if back else x.shape[0] // planes
        shape = (planes, self.rows, self.columns) if back else (self.rows, planes * self.columns)
        self.outputs = [jax.ShapeDtypeStruct(shape, x.dtype)]
        self.copies = planes - 1

    def steps(self, spot, mail, *refs):
        x, out, own_sem = refs[0], refs[-2], refs[-1]
        rows = pl.ds(self.begin, self.size)

        def block(z):
            return pl.ds(pl.multiple_of(z * self.columns, 128), self.columns)

        def source(z):
            if self.back:
                return x.at[rows, block(z)]
            return x.at[pl.ds(pl.multiple_of(z * self.rows + self.begin, 16), self.size), :]

        for _ in range(self.rounds):
            yield
        place = out.at[spot.z, rows] if self.back else out.at[rows, block(spot.z)]
        sent = []
        for k in range(1, self.planes):
            peer, target = spot.plane(k)
            sent.append(mail.start(source(peer), place, target))
        own = pltpu.make_async_copy(source(spot.z), place, own_sem)
        own.start()
        for _ in range(20):
            yield
        own.wait()
        for copy in sent:
            copy.wait_recv()


def communicate(parts, ident):
    planes, side = parts[0].planes, parts[0].side
    counts = [(len(p.inputs), len(p.outputs), len(p.scratch)) for p in parts]
    n_in, n_out = (sum(c[i] for c in counts) for i in range(2))
    copies = sum(p.copies for p in parts)
    aliases, i, o = {}, 0, 0
    for part, (ci, co, _) in zip(parts, counts):
        aliases.update({i + a: o + b for a, b in getattr(part, "aliases", {}).items()})
        i, o = i + ci, o + co

    def kernel(*refs):
        ins, outs, rest = refs[:n_in], refs[n_in : n_in + n_out], refs[n_in + n_out :]
        send, recv = rest[-2:]
        spot = Spot(planes, side)
        spot.greet(parts[0].flat)
        mail = Mail(send, recv)
        running, i, o, s = [], 0, 0, 0
        for part, (ci, co, cs) in zip(parts, counts):
            running.append(
                part.steps(spot, mail, *ins[i : i + ci], *outs[o : o + co], *rest[s : s + cs])
            )
            i, o, s = i + ci, o + co, s + cs
        while running:
            running = [steps for steps in running if next(steps, True) is None]
        mail.finish()

    size = sum(x.size * x.dtype.itemsize for p in parts for x in p.inputs + p.outputs)
    out = pl.pallas_call(
        kernel,
        out_shape=[x for p in parts for x in p.outputs],
        in_specs=[
            pl.BlockSpec(memory_space=space)
            for p in parts
            for space in getattr(p, "in_spaces", (pltpu.VMEM,) * len(p.inputs))
        ],
        out_specs=[
            pl.BlockSpec(memory_space=space)
            for p in parts
            for space in getattr(p, "out_spaces", (pltpu.VMEM,) * len(p.outputs))
        ],
        input_output_aliases=aliases,
        scratch_shapes=[s for p in parts for s in p.scratch]
        + [pltpu.SemaphoreType.DMA((copies,)), pltpu.SemaphoreType.DMA((copies,))],
        compiler_params=pltpu.CompilerParams(
            collective_id=ident, has_side_effects=True, vmem_limit_bytes=62 << 20
        ),
        cost_estimate=pl.CostEstimate(flops=0, bytes_accessed=20 * size, transcendentals=0),
        name="exchange_" + str(ident),
    )(*[x for p in parts for x in p.inputs])
    return list(out)

def expert_gate(gates, lane):
    lanes = lax.broadcasted_iota(jnp.int32, gates.shape, 1)
    return jnp.sum(jnp.where(lanes == lane, gates, 0.0), axis=1, keepdims=True)


CHUNK = 512
BLOCK = 1024
ACROSS = (((1,), (1,)), ((), ()))


def forward_kernel(
    lane_ref, rows_ref, routes_ref, router_ref, in_ref, down_ref, out_ref, mid_ref, gates_ref, cat_ref, down_out, hidden_ref
):
    e, number = pl.program_id(1), pl.num_programs(1)
    units = in_ref.shape[1]
    for j in range(2):
        cat_ref[:, j * units : (j + 1) * units] = in_ref[pl.ds(j, D, stride=2), :].astype(bf16)
    down_out[pl.ds(pl.multiple_of(e * units, units), units), :] = down_ref[0].astype(bf16)

    def chunk(i, carry):
        here = pl.ds(pl.multiple_of(i * CHUNK, CHUNK), CHUNK)
        rows = rows_ref[here, :]

        @pl.when(e == 0)
        def _():
            logits = jnp.dot(rows, router_ref[...], preferred_element_type=f32)
            lanes = lax.broadcasted_iota(jnp.int32, logits.shape, 1)
            mask = lanes == routes_ref[here, 0:1]
            for j in range(1, TOP):
                mask |= lanes == routes_ref[here, j : j + 1]
            top = jnp.max(jnp.where(mask, logits, -3e38), axis=1, keepdims=True)
            weight = jnp.where(mask, jnp.exp(jnp.where(mask, logits - top, 0.0)), 0.0)
            gates_ref[here, :] = weight / jnp.sum(weight, axis=1, keepdims=True)

        mid = jnp.dot(rows, cat_ref[...], preferred_element_type=f32)
        mid_ref[here, :] = mid
        gate, up = mid[:, :units], mid[:, units:]
        hidden = (gate * jax.nn.sigmoid(gate) * up).astype(bf16).astype(f32)
        hidden = (hidden * expert_gate(gates_ref[here, :], lane_ref[0] + e)).astype(bf16)
        hidden_ref[here, pl.ds(pl.multiple_of(e * units, units), units)] = hidden

        @pl.when(e == number - 1)
        def _():
            out_ref[here, :] = jnp.dot(
                hidden_ref[here, :], down_out[...], preferred_element_type=f32
            ).astype(bf16)

        return carry

    lax.fori_loop(0, rows_ref.shape[0] // CHUNK, chunk, 0)


def experts_forward(lane, rows, routes, router, in_rows, down):
    number, units = down.shape[:2]
    total = rows.shape[0]
    block = min(total, BLOCK)
    row = lambda r, e, *_: (r, 0)
    still = lambda r, e, *_: (0, 0)
    return pl.pallas_call(
        forward_kernel,
        grid_spec=pltpu.PrefetchScalarGridSpec(
            num_scalar_prefetch=1,
            grid=(total // block, number),
            in_specs=[
                pl.BlockSpec((block, D), row),
                pl.BlockSpec((block, TOP), row),
                pl.BlockSpec((D, 128), lambda r, e, *_: (0, PACK // 128 - 1)),
                pl.BlockSpec((2 * D, units), lambda r, e, *_: (e, 0)),
                pl.BlockSpec((1, units, D), lambda r, e, *_: (e, 0, 0)),
            ],
            out_specs=[
                pl.BlockSpec((block, D), row),
                pl.BlockSpec((block, 2 * units), lambda r, e, *_: (r, e)),
                pl.BlockSpec((block, 128), row),
                pl.BlockSpec((D, 2 * units), lambda r, e, *_: (0, e)),
                pl.BlockSpec((number * units, D), still),
                pl.BlockSpec((block, number * units), row),
            ],
        ),
        out_shape=[
            jax.ShapeDtypeStruct((total, D), bf16),
            jax.ShapeDtypeStruct((total, 2 * units * number), f32),
            jax.ShapeDtypeStruct((total, 128), f32),
            jax.ShapeDtypeStruct((D, 2 * units * number), bf16),
            jax.ShapeDtypeStruct((number * units, D), bf16),
            jax.ShapeDtypeStruct((total, number * units), bf16),
        ],
        compiler_params=pltpu.CompilerParams(vmem_limit_bytes=60 << 20),
        name="experts_forward",
    )(lane, rows, routes, router, in_rows, down)


def backward_kernel(
    lane_ref, grad_ref, mid_ref, gates_ref, cat_ref, down_ref, out_ref, mid_grad_ref, pulled_ref
):
    number = lane_ref.shape[0]
    units = pulled_ref.shape[1] // number

    def chunk(i, carry):
        here = pl.ds(pl.multiple_of(i * CHUNK, CHUNK), CHUNK)
        pulled_ref[...] = lax.dot_general(
            grad_ref[here, :], down_ref[...], ACROSS, preferred_element_type=f32
        )
        lanes = lax.broadcasted_iota(jnp.int32, (CHUNK, 128), 1)
        gate_part = jnp.zeros((CHUNK, 128), f32)
        for e in range(number):
            lane = lane_ref[e]
            weight = expert_gate(gates_ref[here, :], lane)
            gate = mid_ref[here, 2 * e * units : (2 * e + 1) * units]
            up = mid_ref[here, (2 * e + 1) * units : (2 * e + 2) * units]
            pulled = pulled_ref[:, e * units : (e + 1) * units]
            soft = jax.nn.sigmoid(gate)
            silu = gate * soft
            hidden = (silu * up).astype(bf16).astype(f32)
            gate_grad = jnp.sum(hidden * pulled, axis=1, keepdims=True)
            gate_part = jnp.where(lanes == lane, gate_grad, gate_part)
            hidden_grad = (pulled * weight).astype(bf16).astype(f32)
            turned = hidden_grad * up * (soft * (1.0 + gate * (1.0 - soft)))
            mid_grad_ref[here, 2 * e * units : (2 * e + 1) * units] = turned.astype(bf16)
            mid_grad_ref[here, (2 * e + 1) * units : (2 * e + 2) * units] = (
                hidden_grad * silu
            ).astype(bf16)
        out_ref[here, D:] = gate_part.astype(bf16)
        out_ref[here, :D] = lax.dot_general(
            mid_grad_ref[here, :], cat_ref[...], ACROSS, preferred_element_type=f32
        ).astype(bf16)
        return carry

    lax.fori_loop(0, grad_ref.shape[0] // CHUNK, chunk, 0)


def experts_backward(lanes, grad, mid, gates, cat, down):
    number = lanes.shape[0]
    total = grad.shape[0]
    block = min(total, BLOCK)
    row = lambda r, *_: (r, 0)
    still = lambda r, *_: (0, 0)
    return pl.pallas_call(
        backward_kernel,
        grid_spec=pltpu.PrefetchScalarGridSpec(
            num_scalar_prefetch=1,
            grid=(total // block,),
            in_specs=[
                pl.BlockSpec((block, D), row),
                pl.BlockSpec((block, mid.shape[1]), row),
                pl.BlockSpec((block, 128), row),
                pl.BlockSpec(cat.shape, still),
                pl.BlockSpec(down.shape, still),
            ],
            out_specs=[
                pl.BlockSpec((block, D + 128), row),
                pl.BlockSpec((block, mid.shape[1]), row),
            ],
            scratch_shapes=[pltpu.VMEM((CHUNK, down.shape[0]), f32)],
        ),
        out_shape=[
            jax.ShapeDtypeStruct((total, D + 128), bf16),
            jax.ShapeDtypeStruct(mid.shape, bf16),
        ],
        compiler_params=pltpu.CompilerParams(vmem_limit_bytes=60 << 20),
        name="experts_backward",
    )(lanes, grad, mid, gates, cat, down)


def moments_kernel(scale_ref, grad_ref, w_ref, first_ref, second_ref, new_first, new_second, norms):
    units = w_ref.shape[1]
    part = w_ref.shape[0] // 2

    @pl.when((pl.program_id(0) == 0) & (pl.program_id(1) == 0))
    def _():
        norms[...] = jnp.zeros_like(norms)

    for j in range(2):
        here = pl.ds(j, part, stride=2)
        grad = grad_ref[:, j * units : (j + 1) * units]
        weight = w_ref[here, :]
        one = RATE_ONE * first_ref[here, :] + (1.0 - RATE_ONE) * grad
        two = RATE_TWO * second_ref[here, :] + (1.0 - RATE_TWO) * grad * grad
        update = lamb_update(weight, one, two, scale_ref[0], scale_ref[1])
        new_first[here, :] = one
        new_second[here, :] = two
        norms[0] += jnp.sum((weight * weight).reshape(-1, 8, units), axis=0)
        norms[1] += jnp.sum((update * update).reshape(-1, 8, units), axis=0)


def in_moments(scales, grad, weight, first, second):
    units = weight.shape[1]
    number = grad.shape[1] // (2 * units)
    parts = 2
    row = pl.BlockSpec((2 * D // parts, units), lambda e, p, *_: (e * parts + p, 0))
    return pl.pallas_call(
        moments_kernel,
        grid_spec=pltpu.PrefetchScalarGridSpec(
            num_scalar_prefetch=1,
            grid=(number, parts),
            in_specs=[pl.BlockSpec((D // parts, 2 * units), lambda e, p, *_: (p, e)), row, row, row],
            out_specs=[row, row, pl.BlockSpec((2, 8, units), lambda e, p, *_: (0, 0, 0))],
        ),
        out_shape=[jax.ShapeDtypeStruct(weight.shape, f32)] * 2
        + [jax.ShapeDtypeStruct((2, 8, units), f32)],
        compiler_params=pltpu.CompilerParams(vmem_limit_bytes=40 << 20),
        name="in_moments",
    )(scales, grad, weight, first, second)


HEAD_COLS = QUERY_HEADS * HEAD_WIDTH
KEY_COLS = KEY_VALUE_HEADS * HEAD_WIDTH
PACK = HEAD_COLS + KEY_COLS + 128
ROOT = HEAD_WIDTH ** (-0.5)


def turn(u, cosine, sine):
    width = u.shape[1]
    lanes = lax.broadcasted_iota(jnp.int32, u.shape, 1)
    ahead = pltpu.roll(u, width - HEAD_WIDTH // 2, 1)
    behind = pltpu.roll(u, HEAD_WIDTH // 2, 1)
    other = jnp.where(lax.rem(lanes, HEAD_WIDTH) < HEAD_WIDTH // 2, ahead, behind)
    return u * jnp.tile(cosine, (1, width // 128)) + other * jnp.tile(sine, (1, width // 128))


def rotary_tables():
    half = HEAD_WIDTH // 2
    freqs = jnp.exp(-jnp.log(10000.0) * jnp.arange(half, dtype=f32) / half)
    angles = jnp.arange(SEQUENCE_TOKENS, dtype=f32)[:, None] * freqs[None, :]
    cosine, sine = jnp.cos(angles), jnp.sin(angles)
    return jnp.tile(cosine, (1, 4)), jnp.tile(jnp.concatenate([-sine, sine], axis=1), (1, 2))


def inverse_root(values):
    return lax.rsqrt(jnp.mean(values * values, axis=-1, keepdims=True) + 1e-06)


def norm_back(values, gain, grad):
    root = inverse_root(values)
    scaled = grad * gain
    inner = jnp.mean(scaled * values, axis=-1, keepdims=True)
    return root * scaled - values * (root * root * root * inner), jnp.sum(
        grad * values * root, axis=0, keepdims=True
    )


def dot(a, b):
    return jnp.dot(a, b, preferred_element_type=f32)


def dot_across(a, b):
    return lax.dot_general(a, b, ACROSS, preferred_element_type=f32)


def selector(start, shape, axis):
    row = lax.broadcasted_iota(jnp.int32, shape, 1 - axis) + start
    return (row == lax.broadcasted_iota(jnp.int32, shape, axis)).astype(f32)


def spread(start, rows):
    pick = selector(start, (SEQUENCE_TOKENS, COMP), 0)
    return jnp.dot(pick, rows, preferred_element_type=f32, precision=lax.Precision.HIGHEST)


def head_rows(ref_value, h):
    first = h * GROUP * HEAD_WIDTH
    return jnp.concatenate(
        [
            ref_value[:, first + g * HEAD_WIDTH : first + (g + 1) * HEAD_WIDTH]
            for g in range(GROUP)
        ],
        axis=0,
    )


def head_lanes(parts):
    return jnp.concatenate(
        [part[g * COMP : (g + 1) * COMP] for part in parts for g in range(GROUP)], axis=1
    )


def attend_kernel(
    start_ref, picked_ref, one_ref, two_ref, cos_ref, sin_ref, cos_rows, sin_rows,
    c_ref, resid_ref, probs_ref, query_ref, key_ref, value_ref, mixed_ref, normed_ref, gains_ref,
    embedded,
):
    start = start_ref[0]
    pick_rows = selector(start, (COMP, SEQUENCE_TOKENS), 1).astype(bf16)
    planes, _, columns = picked_ref.shape
    for p in range(planes):
        embedded[:, p * columns : (p + 1) * columns] = picked_ref[p].astype(f32)
    pick = lax.broadcasted_iota(jnp.int32, (8, 128), 0) + EXPERTS
    pick = (pick == lax.broadcasted_iota(jnp.int32, (8, 128), 1)).astype(f32).astype(bf16)
    gains = dot_across(pick, one_ref[:, HEAD_COLS + KEY_COLS :])
    gains_ref[...] = gains
    x = embedded[...]
    a = (x * inverse_root(x) * gains[0:1]).astype(bf16)
    normed_ref[...] = a
    a_rows = dot(pick_rows, a).astype(bf16)
    cosine, sine = cos_ref[...], sin_ref[...]
    query = turn(dot(a_rows, one_ref[:, :HEAD_COLS]), cos_rows[...], sin_rows[...])
    query = query.astype(bf16)
    key = turn(dot(a, one_ref[:, HEAD_COLS : HEAD_COLS + KEY_COLS]), cosine, sine).astype(bf16)
    value = dot(a, two_ref[:, :KEY_COLS]).astype(bf16)
    query_ref[...], key_ref[...], value_ref[...] = query, key, value
    rows = GROUP * COMP
    place = lax.rem(lax.broadcasted_iota(jnp.int32, (rows, SEQUENCE_TOKENS), 0), COMP) + start
    seen = place >= lax.broadcasted_iota(jnp.int32, (rows, SEQUENCE_TOKENS), 1)
    parts = []
    for h in range(KEY_VALUE_HEADS):
        lanes = slice(h * HEAD_WIDTH, (h + 1) * HEAD_WIDTH)
        scores = dot_across(head_rows(query, h), key[:, lanes]) * ROOT
        scores = jnp.where(seen, scores, -1000000000.0)
        expd = jnp.exp(scores - jnp.max(scores, axis=-1, keepdims=True))
        probs = expd / jnp.sum(expd, axis=-1, keepdims=True)
        probs_ref[h] = probs
        parts.append(dot(probs.astype(bf16), value[:, lanes]))
    mixed = head_lanes(parts).astype(bf16)
    mixed_ref[...] = mixed
    resid = dot(pick_rows, embedded[...].astype(bf16)) + dot(mixed, two_ref[:, KEY_COLS : KEY_COLS + D])
    resid_ref[...] = resid
    c_ref[...] = (resid * inverse_root(resid) * gains[1:2]).astype(bf16)


def attend(start, picked, one, two, *tables):
    vm = pl.BlockSpec(memory_space=pltpu.VMEM)
    rows = GROUP * COMP
    return pl.pallas_call(
        attend_kernel,
        in_specs=[pl.BlockSpec(memory_space=pltpu.SMEM)] + [vm] * 7,
        out_specs=[vm] * 9,
        out_shape=[
            jax.ShapeDtypeStruct((COMP, D), bf16),
            jax.ShapeDtypeStruct((COMP, D), f32),
            jax.ShapeDtypeStruct((KEY_VALUE_HEADS, rows, SEQUENCE_TOKENS), f32),
            jax.ShapeDtypeStruct((COMP, HEAD_COLS), bf16),
            jax.ShapeDtypeStruct((SEQUENCE_TOKENS, KEY_COLS), bf16),
            jax.ShapeDtypeStruct((SEQUENCE_TOKENS, KEY_COLS), bf16),
            jax.ShapeDtypeStruct((COMP, HEAD_COLS), bf16),
            jax.ShapeDtypeStruct((SEQUENCE_TOKENS, D), bf16),
            jax.ShapeDtypeStruct((8, D), f32),
        ],
        scratch_shapes=[pltpu.VMEM((SEQUENCE_TOKENS, D), f32)],
        compiler_params=pltpu.CompilerParams(vmem_limit_bytes=56 << 20),
        name="attend",
    )(start, picked, one, two, *tables)


def attend_back_kernel(
    start_ref, back_ref, gates_ref, grad_two_ref, gain_three_ref, c_ref, resid_ref, probs_ref, query_ref,
    key_ref, value_ref, mixed_ref, normed_ref, gains_ref, picked_ref, one_ref, two_ref, cos_ref, sin_ref, cos_rows, sin_rows,
    out_ref, grad_one_ref, grad_pack_ref,
    total,
):
    start = start_ref[0]
    planes, _, columns = picked_ref.shape
    gains = gains_ref[...]
    wide = HEAD_COLS + KEY_COLS
    gates = gates_ref[...]
    gate_grad = back_ref[:, D:]
    router_grad = gates * (gate_grad - jnp.sum(gates * gate_grad, axis=1, keepdims=True))
    router_grad = router_grad.astype(bf16)
    grad = back_ref[:, :D] + dot_across(router_grad, one_ref[:, wide:])
    grad_resid, gain_two = norm_back(resid_ref[...], gains[1:2], grad)
    grad_resid = grad_resid + grad_two_ref[...]
    branch = grad_resid.astype(bf16)
    grad_mixed = dot_across(branch, two_ref[:, KEY_COLS : KEY_COLS + D]).astype(bf16)
    query, key, value = query_ref[...], key_ref[...], value_ref[...]
    query_parts, key_parts, value_parts = [], [], []
    for h in range(KEY_VALUE_HEADS):
        lanes = slice(h * HEAD_WIDTH, (h + 1) * HEAD_WIDTH)
        probs = probs_ref[h]
        grad_head = head_rows(grad_mixed, h)
        grad_probs = dot_across(grad_head, value[:, lanes]).astype(bf16).astype(f32)
        inner = jnp.sum(grad_probs * probs, axis=-1, keepdims=True)
        grad_scores = probs * (grad_probs - inner)
        value_parts.append(dot(probs.T.astype(bf16), grad_head))
        query_parts.append(dot(grad_scores.astype(bf16), key[:, lanes]) * ROOT)
        key_parts.append(dot(grad_scores.T.astype(bf16), head_rows(query, h)) * ROOT)
    grad_query = turn(head_lanes(query_parts), cos_rows[...], -sin_rows[...]).astype(bf16)
    grad_key = jnp.concatenate(key_parts, axis=1)
    grad_key = turn(grad_key, cos_ref[...], -sin_ref[...]).astype(bf16)
    grad_value = jnp.concatenate(value_parts, axis=1).astype(bf16)
    grad_normed = dot_across(grad_key, one_ref[:, HEAD_COLS:wide])
    grad_normed += dot_across(grad_value, two_ref[:, :KEY_COLS])
    grad_normed += spread(start, dot_across(grad_query, one_ref[:, :HEAD_COLS]))
    for p in range(planes):
        total[:, p * columns : (p + 1) * columns] = picked_ref[p].astype(f32)
    grad_embedded, gain_one = norm_back(total[...], gains[0:1], grad_normed)
    total[...] = grad_embedded + spread(start, grad_resid)
    for p in range(planes):
        out_ref[p] = total[:, p * columns : (p + 1) * columns].astype(bf16)
    pick_rows = selector(start, (COMP, SEQUENCE_TOKENS), 1).astype(bf16)
    a_rows = dot(pick_rows, normed_ref[...])
    turned = normed_ref[...].astype(f32).T.astype(bf16)
    grad_one_ref[:, HEAD_COLS:wide] = dot(turned, grad_key).astype(bf16)
    grad_pack_ref[:, :KEY_COLS] = dot(turned, grad_value).astype(bf16)
    grad_one_ref[:, :HEAD_COLS] = dot(a_rows.T.astype(bf16), grad_query).astype(bf16)
    grad_pack_ref[:, KEY_COLS : KEY_COLS + D] = dot(
        mixed_ref[...].astype(f32).T.astype(bf16), branch
    ).astype(bf16)
    grad_pack_ref[:, KEY_COLS + D :] = jnp.zeros((D, PACK - KEY_COLS - D), bf16)
    left = jnp.concatenate(
        [c_ref[...].astype(f32), gain_one, gain_two, gain_three_ref[...], jnp.zeros((5, D), f32)],
        axis=0,
    )
    lane = lax.broadcasted_iota(jnp.int32, (8, 128), 0) + EXPERTS
    lane = (lane == lax.broadcasted_iota(jnp.int32, (8, 128), 1)).astype(f32)
    right = jnp.concatenate([router_grad.astype(f32), lane], axis=0).astype(bf16)
    grad_one_ref[:, wide:] = dot(left.T.astype(bf16), right).astype(bf16)


def attend_back(start, *operands):
    vm = pl.BlockSpec(memory_space=pltpu.VMEM)
    picked = operands[13]
    return pl.pallas_call(
        attend_back_kernel,
        in_specs=[pl.BlockSpec(memory_space=pltpu.SMEM)] + [vm] * len(operands),
        out_specs=[vm] * 3,
        out_shape=[
            jax.ShapeDtypeStruct(picked.shape, bf16),
            jax.ShapeDtypeStruct((D, PACK), bf16),
            jax.ShapeDtypeStruct((D, PACK), bf16),
        ],
        scratch_shapes=[pltpu.VMEM((SEQUENCE_TOKENS, D), f32)],
        compiler_params=pltpu.CompilerParams(vmem_limit_bytes=60 << 20),
        name="attend_back",
    )(start, *operands)


def lamb_update(weight, moment_one, moment_two, scale_one, scale_two):
    return (moment_one * scale_one) / (jnp.sqrt(moment_two * scale_two) + EPSILON) + DECAY * weight


def lamb_parts(weight, moment_one, moment_two, gradient, scales):
    moment_one = RATE_ONE * moment_one + (1.0 - RATE_ONE) * gradient
    moment_two = RATE_TWO * moment_two + (1.0 - RATE_TWO) * gradient * gradient
    return (moment_one, moment_two, lamb_update(weight, moment_one, moment_two, *scales))


STEPS = 4


def row_lists(tokens, base, rows):
    inside = (tokens >= base) & (tokens < base + rows)
    count = jnp.sum(inside.astype(jnp.int32), axis=1)
    place = jnp.arange(SEQUENCE_TOKENS, dtype=jnp.int32)
    before = (place[:, None] < place[None, :]).astype(bf16)
    rank = jnp.dot(inside.astype(bf16), before, preferred_element_type=f32).astype(jnp.int32)
    packed = place[None, :] * 65536 + (tokens - base)
    hit = inside[:, :, None] & (rank[:, :, None] == place[None, None, :])
    entry = jnp.sum(jnp.where(hit, packed[:, :, None], 0), axis=1)
    empty = SEQUENCE_TOKENS * 65536
    return jnp.where(place[None, :] < count[:, None], entry, empty), count


def gather_kernel(list_ref, count_ref, table_ref, out_ref, rows_ref):
    b = pl.program_id(0)
    rows_ref[...] = jnp.zeros_like(rows_ref)

    def step(k, carry):
        for j in range(STEPS):
            entry = list_ref[b, k * STEPS + j]
            rows_ref[pl.ds(entry >> 16, 1), :] = table_ref[pl.ds(entry & 65535, 1), :]
        return carry

    lax.fori_loop(0, (count_ref[b] + STEPS - 1) // STEPS, step, 0)
    out_ref[0] = rows_ref[:SEQUENCE_TOKENS].astype(bf16)


def gather_rows(lists, counts, table):
    blocks = lists.shape[0]
    rows, columns = table.shape
    return pl.pallas_call(
        gather_kernel,
        grid_spec=pltpu.PrefetchScalarGridSpec(
            num_scalar_prefetch=2,
            grid=(blocks,),
            in_specs=[pl.BlockSpec((rows, columns), lambda b, *_: (0, 0))],
            out_specs=pl.BlockSpec((1, SEQUENCE_TOKENS, columns), lambda b, *_: (b, 0, 0)),
            scratch_shapes=[pltpu.VMEM((SEQUENCE_TOKENS + 8, columns), f32)],
        ),
        out_shape=jax.ShapeDtypeStruct((blocks, SEQUENCE_TOKENS, columns), bf16),
        compiler_params=pltpu.CompilerParams(vmem_limit_bytes=40 << 20),
        name="gather_rows",
    )(lists, counts, table)


def scatter_kernel(list_ref, count_ref, grad_ref, head_ref, out_ref, rows_ref):
    b = pl.program_id(0)

    @pl.when(b == 0)
    def _():
        out_ref[...] = head_ref[...].astype(f32)

    rows_ref[:SEQUENCE_TOKENS] = grad_ref[0].astype(f32)
    rows_ref[SEQUENCE_TOKENS:] = jnp.zeros((8, rows_ref.shape[1]), f32)

    def step(k, carry):
        for j in range(STEPS):
            entry = list_ref[b, k * STEPS + j]
            out_ref[pl.ds(entry & 65535, 1), :] += rows_ref[pl.ds(entry >> 16, 1), :]
        return carry

    lax.fori_loop(0, (count_ref[b] + STEPS - 1) // STEPS, step, 0)


def scatter_rows(lists, counts, grads, head):
    blocks = lists.shape[0]
    rows, columns = head.shape
    return pl.pallas_call(
        scatter_kernel,
        grid_spec=pltpu.PrefetchScalarGridSpec(
            num_scalar_prefetch=2,
            grid=(blocks,),
            in_specs=[
                pl.BlockSpec((1, SEQUENCE_TOKENS, columns), lambda b, *_: (b, 0, 0)),
                pl.BlockSpec((rows, columns), lambda b, *_: (0, 0)),
            ],
            out_specs=pl.BlockSpec((rows, columns), lambda b, *_: (0, 0)),
            scratch_shapes=[pltpu.VMEM((SEQUENCE_TOKENS + 8, columns), f32)],
        ),
        out_shape=jax.ShapeDtypeStruct((rows, columns), f32),
        compiler_params=pltpu.CompilerParams(vmem_limit_bytes=50 << 20),
        name="scatter_rows",
    )(lists, counts, grads, head)


def on_device(
    token_ids,
    positions,
    pair_index,
    ref_logps,
    routes,
    step_count,
    embed_table,
    embed_first,
    embed_second,
    qkv_weight,
    qkv_first,
    qkv_second,
    out_weight,
    out_first,
    out_second,
    router_weight,
    router_first,
    router_second,
    norm_gains,
    gains_first,
    gains_second,
    in_weight,
    in_first,
    in_second,
    down_weight,
    down_first,
    down_second,
):
    shard_id = lax.axis_index("shard")
    expert_id = lax.axis_index("expert")
    shards = lax.axis_size("shard")
    planes = lax.axis_size("expert")
    devices = shards * planes
    vocab_rows, columns = embed_table.shape
    vocab_base = shard_id * vocab_rows
    own_rows = vocab_rows // planes
    local_experts = in_weight.shape[0]
    hidden_units = in_weight.shape[3]
    head_cols = QUERY_HEADS * HEAD_WIDTH
    key_cols = KEY_VALUE_HEADS * HEAD_WIDTH
    rows_all = devices * COMP

    side = math.isqrt(shards // 2)
    grid = (planes, side, side, 2)
    together = devices <= 32

    def send(parts, ident):
        if together:
            return communicate(parts, ident)
        return [
            out for n, part in enumerate(parts) for out in communicate([part], ident + 20 * n)
        ]

    unit = own_rows // 24

    def swap(x, start, size, rounds, back=False, held=None):
        return Swap(x, start * unit, size * unit, planes, side, rounds, back, held)

    def gather_completion(rows, ident, *beside):
        part = Gather([rows], split(0, COMP, rows.shape[1], 2, 2), planes, side)
        out = communicate([part, *beside], ident)
        return (out[0].reshape(rows_all, rows.shape[1]), *out[1:])

    def reduce_completion(rows, ident, cuts, *beside):
        rows = rows.reshape(grid + (COMP, rows.shape[1]))
        part = Reduce([rows], split(0, COMP, rows.shape[-1], 2, cuts), planes, side)
        return communicate([part, *beside], ident)

    def gather_tiny(block, ident):
        return communicate([Tiny(block, planes, side)], ident)[0].reshape((devices,) + block.shape)

    weight_rows = qkv_weight.shape[0]
    weight_cols = PACK
    cuts = 3 if weight_rows % 48 == 0 else 1
    weight_groups = [
        [
            (i, slice(n * (weight_rows // cuts), (n + 1) * (weight_rows // cuts)), slice(0, weight_cols), i == 0)
            for i in range(2)
        ]
        for n in range(cuts)
    ]
    embed_groups = split(0, SEQUENCE_TOKENS, columns, 8, 1)

    own_places = lax.dynamic_index_in_dim(positions, shard_id, 0, keepdims=False)
    start = own_places[0]
    own_tokens = lax.dynamic_slice_in_dim(token_ids, shard_id * SEQUENCE_TOKENS, SEQUENCE_TOKENS, 0)
    own_routes = lax.dynamic_slice_in_dim(routes, start, COMP, 0)
    sheet = jnp.concatenate(
        [
            own_tokens,
            own_routes.reshape(-1),
            own_places,
            jnp.zeros((1024 - SEQUENCE_TOKENS - COMP * TOP - COMP,), jnp.int32),
        ]
    )
    sheets = gather_tiny(sheet.reshape(8, 128), 0).reshape(devices, 1024)
    tokens_all = sheets[:, :SEQUENCE_TOKENS]
    routes_all = sheets[:, SEQUENCE_TOKENS : SEQUENCE_TOKENS + COMP * TOP].reshape(rows_all, TOP)
    places_all = sheets[:, SEQUENCE_TOKENS + COMP * TOP : SEQUENCE_TOKENS + COMP * TOP + COMP]
    spots = jnp.arange(SEQUENCE_TOKENS, dtype=jnp.int32)
    targets = jnp.sum(
        jnp.where(
            places_all[:, :, None] + 1 == spots[None, None, :], tokens_all[:, None, :], 0
        ),
        axis=2,
    ).reshape(-1)

    lists, counts = row_lists(tokens_all, vocab_base, vocab_rows)
    picked = gather_rows(lists, counts, embed_table).reshape(grid + (SEQUENCE_TOKENS, columns))
    packs = [
        jnp.concatenate(
            [
                qkv_weight[:, : head_cols + key_cols],
                router_weight,
                norm_gains.T,
                jnp.zeros((weight_rows, 128 - EXPERTS - 3), f32),
            ],
            axis=1,
        ).astype(bf16),
        jnp.concatenate(
            [
                qkv_weight[:, head_cols + key_cols :],
                out_weight,
                jnp.zeros((weight_rows, 128), f32),
            ],
            axis=1,
        ).astype(bf16),
    ]
    table_b = embed_table.astype(bf16)
    picked, first_pack, second_pack, table_one = send(
        [
            Reduce([picked], embed_groups, planes, side, exchange=True),
            Gather(packs, weight_groups, planes, side),
            swap(table_b, 0, 12, 3),
        ],
        1,
    )
    first_pack = first_pack.reshape(D, weight_cols)
    second_pack = second_pack.reshape(D, weight_cols)

    start_at = start.reshape(1)
    tables = rotary_tables()
    tables += tuple(lax.dynamic_slice_in_dim(table, start, COMP, 0) for table in tables)
    normed_two_b, resid, probs, query, key, value, attended, normed_b, gains = attend(
        start_at, picked, first_pack, second_pack, *tables
    )

    expert_rows, table_own = gather_completion(
        normed_two_b, 2, swap(table_b, 12, 4, 2, held=table_one)
    )
    lanes = shard_id * local_experts + jnp.arange(local_experts, dtype=jnp.int32)
    in_rows = in_weight.reshape(-1, hidden_units)
    produced, mid, gates, in_cat, down_b, gated_hidden = experts_forward(
        lanes, expert_rows, routes_all, first_pack, in_rows, down_weight
    )
    own_index = expert_id * shards + shard_id
    own_gates = lax.dynamic_slice(gates, (own_index * COMP, 0), (COMP, 128))
    combined, table_own = reduce_completion(
        produced, 3, 2, swap(table_b, 16, 4, 0, held=table_own)
    )
    resid_two = resid + combined

    final_rows = resid_two * inverse_root(resid_two) * gains[2:3]
    head_rows, table_own = gather_completion(
        final_rows.astype(bf16), 4, swap(table_b, 20, 4, 2, held=table_own)
    )
    logits = jnp.einsum("rd,vd->rv", head_rows, table_own, preferred_element_type=f32) / LOGIT_SCALE
    own_base = vocab_base + expert_id * own_rows
    target_hot = targets[:, None] == own_base + jnp.arange(own_rows, dtype=jnp.int32)[None, :]
    row_top = jnp.max(logits, axis=1)
    row_total = jnp.sum(jnp.exp(logits - row_top[:, None]), axis=1)
    row_hit = jnp.sum(jnp.where(target_hot, logits, 0.0), axis=1)
    stats = jnp.stack([row_top, row_total, row_hit]).reshape(8, 3 * rows_all // 8)
    stats = gather_tiny(stats, 5).reshape(devices, 3, rows_all)
    top_all = jnp.max(stats[:, 0], axis=0)
    total_all = jnp.sum(stats[:, 1] * jnp.exp(stats[:, 0] - top_all[None]), axis=0)
    row_lse = top_all + jnp.log(total_all)
    seq_sums = jnp.sum((jnp.sum(stats[:, 2], axis=0) - row_lse).reshape(-1, COMP), axis=1)

    sequences = jnp.arange(devices, dtype=jnp.int32)[None, :]
    pair_sign = (pair_index[:, :1] == sequences).astype(f32) - (
        pair_index[:, 1:] == sequences
    ).astype(f32)
    scaled = BETA * jnp.sum(pair_sign * (seq_sums - ref_logps)[None, :], axis=1)
    loss_value = -jnp.mean(jax.nn.log_sigmoid(scaled))
    pair_grad = jax.nn.sigmoid(-scaled) * (-BETA / scaled.shape[0])
    seq_grad = jnp.sum(pair_sign * pair_grad[:, None], axis=0)
    row_grad = jnp.repeat(seq_grad, COMP)
    grad_logits = (
        row_grad[:, None] * (target_hot.astype(f32) - jnp.exp(logits - row_lse[:, None]))
    ).astype(bf16)
    grad_rows = jnp.dot(grad_logits, table_own, preferred_element_type=f32) / LOGIT_SCALE
    head_grad = (
        jnp.einsum("rv,rd->vd", grad_logits, head_rows, preferred_element_type=f32) / LOGIT_SCALE
    ).astype(bf16)
    own_grad_rows, head_back = reduce_completion(
        grad_rows.astype(bf16), 6, 2, swap(head_grad, 0, 5, 0, back=True)
    )
    grad_resid_two, grad_gain_three = norm_back(resid_two, gains[2:3], own_grad_rows)

    grad_all, head_back = gather_completion(
        grad_resid_two.astype(bf16), 7, swap(head_grad, 5, 5, 2, back=True, held=head_back)
    )
    back, mid_grad = experts_backward(lanes, grad_all, mid, gates, in_cat, down_b)
    back, head_back = reduce_completion(
        back, 8, 1, swap(head_grad, 10, 5, 0, back=True, held=head_back)
    )

    grad_embedded, *grad_packs = attend_back(
        start_at,
        back,
        own_gates,
        grad_resid_two,
        grad_gain_three,
        normed_two_b,
        resid,
        probs,
        query,
        key,
        value,
        attended,
        normed_b,
        gains,
        picked,
        first_pack,
        second_pack,
        *tables,
    )
    grad_packs = [pack.reshape(grid + (weight_rows, weight_cols)) for pack in grad_packs]
    wide = head_cols + key_cols
    sent, first_grad, second_grad, head_back = send(
        [
            Gather([grad_embedded], embed_groups, planes, side, exchange=True),
            Reduce(grad_packs, weight_groups, planes, side),
            swap(head_grad, 15, 9, 3, back=True, held=head_back),
        ],
        9,
    )
    table_grad = scatter_rows(
        lists,
        counts,
        sent.reshape(devices, SEQUENCE_TOKENS, columns),
        head_back.reshape(vocab_rows, columns),
    )

    step_value = step_count.astype(f32)
    scales = (1.0 / (1.0 - RATE_ONE**step_value), 1.0 / (1.0 - RATE_TWO**step_value))
    grad_in = jnp.einsum("td,tk->dk", expert_rows, mid_grad, preferred_element_type=f32)
    grad_down = jnp.einsum(
        "tk,td->kd", gated_hidden, grad_all, preferred_element_type=f32
    ).reshape(down_weight.shape)
    in_first_new, in_second_new, in_norms = in_moments(
        jnp.stack(scales),
        grad_in,
        in_rows,
        in_first.reshape(in_rows.shape),
        in_second.reshape(in_rows.shape),
    )
    weights = (embed_table, qkv_weight, out_weight, router_weight, norm_gains, down_weight)
    firsts = (embed_first, qkv_first, out_first, router_first, gains_first, down_first)
    seconds = (embed_second, qkv_second, out_second, router_second, gains_second, down_second)
    gradients = (
        table_grad,
        jnp.concatenate([first_grad[:, :wide], second_grad[:, :key_cols]], axis=1),
        second_grad[:, key_cols : key_cols + D],
        first_grad[:, wide : wide + EXPERTS],
        first_grad[:, wide + EXPERTS : wide + EXPERTS + 3].T,
        grad_down,
    )
    moved = [
        lamb_parts(weight, moment_one, moment_two, gradient, scales)
        for weight, moment_one, moment_two, gradient in zip(weights, firsts, seconds, gradients)
    ]
    partial_norms = [
        (jnp.sum(weight * weight), jnp.sum(parts[2] * parts[2]))
        for weight, parts in zip(weights, moved)
    ]
    partial_norms.insert(5, (jnp.sum(in_norms[0]), jnp.sum(in_norms[1])))
    norm_row = lax.broadcasted_iota(jnp.int32, (8, 128), 0)
    norm_lane = lax.broadcasted_iota(jnp.int32, (8, 128), 1)
    norm_block = jnp.zeros((8, 128), f32)
    for n, pair in enumerate(partial_norms):
        for lane, part in enumerate(pair):
            norm_block = jnp.where((norm_row == n) & (norm_lane == lane), part, norm_block)
    norm_values = jnp.sqrt(jnp.sum(gather_tiny(norm_block, 10), axis=0))[:7, :2]
    trust_ratio = norm_values[:, 0] / norm_values[:, 1]
    moved.insert(
        5, (in_first_new, in_second_new, lamb_update(in_rows, in_first_new, in_second_new, *scales))
    )
    weights = weights[:5] + (in_rows,) + weights[5:]
    results = [loss_value]
    for place, (weight, parts) in enumerate(zip(weights, moved)):
        made = [weight - STEP_RATE * trust_ratio[place] * parts[2], parts[0], parts[1]]
        if place == 5:
            made = [x.reshape(in_weight.shape) for x in made]
        results.extend(made)
    results.append(jnp.stack([norm_values[:, 0], norm_values[:, 1], trust_ratio], axis=1))
    return tuple(results)


def solution(mesh):
    rows = P(BOTH, None)
    vocab = P("shard", "expert")
    gains = P(None, BOTH)
    inner = P("shard", None, None, "expert")
    outer = P("shard", "expert", None)
    state = (vocab,) * 3 + (rows,) * 9 + (gains,) * 3 + (inner,) * 3 + (outer,) * 3
    return jax.shard_map(
        on_device,
        mesh=mesh,
        in_specs=(P("expert"), P("expert", None), P(), P(), rows, P()) + state,
        out_specs=(P(),) + state + (P(),),
        check_vma=False,
    )
```

```python
import functools
import math

import jax
import jax.numpy as jnp
from jax import lax
from jax.experimental import pallas as pl
from jax.experimental.pallas import tpu as pltpu
from jax.sharding import PartitionSpec as P

D = 1536
QUERY_HEADS = 24
KEY_VALUE_HEADS = 8
GROUP = QUERY_HEADS // KEY_VALUE_HEADS
HEAD_WIDTH = 64
TOP = 8
EXPERTS = 32
SEQUENCE_TOKENS = 256
COMP = 32
QKV = 2560

BETA = 0.1
LOGIT_SCALE = 6.0
RATE_ONE = 0.9
RATE_TWO = 0.999
EPSILON = 1e-06
DECAY = 0.01
STEP_RATE = 0.3

BOTH = ("expert", "shard")
bf16 = jnp.bfloat16
f32 = jnp.float32


MESH = pl.DeviceIdType.MESH


class Spot:
    def __init__(self, planes, side):
        self.planes, self.side = planes, side
        self.z = lax.axis_index("expert")
        self.shard = lax.axis_index("shard")
        self.core = lax.rem(self.shard, 2)
        self.b = lax.rem(lax.div(self.shard, 2), side)
        self.a = lax.div(self.shard, 2 * side)

    def plane(self, k):
        z = lax.rem(self.z + k, self.planes)
        return z, (z, self.shard)

    def along_a(self, k):
        a = lax.rem(self.a + k, self.side)
        return a, (self.z, (a * self.side + self.b) * 2 + self.core)

    def along_b(self, k):
        b = lax.rem(self.b + k, self.side)
        return b, (self.z, (self.a * self.side + b) * 2 + self.core)

    def along(self, first, k):
        return self.along_a(k) if first else self.along_b(k)

    def mate(self):
        other = 1 - self.core
        return other, (self.z, (self.a * self.side + self.b) * 2 + other)

    def near(self, k):
        return self.z, lax.rem(self.shard + k, 2 * self.side * self.side)

    def greet(self, flat):
        targets = [self.plane(k)[1] for k in range(1, self.planes)]
        if flat:
            targets += [self.near(k) for k in range(1, 2 * self.side * self.side)]
        else:
            targets.append(self.mate()[1])
            for k in range(1, self.side):
                targets += [self.along_a(k)[1], self.along_b(k)[1]]
        barrier = pltpu.get_barrier_semaphore()
        for target in targets:
            pl.semaphore_signal(barrier, inc=1, device_id=target, device_id_type=MESH)
        pl.semaphore_wait(barrier, len(targets))


class Mail:
    def __init__(self, send, recv):
        self.send, self.recv, self.count, self.open = send, recv, 0, []

    def start(self, src, dst, target):
        copy = pltpu.make_async_remote_copy(
            src_ref=src,
            dst_ref=dst,
            send_sem=self.send.at[self.count],
            recv_sem=self.recv.at[self.count],
            device_id=target,
            device_id_type=MESH,
        )
        self.count += 1
        copy.start()
        self.open.append(copy)
        return copy

    def finish(self):
        for copy in self.open:
            copy.wait_send()


def arrive(copies):
    for copy in copies:
        copy.wait_recv()


class Tiny:
    flat = True
    scratch = ()

    def __init__(self, x, planes, side):
        self.planes, self.side, self.inputs = planes, side, [x]
        shape = (planes, 2 * side * side) + x.shape
        self.outputs = [jax.ShapeDtypeStruct(shape, x.dtype)]
        self.copies = planes + 2 * side * side - 2

    def steps(self, spot, mail, x, out):
        out[spot.z, spot.shard] = x[...]
        sent = []
        for k in range(1, self.planes):
            sent.append(mail.start(x, out.at[spot.z, spot.shard], spot.plane(k)[1]))
        yield
        arrive(sent)
        part = out.at[:, spot.shard]
        yield
        arrive([mail.start(part, part, spot.near(k)) for k in range(1, 2 * self.side**2)])


def split(array, rows, columns, row_parts, column_parts):
    r, c = rows // row_parts, columns // column_parts
    cuts = [
        (array, slice(i * r, i * r + r), slice(j * c, j * c + c))
        for j in range(column_parts)
        for i in range(row_parts)
    ]
    cuts = [cut + (n % 2 == 0,) for n, cut in enumerate(cuts)]
    return [cuts[n : n + 2] for n in range(0, len(cuts), 2)]


def pipeline(groups, stage, last):
    sent = [[[] for _ in group] for group in groups]
    for tick in range(len(groups) + last):
        for step in range(last, -1, -1):
            turn = tick - step
            if 0 <= turn < len(groups):
                for n, cut in enumerate(groups[turn]):
                    for copy in sent[turn][n]:
                        copy.wait_recv()
                    sent[turn][n] = stage(step, (turn, n), cut)
        yield


class Gather:
    flat = False
    scratch = ()

    def __init__(self, xs, groups, planes, side, exchange=False, prior=False):
        self.planes, self.side, self.inputs, self.groups = planes, side, xs, groups
        self.exchange, self.prior = exchange, prior
        grid = (planes, side, side, 2)
        self.outputs = [jax.ShapeDtypeStruct(grid + x.shape[-2:], x.dtype) for x in xs]
        self.copies = sum(map(len, groups)) * (planes - 1 + 2 * (side - 1) + 1)

    def steps(self, spot, mail, *refs):
        xs, outs = refs[: len(self.inputs)], refs[len(self.inputs) :]
        z, a, b, core = spot.z, spot.a, spot.b, spot.core
        for x, out in zip(xs, outs):
            if self.prior:
                out[:, a, b, core] = x[...]
            else:
                out[z, a, b, core] = x[z] if self.exchange else x[...]

        def stage(step, key, cut):
            i, rows, columns, first = cut
            x, out = xs[i], outs[i]
            if step == 0 and self.prior:
                return []
            if step == 0:
                place = out.at[z, a, b, core, rows, columns]
                sent = []
                for k in range(1, self.planes):
                    peer, target = spot.plane(k)
                    own = x.at[peer, rows, columns] if self.exchange else x.at[rows, columns]
                    sent.append(mail.start(own, place, target))
                return sent
            if step in (1, 2):
                if step == 1:
                    part = out.at[:, a, b, core, rows, columns]
                elif first:
                    part = out.at[:, :, b, core, rows, columns]
                else:
                    part = out.at[:, a, :, core, rows, columns]
                return [
                    mail.start(part, part, spot.along(first == (step == 1), k)[1])
                    for k in range(1, self.side)
                ]
            if step == 3:
                part = out.at[:, :, :, core, rows, columns]
                return [mail.start(part, part, spot.mate()[1])]
            return []

        return pipeline(self.groups, stage, 4)


class Reduce:
    flat = False

    def __init__(self, xs, groups, planes, side, exchange=False, partial=False):
        self.planes, self.side, self.inputs, self.groups = planes, side, xs, groups
        self.exchange, self.partial = exchange or partial, partial
        self.outputs = [
            jax.ShapeDtypeStruct((planes,) + x.shape[-2:], x.dtype)
            if self.exchange
            else jax.ShapeDtypeStruct(x.shape[-2:], f32)
            for x in xs
        ]
        self.scratch = []
        for i, rows, columns, _ in [cut for group in groups for cut in group]:
            block = (rows.stop - rows.start, columns.stop - columns.start)
            self.scratch += [
                pltpu.VMEM(shape + block, xs[i].dtype)
                for shape in (
                    (planes, side, side),
                    (side - 1, planes, side),
                    (planes, side),
                    (side - 1, planes),
                    (planes,),
                )
                + (() if self.exchange else ((planes - 1,),))
            ]
        self.copies = sum(map(len, groups)) * (planes - 1 + 2 * (side - 1) + 1)

    def steps(self, spot, mail, *refs):
        planes, side, number = self.planes, self.side, len(self.inputs)
        xs, outs, rest = refs[:number], refs[number : 2 * number], refs[2 * number :]
        each = 5 if self.exchange else 6
        order = [(t, n) for t, group in enumerate(self.groups) for n in range(len(group))]
        held = {key: rest[each * p : each * (p + 1)] for p, key in enumerate(order)}
        core, z = spot.core, spot.z
        other, mate = spot.mate()

        def stage(step, key, cut):
            i, rows, columns, first = cut
            x, out = xs[i], outs[i]
            one, hop_two, two, hop_three, three = held[key][:5]
            if step == 0:
                return [mail.start(x.at[:, :, :, other, rows, columns], one, mate)]
            sent = []
            if step == 1:

                def add(n, carry):
                    ia, ib = lax.rem(lax.div(n, side), side), lax.rem(n, side)
                    iz = lax.div(n, side * side)
                    total = x[iz, ia, ib, core, rows, columns].astype(f32)
                    one[iz, ia, ib] = (total + one[iz, ia, ib].astype(f32)).astype(one.dtype)
                    return carry

                lax.fori_loop(0, planes * side * side, add, 0)
                for k in range(1, side):
                    peer, target = spot.along(first, k)
                    part = one.at[:, peer] if first else one.at[:, :, peer]
                    sent.append(mail.start(part, hop_two.at[k - 1], target))
            elif step == 2:

                def add(n, carry):
                    iz, ir = lax.div(n, side), lax.rem(n, side)
                    total = (one[iz, spot.a, ir] if first else one[iz, ir, spot.b]).astype(f32)
                    for k in range(side - 1):
                        total += hop_two[k, iz, ir].astype(f32)
                    two[iz, ir] = total.astype(two.dtype)
                    return carry

                lax.fori_loop(0, planes * side, add, 0)
                for k in range(1, side):
                    peer, target = spot.along(not first, k)
                    sent.append(mail.start(two.at[:, peer], hop_three.at[k - 1], target))
            elif step == 3:
                mine = spot.b if first else spot.a

                def add(iz, carry):
                    total = two[iz, mine].astype(f32)
                    for k in range(side - 1):
                        total += hop_three[k, iz].astype(f32)
                    if self.partial:
                        out[iz, rows, columns] = total.astype(out.dtype)
                    else:
                        three[iz] = total.astype(three.dtype)
                    return carry

                lax.fori_loop(0, planes, add, 0)
                if self.partial:
                    return []
                for k in range(1, planes):
                    peer, target = spot.plane(k)
                    if self.exchange:
                        place = out.at[z, rows, columns]
                    else:
                        place = held[key][5].at[k - 1]
                    sent.append(mail.start(three.at[peer], place, target))
                if self.exchange:
                    out[z, rows, columns] = three[z]
            elif not self.exchange:
                total = three[z].astype(f32)
                for k in range(planes - 1):
                    total += held[key][5][k].astype(f32)
                out[rows, columns] = total
            return sent

        return pipeline(self.groups, stage, 4)


class Swap:
    flat = False
    def __init__(self, x, turns, planes, side, back=False, held=None):
        self.planes, self.side = planes, side
        self.inputs = [x] if held is None else [x, held]
        self.in_spaces, self.out_spaces = (pl.ANY,) * len(self.inputs), (pl.ANY,)
        self.aliases = {} if held is None else {1: 0}
        self.turns, self.back = turns, back
        self.scratch = [pltpu.SemaphoreType.DMA((len(turns),))]
        self.columns = x.shape[1] // planes if back else x.shape[1]
        self.rows = x.shape[0] if back else x.shape[0] // planes
        shape = (planes, self.rows, self.columns) if back else (self.rows, planes * self.columns)
        self.outputs = [jax.ShapeDtypeStruct(shape, x.dtype)]
        self.copies = len(turns) * (planes - 1)

    def steps(self, spot, mail, *refs):
        x, out, own_sem = refs[0], refs[-2], refs[-1]
        def block(z):
            return pl.ds(pl.multiple_of(z * self.columns, 128), self.columns)

        def source(z, begin, size):
            if self.back:
                return x.at[pl.ds(begin, size), block(z)]
            return x.at[pl.ds(pl.multiple_of(z * self.rows + begin, 16), size), :]

        sent, own, now = [], [], 0
        for n, (begin, size, rounds) in enumerate(self.turns):
            while now < rounds:
                now += 1
                yield
            rows = pl.ds(begin, size)
            place = out.at[spot.z, rows] if self.back else out.at[rows, block(spot.z)]
            for k in range(1, self.planes):
                peer, target = spot.plane(k)
                sent.append(mail.start(source(peer, begin, size), place, target))
            own.append(pltpu.make_async_copy(source(spot.z, begin, size), place, own_sem.at[n]))
            own[-1].start()
        while now < 24:
            now += 1
            yield
        for copy in own:
            copy.wait()
        for copy in sent:
            copy.wait_recv()


class Chain:
    flat = False

    def __init__(self, reduce, extra, extra_out, middle, gather):
        self.planes, self.side = reduce.planes, reduce.side
        self.reduce, self.middle, self.gather = reduce, middle, gather
        self.inputs = reduce.inputs + extra
        self.outputs = gather.outputs + extra_out
        self.scratch = reduce.scratch + [
            pltpu.VMEM(x.shape, x.dtype) for x in reduce.outputs + gather.inputs
        ]
        self.copies = reduce.copies + gather.copies

    def steps(self, spot, mail, *refs):
        n_in, n_out = len(self.inputs), len(self.outputs)
        (x, *extra), (out, *extra_out) = refs[:n_in], refs[n_in : n_in + n_out]
        *held, sums, made = refs[n_in + n_out :]
        yield from self.reduce.steps(spot, mail, x, sums, *held)
        self.middle(sums, made, *extra, *extra_out)
        yield from self.gather.steps(spot, mail, made, out)


def final_norm(sums, made, resid, gains, resid_two):
    values = resid[...] + sums[...]
    resid_two[...] = values
    made[...] = (values * inverse_root(values) * gains[2:3]).astype(bf16)


def final_norm_back(sums, made, resid_two, gains, grad_two, gain_grad):
    grad, gain_grad[...] = norm_back(resid_two[...], gains[2:3], sums[...])
    grad_two[...] = grad
    made[...] = grad.astype(bf16)


def communicate(parts, ident):
    planes, side = parts[0].planes, parts[0].side
    counts = [(len(p.inputs), len(p.outputs), len(p.scratch)) for p in parts]
    n_in, n_out = (sum(c[i] for c in counts) for i in range(2))
    copies = sum(p.copies for p in parts)
    aliases, i, o = {}, 0, 0
    for part, (ci, co, _) in zip(parts, counts):
        aliases.update({i + a: o + b for a, b in getattr(part, "aliases", {}).items()})
        i, o = i + ci, o + co

    def kernel(*refs):
        ins, outs, rest = refs[:n_in], refs[n_in : n_in + n_out], refs[n_in + n_out :]
        send, recv = rest[-2:]
        spot = Spot(planes, side)
        spot.greet(parts[0].flat)
        mail = Mail(send, recv)
        running, i, o, s = [], 0, 0, 0
        for part, (ci, co, cs) in zip(parts, counts):
            running.append(
                part.steps(spot, mail, *ins[i : i + ci], *outs[o : o + co], *rest[s : s + cs])
            )
            i, o, s = i + ci, o + co, s + cs
        while running:
            running = [steps for steps in running if next(steps, True) is None]
        mail.finish()

    size = sum(x.size * x.dtype.itemsize for p in parts for x in p.inputs + p.outputs)
    out = pl.pallas_call(
        kernel,
        out_shape=[x for p in parts for x in p.outputs],
        in_specs=[
            pl.BlockSpec(memory_space=space)
            for p in parts
            for space in getattr(p, "in_spaces", (pltpu.VMEM,) * len(p.inputs))
        ],
        out_specs=[
            pl.BlockSpec(memory_space=space)
            for p in parts
            for space in getattr(p, "out_spaces", (pltpu.VMEM,) * len(p.outputs))
        ],
        input_output_aliases=aliases,
        scratch_shapes=[s for p in parts for s in p.scratch]
        + [pltpu.SemaphoreType.DMA((copies,)), pltpu.SemaphoreType.DMA((copies,))],
        compiler_params=pltpu.CompilerParams(
            collective_id=ident, has_side_effects=True, vmem_limit_bytes=62 << 20
        ),
        cost_estimate=pl.CostEstimate(flops=0, bytes_accessed=20 * size, transcendentals=0),
        name="exchange_" + str(ident),
    )(*[x for p in parts for x in p.inputs])
    return list(out)

def expert_gate(gates, lane):
    lanes = lax.broadcasted_iota(jnp.int32, gates.shape, 1)
    return jnp.sum(jnp.where(lanes == lane, gates, 0.0), axis=1, keepdims=True)


CHUNK = 512
BLOCK = 1024
ACROSS = (((1,), (1,)), ((), ()))


def forward_kernel(
    lane_ref, rows_ref, routes_ref, router_ref, in_ref, down_ref, out_ref, mid_ref, gates_ref, cat_ref, down_out, hidden_ref
):
    e, number = pl.program_id(1), pl.num_programs(1)
    units = in_ref.shape[1]
    for j in range(2):
        cat_ref[:, j * units : (j + 1) * units] = in_ref[pl.ds(j, D, stride=2), :].astype(bf16)
    down_out[pl.ds(pl.multiple_of(e * units, units), units), :] = down_ref[0].astype(bf16)

    def chunk(i, carry):
        here = pl.ds(pl.multiple_of(i * CHUNK, CHUNK), CHUNK)
        rows = rows_ref[here, :]

        @pl.when(e == 0)
        def _():
            logits = jnp.dot(rows, router_ref[...], preferred_element_type=f32)
            lanes = lax.broadcasted_iota(jnp.int32, logits.shape, 1)
            mask = lanes == routes_ref[here, 0:1]
            for j in range(1, TOP):
                mask |= lanes == routes_ref[here, j : j + 1]
            top = jnp.max(jnp.where(mask, logits, -3e38), axis=1, keepdims=True)
            weight = jnp.where(mask, jnp.exp(jnp.where(mask, logits - top, 0.0)), 0.0)
            gates_ref[here, :] = weight / jnp.sum(weight, axis=1, keepdims=True)

        mid = jnp.dot(rows, cat_ref[...], preferred_element_type=f32)
        mid_ref[here, :] = mid
        gate, up = mid[:, :units], mid[:, units:]
        hidden = (gate * jax.nn.sigmoid(gate) * up).astype(bf16).astype(f32)
        hidden = (hidden * expert_gate(gates_ref[here, :], lane_ref[0] + e)).astype(bf16)
        hidden_ref[here, pl.ds(pl.multiple_of(e * units, units), units)] = hidden

        @pl.when(e == number - 1)
        def _():
            out_ref[here, :] = jnp.dot(
                hidden_ref[here, :], down_out[...], preferred_element_type=f32
            ).astype(bf16)

        return carry

    lax.fori_loop(0, rows_ref.shape[0] // CHUNK, chunk, 0)


def experts_forward(lane, rows, routes, router, in_rows, down):
    number, units = down.shape[:2]
    total = rows.shape[0]
    block = min(total, BLOCK)
    row = lambda r, e, *_: (r, 0)
    still = lambda r, e, *_: (0, 0)
    return pl.pallas_call(
        forward_kernel,
        grid_spec=pltpu.PrefetchScalarGridSpec(
            num_scalar_prefetch=1,
            grid=(total // block, number),
            in_specs=[
                pl.BlockSpec((block, D), row),
                pl.BlockSpec((block, TOP), row),
                pl.BlockSpec((D, 128), lambda r, e, *_: (0, PACK // 128 - 1)),
                pl.BlockSpec((2 * D, units), lambda r, e, *_: (e, 0)),
                pl.BlockSpec((1, units, D), lambda r, e, *_: (e, 0, 0)),
            ],
            out_specs=[
                pl.BlockSpec((block, D), row),
                pl.BlockSpec((block, 2 * units), lambda r, e, *_: (r, e)),
                pl.BlockSpec((block, 128), row),
                pl.BlockSpec((D, 2 * units), lambda r, e, *_: (0, e)),
                pl.BlockSpec((number * units, D), still),
                pl.BlockSpec((block, number * units), row),
            ],
        ),
        out_shape=[
            jax.ShapeDtypeStruct((total, D), bf16),
            jax.ShapeDtypeStruct((total, 2 * units * number), f32),
            jax.ShapeDtypeStruct((total, 128), f32),
            jax.ShapeDtypeStruct((D, 2 * units * number), bf16),
            jax.ShapeDtypeStruct((number * units, D), bf16),
            jax.ShapeDtypeStruct((total, number * units), bf16),
        ],
        compiler_params=pltpu.CompilerParams(vmem_limit_bytes=60 << 20),
        name="experts_forward",
    )(lane, rows, routes, router, in_rows, down)


def backward_kernel(
    lane_ref, grad_ref, mid_ref, gates_ref, cat_ref, down_ref, out_ref, mid_grad_ref, pulled_ref
):
    number = lane_ref.shape[0]
    units = pulled_ref.shape[1] // number

    def chunk(i, carry):
        here = pl.ds(pl.multiple_of(i * CHUNK, CHUNK), CHUNK)
        pulled_ref[...] = lax.dot_general(
            grad_ref[here, :], down_ref[...], ACROSS, preferred_element_type=f32
        )
        lanes = lax.broadcasted_iota(jnp.int32, (CHUNK, 128), 1)
        gate_part = jnp.zeros((CHUNK, 128), f32)
        for e in range(number):
            lane = lane_ref[e]
            weight = expert_gate(gates_ref[here, :], lane)
            gate = mid_ref[here, 2 * e * units : (2 * e + 1) * units]
            up = mid_ref[here, (2 * e + 1) * units : (2 * e + 2) * units]
            pulled = pulled_ref[:, e * units : (e + 1) * units]
            soft = jax.nn.sigmoid(gate)
            silu = gate * soft
            hidden = (silu * up).astype(bf16).astype(f32)
            gate_grad = jnp.sum(hidden * pulled, axis=1, keepdims=True)
            gate_part = jnp.where(lanes == lane, gate_grad, gate_part)
            hidden_grad = (pulled * weight).astype(bf16).astype(f32)
            turned = hidden_grad * up * (soft * (1.0 + gate * (1.0 - soft)))
            mid_grad_ref[here, 2 * e * units : (2 * e + 1) * units] = turned.astype(bf16)
            mid_grad_ref[here, (2 * e + 1) * units : (2 * e + 2) * units] = (
                hidden_grad * silu
            ).astype(bf16)
        out_ref[here, D:] = gate_part.astype(bf16)
        out_ref[here, :D] = lax.dot_general(
            mid_grad_ref[here, :], cat_ref[...], ACROSS, preferred_element_type=f32
        ).astype(bf16)
        return carry

    lax.fori_loop(0, grad_ref.shape[0] // CHUNK, chunk, 0)


def experts_backward(lanes, grad, mid, gates, cat, down):
    number = lanes.shape[0]
    total = grad.shape[0]
    block = min(total, BLOCK)
    row = lambda r, *_: (r, 0)
    still = lambda r, *_: (0, 0)
    return pl.pallas_call(
        backward_kernel,
        grid_spec=pltpu.PrefetchScalarGridSpec(
            num_scalar_prefetch=1,
            grid=(total // block,),
            in_specs=[
                pl.BlockSpec((block, D), row),
                pl.BlockSpec((block, mid.shape[1]), row),
                pl.BlockSpec((block, 128), row),
                pl.BlockSpec(cat.shape, still),
                pl.BlockSpec(down.shape, still),
            ],
            out_specs=[
                pl.BlockSpec((block, D + 128), row),
                pl.BlockSpec((block, mid.shape[1]), row),
            ],
            scratch_shapes=[pltpu.VMEM((CHUNK, down.shape[0]), f32)],
        ),
        out_shape=[
            jax.ShapeDtypeStruct((total, D + 128), bf16),
            jax.ShapeDtypeStruct(mid.shape, bf16),
        ],
        compiler_params=pltpu.CompilerParams(vmem_limit_bytes=60 << 20),
        name="experts_backward",
    )(lanes, grad, mid, gates, cat, down)


def moments_kernel(scale_ref, grad_ref, w_ref, first_ref, second_ref, new_first, new_second, norms):
    units = w_ref.shape[1]
    part = w_ref.shape[0] // 2

    @pl.when((pl.program_id(0) == 0) & (pl.program_id(1) == 0))
    def _():
        norms[...] = jnp.zeros_like(norms)

    for j in range(2):
        here = pl.ds(j, part, stride=2)
        grad = grad_ref[:, j * units : (j + 1) * units]
        weight = w_ref[here, :]
        one = RATE_ONE * first_ref[here, :] + (1.0 - RATE_ONE) * grad
        two = RATE_TWO * second_ref[here, :] + (1.0 - RATE_TWO) * grad * grad
        update = lamb_update(weight, one, two, scale_ref[0], scale_ref[1])
        new_first[here, :] = one
        new_second[here, :] = two
        norms[0] += jnp.sum((weight * weight).reshape(-1, 8, units), axis=0)
        norms[1] += jnp.sum((update * update).reshape(-1, 8, units), axis=0)


def in_moments(scales, grad, weight, first, second):
    units = weight.shape[1]
    number = grad.shape[1] // (2 * units)
    parts = 2
    row = pl.BlockSpec((2 * D // parts, units), lambda e, p, *_: (e * parts + p, 0))
    return pl.pallas_call(
        moments_kernel,
        grid_spec=pltpu.PrefetchScalarGridSpec(
            num_scalar_prefetch=1,
            grid=(number, parts),
            in_specs=[pl.BlockSpec((D // parts, 2 * units), lambda e, p, *_: (p, e)), row, row, row],
            out_specs=[row, row, pl.BlockSpec((2, 8, units), lambda e, p, *_: (0, 0, 0))],
        ),
        out_shape=[jax.ShapeDtypeStruct(weight.shape, f32)] * 2
        + [jax.ShapeDtypeStruct((2, 8, units), f32)],
        compiler_params=pltpu.CompilerParams(vmem_limit_bytes=40 << 20),
        name="in_moments",
    )(scales, grad, weight, first, second)


HEAD_COLS = QUERY_HEADS * HEAD_WIDTH
KEY_COLS = KEY_VALUE_HEADS * HEAD_WIDTH
PACK = HEAD_COLS + KEY_COLS + 128
ROOT = HEAD_WIDTH ** (-0.5)


def turn(u, cosine, sine):
    width = u.shape[1]
    lanes = lax.broadcasted_iota(jnp.int32, u.shape, 1)
    ahead = pltpu.roll(u, width - HEAD_WIDTH // 2, 1)
    behind = pltpu.roll(u, HEAD_WIDTH // 2, 1)
    other = jnp.where(lax.rem(lanes, HEAD_WIDTH) < HEAD_WIDTH // 2, ahead, behind)
    return u * jnp.tile(cosine, (1, width // 128)) + other * jnp.tile(sine, (1, width // 128))


def rotary_tables():
    half = HEAD_WIDTH // 2
    freqs = jnp.exp(-jnp.log(10000.0) * jnp.arange(half, dtype=f32) / half)
    angles = jnp.arange(SEQUENCE_TOKENS, dtype=f32)[:, None] * freqs[None, :]
    cosine, sine = jnp.cos(angles), jnp.sin(angles)
    return jnp.tile(cosine, (1, 4)), jnp.tile(jnp.concatenate([-sine, sine], axis=1), (1, 2))


def inverse_root(values):
    return lax.rsqrt(jnp.mean(values * values, axis=-1, keepdims=True) + 1e-06)


def norm_back(values, gain, grad):
    root = inverse_root(values)
    scaled = grad * gain
    inner = jnp.mean(scaled * values, axis=-1, keepdims=True)
    return root * scaled - values * (root * root * root * inner), jnp.sum(
        grad * values * root, axis=0, keepdims=True
    )


def dot(a, b):
    return jnp.dot(a, b, preferred_element_type=f32)


def dot_across(a, b):
    return lax.dot_general(a, b, ACROSS, preferred_element_type=f32)


def selector(start, shape, axis):
    row = lax.broadcasted_iota(jnp.int32, shape, 1 - axis) + start
    return (row == lax.broadcasted_iota(jnp.int32, shape, axis)).astype(f32)


def spread(start, rows):
    pick = selector(start, (SEQUENCE_TOKENS, COMP), 0)
    return jnp.dot(pick, rows, preferred_element_type=f32, precision=lax.Precision.HIGHEST)


def head_rows(ref_value, h):
    first = h * GROUP * HEAD_WIDTH
    return jnp.concatenate(
        [
            ref_value[:, first + g * HEAD_WIDTH : first + (g + 1) * HEAD_WIDTH]
            for g in range(GROUP)
        ],
        axis=0,
    )


def head_lanes(parts):
    return jnp.concatenate(
        [part[g * COMP : (g + 1) * COMP] for part in parts for g in range(GROUP)], axis=1
    )


def attend_kernel(
    start_ref, picked_ref, one_ref, two_ref, cos_ref, sin_ref, cos_rows, sin_rows,
    c_ref, resid_ref, probs_ref, query_ref, key_ref, value_ref, mixed_ref, normed_ref, gains_ref,
    embedded,
):
    start = start_ref[0]
    pick_rows = selector(start, (COMP, SEQUENCE_TOKENS), 1).astype(bf16)
    planes, _, columns = picked_ref.shape
    for p in range(planes):
        embedded[:, p * columns : (p + 1) * columns] = picked_ref[p].astype(f32)
    pick = lax.broadcasted_iota(jnp.int32, (8, 128), 0) + EXPERTS
    pick = (pick == lax.broadcasted_iota(jnp.int32, (8, 128), 1)).astype(f32).astype(bf16)
    gains = dot_across(pick, one_ref[:, HEAD_COLS + KEY_COLS :])
    gains_ref[...] = gains
    x = embedded[...]
    a = (x * inverse_root(x) * gains[0:1]).astype(bf16)
    normed_ref[...] = a
    a_rows = dot(pick_rows, a).astype(bf16)
    cosine, sine = cos_ref[...], sin_ref[...]
    query = turn(dot(a_rows, one_ref[:, :HEAD_COLS]), cos_rows[...], sin_rows[...])
    query = query.astype(bf16)
    key = turn(dot(a, one_ref[:, HEAD_COLS : HEAD_COLS + KEY_COLS]), cosine, sine).astype(bf16)
    value = dot(a, two_ref[:, :KEY_COLS]).astype(bf16)
    query_ref[...], key_ref[...], value_ref[...] = query, key, value
    rows = GROUP * COMP
    place = lax.rem(lax.broadcasted_iota(jnp.int32, (rows, SEQUENCE_TOKENS), 0), COMP) + start
    seen = place >= lax.broadcasted_iota(jnp.int32, (rows, SEQUENCE_TOKENS), 1)
    parts = []
    for h in range(KEY_VALUE_HEADS):
        lanes = slice(h * HEAD_WIDTH, (h + 1) * HEAD_WIDTH)
        scores = dot_across(head_rows(query, h), key[:, lanes]) * ROOT
        scores = jnp.where(seen, scores, -1000000000.0)
        expd = jnp.exp(scores - jnp.max(scores, axis=-1, keepdims=True))
        probs = expd / jnp.sum(expd, axis=-1, keepdims=True)
        probs_ref[h] = probs
        parts.append(dot(probs.astype(bf16), value[:, lanes]))
    mixed = head_lanes(parts).astype(bf16)
    mixed_ref[...] = mixed
    resid = dot(pick_rows, embedded[...].astype(bf16)) + dot(mixed, two_ref[:, KEY_COLS : KEY_COLS + D])
    resid_ref[...] = resid
    c_ref[...] = (resid * inverse_root(resid) * gains[1:2]).astype(bf16)


def attend(start, picked, one, two, *tables):
    vm = pl.BlockSpec(memory_space=pltpu.VMEM)
    rows = GROUP * COMP
    return pl.pallas_call(
        attend_kernel,
        in_specs=[pl.BlockSpec(memory_space=pltpu.SMEM)] + [vm] * 7,
        out_specs=[vm] * 9,
        out_shape=[
            jax.ShapeDtypeStruct((COMP, D), bf16),
            jax.ShapeDtypeStruct((COMP, D), f32),
            jax.ShapeDtypeStruct((KEY_VALUE_HEADS, rows, SEQUENCE_TOKENS), f32),
            jax.ShapeDtypeStruct((COMP, HEAD_COLS), bf16),
            jax.ShapeDtypeStruct((SEQUENCE_TOKENS, KEY_COLS), bf16),
            jax.ShapeDtypeStruct((SEQUENCE_TOKENS, KEY_COLS), bf16),
            jax.ShapeDtypeStruct((COMP, HEAD_COLS), bf16),
            jax.ShapeDtypeStruct((SEQUENCE_TOKENS, D), bf16),
            jax.ShapeDtypeStruct((8, D), f32),
        ],
        scratch_shapes=[pltpu.VMEM((SEQUENCE_TOKENS, D), f32)],
        compiler_params=pltpu.CompilerParams(vmem_limit_bytes=56 << 20),
        name="attend",
    )(start, picked, one, two, *tables)


def attend_back_kernel(
    start_ref, back_ref, gates_ref, grad_two_ref, gain_three_ref, c_ref, resid_ref, probs_ref, query_ref,
    key_ref, value_ref, mixed_ref, normed_ref, gains_ref, picked_ref, one_ref, two_ref, cos_ref, sin_ref, cos_rows, sin_rows,
    out_ref, grad_one_ref, grad_pack_ref,
    total,
):
    start = start_ref[0]
    planes, _, columns = picked_ref.shape
    gains = gains_ref[...]
    wide = HEAD_COLS + KEY_COLS
    gates = gates_ref[...]
    gate_grad = back_ref[:, D:]
    router_grad = gates * (gate_grad - jnp.sum(gates * gate_grad, axis=1, keepdims=True))
    router_grad = router_grad.astype(bf16)
    grad = back_ref[:, :D] + dot_across(router_grad, one_ref[:, wide:])
    grad_resid, gain_two = norm_back(resid_ref[...], gains[1:2], grad)
    grad_resid = grad_resid + grad_two_ref[...]
    branch = grad_resid.astype(bf16)
    grad_mixed = dot_across(branch, two_ref[:, KEY_COLS : KEY_COLS + D]).astype(bf16)
    query, key, value = query_ref[...], key_ref[...], value_ref[...]
    query_parts, key_parts, value_parts = [], [], []
    for h in range(KEY_VALUE_HEADS):
        lanes = slice(h * HEAD_WIDTH, (h + 1) * HEAD_WIDTH)
        probs = probs_ref[h]
        grad_head = head_rows(grad_mixed, h)
        grad_probs = dot_across(grad_head, value[:, lanes]).astype(bf16).astype(f32)
        inner = jnp.sum(grad_probs * probs, axis=-1, keepdims=True)
        grad_scores = probs * (grad_probs - inner)
        value_parts.append(dot(probs.T.astype(bf16), grad_head))
        query_parts.append(dot(grad_scores.astype(bf16), key[:, lanes]) * ROOT)
        key_parts.append(dot(grad_scores.T.astype(bf16), head_rows(query, h)) * ROOT)
    grad_query = turn(head_lanes(query_parts), cos_rows[...], -sin_rows[...]).astype(bf16)
    grad_key = jnp.concatenate(key_parts, axis=1)
    grad_key = turn(grad_key, cos_ref[...], -sin_ref[...]).astype(bf16)
    grad_value = jnp.concatenate(value_parts, axis=1).astype(bf16)
    grad_normed = dot_across(grad_key, one_ref[:, HEAD_COLS:wide])
    grad_normed += dot_across(grad_value, two_ref[:, :KEY_COLS])
    grad_normed += spread(start, dot_across(grad_query, one_ref[:, :HEAD_COLS]))
    for p in range(planes):
        total[:, p * columns : (p + 1) * columns] = picked_ref[p].astype(f32)
    grad_embedded, gain_one = norm_back(total[...], gains[0:1], grad_normed)
    total[...] = grad_embedded + spread(start, grad_resid)
    for p in range(planes):
        out_ref[p] = total[:, p * columns : (p + 1) * columns].astype(bf16)
    pick_rows = selector(start, (COMP, SEQUENCE_TOKENS), 1).astype(bf16)
    a_rows = dot(pick_rows, normed_ref[...])
    turned = normed_ref[...].astype(f32).T.astype(bf16)
    grad_one_ref[:, HEAD_COLS:wide] = dot(turned, grad_key).astype(bf16)
    grad_pack_ref[:, :KEY_COLS] = dot(turned, grad_value).astype(bf16)
    grad_one_ref[:, :HEAD_COLS] = dot(a_rows.T.astype(bf16), grad_query).astype(bf16)
    grad_pack_ref[:, KEY_COLS : KEY_COLS + D] = dot(
        mixed_ref[...].astype(f32).T.astype(bf16), branch
    ).astype(bf16)
    grad_pack_ref[:, KEY_COLS + D :] = jnp.zeros((D, PACK - KEY_COLS - D), bf16)
    left = jnp.concatenate(
        [c_ref[...].astype(f32), gain_one, gain_two, gain_three_ref[...], jnp.zeros((5, D), f32)],
        axis=0,
    )
    lane = lax.broadcasted_iota(jnp.int32, (8, 128), 0) + EXPERTS
    lane = (lane == lax.broadcasted_iota(jnp.int32, (8, 128), 1)).astype(f32)
    right = jnp.concatenate([router_grad.astype(f32), lane], axis=0).astype(bf16)
    grad_one_ref[:, wide:] = dot(left.T.astype(bf16), right).astype(bf16)


def attend_back(start, *operands):
    vm = pl.BlockSpec(memory_space=pltpu.VMEM)
    picked = operands[13]
    return pl.pallas_call(
        attend_back_kernel,
        in_specs=[pl.BlockSpec(memory_space=pltpu.SMEM)] + [vm] * len(operands),
        out_specs=[vm] * 3,
        out_shape=[
            jax.ShapeDtypeStruct(picked.shape, bf16),
            jax.ShapeDtypeStruct((D, PACK), bf16),
            jax.ShapeDtypeStruct((D, PACK), bf16),
        ],
        scratch_shapes=[pltpu.VMEM((SEQUENCE_TOKENS, D), f32)],
        compiler_params=pltpu.CompilerParams(vmem_limit_bytes=60 << 20),
        name="attend_back",
    )(start, *operands)


def lamb_update(weight, moment_one, moment_two, scale_one, scale_two):
    return (moment_one * scale_one) / (jnp.sqrt(moment_two * scale_two) + EPSILON) + DECAY * weight


def lamb_parts(weight, moment_one, moment_two, gradient, scales):
    moment_one = RATE_ONE * moment_one + (1.0 - RATE_ONE) * gradient
    moment_two = RATE_TWO * moment_two + (1.0 - RATE_TWO) * gradient * gradient
    return (moment_one, moment_two, lamb_update(weight, moment_one, moment_two, *scales))


STEPS = 4


def row_lists(tokens, base, rows):
    inside = (tokens >= base) & (tokens < base + rows)
    count = jnp.sum(inside.astype(jnp.int32), axis=1)
    place = jnp.arange(SEQUENCE_TOKENS, dtype=jnp.int32)
    before = (place[:, None] < place[None, :]).astype(bf16)
    rank = jnp.dot(inside.astype(bf16), before, preferred_element_type=f32).astype(jnp.int32)
    packed = place[None, :] * 65536 + (tokens - base)
    hit = inside[:, :, None] & (rank[:, :, None] == place[None, None, :])
    entry = jnp.sum(jnp.where(hit, packed[:, :, None], 0), axis=1)
    empty = SEQUENCE_TOKENS * 65536
    return jnp.where(place[None, :] < count[:, None], entry, empty), count


def gather_kernel(list_ref, count_ref, table_ref, out_ref, rows_ref):
    b = pl.program_id(0)
    rows_ref[...] = jnp.zeros_like(rows_ref)

    def step(k, carry):
        for j in range(STEPS):
            entry = list_ref[b, k * STEPS + j]
            rows_ref[pl.ds(entry >> 16, 1), :] = table_ref[pl.ds(entry & 65535, 1), :]
        return carry

    lax.fori_loop(0, (count_ref[b] + STEPS - 1) // STEPS, step, 0)
    out_ref[0] = rows_ref[:SEQUENCE_TOKENS].astype(bf16)


def gather_rows(lists, counts, table):
    blocks = lists.shape[0]
    rows, columns = table.shape
    return pl.pallas_call(
        gather_kernel,
        grid_spec=pltpu.PrefetchScalarGridSpec(
            num_scalar_prefetch=2,
            grid=(blocks,),
            in_specs=[pl.BlockSpec((rows, columns), lambda b, *_: (0, 0))],
            out_specs=pl.BlockSpec((1, SEQUENCE_TOKENS, columns), lambda b, *_: (b, 0, 0)),
            scratch_shapes=[pltpu.VMEM((SEQUENCE_TOKENS + 8, columns), f32)],
        ),
        out_shape=jax.ShapeDtypeStruct((blocks, SEQUENCE_TOKENS, columns), bf16),
        compiler_params=pltpu.CompilerParams(vmem_limit_bytes=40 << 20),
        name="gather_rows",
    )(lists, counts, table)


def scatter_kernel(list_ref, count_ref, grad_ref, head_ref, out_ref, rows_ref):
    b = pl.program_id(0)

    @pl.when(b == 0)
    def _():
        out_ref[...] = head_ref[...].astype(f32)

    rows_ref[:SEQUENCE_TOKENS] = grad_ref[0].astype(f32)
    rows_ref[SEQUENCE_TOKENS:] = jnp.zeros((8, rows_ref.shape[1]), f32)

    def step(k, carry):
        for j in range(STEPS):
            entry = list_ref[b, k * STEPS + j]
            out_ref[pl.ds(entry & 65535, 1), :] += rows_ref[pl.ds(entry >> 16, 1), :]
        return carry

    lax.fori_loop(0, (count_ref[b] + STEPS - 1) // STEPS, step, 0)


def scatter_rows(lists, counts, grads, head):
    blocks = lists.shape[0]
    rows, columns = head.shape
    return pl.pallas_call(
        scatter_kernel,
        grid_spec=pltpu.PrefetchScalarGridSpec(
            num_scalar_prefetch=2,
            grid=(blocks,),
            in_specs=[
                pl.BlockSpec((1, SEQUENCE_TOKENS, columns), lambda b, *_: (b, 0, 0)),
                pl.BlockSpec((rows, columns), lambda b, *_: (0, 0)),
            ],
            out_specs=pl.BlockSpec((rows, columns), lambda b, *_: (0, 0)),
            scratch_shapes=[pltpu.VMEM((SEQUENCE_TOKENS + 8, columns), f32)],
        ),
        out_shape=jax.ShapeDtypeStruct((rows, columns), f32),
        compiler_params=pltpu.CompilerParams(vmem_limit_bytes=50 << 20),
        name="scatter_rows",
    )(lists, counts, grads, head)


def on_device(
    token_ids,
    positions,
    pair_index,
    ref_logps,
    routes,
    step_count,
    embed_table,
    embed_first,
    embed_second,
    qkv_weight,
    qkv_first,
    qkv_second,
    out_weight,
    out_first,
    out_second,
    router_weight,
    router_first,
    router_second,
    norm_gains,
    gains_first,
    gains_second,
    in_weight,
    in_first,
    in_second,
    down_weight,
    down_first,
    down_second,
):
    shard_id = lax.axis_index("shard")
    expert_id = lax.axis_index("expert")
    shards = lax.axis_size("shard")
    planes = lax.axis_size("expert")
    devices = shards * planes
    vocab_rows, columns = embed_table.shape
    vocab_base = shard_id * vocab_rows
    own_rows = vocab_rows // planes
    local_experts = in_weight.shape[0]
    hidden_units = in_weight.shape[3]
    head_cols = QUERY_HEADS * HEAD_WIDTH
    key_cols = KEY_VALUE_HEADS * HEAD_WIDTH
    rows_all = devices * COMP

    side = math.isqrt(shards // 2)
    grid = (planes, side, side, 2)
    together = devices <= 32

    def send(parts, ident):
        if together:
            return communicate(parts, ident)
        return [
            out for n, part in enumerate(parts) for out in communicate([part], ident + 20 * n)
        ]

    unit = own_rows // 24

    def swap(x, *turns, back=False, held=None):
        turns = [(start * unit, size * unit, rounds) for start, size, rounds in turns]
        return Swap(x, turns, planes, side, back, held)

    def gather_part(rows):
        return Gather([rows], split(0, COMP, rows.shape[1], 2, 2), planes, side)

    def reduce_part(rows, cuts):
        rows = rows.reshape(grid + (COMP, rows.shape[1]))
        return Reduce([rows], split(0, COMP, rows.shape[-1], 2, cuts), planes, side)

    def chain(rows, extra, extra_out, middle, beside, ident):
        gather = gather_part(jax.ShapeDtypeStruct((COMP, D), bf16))
        part = Chain(reduce_part(rows, 2), extra, extra_out, middle, gather)
        out = communicate([part, beside], ident)
        return (out[0].reshape(rows_all, D), *out[1:])

    def gather_tiny(block, ident):
        return communicate([Tiny(block, planes, side)], ident)[0].reshape((devices,) + block.shape)

    weight_rows = qkv_weight.shape[0]
    weight_cols = PACK
    cuts = 3 if weight_rows % 48 == 0 else 1
    weight_groups = [
        [
            (i, slice(n * (weight_rows // cuts), (n + 1) * (weight_rows // cuts)), slice(0, weight_cols), i == 0)
            for i in range(2)
        ]
        for n in range(cuts)
    ]
    embed_groups = split(0, SEQUENCE_TOKENS, columns, 8, 1)

    own_places = lax.dynamic_index_in_dim(positions, shard_id, 0, keepdims=False)
    start = own_places[0]
    own_tokens = lax.dynamic_slice_in_dim(token_ids, shard_id * SEQUENCE_TOKENS, SEQUENCE_TOKENS, 0)
    own_routes = lax.dynamic_slice_in_dim(routes, start, COMP, 0)
    sheet = jnp.concatenate(
        [
            own_tokens,
            own_routes.reshape(-1),
            own_places,
            jnp.zeros((1024 - SEQUENCE_TOKENS - COMP * TOP - COMP,), jnp.int32),
        ]
    )
    sheets = gather_tiny(sheet.reshape(8, 128), 0).reshape(devices, 1024)
    tokens_all = sheets[:, :SEQUENCE_TOKENS]
    routes_all = sheets[:, SEQUENCE_TOKENS : SEQUENCE_TOKENS + COMP * TOP].reshape(rows_all, TOP)
    places_all = sheets[:, SEQUENCE_TOKENS + COMP * TOP : SEQUENCE_TOKENS + COMP * TOP + COMP]
    spots = jnp.arange(SEQUENCE_TOKENS, dtype=jnp.int32)
    targets = jnp.sum(
        jnp.where(
            places_all[:, :, None] + 1 == spots[None, None, :], tokens_all[:, None, :], 0
        ),
        axis=2,
    ).reshape(-1)

    lists, counts = row_lists(tokens_all, vocab_base, vocab_rows)
    picked = gather_rows(lists, counts, embed_table).reshape(grid + (SEQUENCE_TOKENS, columns))
    packs = [
        jnp.concatenate(
            [
                qkv_weight[:, : head_cols + key_cols],
                router_weight,
                norm_gains.T,
                jnp.zeros((weight_rows, 128 - EXPERTS - 3), f32),
            ],
            axis=1,
        ).astype(bf16),
        jnp.concatenate(
            [
                qkv_weight[:, head_cols + key_cols :],
                out_weight,
                jnp.zeros((weight_rows, 128), f32),
            ],
            axis=1,
        ).astype(bf16),
    ]
    table_b = embed_table.astype(bf16)
    packs = jnp.concatenate(packs, axis=0)
    packs, sheets = lax.optimization_barrier((packs, sheets))
    packs = lax.all_to_all(
        jnp.broadcast_to(packs[None], (planes,) + packs.shape),
        "expert",
        split_axis=0,
        concat_axis=0,
        tiled=True,
    )
    table_b = embed_table.astype(bf16)
    picked, first_pack, second_pack, table_own = send(
        [
            Reduce([picked], embed_groups, planes, side, exchange=True),
            Gather(
                [packs[:, :weight_rows], packs[:, weight_rows:]],
                weight_groups,
                planes,
                side,
                prior=True,
            ),
            swap(table_b, (0, 16, 0)),
        ],
        1,
    )
    first_pack = first_pack.reshape(D, weight_cols)
    second_pack = second_pack.reshape(D, weight_cols)

    start_at = start.reshape(1)
    tables = rotary_tables()
    tables += tuple(lax.dynamic_slice_in_dim(table, start, COMP, 0) for table in tables)
    normed_two_b, resid, probs, query, key, value, attended, normed_b, gains = attend(
        start_at, picked, first_pack, second_pack, *tables
    )

    expert_rows, table_own = communicate(
        [gather_part(normed_two_b), swap(table_b, (16, 2, 2), held=table_own)], 2
    )
    expert_rows = expert_rows.reshape(rows_all, D)
    lanes = shard_id * local_experts + jnp.arange(local_experts, dtype=jnp.int32)
    in_rows = in_weight.reshape(-1, hidden_units)
    produced, mid, gates, in_cat, down_b, gated_hidden = experts_forward(
        lanes, expert_rows, routes_all, first_pack, in_rows, down_weight
    )
    own_index = expert_id * shards + shard_id
    own_gates = lax.dynamic_slice(gates, (own_index * COMP, 0), (COMP, 128))
    row_block = jax.ShapeDtypeStruct((COMP, D), f32)
    head_rows, resid_two, table_own = chain(
        produced,
        [resid, gains],
        [row_block],
        final_norm,
        swap(table_b, (18, 3, 0), (21, 3, 8), held=table_own),
        3,
    )

    logits = jnp.einsum("rd,vd->rv", head_rows, table_own, preferred_element_type=f32) / LOGIT_SCALE
    own_base = vocab_base + expert_id * own_rows
    target_hot = targets[:, None] == own_base + jnp.arange(own_rows, dtype=jnp.int32)[None, :]
    row_top = jnp.max(logits, axis=1)
    row_total = jnp.sum(jnp.exp(logits - row_top[:, None]), axis=1)
    row_hit = jnp.sum(jnp.where(target_hot, logits, 0.0), axis=1)
    stats = jnp.stack([row_top, row_total, row_hit]).reshape(8, 3 * rows_all // 8)
    stats = gather_tiny(stats, 5).reshape(devices, 3, rows_all)
    top_all = jnp.max(stats[:, 0], axis=0)
    total_all = jnp.sum(stats[:, 1] * jnp.exp(stats[:, 0] - top_all[None]), axis=0)
    row_lse = top_all + jnp.log(total_all)
    seq_sums = jnp.sum((jnp.sum(stats[:, 2], axis=0) - row_lse).reshape(-1, COMP), axis=1)

    sequences = jnp.arange(devices, dtype=jnp.int32)[None, :]
    pair_sign = (pair_index[:, :1] == sequences).astype(f32) - (
        pair_index[:, 1:] == sequences
    ).astype(f32)
    scaled = BETA * jnp.sum(pair_sign * (seq_sums - ref_logps)[None, :], axis=1)
    loss_value = -jnp.mean(jax.nn.log_sigmoid(scaled))
    pair_grad = jax.nn.sigmoid(-scaled) * (-BETA / scaled.shape[0])
    seq_grad = jnp.sum(pair_sign * pair_grad[:, None], axis=0)
    row_grad = jnp.repeat(seq_grad, COMP)
    grad_logits = (
        row_grad[:, None] * (target_hot.astype(f32) - jnp.exp(logits - row_lse[:, None]))
    ).astype(bf16)
    grad_logits = lax.optimization_barrier(grad_logits)
    grad_rows = jnp.dot(grad_logits, table_own, preferred_element_type=f32) / LOGIT_SCALE
    head_grad = (
        jnp.einsum("rv,rd->vd", grad_logits, head_rows, preferred_element_type=f32) / LOGIT_SCALE
    ).astype(bf16)
    grad_all, grad_resid_two, grad_gain_three, head_back = chain(
        grad_rows.astype(bf16),
        [resid_two, gains],
        [row_block, jax.ShapeDtypeStruct((1, D), f32)],
        final_norm_back,
        swap(head_grad, (0, 3, 0), (3, 3, 8), back=True),
        6,
    )

    back, mid_grad = experts_backward(lanes, grad_all, mid, gates, in_cat, down_b)
    back, head_back = communicate(
        [reduce_part(back, 1), swap(head_grad, (6, 3, 0), back=True, held=head_back)], 8
    )

    grad_embedded, *grad_packs = attend_back(
        start_at,
        back,
        own_gates,
        grad_resid_two,
        grad_gain_three,
        normed_two_b,
        resid,
        probs,
        query,
        key,
        value,
        attended,
        normed_b,
        gains,
        picked,
        first_pack,
        second_pack,
        *tables,
    )
    grad_packs = [pack.reshape(grid + (weight_rows, weight_cols)) for pack in grad_packs]
    wide = head_cols + key_cols
    sent, first_grad, second_grad, head_back = send(
        [
            Gather([grad_embedded], embed_groups, planes, side, exchange=True),
            Reduce(grad_packs, weight_groups, planes, side, partial=True),
            swap(head_grad, (9, 15, 4), back=True, held=head_back),
        ],
        9,
    )
    plane_sums = lax.all_to_all(
        jnp.concatenate([first_grad, second_grad], axis=1),
        "expert",
        split_axis=0,
        concat_axis=0,
        tiled=True,
    ).astype(f32)
    first_grad = jnp.sum(plane_sums[:, :weight_rows], axis=0)
    second_grad = jnp.sum(plane_sums[:, weight_rows:], axis=0)
    table_grad = scatter_rows(
        lists,
        counts,
        sent.reshape(devices, SEQUENCE_TOKENS, columns),
        head_back.reshape(vocab_rows, columns),
    )

    step_value = step_count.astype(f32)
    scales = (1.0 / (1.0 - RATE_ONE**step_value), 1.0 / (1.0 - RATE_TWO**step_value))
    grad_in = jnp.einsum("td,tk->dk", expert_rows, mid_grad, preferred_element_type=f32)
    grad_down = jnp.einsum(
        "tk,td->kd", gated_hidden, grad_all, preferred_element_type=f32
    ).reshape(down_weight.shape)
    in_first_new, in_second_new, in_norms = in_moments(
        jnp.stack(scales),
        grad_in,
        in_rows,
        in_first.reshape(in_rows.shape),
        in_second.reshape(in_rows.shape),
    )
    weights = (embed_table, qkv_weight, out_weight, router_weight, norm_gains, down_weight)
    firsts = (embed_first, qkv_first, out_first, router_first, gains_first, down_first)
    seconds = (embed_second, qkv_second, out_second, router_second, gains_second, down_second)
    gradients = (
        table_grad,
        jnp.concatenate([first_grad[:, :wide], second_grad[:, :key_cols]], axis=1),
        second_grad[:, key_cols : key_cols + D],
        first_grad[:, wide : wide + EXPERTS],
        first_grad[:, wide + EXPERTS : wide + EXPERTS + 3].T,
        grad_down,
    )
    moved = [
        lamb_parts(weight, moment_one, moment_two, gradient, scales)
        for weight, moment_one, moment_two, gradient in zip(weights, firsts, seconds, gradients)
    ]
    partial_norms = [
        (jnp.sum(weight * weight), jnp.sum(parts[2] * parts[2]))
        for weight, parts in zip(weights, moved)
    ]
    partial_norms.insert(5, (jnp.sum(in_norms[0]), jnp.sum(in_norms[1])))
    norm_row = lax.broadcasted_iota(jnp.int32, (8, 128), 0)
    norm_lane = lax.broadcasted_iota(jnp.int32, (8, 128), 1)
    norm_block = jnp.zeros((8, 128), f32)
    for n, pair in enumerate(partial_norms):
        for lane, part in enumerate(pair):
            norm_block = jnp.where((norm_row == n) & (norm_lane == lane), part, norm_block)
    norm_values = jnp.sqrt(jnp.sum(gather_tiny(norm_block, 10), axis=0))[:7, :2]
    trust_ratio = norm_values[:, 0] / norm_values[:, 1]
    moved.insert(
        5, (in_first_new, in_second_new, lamb_update(in_rows, in_first_new, in_second_new, *scales))
    )
    weights = weights[:5] + (in_rows,) + weights[5:]
    results = [loss_value]
    for place, (weight, parts) in enumerate(zip(weights, moved)):
        made = [weight - STEP_RATE * trust_ratio[place] * parts[2], parts[0], parts[1]]
        if place == 5:
            made = [x.reshape(in_weight.shape) for x in made]
        results.extend(made)
    results.append(jnp.stack([norm_values[:, 0], norm_values[:, 1], trust_ratio], axis=1))
    return tuple(results)


def solution(mesh):
    rows = P(BOTH, None)
    vocab = P("shard", "expert")
    gains = P(None, BOTH)
    inner = P("shard", None, None, "expert")
    outer = P("shard", "expert", None)
    state = (vocab,) * 3 + (rows,) * 9 + (gains,) * 3 + (inner,) * 3 + (outer,) * 3
    return jax.shard_map(
        on_device,
        mesh=mesh,
        in_specs=(P("expert"), P("expert", None), P(), P(), rows, P()) + state,
        out_specs=(P(),) + state + (P(),),
        check_vma=False,
    )
```

```python
import functools
import math

import jax
import jax.numpy as jnp
from jax import lax
from jax.experimental import pallas as pl
from jax.experimental.pallas import tpu as pltpu
from jax.sharding import PartitionSpec as P

D = 1536
QUERY_HEADS = 24
KEY_VALUE_HEADS = 8
GROUP = QUERY_HEADS // KEY_VALUE_HEADS
HEAD_WIDTH = 64
TOP = 8
EXPERTS = 32
SEQUENCE_TOKENS = 256
COMP = 32
QKV = 2560

BETA = 0.1
LOGIT_SCALE = 6.0
RATE_ONE = 0.9
RATE_TWO = 0.999
EPSILON = 1e-06
DECAY = 0.01
STEP_RATE = 0.3

BOTH = ("expert", "shard")
bf16 = jnp.bfloat16
f32 = jnp.float32


MESH = pl.DeviceIdType.MESH


class Spot:
    def __init__(self, planes, side):
        self.planes, self.side = planes, side
        self.z = lax.axis_index("expert")
        self.shard = lax.axis_index("shard")
        self.core = lax.rem(self.shard, 2)
        self.b = lax.rem(lax.div(self.shard, 2), side)
        self.a = lax.div(self.shard, 2 * side)

    def plane(self, k):
        z = lax.rem(self.z + k, self.planes)
        return z, (z, self.shard)

    def along_a(self, k):
        a = lax.rem(self.a + k, self.side)
        return a, (self.z, (a * self.side + self.b) * 2 + self.core)

    def along_b(self, k):
        b = lax.rem(self.b + k, self.side)
        return b, (self.z, (self.a * self.side + b) * 2 + self.core)

    def along(self, first, k):
        return self.along_a(k) if first else self.along_b(k)

    def mate(self):
        other = 1 - self.core
        return other, (self.z, (self.a * self.side + self.b) * 2 + other)

    def near(self, k):
        return self.z, lax.rem(self.shard + k, 2 * self.side * self.side)

    def greet(self, flat):
        targets = [self.plane(k)[1] for k in range(1, self.planes)]
        if flat:
            targets += [self.near(k) for k in range(1, 2 * self.side * self.side)]
        else:
            targets.append(self.mate()[1])
            for k in range(1, self.side):
                targets += [self.along_a(k)[1], self.along_b(k)[1]]
        barrier = pltpu.get_barrier_semaphore()
        for target in targets:
            pl.semaphore_signal(barrier, inc=1, device_id=target, device_id_type=MESH)
        pl.semaphore_wait(barrier, len(targets))


class Mail:
    def __init__(self, send, recv):
        self.send, self.recv, self.count, self.open = send, recv, 0, []

    def start(self, src, dst, target):
        copy = pltpu.make_async_remote_copy(
            src_ref=src,
            dst_ref=dst,
            send_sem=self.send.at[self.count],
            recv_sem=self.recv.at[self.count],
            device_id=target,
            device_id_type=MESH,
        )
        self.count += 1
        copy.start()
        self.open.append(copy)
        return copy

    def finish(self):
        for copy in self.open:
            copy.wait_send()


def arrive(copies):
    for copy in copies:
        copy.wait_recv()


class Tiny:
    flat = True
    scratch = ()

    def __init__(self, x, planes, side):
        self.planes, self.side, self.inputs = planes, side, [x]
        shape = (planes, 2 * side * side) + x.shape
        self.outputs = [jax.ShapeDtypeStruct(shape, x.dtype)]
        self.copies = planes + 2 * side * side - 2

    def steps(self, spot, mail, x, out):
        out[spot.z, spot.shard] = x[...]
        sent = []
        for k in range(1, self.planes):
            sent.append(mail.start(x, out.at[spot.z, spot.shard], spot.plane(k)[1]))
        yield
        arrive(sent)
        part = out.at[:, spot.shard]
        yield
        arrive([mail.start(part, part, spot.near(k)) for k in range(1, 2 * self.side**2)])


def split(array, rows, columns, row_parts, column_parts):
    r, c = rows // row_parts, columns // column_parts
    cuts = [
        (array, slice(i * r, i * r + r), slice(j * c, j * c + c))
        for j in range(column_parts)
        for i in range(row_parts)
    ]
    cuts = [cut + (n % 2 == 0,) for n, cut in enumerate(cuts)]
    return [cuts[n : n + 2] for n in range(0, len(cuts), 2)]


def pipeline(groups, stage, last):
    sent = [[[] for _ in group] for group in groups]
    for tick in range(len(groups) + last):
        for step in range(last, -1, -1):
            turn = tick - step
            if 0 <= turn < len(groups):
                for n, cut in enumerate(groups[turn]):
                    for copy in sent[turn][n]:
                        copy.wait_recv()
                    sent[turn][n] = stage(step, (turn, n), cut)
        yield


class Gather:
    flat = False
    scratch = ()

    def __init__(self, xs, groups, planes, side, exchange=False, prior=False):
        self.planes, self.side, self.inputs, self.groups = planes, side, xs, groups
        self.exchange, self.prior = exchange, prior
        grid = (planes, side, side, 2)
        self.outputs = [jax.ShapeDtypeStruct(grid + x.shape[-2:], x.dtype) for x in xs]
        self.copies = sum(map(len, groups)) * (planes - 1 + 2 * (side - 1) + 1)

    def steps(self, spot, mail, *refs):
        xs, outs = refs[: len(self.inputs)], refs[len(self.inputs) :]
        z, a, b, core = spot.z, spot.a, spot.b, spot.core
        for x, out in zip(xs, outs):
            if self.prior:
                out[:, a, b, core] = x[...]
            else:
                out[z, a, b, core] = x[z] if self.exchange else x[...]

        def stage(step, key, cut):
            i, rows, columns, first = cut
            x, out = xs[i], outs[i]
            if step == 0 and self.prior:
                return []
            if step == 0:
                place = out.at[z, a, b, core, rows, columns]
                sent = []
                for k in range(1, self.planes):
                    peer, target = spot.plane(k)
                    own = x.at[peer, rows, columns] if self.exchange else x.at[rows, columns]
                    sent.append(mail.start(own, place, target))
                return sent
            if step in (1, 2):
                if step == 1:
                    part = out.at[:, a, b, core, rows, columns]
                elif first:
                    part = out.at[:, :, b, core, rows, columns]
                else:
                    part = out.at[:, a, :, core, rows, columns]
                return [
                    mail.start(part, part, spot.along(first == (step == 1), k)[1])
                    for k in range(1, self.side)
                ]
            if step == 3:
                part = out.at[:, :, :, core, rows, columns]
                return [mail.start(part, part, spot.mate()[1])]
            return []

        return pipeline(self.groups, stage, 4)


class Reduce:
    flat = False

    def __init__(self, xs, groups, planes, side, exchange=False, partial=False):
        self.planes, self.side, self.inputs, self.groups = planes, side, xs, groups
        self.exchange, self.partial = exchange or partial, partial
        self.outputs = [
            jax.ShapeDtypeStruct((planes,) + x.shape[-2:], x.dtype)
            if self.exchange
            else jax.ShapeDtypeStruct(x.shape[-2:], f32)
            for x in xs
        ]
        self.scratch = []
        for i, rows, columns, _ in [cut for group in groups for cut in group]:
            block = (rows.stop - rows.start, columns.stop - columns.start)
            self.scratch += [
                pltpu.VMEM(shape + block, xs[i].dtype)
                for shape in (
                    (planes, side, side),
                    (side - 1, planes, side),
                    (planes, side),
                    (side - 1, planes),
                    (planes,),
                )
                + (() if self.exchange else ((planes - 1,),))
            ]
        self.copies = sum(map(len, groups)) * (planes - 1 + 2 * (side - 1) + 1)

    def steps(self, spot, mail, *refs):
        planes, side, number = self.planes, self.side, len(self.inputs)
        xs, outs, rest = refs[:number], refs[number : 2 * number], refs[2 * number :]
        each = 5 if self.exchange else 6
        order = [(t, n) for t, group in enumerate(self.groups) for n in range(len(group))]
        held = {key: rest[each * p : each * (p + 1)] for p, key in enumerate(order)}
        core, z = spot.core, spot.z
        other, mate = spot.mate()

        def stage(step, key, cut):
            i, rows, columns, first = cut
            x, out = xs[i], outs[i]
            one, hop_two, two, hop_three, three = held[key][:5]
            if step == 0:
                return [mail.start(x.at[:, :, :, other, rows, columns], one, mate)]
            sent = []
            if step == 1:

                def add(n, carry):
                    ia, ib = lax.rem(lax.div(n, side), side), lax.rem(n, side)
                    iz = lax.div(n, side * side)
                    total = x[iz, ia, ib, core, rows, columns].astype(f32)
                    one[iz, ia, ib] = (total + one[iz, ia, ib].astype(f32)).astype(one.dtype)
                    return carry

                lax.fori_loop(0, planes * side * side, add, 0)
                for k in range(1, side):
                    peer, target = spot.along(first, k)
                    part = one.at[:, peer] if first else one.at[:, :, peer]
                    sent.append(mail.start(part, hop_two.at[k - 1], target))
            elif step == 2:

                def add(n, carry):
                    iz, ir = lax.div(n, side), lax.rem(n, side)
                    total = (one[iz, spot.a, ir] if first else one[iz, ir, spot.b]).astype(f32)
                    for k in range(side - 1):
                        total += hop_two[k, iz, ir].astype(f32)
                    two[iz, ir] = total.astype(two.dtype)
                    return carry

                lax.fori_loop(0, planes * side, add, 0)
                for k in range(1, side):
                    peer, target = spot.along(not first, k)
                    sent.append(mail.start(two.at[:, peer], hop_three.at[k - 1], target))
            elif step == 3:
                mine = spot.b if first else spot.a

                def add(iz, carry):
                    total = two[iz, mine].astype(f32)
                    for k in range(side - 1):
                        total += hop_three[k, iz].astype(f32)
                    if self.partial:
                        out[iz, rows, columns] = total.astype(out.dtype)
                    else:
                        three[iz] = total.astype(three.dtype)
                    return carry

                lax.fori_loop(0, planes, add, 0)
                if self.partial:
                    return []
                for k in range(1, planes):
                    peer, target = spot.plane(k)
                    if self.exchange:
                        place = out.at[z, rows, columns]
                    else:
                        place = held[key][5].at[k - 1]
                    sent.append(mail.start(three.at[peer], place, target))
                if self.exchange:
                    out[z, rows, columns] = three[z]
            elif not self.exchange:
                total = three[z].astype(f32)
                for k in range(planes - 1):
                    total += held[key][5][k].astype(f32)
                out[rows, columns] = total
            return sent

        return pipeline(self.groups, stage, 4)


class Swap:
    flat = False
    def __init__(self, x, turns, planes, side, back=False, held=None):
        self.planes, self.side = planes, side
        self.inputs = [x] if held is None else [x, held]
        self.in_spaces, self.out_spaces = (pl.ANY,) * len(self.inputs), (pl.ANY,)
        self.aliases = {} if held is None else {1: 0}
        self.turns, self.back = turns, back
        self.scratch = [pltpu.SemaphoreType.DMA((len(turns),))]
        self.columns = x.shape[1] // planes if back else x.shape[1]
        self.rows = x.shape[0] if back else x.shape[0] // planes
        shape = (planes, self.rows, self.columns) if back else (self.rows, planes * self.columns)
        self.outputs = [jax.ShapeDtypeStruct(shape, x.dtype)]
        self.copies = len(turns) * (planes - 1)

    def steps(self, spot, mail, *refs):
        x, out, own_sem = refs[0], refs[-2], refs[-1]
        def block(z):
            return pl.ds(pl.multiple_of(z * self.columns, 128), self.columns)

        def source(z, begin, size):
            if self.back:
                return x.at[pl.ds(begin, size), block(z)]
            return x.at[pl.ds(pl.multiple_of(z * self.rows + begin, 16), size), :]

        sent, own, now = [], [], 0
        for n, (begin, size, rounds) in enumerate(self.turns):
            while now < rounds:
                now += 1
                yield
            rows = pl.ds(begin, size)
            place = out.at[spot.z, rows] if self.back else out.at[rows, block(spot.z)]
            for k in range(1, self.planes):
                peer, target = spot.plane(k)
                sent.append(mail.start(source(peer, begin, size), place, target))
            own.append(pltpu.make_async_copy(source(spot.z, begin, size), place, own_sem.at[n]))
            own[-1].start()
        while now < 24:
            now += 1
            yield
        for copy in own:
            copy.wait()
        for copy in sent:
            copy.wait_recv()


class Chain:
    flat = False

    def __init__(self, reduce, extra, extra_out, middle, gather):
        self.planes, self.side = reduce.planes, reduce.side
        self.reduce, self.middle, self.gather = reduce, middle, gather
        self.inputs = reduce.inputs + extra
        self.outputs = gather.outputs + extra_out
        self.scratch = reduce.scratch + [
            pltpu.VMEM(x.shape, x.dtype) for x in reduce.outputs + gather.inputs
        ]
        self.copies = reduce.copies + gather.copies

    def steps(self, spot, mail, *refs):
        n_in, n_out = len(self.inputs), len(self.outputs)
        (x, *extra), (out, *extra_out) = refs[:n_in], refs[n_in : n_in + n_out]
        *held, sums, made = refs[n_in + n_out :]
        yield from self.reduce.steps(spot, mail, x, sums, *held)
        self.middle(sums, made, *extra, *extra_out)
        yield from self.gather.steps(spot, mail, made, out)


def final_norm(sums, made, resid, gains, resid_two):
    values = resid[...] + sums[...]
    resid_two[...] = values
    made[...] = (values * inverse_root(values) * gains[2:3]).astype(bf16)


def final_norm_back(sums, made, resid_two, gains, grad_two, gain_grad):
    grad, gain_grad[...] = norm_back(resid_two[...], gains[2:3], sums[...])
    grad_two[...] = grad
    made[...] = grad.astype(bf16)


def communicate(parts, ident):
    planes, side = parts[0].planes, parts[0].side
    counts = [(len(p.inputs), len(p.outputs), len(p.scratch)) for p in parts]
    n_in, n_out = (sum(c[i] for c in counts) for i in range(2))
    copies = sum(p.copies for p in parts)
    aliases, i, o = {}, 0, 0
    for part, (ci, co, _) in zip(parts, counts):
        aliases.update({i + a: o + b for a, b in getattr(part, "aliases", {}).items()})
        i, o = i + ci, o + co

    def kernel(*refs):
        ins, outs, rest = refs[:n_in], refs[n_in : n_in + n_out], refs[n_in + n_out :]
        send, recv = rest[-2:]
        spot = Spot(planes, side)
        spot.greet(parts[0].flat)
        mail = Mail(send, recv)
        running, i, o, s = [], 0, 0, 0
        for part, (ci, co, cs) in zip(parts, counts):
            running.append(
                part.steps(spot, mail, *ins[i : i + ci], *outs[o : o + co], *rest[s : s + cs])
            )
            i, o, s = i + ci, o + co, s + cs
        while running:
            running = [steps for steps in running if next(steps, True) is None]
        mail.finish()

    size = sum(x.size * x.dtype.itemsize for p in parts for x in p.inputs + p.outputs)
    need = size + sum(
        math.prod(x.shape) * x.dtype.itemsize
        for p in parts
        for x in p.scratch
        if x.memory_space == pltpu.VMEM
    )
    out = pl.pallas_call(
        kernel,
        out_shape=[x for p in parts for x in p.outputs],
        in_specs=[
            pl.BlockSpec(memory_space=space)
            for p in parts
            for space in getattr(p, "in_spaces", (pltpu.VMEM,) * len(p.inputs))
        ],
        out_specs=[
            pl.BlockSpec(memory_space=space)
            for p in parts
            for space in getattr(p, "out_spaces", (pltpu.VMEM,) * len(p.outputs))
        ],
        input_output_aliases=aliases,
        scratch_shapes=[s for p in parts for s in p.scratch]
        + [pltpu.SemaphoreType.DMA((copies,)), pltpu.SemaphoreType.DMA((copies,))],
        compiler_params=pltpu.CompilerParams(
            collective_id=ident,
            has_side_effects=True,
            vmem_limit_bytes=min(62 << 20, need * 9 // 8 + (4 << 20)),
        ),
        cost_estimate=pl.CostEstimate(flops=0, bytes_accessed=20 * size, transcendentals=0),
        name="exchange_" + str(ident),
    )(*[x for p in parts for x in p.inputs])
    return list(out)

def expert_gate(gates, lane):
    lanes = lax.broadcasted_iota(jnp.int32, gates.shape, 1)
    return jnp.sum(jnp.where(lanes == lane, gates, 0.0), axis=1, keepdims=True)


CHUNK = 512
BLOCK = 1024
ACROSS = (((1,), (1,)), ((), ()))


def forward_kernel(
    lane_ref, rows_ref, routes_ref, router_ref, in_ref, down_ref, out_ref, mid_ref, gates_ref, cat_ref, down_out, hidden_ref
):
    e, number = pl.program_id(1), pl.num_programs(1)
    units = in_ref.shape[1]
    for j in range(2):
        cat_ref[:, j * units : (j + 1) * units] = in_ref[pl.ds(j, D, stride=2), :].astype(bf16)
    down_out[pl.ds(pl.multiple_of(e * units, units), units), :] = down_ref[0].astype(bf16)

    def chunk(i, carry):
        here = pl.ds(pl.multiple_of(i * CHUNK, CHUNK), CHUNK)
        rows = rows_ref[here, :]

        @pl.when(e == 0)
        def _():
            logits = jnp.dot(rows, router_ref[...], preferred_element_type=f32)
            lanes = lax.broadcasted_iota(jnp.int32, logits.shape, 1)
            mask = lanes == routes_ref[here, 0:1]
            for j in range(1, TOP):
                mask |= lanes == routes_ref[here, j : j + 1]
            top = jnp.max(jnp.where(mask, logits, -3e38), axis=1, keepdims=True)
            weight = jnp.where(mask, jnp.exp(jnp.where(mask, logits - top, 0.0)), 0.0)
            gates_ref[here, :] = weight / jnp.sum(weight, axis=1, keepdims=True)

        mid = jnp.dot(rows, cat_ref[...], preferred_element_type=f32)
        mid_ref[here, :] = mid
        gate, up = mid[:, :units], mid[:, units:]
        hidden = (gate * jax.nn.sigmoid(gate) * up).astype(bf16).astype(f32)
        hidden = (hidden * expert_gate(gates_ref[here, :], lane_ref[0] + e)).astype(bf16)
        hidden_ref[here, pl.ds(pl.multiple_of(e * units, units), units)] = hidden

        @pl.when(e == number - 1)
        def _():
            out_ref[here, :] = jnp.dot(
                hidden_ref[here, :], down_out[...], preferred_element_type=f32
            ).astype(bf16)

        return carry

    lax.fori_loop(0, rows_ref.shape[0] // CHUNK, chunk, 0)


def experts_forward(lane, rows, routes, router, in_rows, down):
    number, units = down.shape[:2]
    total = rows.shape[0]
    block = min(total, BLOCK)
    row = lambda r, e, *_: (r, 0)
    still = lambda r, e, *_: (0, 0)
    return pl.pallas_call(
        forward_kernel,
        grid_spec=pltpu.PrefetchScalarGridSpec(
            num_scalar_prefetch=1,
            grid=(total // block, number),
            in_specs=[
                pl.BlockSpec((block, D), row),
                pl.BlockSpec((block, TOP), row),
                pl.BlockSpec((D, 128), lambda r, e, *_: (0, PACK // 128 - 1)),
                pl.BlockSpec((2 * D, units), lambda r, e, *_: (e, 0)),
                pl.BlockSpec((1, units, D), lambda r, e, *_: (e, 0, 0)),
            ],
            out_specs=[
                pl.BlockSpec((block, D), row),
                pl.BlockSpec((block, 2 * units), lambda r, e, *_: (r, e)),
                pl.BlockSpec((block, 128), row),
                pl.BlockSpec((D, 2 * units), lambda r, e, *_: (0, e)),
                pl.BlockSpec((number * units, D), still),
                pl.BlockSpec((block, number * units), row),
            ],
        ),
        out_shape=[
            jax.ShapeDtypeStruct((total, D), bf16),
            jax.ShapeDtypeStruct((total, 2 * units * number), f32),
            jax.ShapeDtypeStruct((total, 128), f32),
            jax.ShapeDtypeStruct((D, 2 * units * number), bf16),
            jax.ShapeDtypeStruct((number * units, D), bf16),
            jax.ShapeDtypeStruct((total, number * units), bf16),
        ],
        compiler_params=pltpu.CompilerParams(vmem_limit_bytes=42 << 20),
        name="experts_forward",
    )(lane, rows, routes, router, in_rows, down)


def backward_kernel(
    lane_ref, grad_ref, mid_ref, gates_ref, cat_ref, down_ref, out_ref, mid_grad_ref, pulled_ref
):
    number = lane_ref.shape[0]
    units = pulled_ref.shape[1] // number

    def chunk(i, carry):
        here = pl.ds(pl.multiple_of(i * CHUNK, CHUNK), CHUNK)
        pulled_ref[...] = lax.dot_general(
            grad_ref[here, :], down_ref[...], ACROSS, preferred_element_type=f32
        )
        lanes = lax.broadcasted_iota(jnp.int32, (CHUNK, 128), 1)
        gate_part = jnp.zeros((CHUNK, 128), f32)
        for e in range(number):
            lane = lane_ref[e]
            weight = expert_gate(gates_ref[here, :], lane)
            gate = mid_ref[here, 2 * e * units : (2 * e + 1) * units]
            up = mid_ref[here, (2 * e + 1) * units : (2 * e + 2) * units]
            pulled = pulled_ref[:, e * units : (e + 1) * units]
            soft = jax.nn.sigmoid(gate)
            silu = gate * soft
            hidden = (silu * up).astype(bf16).astype(f32)
            gate_grad = jnp.sum(hidden * pulled, axis=1, keepdims=True)
            gate_part = jnp.where(lanes == lane, gate_grad, gate_part)
            hidden_grad = (pulled * weight).astype(bf16).astype(f32)
            turned = hidden_grad * up * (soft * (1.0 + gate * (1.0 - soft)))
            mid_grad_ref[here, 2 * e * units : (2 * e + 1) * units] = turned.astype(bf16)
            mid_grad_ref[here, (2 * e + 1) * units : (2 * e + 2) * units] = (
                hidden_grad * silu
            ).astype(bf16)
        out_ref[here, D:] = gate_part.astype(bf16)
        out_ref[here, :D] = lax.dot_general(
            mid_grad_ref[here, :], cat_ref[...], ACROSS, preferred_element_type=f32
        ).astype(bf16)
        return carry

    lax.fori_loop(0, grad_ref.shape[0] // CHUNK, chunk, 0)


def experts_backward(lanes, grad, mid, gates, cat, down):
    number = lanes.shape[0]
    total = grad.shape[0]
    block = min(total, BLOCK)
    row = lambda r, *_: (r, 0)
    still = lambda r, *_: (0, 0)
    return pl.pallas_call(
        backward_kernel,
        grid_spec=pltpu.PrefetchScalarGridSpec(
            num_scalar_prefetch=1,
            grid=(total // block,),
            in_specs=[
                pl.BlockSpec((block, D), row),
                pl.BlockSpec((block, mid.shape[1]), row),
                pl.BlockSpec((block, 128), row),
                pl.BlockSpec(cat.shape, still),
                pl.BlockSpec(down.shape, still),
            ],
            out_specs=[
                pl.BlockSpec((block, D + 128), row),
                pl.BlockSpec((block, mid.shape[1]), row),
            ],
            scratch_shapes=[pltpu.VMEM((CHUNK, down.shape[0]), f32)],
        ),
        out_shape=[
            jax.ShapeDtypeStruct((total, D + 128), bf16),
            jax.ShapeDtypeStruct(mid.shape, bf16),
        ],
        compiler_params=pltpu.CompilerParams(vmem_limit_bytes=50 << 20),
        name="experts_backward",
    )(lanes, grad, mid, gates, cat, down)


def moments_kernel(
    scale_ref, grad_ref, w_ref, first_ref, second_ref, down_grad, down_w, down_first, down_second,
    new_first, new_second, new_down_first, new_down_second, norms, sums, down_sums,
):
    units = w_ref.shape[1]
    part = w_ref.shape[0] // 2
    scales = (scale_ref[0], scale_ref[1])
    step = pl.program_id(0) * pl.num_programs(1) + pl.program_id(1)

    @pl.when(step == 0)
    def _():
        sums[...] = jnp.zeros_like(sums)
        down_sums[...] = jnp.zeros_like(down_sums)

    for j in range(2):
        here = pl.ds(j, part, stride=2)
        grad = grad_ref[:, j * units : (j + 1) * units]
        weight = w_ref[here, :]
        one, two, update = lamb_parts(weight, first_ref[here, :], second_ref[here, :], grad, scales)
        new_first[here, :] = one
        new_second[here, :] = two
        sums[0] += fold(weight * weight)
        sums[1] += fold(update * update)
    weight = down_w[...]
    one, two, update = lamb_parts(weight, down_first[...], down_second[...], down_grad[...], scales)
    new_down_first[...] = one
    new_down_second[...] = two
    down_sums[0] += fold(weight * weight)
    down_sums[1] += fold(update * update)

    @pl.when(step == pl.num_programs(0) * pl.num_programs(1) - 1)
    def _():
        norms[...] = norm_cells(5, total_of(sums[0]), total_of(sums[1])) + norm_cells(
            6, total_of(down_sums[0]), total_of(down_sums[1])
        )


def expert_moments(scales, grad, weight, first, second, down_grad, down, down_first, down_second):
    units = weight.shape[1]
    number = grad.shape[1] // (2 * units)
    parts = 2
    row = pl.BlockSpec((2 * D // parts, units), lambda e, p, *_: (e * parts + p, 0))
    down_row = pl.BlockSpec((units // parts, D), lambda e, p, *_: (e * parts + p, 0))
    return pl.pallas_call(
        moments_kernel,
        grid_spec=pltpu.PrefetchScalarGridSpec(
            num_scalar_prefetch=1,
            grid=(number, parts),
            in_specs=[pl.BlockSpec((D // parts, 2 * units), lambda e, p, *_: (p, e)), row, row, row]
            + [down_row] * 4,
            out_specs=[row, row, down_row, down_row, pl.BlockSpec((8, 128), lambda e, p, *_: (0, 0))],
            scratch_shapes=[pltpu.VMEM((2, 8, units), f32), pltpu.VMEM((2, 8, D), f32)],
        ),
        out_shape=[jax.ShapeDtypeStruct(weight.shape, f32)] * 2
        + [jax.ShapeDtypeStruct(down.shape, f32)] * 2
        + [jax.ShapeDtypeStruct((8, 128), f32)],
        compiler_params=pltpu.CompilerParams(vmem_limit_bytes=36 << 20),
        name="expert_moments",
    )(scales, grad, weight, first, second, down_grad, down, down_first, down_second)


HEAD_COLS = QUERY_HEADS * HEAD_WIDTH
KEY_COLS = KEY_VALUE_HEADS * HEAD_WIDTH
PACK = HEAD_COLS + KEY_COLS + 128
ROOT = HEAD_WIDTH ** (-0.5)


def turn(u, cosine, sine):
    width = u.shape[1]
    lanes = lax.broadcasted_iota(jnp.int32, u.shape, 1)
    ahead = pltpu.roll(u, width - HEAD_WIDTH // 2, 1)
    behind = pltpu.roll(u, HEAD_WIDTH // 2, 1)
    other = jnp.where(lax.rem(lanes, HEAD_WIDTH) < HEAD_WIDTH // 2, ahead, behind)
    return u * jnp.tile(cosine, (1, width // 128)) + other * jnp.tile(sine, (1, width // 128))


def rotary_tables():
    half = HEAD_WIDTH // 2
    freqs = jnp.exp(-jnp.log(10000.0) * jnp.arange(half, dtype=f32) / half)
    angles = jnp.arange(SEQUENCE_TOKENS, dtype=f32)[:, None] * freqs[None, :]
    cosine, sine = jnp.cos(angles), jnp.sin(angles)
    return jnp.tile(cosine, (1, 4)), jnp.tile(jnp.concatenate([-sine, sine], axis=1), (1, 2))


def inverse_root(values):
    return lax.rsqrt(jnp.mean(values * values, axis=-1, keepdims=True) + 1e-06)


def norm_back(values, gain, grad):
    root = inverse_root(values)
    scaled = grad * gain
    inner = jnp.mean(scaled * values, axis=-1, keepdims=True)
    return root * scaled - values * (root * root * root * inner), jnp.sum(
        grad * values * root, axis=0, keepdims=True
    )


def dot(a, b):
    return jnp.dot(a, b, preferred_element_type=f32)


def dot_across(a, b):
    return lax.dot_general(a, b, ACROSS, preferred_element_type=f32)


def selector(start, shape, axis):
    row = lax.broadcasted_iota(jnp.int32, shape, 1 - axis) + start
    return (row == lax.broadcasted_iota(jnp.int32, shape, axis)).astype(f32)


def spread(start, rows):
    pick = selector(start, (SEQUENCE_TOKENS, COMP), 0)
    return jnp.dot(pick, rows, preferred_element_type=f32, precision=lax.Precision.HIGHEST)


def head_rows(ref_value, h):
    first = h * GROUP * HEAD_WIDTH
    return jnp.concatenate(
        [
            ref_value[:, first + g * HEAD_WIDTH : first + (g + 1) * HEAD_WIDTH]
            for g in range(GROUP)
        ],
        axis=0,
    )


def head_lanes(parts):
    return jnp.concatenate(
        [part[g * COMP : (g + 1) * COMP] for part in parts for g in range(GROUP)], axis=1
    )


def attend_kernel(
    start_ref, picked_ref, one_ref, two_ref, cos_ref, sin_ref, cos_rows, sin_rows,
    c_ref, resid_ref, probs_ref, query_ref, key_ref, value_ref, mixed_ref, normed_ref, gains_ref,
    embedded,
):
    start = start_ref[0]
    pick_rows = selector(start, (COMP, SEQUENCE_TOKENS), 1).astype(bf16)
    planes, _, columns = picked_ref.shape
    for p in range(planes):
        embedded[:, p * columns : (p + 1) * columns] = picked_ref[p].astype(f32)
    pick = lax.broadcasted_iota(jnp.int32, (8, 128), 0) + EXPERTS
    pick = (pick == lax.broadcasted_iota(jnp.int32, (8, 128), 1)).astype(f32).astype(bf16)
    gains = dot_across(pick, one_ref[:, HEAD_COLS + KEY_COLS :])
    gains_ref[...] = gains
    x = embedded[...]
    a = (x * inverse_root(x) * gains[0:1]).astype(bf16)
    normed_ref[...] = a
    a_rows = dot(pick_rows, a).astype(bf16)
    cosine, sine = cos_ref[...], sin_ref[...]
    query = turn(dot(a_rows, one_ref[:, :HEAD_COLS]), cos_rows[...], sin_rows[...])
    query = query.astype(bf16)
    key = turn(dot(a, one_ref[:, HEAD_COLS : HEAD_COLS + KEY_COLS]), cosine, sine).astype(bf16)
    value = dot(a, two_ref[:, :KEY_COLS]).astype(bf16)
    query_ref[...], key_ref[...], value_ref[...] = query, key, value
    rows = GROUP * COMP
    place = lax.rem(lax.broadcasted_iota(jnp.int32, (rows, SEQUENCE_TOKENS), 0), COMP) + start
    seen = place >= lax.broadcasted_iota(jnp.int32, (rows, SEQUENCE_TOKENS), 1)
    parts = []
    for h in range(KEY_VALUE_HEADS):
        lanes = slice(h * HEAD_WIDTH, (h + 1) * HEAD_WIDTH)
        scores = dot_across(head_rows(query, h), key[:, lanes]) * ROOT
        scores = jnp.where(seen, scores, -1000000000.0)
        expd = jnp.exp(scores - jnp.max(scores, axis=-1, keepdims=True))
        probs = expd / jnp.sum(expd, axis=-1, keepdims=True)
        probs_ref[h] = probs
        parts.append(dot(probs.astype(bf16), value[:, lanes]))
    mixed = head_lanes(parts).astype(bf16)
    mixed_ref[...] = mixed
    resid = dot(pick_rows, embedded[...].astype(bf16)) + dot(mixed, two_ref[:, KEY_COLS : KEY_COLS + D])
    resid_ref[...] = resid
    c_ref[...] = (resid * inverse_root(resid) * gains[1:2]).astype(bf16)


def attend(start, picked, one, two, *tables):
    vm = pl.BlockSpec(memory_space=pltpu.VMEM)
    rows = GROUP * COMP
    return pl.pallas_call(
        attend_kernel,
        in_specs=[pl.BlockSpec(memory_space=pltpu.SMEM)] + [vm] * 7,
        out_specs=[vm] * 9,
        out_shape=[
            jax.ShapeDtypeStruct((COMP, D), bf16),
            jax.ShapeDtypeStruct((COMP, D), f32),
            jax.ShapeDtypeStruct((KEY_VALUE_HEADS, rows, SEQUENCE_TOKENS), f32),
            jax.ShapeDtypeStruct((COMP, HEAD_COLS), bf16),
            jax.ShapeDtypeStruct((SEQUENCE_TOKENS, KEY_COLS), bf16),
            jax.ShapeDtypeStruct((SEQUENCE_TOKENS, KEY_COLS), bf16),
            jax.ShapeDtypeStruct((COMP, HEAD_COLS), bf16),
            jax.ShapeDtypeStruct((SEQUENCE_TOKENS, D), bf16),
            jax.ShapeDtypeStruct((8, D), f32),
        ],
        scratch_shapes=[pltpu.VMEM((SEQUENCE_TOKENS, D), f32)],
        compiler_params=pltpu.CompilerParams(vmem_limit_bytes=56 << 20),
        name="attend",
    )(start, picked, one, two, *tables)


def attend_back_kernel(
    start_ref, back_ref, gates_ref, grad_two_ref, gain_three_ref, c_ref, resid_ref, probs_ref, query_ref,
    key_ref, value_ref, mixed_ref, normed_ref, gains_ref, picked_ref, one_ref, two_ref, cos_ref, sin_ref, cos_rows, sin_rows,
    out_ref, grad_one_ref, grad_pack_ref,
    total,
):
    start = start_ref[0]
    planes, _, columns = picked_ref.shape
    gains = gains_ref[...]
    wide = HEAD_COLS + KEY_COLS
    gates = gates_ref[...]
    gate_grad = back_ref[:, D:]
    router_grad = gates * (gate_grad - jnp.sum(gates * gate_grad, axis=1, keepdims=True))
    router_grad = router_grad.astype(bf16)
    grad = back_ref[:, :D] + dot_across(router_grad, one_ref[:, wide:])
    grad_resid, gain_two = norm_back(resid_ref[...], gains[1:2], grad)
    grad_resid = grad_resid + grad_two_ref[...]
    branch = grad_resid.astype(bf16)
    grad_mixed = dot_across(branch, two_ref[:, KEY_COLS : KEY_COLS + D]).astype(bf16)
    query, key, value = query_ref[...], key_ref[...], value_ref[...]
    query_parts, key_parts, value_parts = [], [], []
    for h in range(KEY_VALUE_HEADS):
        lanes = slice(h * HEAD_WIDTH, (h + 1) * HEAD_WIDTH)
        probs = probs_ref[h]
        grad_head = head_rows(grad_mixed, h)
        grad_probs = dot_across(grad_head, value[:, lanes]).astype(bf16).astype(f32)
        inner = jnp.sum(grad_probs * probs, axis=-1, keepdims=True)
        grad_scores = probs * (grad_probs - inner)
        value_parts.append(dot(probs.T.astype(bf16), grad_head))
        query_parts.append(dot(grad_scores.astype(bf16), key[:, lanes]) * ROOT)
        key_parts.append(dot(grad_scores.T.astype(bf16), head_rows(query, h)) * ROOT)
    grad_query = turn(head_lanes(query_parts), cos_rows[...], -sin_rows[...]).astype(bf16)
    grad_key = jnp.concatenate(key_parts, axis=1)
    grad_key = turn(grad_key, cos_ref[...], -sin_ref[...]).astype(bf16)
    grad_value = jnp.concatenate(value_parts, axis=1).astype(bf16)
    grad_normed = dot_across(grad_key, one_ref[:, HEAD_COLS:wide])
    grad_normed += dot_across(grad_value, two_ref[:, :KEY_COLS])
    grad_normed += spread(start, dot_across(grad_query, one_ref[:, :HEAD_COLS]))
    for p in range(planes):
        total[:, p * columns : (p + 1) * columns] = picked_ref[p].astype(f32)
    grad_embedded, gain_one = norm_back(total[...], gains[0:1], grad_normed)
    total[...] = grad_embedded + spread(start, grad_resid)
    for p in range(planes):
        out_ref[p] = total[:, p * columns : (p + 1) * columns].astype(bf16)
    pick_rows = selector(start, (COMP, SEQUENCE_TOKENS), 1).astype(bf16)
    a_rows = dot(pick_rows, normed_ref[...])
    turned = normed_ref[...].astype(f32).T.astype(bf16)
    grad_one_ref[:, HEAD_COLS:wide] = dot(turned, grad_key).astype(bf16)
    grad_pack_ref[:, :KEY_COLS] = dot(turned, grad_value).astype(bf16)
    grad_one_ref[:, :HEAD_COLS] = dot(a_rows.T.astype(bf16), grad_query).astype(bf16)
    grad_pack_ref[:, KEY_COLS : KEY_COLS + D] = dot(
        mixed_ref[...].astype(f32).T.astype(bf16), branch
    ).astype(bf16)
    grad_pack_ref[:, KEY_COLS + D :] = jnp.zeros((D, PACK - KEY_COLS - D), bf16)
    left = jnp.concatenate(
        [c_ref[...].astype(f32), gain_one, gain_two, gain_three_ref[...], jnp.zeros((5, D), f32)],
        axis=0,
    )
    lane = lax.broadcasted_iota(jnp.int32, (8, 128), 0) + EXPERTS
    lane = (lane == lax.broadcasted_iota(jnp.int32, (8, 128), 1)).astype(f32)
    right = jnp.concatenate([router_grad.astype(f32), lane], axis=0).astype(bf16)
    grad_one_ref[:, wide:] = dot(left.T.astype(bf16), right).astype(bf16)


def attend_back(start, *operands):
    vm = pl.BlockSpec(memory_space=pltpu.VMEM)
    picked = operands[13]
    return pl.pallas_call(
        attend_back_kernel,
        in_specs=[pl.BlockSpec(memory_space=pltpu.SMEM)] + [vm] * len(operands),
        out_specs=[vm] * 3,
        out_shape=[
            jax.ShapeDtypeStruct(picked.shape, bf16),
            jax.ShapeDtypeStruct((D, PACK), bf16),
            jax.ShapeDtypeStruct((D, PACK), bf16),
        ],
        scratch_shapes=[pltpu.VMEM((SEQUENCE_TOKENS, D), f32)],
        compiler_params=pltpu.CompilerParams(vmem_limit_bytes=60 << 20),
        name="attend_back",
    )(start, *operands)


def lamb_update(weight, moment_one, moment_two, scale_one, scale_two):
    return (moment_one * scale_one) / (jnp.sqrt(moment_two * scale_two) + EPSILON) + DECAY * weight


def lamb_parts(weight, moment_one, moment_two, gradient, scales):
    moment_one = RATE_ONE * moment_one + (1.0 - RATE_ONE) * gradient
    moment_two = RATE_TWO * moment_two + (1.0 - RATE_TWO) * gradient * gradient
    return (moment_one, moment_two, lamb_update(weight, moment_one, moment_two, *scales))


STEPS = 4


def row_lists(tokens, base, rows):
    inside = (tokens >= base) & (tokens < base + rows)
    count = jnp.sum(inside.astype(jnp.int32), axis=1)
    place = jnp.arange(SEQUENCE_TOKENS, dtype=jnp.int32)
    before = (place[:, None] < place[None, :]).astype(bf16)
    rank = jnp.dot(inside.astype(bf16), before, preferred_element_type=f32).astype(jnp.int32)
    packed = place[None, :] * 65536 + (tokens - base)
    hit = inside[:, :, None] & (rank[:, :, None] == place[None, None, :])
    entry = jnp.sum(jnp.where(hit, packed[:, :, None], 0), axis=1)
    empty = SEQUENCE_TOKENS * 65536
    return jnp.where(place[None, :] < count[:, None], entry, empty), count


def gather_kernel(list_ref, count_ref, table_ref, out_ref, rows_ref):
    b = pl.program_id(0)
    rows_ref[...] = jnp.zeros_like(rows_ref)

    def step(k, carry):
        for j in range(STEPS):
            entry = list_ref[b, k * STEPS + j]
            rows_ref[pl.ds(entry >> 16, 1), :] = table_ref[pl.ds(entry & 65535, 1), :]
        return carry

    lax.fori_loop(0, (count_ref[b] + STEPS - 1) // STEPS, step, 0)
    out_ref[0] = rows_ref[:SEQUENCE_TOKENS].astype(bf16)


def gather_rows(lists, counts, table):
    blocks = lists.shape[0]
    rows, columns = table.shape
    return pl.pallas_call(
        gather_kernel,
        grid_spec=pltpu.PrefetchScalarGridSpec(
            num_scalar_prefetch=2,
            grid=(blocks,),
            in_specs=[pl.BlockSpec((rows, columns), lambda b, *_: (0, 0))],
            out_specs=pl.BlockSpec((1, SEQUENCE_TOKENS, columns), lambda b, *_: (b, 0, 0)),
            scratch_shapes=[pltpu.VMEM((SEQUENCE_TOKENS + 8, columns), f32)],
        ),
        out_shape=jax.ShapeDtypeStruct((blocks, SEQUENCE_TOKENS, columns), bf16),
        compiler_params=pltpu.CompilerParams(vmem_limit_bytes=40 << 20),
        name="gather_rows",
    )(lists, counts, table)


TABLE_PARTS = 16


def norm_cells(row, weight_sum, update_sum):
    rows = lax.broadcasted_iota(jnp.int32, (8, 128), 0)
    lanes = lax.broadcasted_iota(jnp.int32, (8, 128), 1)
    block = jnp.where(lanes == 0, weight_sum, jnp.where(lanes == 1, update_sum, 0.0))
    return jnp.where(rows == row, block, 0.0)


def total_of(values):
    return jnp.sum(jnp.sum(values, axis=1, keepdims=True), axis=0, keepdims=True)


def fold(values):
    return jnp.sum(values.reshape(-1, 8, values.shape[1]), axis=0)


def table_kernel(
    list_ref, count_ref, scale_ref, grad_ref, head_ref, w_in, first_in, second_in,
    new_first, new_second, norms,
    rows_ref, acc, w, first, second, sums, sems,
):
    b = pl.program_id(0)
    blocks = pl.num_programs(0) - TABLE_PARTS
    loads = [
        pltpu.make_async_copy(src, dst, sems.at[n])
        for n, (src, dst) in enumerate([(w_in, w), (first_in, first), (second_in, second)])
    ]

    @pl.when(b == 0)
    def _():
        for load in loads:
            load.start()
        acc[...] = head_ref[...].astype(f32)
        sums[...] = jnp.zeros_like(sums)

    @pl.when(b < blocks)
    def _():
        rows_ref[:SEQUENCE_TOKENS] = grad_ref[0].astype(f32)
        rows_ref[SEQUENCE_TOKENS:] = jnp.zeros((8, rows_ref.shape[1]), f32)

        def step(k, carry):
            entries = [list_ref[b, k * STEPS + j] for j in range(STEPS)]
            spots = [entry & 65535 for entry in entries]
            grads = [rows_ref[pl.ds(entry >> 16, 1), :] for entry in entries]
            olds = [acc[pl.ds(spot, 1), :] for spot in spots]
            for j in range(STEPS):
                total = olds[j] + grads[j]
                for i in range(j):
                    total += jnp.where(spots[i] == spots[j], grads[i], 0.0)
                acc[pl.ds(spots[j], 1), :] = total
            return carry

        lax.fori_loop(0, (count_ref[b] + STEPS - 1) // STEPS, step, 0)

    @pl.when(b == blocks)
    def _():
        for load in loads:
            load.wait()

    @pl.when(b >= blocks)
    def _():
        size = new_first.shape[0]
        here = pl.ds(pl.multiple_of((b - blocks) * size, 8), size)
        one, two, update = lamb_parts(
            w[here, :], first[here, :], second[here, :], acc[here, :], (scale_ref[0], scale_ref[1])
        )
        new_first[...] = one
        new_second[...] = two
        sums[0] += fold(w[here, :] * w[here, :])
        sums[1] += fold(update * update)

    @pl.when(b == blocks + TABLE_PARTS - 1)
    def _():
        norms[...] = norm_cells(0, total_of(sums[0]), total_of(sums[1]))


def table_moments(lists, counts, scales, grads, head, weight, first, second):
    blocks = lists.shape[0]
    rows, columns = weight.shape
    part = rows // TABLE_PARTS
    out = pl.BlockSpec((part, columns), lambda b, *_: (jnp.maximum(b - blocks, 0), 0))
    return pl.pallas_call(
        table_kernel,
        grid_spec=pltpu.PrefetchScalarGridSpec(
            num_scalar_prefetch=3,
            grid=(blocks + TABLE_PARTS,),
            in_specs=[
                pl.BlockSpec(
                    (1, SEQUENCE_TOKENS, columns),
                    lambda b, *_: (jnp.minimum(b, blocks - 1), 0, 0),
                ),
                pl.BlockSpec(
                    (rows, columns), lambda b, *_: (0, 0), pipeline_mode=pl.Buffered(1)
                ),
            ]
            + [pl.BlockSpec(memory_space=pl.ANY)] * 3,
            out_specs=[out, out, pl.BlockSpec((8, 128), lambda b, *_: (0, 0))],
            scratch_shapes=[pltpu.VMEM((SEQUENCE_TOKENS + 8, columns), f32)]
            + [pltpu.VMEM((rows, columns), f32)] * 4
            + [pltpu.VMEM((2, 8, columns), f32), pltpu.SemaphoreType.DMA((3,))],
        ),
        out_shape=[jax.ShapeDtypeStruct((rows, columns), f32)] * 2
        + [jax.ShapeDtypeStruct((8, 128), f32)],
        compiler_params=pltpu.CompilerParams(vmem_limit_bytes=54 << 20),
        name="table_moments",
    )(lists, counts, scales, grads, head, weight, first, second)


def small_kernel(
    scale_ref, grad_ref, qkv, qkv_one, qkv_two, out, out_one, out_two, router, router_one, router_two,
    gains, gains_one, gains_two, *results
):
    scales = (scale_ref[0], scale_ref[1])
    planes = grad_ref.shape[0]
    packs = []
    for n in range(2):
        pack = grad_ref[0, n].astype(f32)
        for z in range(1, planes):
            pack += grad_ref[z, n].astype(f32)
        packs.append(pack)
    wide = HEAD_COLS + KEY_COLS
    pick = lax.broadcasted_iota(jnp.int32, (8, 128), 0) + EXPERTS
    pick = (pick == lax.broadcasted_iota(jnp.int32, (8, 128), 1)).astype(f32)
    gains_grad = lax.dot_general(
        pick,
        packs[0][:, wide:],
        ACROSS,
        preferred_element_type=f32,
        precision=lax.Precision.HIGHEST,
    )[:3]
    block = jnp.zeros((8, 128), f32)
    sets = [
        (qkv, qkv_one, qkv_two, jnp.concatenate([packs[0][:, :wide], packs[1][:, :KEY_COLS]], axis=1)),
        (out, out_one, out_two, packs[1][:, KEY_COLS : KEY_COLS + D]),
        (router, router_one, router_two, packs[0][:, wide : wide + EXPERTS]),
        (gains, gains_one, gains_two, gains_grad),
    ]
    for n, (weight, first, second, grad) in enumerate(sets):
        one, two, update = lamb_parts(weight[...], first[...], second[...], grad, scales)
        results[2 * n][...] = one
        results[2 * n + 1][...] = two
        block += norm_cells(n + 1, total_of(weight[...] * weight[...]), total_of(update * update))
    results[8][...] = block


def small_moments(scales, sums, *state):
    vm = pl.BlockSpec(memory_space=pltpu.VMEM)
    return pl.pallas_call(
        small_kernel,
        in_specs=[pl.BlockSpec(memory_space=pltpu.SMEM)] + [vm] * (1 + len(state)),
        out_specs=[vm] * 9,
        out_shape=[jax.ShapeDtypeStruct(x.shape, f32) for x in state[::3] for _ in range(2)]
        + [jax.ShapeDtypeStruct((8, 128), f32)],
        compiler_params=pltpu.CompilerParams(vmem_limit_bytes=16 << 20),
        name="small_moments",
    )(scales, sums, *state)


FINISH_PARTS = 16


def finish_kernel(scale_ref, norms_ref, *refs):
    norms = jnp.sqrt(jnp.sum(norms_ref[...], axis=0))
    count = len(refs) // 4

    def apply(n, row):
        weight = refs[3 * n][...]
        update = lamb_update(
            weight, refs[3 * n + 1][...], refs[3 * n + 2][...], scale_ref[0], scale_ref[1]
        )
        ratio = norms[row : row + 1, 0:1] / norms[row : row + 1, 1:2]
        refs[3 * count + n][...] = weight - (STEP_RATE * ratio) * update

    apply(0, 0)
    apply(1, 5)
    apply(2, 6)

    @pl.when(pl.program_id(0) == 0)
    def _():
        apply(3, 1)
        apply(4, 2)


def finish(scales, norms, *state):
    weights = state[::3]

    def spec(n):
        rows, columns = weights[n].shape
        if n < 3:
            return pl.BlockSpec((rows // FINISH_PARTS, columns), lambda i, *_: (i, 0))
        return pl.BlockSpec((rows, columns), lambda i, *_: (0, 0))

    return pl.pallas_call(
        finish_kernel,
        grid_spec=pltpu.PrefetchScalarGridSpec(
            num_scalar_prefetch=1,
            grid=(FINISH_PARTS,),
            in_specs=[pl.BlockSpec(norms.shape, lambda i, *_: (0, 0, 0))]
            + [spec(n) for n in range(5) for _ in range(3)],
            out_specs=[spec(n) for n in range(5)],
        ),
        out_shape=[jax.ShapeDtypeStruct(x.shape, f32) for x in weights],
        compiler_params=pltpu.CompilerParams(vmem_limit_bytes=40 << 20),
        name="finish",
    )(scales, norms, *state)


def on_device(
    token_ids,
    positions,
    pair_index,
    ref_logps,
    routes,
    step_count,
    embed_table,
    embed_first,
    embed_second,
    qkv_weight,
    qkv_first,
    qkv_second,
    out_weight,
    out_first,
    out_second,
    router_weight,
    router_first,
    router_second,
    norm_gains,
    gains_first,
    gains_second,
    in_weight,
    in_first,
    in_second,
    down_weight,
    down_first,
    down_second,
):
    shard_id = lax.axis_index("shard")
    expert_id = lax.axis_index("expert")
    shards = lax.axis_size("shard")
    planes = lax.axis_size("expert")
    devices = shards * planes
    vocab_rows, columns = embed_table.shape
    vocab_base = shard_id * vocab_rows
    own_rows = vocab_rows // planes
    local_experts = in_weight.shape[0]
    hidden_units = in_weight.shape[3]
    head_cols = QUERY_HEADS * HEAD_WIDTH
    key_cols = KEY_VALUE_HEADS * HEAD_WIDTH
    rows_all = devices * COMP

    side = math.isqrt(shards // 2)
    grid = (planes, side, side, 2)
    together = devices <= 32

    def send(parts, ident):
        if together:
            return communicate(parts, ident)
        return [
            out for n, part in enumerate(parts) for out in communicate([part], ident + 20 * n)
        ]

    unit = own_rows // 24

    def swap(x, *turns, back=False, held=None):
        turns = [(start * unit, size * unit, rounds) for start, size, rounds in turns]
        return Swap(x, turns, planes, side, back, held)

    def gather_part(rows):
        return Gather([rows], split(0, COMP, rows.shape[1], 2, 2), planes, side)

    def reduce_part(rows, cuts):
        rows = rows.reshape(grid + (COMP, rows.shape[1]))
        return Reduce([rows], split(0, COMP, rows.shape[-1], 2, cuts), planes, side)

    def chain(rows, extra, extra_out, middle, beside, ident):
        gather = gather_part(jax.ShapeDtypeStruct((COMP, D), bf16))
        part = Chain(reduce_part(rows, 2), extra, extra_out, middle, gather)
        out = communicate([part, beside], ident)
        return (out[0].reshape(rows_all, D), *out[1:])

    def gather_tiny(block, ident):
        return communicate([Tiny(block, planes, side)], ident)[0].reshape((devices,) + block.shape)

    weight_rows = qkv_weight.shape[0]
    weight_cols = PACK
    cuts = 3 if weight_rows % 48 == 0 else 1
    weight_groups = [
        [
            (i, slice(n * (weight_rows // cuts), (n + 1) * (weight_rows // cuts)), slice(0, weight_cols), i == 0)
            for i in range(2)
        ]
        for n in range(cuts)
    ]
    embed_groups = split(0, SEQUENCE_TOKENS, columns, 4, 1)

    own_places = lax.dynamic_index_in_dim(positions, shard_id, 0, keepdims=False)
    start = own_places[0]
    own_tokens = lax.dynamic_slice_in_dim(token_ids, shard_id * SEQUENCE_TOKENS, SEQUENCE_TOKENS, 0)
    own_routes = lax.dynamic_slice_in_dim(routes, start, COMP, 0)
    sheet = jnp.concatenate(
        [
            own_tokens,
            own_routes.reshape(-1),
            own_places,
            jnp.zeros((1024 - SEQUENCE_TOKENS - COMP * TOP - COMP,), jnp.int32),
        ]
    )
    sheets = gather_tiny(sheet.reshape(8, 128), 0).reshape(devices, 1024)
    tokens_all = sheets[:, :SEQUENCE_TOKENS]
    routes_all = sheets[:, SEQUENCE_TOKENS : SEQUENCE_TOKENS + COMP * TOP].reshape(rows_all, TOP)
    places_all = sheets[:, SEQUENCE_TOKENS + COMP * TOP : SEQUENCE_TOKENS + COMP * TOP + COMP]
    spots = jnp.arange(SEQUENCE_TOKENS, dtype=jnp.int32)
    targets = jnp.sum(
        jnp.where(
            places_all[:, :, None] + 1 == spots[None, None, :], tokens_all[:, None, :], 0
        ),
        axis=2,
    ).reshape(-1)

    lists, counts = row_lists(tokens_all, vocab_base, vocab_rows)
    picked = gather_rows(lists, counts, embed_table).reshape(grid + (SEQUENCE_TOKENS, columns))
    packs = [
        jnp.concatenate(
            [
                qkv_weight[:, : head_cols + key_cols],
                router_weight,
                norm_gains.T,
                jnp.zeros((weight_rows, 128 - EXPERTS - 3), f32),
            ],
            axis=1,
        ).astype(bf16),
        jnp.concatenate(
            [
                qkv_weight[:, head_cols + key_cols :],
                out_weight,
                jnp.zeros((weight_rows, 128), f32),
            ],
            axis=1,
        ).astype(bf16),
    ]
    table_b = embed_table.astype(bf16)
    packs = jnp.concatenate(packs, axis=0)
    packs, sheets = lax.optimization_barrier((packs, sheets))
    packs = lax.all_to_all(
        jnp.broadcast_to(packs[None], (planes,) + packs.shape),
        "expert",
        split_axis=0,
        concat_axis=0,
        tiled=True,
    )
    table_b = embed_table.astype(bf16)
    first_pack, second_pack, picked, table_own = send(
        [
            Gather(
                [packs[:, :weight_rows], packs[:, weight_rows:]],
                weight_groups,
                planes,
                side,
                prior=True,
            ),
            Reduce([picked], embed_groups, planes, side, exchange=True),
            swap(table_b, (0, 16, 0)),
        ],
        1,
    )
    first_pack = first_pack.reshape(D, weight_cols)
    second_pack = second_pack.reshape(D, weight_cols)

    start_at = start.reshape(1)
    tables = rotary_tables()
    tables += tuple(lax.dynamic_slice_in_dim(table, start, COMP, 0) for table in tables)
    normed_two_b, resid, probs, query, key, value, attended, normed_b, gains = attend(
        start_at, picked, first_pack, second_pack, *tables
    )

    expert_rows, table_own = communicate(
        [gather_part(normed_two_b), swap(table_b, (16, 2, 2), held=table_own)], 2
    )
    expert_rows = expert_rows.reshape(rows_all, D)
    lanes = shard_id * local_experts + jnp.arange(local_experts, dtype=jnp.int32)
    in_rows = in_weight.reshape(-1, hidden_units)
    produced, mid, gates, in_cat, down_b, gated_hidden = experts_forward(
        lanes, expert_rows, routes_all, first_pack, in_rows, down_weight
    )
    own_index = expert_id * shards + shard_id
    own_gates = lax.dynamic_slice(gates, (own_index * COMP, 0), (COMP, 128))
    row_block = jax.ShapeDtypeStruct((COMP, D), f32)
    head_rows, resid_two, table_own = chain(
        produced,
        [resid, gains],
        [row_block],
        final_norm,
        swap(table_b, (18, 3, 0), (21, 3, 8), held=table_own),
        3,
    )

    logits = jnp.einsum("rd,vd->rv", head_rows, table_own, preferred_element_type=f32) / LOGIT_SCALE
    own_base = vocab_base + expert_id * own_rows
    target_hot = targets[:, None] == own_base + jnp.arange(own_rows, dtype=jnp.int32)[None, :]
    row_top = jnp.max(logits, axis=1)
    row_total = jnp.sum(jnp.exp(logits - row_top[:, None]), axis=1)
    row_hit = jnp.sum(jnp.where(target_hot, logits, 0.0), axis=1)
    stats = jnp.stack([row_top, row_total, row_hit]).reshape(8, 3 * rows_all // 8)
    stats = gather_tiny(stats, 5).reshape(devices, 3, rows_all)
    top_all = jnp.max(stats[:, 0], axis=0)
    total_all = jnp.sum(stats[:, 1] * jnp.exp(stats[:, 0] - top_all[None]), axis=0)
    row_lse = top_all + jnp.log(total_all)
    seq_sums = jnp.sum((jnp.sum(stats[:, 2], axis=0) - row_lse).reshape(-1, COMP), axis=1)

    sequences = jnp.arange(devices, dtype=jnp.int32)[None, :]
    pair_sign = (pair_index[:, :1] == sequences).astype(f32) - (
        pair_index[:, 1:] == sequences
    ).astype(f32)
    scaled = BETA * jnp.sum(pair_sign * (seq_sums - ref_logps)[None, :], axis=1)
    loss_value = -jnp.mean(jax.nn.log_sigmoid(scaled))
    pair_grad = jax.nn.sigmoid(-scaled) * (-BETA / scaled.shape[0])
    seq_grad = jnp.sum(pair_sign * pair_grad[:, None], axis=0)
    row_grad = jnp.repeat(seq_grad, COMP)
    grad_logits = (
        row_grad[:, None] * (target_hot.astype(f32) - jnp.exp(logits - row_lse[:, None]))
    ).astype(bf16)
    grad_logits = lax.optimization_barrier(grad_logits)
    grad_rows = jnp.dot(grad_logits, table_own, preferred_element_type=f32) / LOGIT_SCALE
    head_grad = (
        jnp.einsum("rv,rd->vd", grad_logits, head_rows, preferred_element_type=f32) / LOGIT_SCALE
    ).astype(bf16)
    grad_all, grad_resid_two, grad_gain_three, head_back = chain(
        grad_rows.astype(bf16),
        [resid_two, gains],
        [row_block, jax.ShapeDtypeStruct((1, D), f32)],
        final_norm_back,
        swap(head_grad, (0, 3, 0), (3, 3, 8), back=True),
        6,
    )

    back, mid_grad = experts_backward(lanes, grad_all, mid, gates, in_cat, down_b)
    back, head_back = communicate(
        [reduce_part(back, 1), swap(head_grad, (6, 3, 0), back=True, held=head_back)], 8
    )

    grad_embedded, *grad_packs = attend_back(
        start_at,
        back,
        own_gates,
        grad_resid_two,
        grad_gain_three,
        normed_two_b,
        resid,
        probs,
        query,
        key,
        value,
        attended,
        normed_b,
        gains,
        picked,
        first_pack,
        second_pack,
        *tables,
    )
    grad_packs = [pack.reshape(grid + (weight_rows, weight_cols)) for pack in grad_packs]
    wide = head_cols + key_cols
    first_grad, second_grad, sent, head_back = send(
        [
            Reduce(grad_packs, weight_groups, planes, side, partial=True),
            Gather([grad_embedded], embed_groups, planes, side, exchange=True),
            swap(head_grad, (9, 5, 1), (14, 5, 2), (19, 5, 3), back=True, held=head_back),
        ],
        9,
    )
    plane_sums = lax.all_to_all(
        jnp.concatenate([first_grad, second_grad], axis=1),
        "expert",
        split_axis=0,
        concat_axis=0,
        tiled=True,
    ).reshape(planes, 2, weight_rows, weight_cols)

    step_value = step_count.astype(f32)
    scales = jnp.stack([1.0 / (1.0 - RATE_ONE**step_value), 1.0 / (1.0 - RATE_TWO**step_value)])
    grad_in = jnp.einsum("td,tk->dk", expert_rows, mid_grad, preferred_element_type=f32)
    grad_down = jnp.einsum("tk,td->kd", gated_hidden, grad_all, preferred_element_type=f32)
    down_rows = down_weight.reshape(-1, D)
    in_one, in_two, down_one, down_two, expert_norms = expert_moments(
        scales,
        grad_in,
        in_rows,
        in_first.reshape(in_rows.shape),
        in_second.reshape(in_rows.shape),
        grad_down,
        down_rows,
        down_first.reshape(down_rows.shape),
        down_second.reshape(down_rows.shape),
    )
    table_one, table_two, table_norms = table_moments(
        lists,
        counts,
        scales,
        sent.reshape(devices, SEQUENCE_TOKENS, columns),
        head_back.reshape(vocab_rows, columns),
        embed_table,
        embed_first,
        embed_second,
    )
    *small, small_norms = small_moments(
        scales,
        plane_sums,
        qkv_weight,
        qkv_first,
        qkv_second,
        out_weight,
        out_first,
        out_second,
        router_weight,
        router_first,
        router_second,
        norm_gains,
        gains_first,
        gains_second,
    )
    norm_blocks = gather_tiny(expert_norms + table_norms + small_norms, 10)
    norm_values = jnp.sqrt(jnp.sum(norm_blocks, axis=0))[:7, :2]
    trust_ratio = norm_values[:, 0] / norm_values[:, 1]
    new_table, new_in, new_down, new_qkv, new_out = finish(
        scales,
        norm_blocks,
        embed_table,
        table_one,
        table_two,
        in_rows,
        in_one,
        in_two,
        down_rows,
        down_one,
        down_two,
        qkv_weight,
        small[0],
        small[1],
        out_weight,
        small[2],
        small[3],
    )

    def renew(place, weight, one, two):
        update = lamb_update(weight, one, two, scales[0], scales[1])
        return weight - STEP_RATE * trust_ratio[place] * update

    new_router = renew(3, router_weight, small[4], small[5])
    new_gains = renew(4, norm_gains, small[6], small[7])
    stats = jnp.stack([norm_values[:, 0], norm_values[:, 1], trust_ratio], axis=1)
    return (
        loss_value,
        new_table,
        table_one,
        table_two,
        new_qkv,
        small[0],
        small[1],
        new_out,
        small[2],
        small[3],
        new_router,
        small[4],
        small[5],
        new_gains,
        small[6],
        small[7],
        new_in.reshape(in_weight.shape),
        in_one.reshape(in_weight.shape),
        in_two.reshape(in_weight.shape),
        new_down.reshape(down_weight.shape),
        down_one.reshape(down_weight.shape),
        down_two.reshape(down_weight.shape),
        stats,
    )


def solution(mesh):
    rows = P(BOTH, None)
    vocab = P("shard", "expert")
    gains = P(None, BOTH)
    inner = P("shard", None, None, "expert")
    outer = P("shard", "expert", None)
    state = (vocab,) * 3 + (rows,) * 9 + (gains,) * 3 + (inner,) * 3 + (outer,) * 3
    return jax.shard_map(
        on_device,
        mesh=mesh,
        in_specs=(P("expert"), P("expert", None), P(), P(), rows, P()) + state,
        out_specs=(P(),) + state + (P(),),
        check_vma=False,
    )
```

```python
import functools
import math

import jax
import jax.numpy as jnp
from jax import lax
from jax.experimental import pallas as pl
from jax.experimental.pallas import tpu as pltpu
from jax.sharding import PartitionSpec as P

D = 1536
QUERY_HEADS = 24
KEY_VALUE_HEADS = 8
GROUP = QUERY_HEADS // KEY_VALUE_HEADS
HEAD_WIDTH = 64
TOP = 8
EXPERTS = 32
SEQUENCE_TOKENS = 256
COMP = 32
QKV = 2560

BETA = 0.1
LOGIT_SCALE = 6.0
RATE_ONE = 0.9
RATE_TWO = 0.999
EPSILON = 1e-06
DECAY = 0.01
STEP_RATE = 0.3

BOTH = ("expert", "shard")
bf16 = jnp.bfloat16
f32 = jnp.float32


MESH = pl.DeviceIdType.MESH


class Spot:
    def __init__(self, planes, side):
        self.planes, self.side = planes, side
        self.z = lax.axis_index("expert")
        self.shard = lax.axis_index("shard")
        self.core = lax.rem(self.shard, 2)
        self.b = lax.rem(lax.div(self.shard, 2), side)
        self.a = lax.div(self.shard, 2 * side)

    def plane(self, k):
        z = lax.rem(self.z + k, self.planes)
        return z, (z, self.shard)

    def along_a(self, k):
        a = lax.rem(self.a + k, self.side)
        return a, (self.z, (a * self.side + self.b) * 2 + self.core)

    def along_b(self, k):
        b = lax.rem(self.b + k, self.side)
        return b, (self.z, (self.a * self.side + b) * 2 + self.core)

    def along(self, first, k):
        return self.along_a(k) if first else self.along_b(k)

    def mate(self):
        other = 1 - self.core
        return other, (self.z, (self.a * self.side + self.b) * 2 + other)

    def near(self, k):
        return self.z, lax.rem(self.shard + k, 2 * self.side * self.side)

    def greet(self, flat):
        targets = [self.plane(k)[1] for k in range(1, self.planes)]
        if flat:
            targets += [self.near(k) for k in range(1, 2 * self.side * self.side)]
        else:
            targets.append(self.mate()[1])
            for k in range(1, self.side):
                targets += [self.along_a(k)[1], self.along_b(k)[1]]
        barrier = pltpu.get_barrier_semaphore()
        for target in targets:
            pl.semaphore_signal(barrier, inc=1, device_id=target, device_id_type=MESH)
        pl.semaphore_wait(barrier, len(targets))


class Mail:
    def __init__(self, send, recv):
        self.send, self.recv, self.count, self.open = send, recv, 0, []

    def start(self, src, dst, target):
        copy = pltpu.make_async_remote_copy(
            src_ref=src,
            dst_ref=dst,
            send_sem=self.send.at[self.count],
            recv_sem=self.recv.at[self.count],
            device_id=target,
            device_id_type=MESH,
        )
        self.count += 1
        copy.start()
        self.open.append(copy)
        return copy

    def finish(self):
        for copy in self.open:
            copy.wait_send()


def arrive(copies):
    for copy in copies:
        copy.wait_recv()


class Tiny:
    flat = True
    scratch = ()

    def __init__(self, x, planes, side):
        self.planes, self.side, self.inputs = planes, side, [x]
        shape = (planes, 2 * side * side) + x.shape
        self.outputs = [jax.ShapeDtypeStruct(shape, x.dtype)]
        self.copies = planes + 2 * side * side - 2

    def steps(self, spot, mail, x, out):
        out[spot.z, spot.shard] = x[...]
        sent = []
        for k in range(1, self.planes):
            sent.append(mail.start(x, out.at[spot.z, spot.shard], spot.plane(k)[1]))
        yield
        arrive(sent)
        part = out.at[:, spot.shard]
        yield
        arrive([mail.start(part, part, spot.near(k)) for k in range(1, 2 * self.side**2)])


def split(array, rows, columns, row_parts, column_parts):
    r, c = rows // row_parts, columns // column_parts
    cuts = [
        (array, slice(i * r, i * r + r), slice(j * c, j * c + c))
        for j in range(column_parts)
        for i in range(row_parts)
    ]
    cuts = [cut + (n % 2 == 0,) for n, cut in enumerate(cuts)]
    return [cuts[n : n + 2] for n in range(0, len(cuts), 2)]


def pipeline(groups, stage, last):
    sent = [[[] for _ in group] for group in groups]
    for tick in range(len(groups) + last):
        for step in range(last, -1, -1):
            turn = tick - step
            if 0 <= turn < len(groups):
                for n, cut in enumerate(groups[turn]):
                    for copy in sent[turn][n]:
                        copy.wait_recv()
                    sent[turn][n] = stage(step, (turn, n), cut)
        yield


class Gather:
    flat = False
    scratch = ()

    def __init__(self, xs, groups, planes, side, exchange=False, prior=False):
        self.planes, self.side, self.inputs, self.groups = planes, side, xs, groups
        self.exchange, self.prior = exchange, prior
        grid = (planes, side, side, 2)
        self.outputs = [jax.ShapeDtypeStruct(grid + x.shape[-2:], x.dtype) for x in xs]
        self.copies = sum(map(len, groups)) * (planes - 1 + 2 * (side - 1) + 1)

    def steps(self, spot, mail, *refs):
        xs, outs = refs[: len(self.inputs)], refs[len(self.inputs) :]
        z, a, b, core = spot.z, spot.a, spot.b, spot.core
        for x, out in zip(xs, outs):
            if self.prior:
                out[:, a, b, core] = x[...]
            else:
                out[z, a, b, core] = x[z] if self.exchange else x[...]

        def stage(step, key, cut):
            i, rows, columns, first = cut
            x, out = xs[i], outs[i]
            if step == 0 and self.prior:
                return []
            if step == 0:
                place = out.at[z, a, b, core, rows, columns]
                sent = []
                for k in range(1, self.planes):
                    peer, target = spot.plane(k)
                    own = x.at[peer, rows, columns] if self.exchange else x.at[rows, columns]
                    sent.append(mail.start(own, place, target))
                return sent
            if step in (1, 2):
                if step == 1:
                    part = out.at[:, a, b, core, rows, columns]
                elif first:
                    part = out.at[:, :, b, core, rows, columns]
                else:
                    part = out.at[:, a, :, core, rows, columns]
                return [
                    mail.start(part, part, spot.along(first == (step == 1), k)[1])
                    for k in range(1, self.side)
                ]
            if step == 3:
                part = out.at[:, :, :, core, rows, columns]
                return [mail.start(part, part, spot.mate()[1])]
            return []

        return pipeline(self.groups, stage, 4)


class Reduce:
    flat = False

    def __init__(self, xs, groups, planes, side, exchange=False, partial=False):
        self.planes, self.side, self.inputs, self.groups = planes, side, xs, groups
        self.exchange, self.partial = exchange or partial, partial
        self.outputs = [
            jax.ShapeDtypeStruct((planes,) + x.shape[-2:], x.dtype)
            if self.exchange
            else jax.ShapeDtypeStruct(x.shape[-2:], f32)
            for x in xs
        ]
        self.scratch = []
        for i, rows, columns, _ in [cut for group in groups for cut in group]:
            block = (rows.stop - rows.start, columns.stop - columns.start)
            self.scratch += [
                pltpu.VMEM(shape + block, xs[i].dtype)
                for shape in (
                    (planes, side, side),
                    (side - 1, planes, side),
                    (planes, side),
                    (side - 1, planes),
                    (planes,),
                )
                + (() if self.exchange else ((planes - 1,),))
            ]
        self.copies = sum(map(len, groups)) * (planes - 1 + 2 * (side - 1) + 1)

    def steps(self, spot, mail, *refs):
        planes, side, number = self.planes, self.side, len(self.inputs)
        xs, outs, rest = refs[:number], refs[number : 2 * number], refs[2 * number :]
        each = 5 if self.exchange else 6
        order = [(t, n) for t, group in enumerate(self.groups) for n in range(len(group))]
        held = {key: rest[each * p : each * (p + 1)] for p, key in enumerate(order)}
        core, z = spot.core, spot.z
        other, mate = spot.mate()

        def stage(step, key, cut):
            i, rows, columns, first = cut
            x, out = xs[i], outs[i]
            one, hop_two, two, hop_three, three = held[key][:5]
            if step == 0:
                return [mail.start(x.at[:, :, :, other, rows, columns], one, mate)]
            sent = []
            if step == 1:

                def add(n, carry):
                    ia, ib = lax.rem(lax.div(n, side), side), lax.rem(n, side)
                    iz = lax.div(n, side * side)
                    total = x[iz, ia, ib, core, rows, columns].astype(f32)
                    one[iz, ia, ib] = (total + one[iz, ia, ib].astype(f32)).astype(one.dtype)
                    return carry

                lax.fori_loop(0, planes * side * side, add, 0)
                for k in range(1, side):
                    peer, target = spot.along(first, k)
                    part = one.at[:, peer] if first else one.at[:, :, peer]
                    sent.append(mail.start(part, hop_two.at[k - 1], target))
            elif step == 2:

                def add(n, carry):
                    iz, ir = lax.div(n, side), lax.rem(n, side)
                    total = (one[iz, spot.a, ir] if first else one[iz, ir, spot.b]).astype(f32)
                    for k in range(side - 1):
                        total += hop_two[k, iz, ir].astype(f32)
                    two[iz, ir] = total.astype(two.dtype)
                    return carry

                lax.fori_loop(0, planes * side, add, 0)
                for k in range(1, side):
                    peer, target = spot.along(not first, k)
                    sent.append(mail.start(two.at[:, peer], hop_three.at[k - 1], target))
            elif step == 3:
                mine = spot.b if first else spot.a

                def add(iz, carry):
                    total = two[iz, mine].astype(f32)
                    for k in range(side - 1):
                        total += hop_three[k, iz].astype(f32)
                    if self.partial:
                        out[iz, rows, columns] = total.astype(out.dtype)
                    else:
                        three[iz] = total.astype(three.dtype)
                    return carry

                lax.fori_loop(0, planes, add, 0)
                if self.partial:
                    return []
                for k in range(1, planes):
                    peer, target = spot.plane(k)
                    if self.exchange:
                        place = out.at[z, rows, columns]
                    else:
                        place = held[key][5].at[k - 1]
                    sent.append(mail.start(three.at[peer], place, target))
                if self.exchange:
                    out[z, rows, columns] = three[z]
            elif not self.exchange:
                total = three[z].astype(f32)
                for k in range(planes - 1):
                    total += held[key][5][k].astype(f32)
                out[rows, columns] = total
            return sent

        return pipeline(self.groups, stage, 4)


class Swap:
    flat = False
    def __init__(self, x, turns, planes, side, back=False, held=None):
        self.planes, self.side = planes, side
        self.inputs = [x] if held is None else [x, held]
        self.in_spaces, self.out_spaces = (pltpu.HBM,) * len(self.inputs), (pltpu.HBM,)
        self.aliases = {} if held is None else {1: 0}
        self.turns, self.back = turns, back
        self.scratch = [pltpu.SemaphoreType.DMA((len(turns),))]
        self.columns = x.shape[1] // planes if back else x.shape[1]
        self.rows = x.shape[0] if back else x.shape[0] // planes
        shape = (planes, self.rows, self.columns) if back else (self.rows, planes * self.columns)
        self.outputs = [jax.ShapeDtypeStruct(shape, x.dtype)]
        self.copies = len(turns) * (planes - 1)

    def steps(self, spot, mail, *refs):
        x, out, own_sem = refs[0], refs[-2], refs[-1]
        def block(z):
            return pl.ds(pl.multiple_of(z * self.columns, 128), self.columns)

        def source(z, begin, size):
            if self.back:
                return x.at[pl.ds(begin, size), block(z)]
            return x.at[pl.ds(pl.multiple_of(z * self.rows + begin, 16), size), :]

        sent, own, now = [], [], 0
        for n, (begin, size, rounds) in enumerate(self.turns):
            while now < rounds:
                now += 1
                yield
            rows = pl.ds(begin, size)
            place = out.at[spot.z, rows] if self.back else out.at[rows, block(spot.z)]
            for k in range(1, self.planes):
                peer, target = spot.plane(k)
                sent.append(mail.start(source(peer, begin, size), place, target))
            own.append(pltpu.make_async_copy(source(spot.z, begin, size), place, own_sem.at[n]))
            own[-1].start()
        while now < 24:
            now += 1
            yield
        for copy in own:
            copy.wait()
        for copy in sent:
            copy.wait_recv()


class Chain:
    flat = False

    def __init__(self, reduce, extra, extra_out, middle, gather):
        self.planes, self.side = reduce.planes, reduce.side
        self.reduce, self.middle, self.gather = reduce, middle, gather
        self.inputs = reduce.inputs + extra
        self.outputs = gather.outputs + extra_out
        self.scratch = reduce.scratch + [
            pltpu.VMEM(x.shape, x.dtype) for x in reduce.outputs + gather.inputs
        ]
        self.copies = reduce.copies + gather.copies

    def steps(self, spot, mail, *refs):
        n_in, n_out = len(self.inputs), len(self.outputs)
        (x, *extra), (out, *extra_out) = refs[:n_in], refs[n_in : n_in + n_out]
        *held, sums, made = refs[n_in + n_out :]
        yield from self.reduce.steps(spot, mail, x, sums, *held)
        self.middle(sums, made, *extra, *extra_out)
        yield from self.gather.steps(spot, mail, made, out)


def final_norm(sums, made, resid, gains, resid_two):
    values = resid[...] + sums[...]
    resid_two[...] = values
    made[...] = (values * inverse_root(values) * gains[2:3]).astype(bf16)


def final_norm_back(sums, made, resid_two, gains, grad_two, gain_grad):
    grad, gain_grad[...] = norm_back(resid_two[...], gains[2:3], sums[...])
    grad_two[...] = grad
    made[...] = grad.astype(bf16)


def communicate(parts, ident):
    planes, side = parts[0].planes, parts[0].side
    counts = [(len(p.inputs), len(p.outputs), len(p.scratch)) for p in parts]
    n_in, n_out = (sum(c[i] for c in counts) for i in range(2))
    copies = sum(p.copies for p in parts)
    aliases, i, o = {}, 0, 0
    for part, (ci, co, _) in zip(parts, counts):
        aliases.update({i + a: o + b for a, b in getattr(part, "aliases", {}).items()})
        i, o = i + ci, o + co

    def kernel(*refs):
        ins, outs, rest = refs[:n_in], refs[n_in : n_in + n_out], refs[n_in + n_out :]
        send, recv = rest[-2:]
        spot = Spot(planes, side)
        spot.greet(parts[0].flat)
        mail = Mail(send, recv)
        running, i, o, s = [], 0, 0, 0
        for part, (ci, co, cs) in zip(parts, counts):
            running.append(
                part.steps(spot, mail, *ins[i : i + ci], *outs[o : o + co], *rest[s : s + cs])
            )
            i, o, s = i + ci, o + co, s + cs
        while running:
            running = [steps for steps in running if next(steps, True) is None]
        mail.finish()

    size = sum(x.size * x.dtype.itemsize for p in parts for x in p.inputs + p.outputs)
    need = size + sum(
        math.prod(x.shape) * x.dtype.itemsize
        for p in parts
        for x in p.scratch
        if x.memory_space == pltpu.VMEM
    )
    out = pl.pallas_call(
        kernel,
        out_shape=[x for p in parts for x in p.outputs],
        in_specs=[
            pl.BlockSpec(memory_space=space)
            for p in parts
            for space in getattr(p, "in_spaces", (pltpu.VMEM,) * len(p.inputs))
        ],
        out_specs=[
            pl.BlockSpec(memory_space=space)
            for p in parts
            for space in getattr(p, "out_spaces", (pltpu.VMEM,) * len(p.outputs))
        ],
        input_output_aliases=aliases,
        scratch_shapes=[s for p in parts for s in p.scratch]
        + [pltpu.SemaphoreType.DMA((copies,)), pltpu.SemaphoreType.DMA((copies,))],
        compiler_params=pltpu.CompilerParams(
            collective_id=ident,
            has_side_effects=True,
            vmem_limit_bytes=min(62 << 20, need * 9 // 8 + (4 << 20)),
        ),
        cost_estimate=pl.CostEstimate(flops=0, bytes_accessed=20 * size, transcendentals=0),
        name="exchange_" + str(ident),
    )(*[x for p in parts for x in p.inputs])
    return list(out)

def expert_gate(gates, lane):
    lanes = lax.broadcasted_iota(jnp.int32, gates.shape, 1)
    return jnp.sum(jnp.where(lanes == lane, gates, 0.0), axis=1, keepdims=True)


CHUNK = 512
BLOCK = 1024
ACROSS = (((1,), (1,)), ((), ()))


def forward_kernel(
    lane_ref, rows_ref, routes_ref, router_ref, in_ref, down_ref, out_ref, mid_ref, gates_ref, cat_ref, down_out, hidden_ref
):
    e, number = pl.program_id(1), pl.num_programs(1)
    units = in_ref.shape[1]
    for j in range(2):
        cat_ref[:, j * units : (j + 1) * units] = in_ref[pl.ds(j, D, stride=2), :].astype(bf16)
    down_out[pl.ds(pl.multiple_of(e * units, units), units), :] = down_ref[0].astype(bf16)

    def chunk(i, carry):
        here = pl.ds(pl.multiple_of(i * CHUNK, CHUNK), CHUNK)
        rows = rows_ref[here, :]

        @pl.when(e == 0)
        def _():
            logits = jnp.dot(rows, router_ref[...], preferred_element_type=f32)
            lanes = lax.broadcasted_iota(jnp.int32, logits.shape, 1)
            mask = lanes == routes_ref[here, 0:1]
            for j in range(1, TOP):
                mask |= lanes == routes_ref[here, j : j + 1]
            top = jnp.max(jnp.where(mask, logits, -3e38), axis=1, keepdims=True)
            weight = jnp.where(mask, jnp.exp(jnp.where(mask, logits - top, 0.0)), 0.0)
            gates_ref[here, :] = weight / jnp.sum(weight, axis=1, keepdims=True)

        mid = jnp.dot(rows, cat_ref[...], preferred_element_type=f32)
        mid_ref[here, :] = mid
        gate, up = mid[:, :units], mid[:, units:]
        hidden = (gate * jax.nn.sigmoid(gate) * up).astype(bf16).astype(f32)
        hidden = (hidden * expert_gate(gates_ref[here, :], lane_ref[0] + e)).astype(bf16)
        hidden_ref[here, pl.ds(pl.multiple_of(e * units, units), units)] = hidden

        @pl.when(e == number - 1)
        def _():
            out_ref[here, :] = jnp.dot(
                hidden_ref[here, :], down_out[...], preferred_element_type=f32
            ).astype(bf16)

        return carry

    lax.fori_loop(0, rows_ref.shape[0] // CHUNK, chunk, 0)


def experts_forward(lane, rows, routes, router, in_rows, down):
    number, units = down.shape[:2]
    total = rows.shape[0]
    block = min(total, BLOCK)
    row = lambda r, e, *_: (r, 0)
    still = lambda r, e, *_: (0, 0)
    return pl.pallas_call(
        forward_kernel,
        grid_spec=pltpu.PrefetchScalarGridSpec(
            num_scalar_prefetch=1,
            grid=(total // block, number),
            in_specs=[
                pl.BlockSpec((block, D), row),
                pl.BlockSpec((block, TOP), row),
                pl.BlockSpec((D, 128), lambda r, e, *_: (0, PACK // 128 - 1)),
                pl.BlockSpec((2 * D, units), lambda r, e, *_: (e, 0)),
                pl.BlockSpec((1, units, D), lambda r, e, *_: (e, 0, 0)),
            ],
            out_specs=[
                pl.BlockSpec((block, D), row),
                pl.BlockSpec((block, 2 * units), lambda r, e, *_: (r, e)),
                pl.BlockSpec((block, 128), row),
                pl.BlockSpec((D, 2 * units), lambda r, e, *_: (0, e)),
                pl.BlockSpec((number * units, D), still),
                pl.BlockSpec((block, number * units), row),
            ],
        ),
        out_shape=[
            jax.ShapeDtypeStruct((total, D), bf16),
            jax.ShapeDtypeStruct((total, 2 * units * number), f32),
            jax.ShapeDtypeStruct((total, 128), f32),
            jax.ShapeDtypeStruct((D, 2 * units * number), bf16),
            jax.ShapeDtypeStruct((number * units, D), bf16),
            jax.ShapeDtypeStruct((total, number * units), bf16),
        ],
        compiler_params=pltpu.CompilerParams(vmem_limit_bytes=42 << 20),
        name="experts_forward",
    )(lane, rows, routes, router, in_rows, down)


def backward_kernel(
    lane_ref, grad_ref, mid_ref, gates_ref, cat_ref, down_ref, out_ref, mid_grad_ref, pulled_ref
):
    number = lane_ref.shape[0]
    units = pulled_ref.shape[1] // number

    def chunk(i, carry):
        here = pl.ds(pl.multiple_of(i * CHUNK, CHUNK), CHUNK)
        pulled_ref[...] = lax.dot_general(
            grad_ref[here, :], down_ref[...], ACROSS, preferred_element_type=f32
        )
        lanes = lax.broadcasted_iota(jnp.int32, (CHUNK, 128), 1)
        gate_part = jnp.zeros((CHUNK, 128), f32)
        for e in range(number):
            lane = lane_ref[e]
            weight = expert_gate(gates_ref[here, :], lane)
            gate = mid_ref[here, 2 * e * units : (2 * e + 1) * units]
            up = mid_ref[here, (2 * e + 1) * units : (2 * e + 2) * units]
            pulled = pulled_ref[:, e * units : (e + 1) * units]
            soft = jax.nn.sigmoid(gate)
            silu = gate * soft
            hidden = (silu * up).astype(bf16).astype(f32)
            gate_grad = jnp.sum(hidden * pulled, axis=1, keepdims=True)
            gate_part = jnp.where(lanes == lane, gate_grad, gate_part)
            hidden_grad = (pulled * weight).astype(bf16).astype(f32)
            turned = hidden_grad * up * (soft * (1.0 + gate * (1.0 - soft)))
            mid_grad_ref[here, 2 * e * units : (2 * e + 1) * units] = turned.astype(bf16)
            mid_grad_ref[here, (2 * e + 1) * units : (2 * e + 2) * units] = (
                hidden_grad * silu
            ).astype(bf16)
        out_ref[here, D:] = gate_part.astype(bf16)
        out_ref[here, :D] = lax.dot_general(
            mid_grad_ref[here, :], cat_ref[...], ACROSS, preferred_element_type=f32
        ).astype(bf16)
        return carry

    lax.fori_loop(0, grad_ref.shape[0] // CHUNK, chunk, 0)


def experts_backward(lanes, grad, mid, gates, cat, down):
    number = lanes.shape[0]
    total = grad.shape[0]
    block = min(total, BLOCK)
    row = lambda r, *_: (r, 0)
    still = lambda r, *_: (0, 0)
    return pl.pallas_call(
        backward_kernel,
        grid_spec=pltpu.PrefetchScalarGridSpec(
            num_scalar_prefetch=1,
            grid=(total // block,),
            in_specs=[
                pl.BlockSpec((block, D), row),
                pl.BlockSpec((block, mid.shape[1]), row),
                pl.BlockSpec((block, 128), row),
                pl.BlockSpec(cat.shape, still),
                pl.BlockSpec(down.shape, still),
            ],
            out_specs=[
                pl.BlockSpec((block, D + 128), row),
                pl.BlockSpec((block, mid.shape[1]), row),
            ],
            scratch_shapes=[pltpu.VMEM((CHUNK, down.shape[0]), f32)],
        ),
        out_shape=[
            jax.ShapeDtypeStruct((total, D + 128), bf16),
            jax.ShapeDtypeStruct(mid.shape, bf16),
        ],
        compiler_params=pltpu.CompilerParams(vmem_limit_bytes=50 << 20),
        name="experts_backward",
    )(lanes, grad, mid, gates, cat, down)


def moments_kernel(
    scale_ref, other_norms, grad_ref, w_ref, first_ref, second_ref, down_grad, down_w, down_first, down_second,
    new_first, new_second, updates, new_down_first, new_down_second, down_updates, norms, sums, down_sums,
):
    units = w_ref.shape[1]
    part = w_ref.shape[0] // 2
    scales = (scale_ref[0], scale_ref[1])
    step = pl.program_id(0) * pl.num_programs(1) + pl.program_id(1)

    @pl.when(step == 0)
    def _():
        sums[...] = jnp.zeros_like(sums)
        down_sums[...] = jnp.zeros_like(down_sums)

    for j in range(2):
        here = pl.ds(j, part, stride=2)
        grad = grad_ref[:, j * units : (j + 1) * units]
        weight = w_ref[here, :]
        one, two, update = lamb_parts(weight, first_ref[here, :], second_ref[here, :], grad, scales)
        new_first[here, :] = one
        new_second[here, :] = two
        updates[here, :] = update
        sums[0] += fold(weight * weight)
        sums[1] += fold(update * update)
    weight = down_w[...]
    one, two, update = lamb_parts(weight, down_first[...], down_second[...], down_grad[...], scales)
    new_down_first[...] = one
    new_down_second[...] = two
    down_updates[...] = update
    down_sums[0] += fold(weight * weight)
    down_sums[1] += fold(update * update)

    @pl.when(step == pl.num_programs(0) * pl.num_programs(1) - 1)
    def _():
        block = norm_cells(5, total_of(sums[0]), total_of(sums[1]))
        block += norm_cells(6, total_of(down_sums[0]), total_of(down_sums[1]))
        norms[...] = other_norms[...] + block


def expert_moments(scales, norms, grad, weight, first, second, *down_state):
    units = weight.shape[1]
    down = down_state[1]
    number = grad.shape[1] // (2 * units)
    parts = 2
    cells = pl.BlockSpec((8, 128), lambda e, p, *_: (0, 0))
    row = pl.BlockSpec((2 * D // parts, units), lambda e, p, *_: (e * parts + p, 0))
    down_row = pl.BlockSpec((units // parts, D), lambda e, p, *_: (e * parts + p, 0))
    return pl.pallas_call(
        moments_kernel,
        grid_spec=pltpu.PrefetchScalarGridSpec(
            num_scalar_prefetch=1,
            grid=(number, parts),
            in_specs=[cells, pl.BlockSpec((D // parts, 2 * units), lambda e, p, *_: (p, e))]
            + [row] * 3
            + [down_row] * 4,
            out_specs=[row] * 3 + [down_row] * 3 + [cells],
            scratch_shapes=[pltpu.VMEM((2, 8, units), f32), pltpu.VMEM((2, 8, D), f32)],
        ),
        out_shape=[jax.ShapeDtypeStruct(weight.shape, f32)] * 3
        + [jax.ShapeDtypeStruct(down.shape, f32)] * 3
        + [jax.ShapeDtypeStruct((8, 128), f32)],
        compiler_params=pltpu.CompilerParams(vmem_limit_bytes=62 << 20),
        name="expert_moments",
    )(scales, norms, grad, weight, first, second, *down_state)


HEAD_COLS = QUERY_HEADS * HEAD_WIDTH
KEY_COLS = KEY_VALUE_HEADS * HEAD_WIDTH
PACK = HEAD_COLS + KEY_COLS + 128
ROOT = HEAD_WIDTH ** (-0.5)


def turn(u, cosine, sine):
    width = u.shape[1]
    lanes = lax.broadcasted_iota(jnp.int32, u.shape, 1)
    ahead = pltpu.roll(u, width - HEAD_WIDTH // 2, 1)
    behind = pltpu.roll(u, HEAD_WIDTH // 2, 1)
    other = jnp.where(lax.rem(lanes, HEAD_WIDTH) < HEAD_WIDTH // 2, ahead, behind)
    return u * jnp.tile(cosine, (1, width // 128)) + other * jnp.tile(sine, (1, width // 128))


def rotary_tables():
    half = HEAD_WIDTH // 2
    freqs = jnp.exp(-jnp.log(10000.0) * jnp.arange(half, dtype=f32) / half)
    angles = jnp.arange(SEQUENCE_TOKENS, dtype=f32)[:, None] * freqs[None, :]
    cosine, sine = jnp.cos(angles), jnp.sin(angles)
    return jnp.tile(cosine, (1, 4)), jnp.tile(jnp.concatenate([-sine, sine], axis=1), (1, 2))


def inverse_root(values):
    return lax.rsqrt(jnp.mean(values * values, axis=-1, keepdims=True) + 1e-06)


def norm_back(values, gain, grad):
    root = inverse_root(values)
    scaled = grad * gain
    inner = jnp.mean(scaled * values, axis=-1, keepdims=True)
    return root * scaled - values * (root * root * root * inner), jnp.sum(
        grad * values * root, axis=0, keepdims=True
    )


def dot(a, b):
    return jnp.dot(a, b, preferred_element_type=f32)


def dot_across(a, b):
    return lax.dot_general(a, b, ACROSS, preferred_element_type=f32)


def selector(start, shape, axis):
    row = lax.broadcasted_iota(jnp.int32, shape, 1 - axis) + start
    return (row == lax.broadcasted_iota(jnp.int32, shape, axis)).astype(f32)


def spread(start, rows):
    pick = selector(start, (SEQUENCE_TOKENS, COMP), 0)
    return jnp.dot(pick, rows, preferred_element_type=f32, precision=lax.Precision.HIGHEST)


def head_rows(ref_value, h):
    first = h * GROUP * HEAD_WIDTH
    return jnp.concatenate(
        [
            ref_value[:, first + g * HEAD_WIDTH : first + (g + 1) * HEAD_WIDTH]
            for g in range(GROUP)
        ],
        axis=0,
    )


def head_lanes(parts):
    return jnp.concatenate(
        [part[g * COMP : (g + 1) * COMP] for part in parts for g in range(GROUP)], axis=1
    )


def attend_kernel(
    start_ref, picked_ref, one_ref, two_ref, cos_ref, sin_ref, cos_rows, sin_rows,
    c_ref, resid_ref, probs_ref, query_ref, key_ref, value_ref, mixed_ref, normed_ref, gains_ref,
    embedded,
):
    start = start_ref[0]
    pick_rows = selector(start, (COMP, SEQUENCE_TOKENS), 1).astype(bf16)
    planes, _, columns = picked_ref.shape
    for p in range(planes):
        embedded[:, p * columns : (p + 1) * columns] = picked_ref[p].astype(f32)
    pick = lax.broadcasted_iota(jnp.int32, (8, 128), 0) + EXPERTS
    pick = (pick == lax.broadcasted_iota(jnp.int32, (8, 128), 1)).astype(f32).astype(bf16)
    gains = dot_across(pick, one_ref[:, HEAD_COLS + KEY_COLS :])
    gains_ref[...] = gains
    x = embedded[...]
    a = (x * inverse_root(x) * gains[0:1]).astype(bf16)
    normed_ref[...] = a
    a_rows = dot(pick_rows, a).astype(bf16)
    cosine, sine = cos_ref[...], sin_ref[...]
    query = turn(dot(a_rows, one_ref[:, :HEAD_COLS]), cos_rows[...], sin_rows[...])
    query = query.astype(bf16)
    key = turn(dot(a, one_ref[:, HEAD_COLS : HEAD_COLS + KEY_COLS]), cosine, sine).astype(bf16)
    value = dot(a, two_ref[:, :KEY_COLS]).astype(bf16)
    query_ref[...], key_ref[...], value_ref[...] = query, key, value
    rows = GROUP * COMP
    place = lax.rem(lax.broadcasted_iota(jnp.int32, (rows, SEQUENCE_TOKENS), 0), COMP) + start
    seen = place >= lax.broadcasted_iota(jnp.int32, (rows, SEQUENCE_TOKENS), 1)
    parts = []
    for h in range(KEY_VALUE_HEADS):
        lanes = slice(h * HEAD_WIDTH, (h + 1) * HEAD_WIDTH)
        scores = dot_across(head_rows(query, h), key[:, lanes]) * ROOT
        scores = jnp.where(seen, scores, -1000000000.0)
        expd = jnp.exp(scores - jnp.max(scores, axis=-1, keepdims=True))
        probs = expd / jnp.sum(expd, axis=-1, keepdims=True)
        probs_ref[h] = probs
        parts.append(dot(probs.astype(bf16), value[:, lanes]))
    mixed = head_lanes(parts).astype(bf16)
    mixed_ref[...] = mixed
    resid = dot(pick_rows, embedded[...].astype(bf16)) + dot(mixed, two_ref[:, KEY_COLS : KEY_COLS + D])
    resid_ref[...] = resid
    c_ref[...] = (resid * inverse_root(resid) * gains[1:2]).astype(bf16)


def attend(start, picked, one, two, *tables):
    vm = pl.BlockSpec(memory_space=pltpu.VMEM)
    rows = GROUP * COMP
    return pl.pallas_call(
        attend_kernel,
        in_specs=[pl.BlockSpec(memory_space=pltpu.SMEM)] + [vm] * 7,
        out_specs=[vm] * 9,
        out_shape=[
            jax.ShapeDtypeStruct((COMP, D), bf16),
            jax.ShapeDtypeStruct((COMP, D), f32),
            jax.ShapeDtypeStruct((KEY_VALUE_HEADS, rows, SEQUENCE_TOKENS), f32),
            jax.ShapeDtypeStruct((COMP, HEAD_COLS), bf16),
            jax.ShapeDtypeStruct((SEQUENCE_TOKENS, KEY_COLS), bf16),
            jax.ShapeDtypeStruct((SEQUENCE_TOKENS, KEY_COLS), bf16),
            jax.ShapeDtypeStruct((COMP, HEAD_COLS), bf16),
            jax.ShapeDtypeStruct((SEQUENCE_TOKENS, D), bf16),
            jax.ShapeDtypeStruct((8, D), f32),
        ],
        scratch_shapes=[pltpu.VMEM((SEQUENCE_TOKENS, D), f32)],
        compiler_params=pltpu.CompilerParams(vmem_limit_bytes=28 << 20),
        name="attend",
    )(start, picked, one, two, *tables)


def attend_back_kernel(
    start_ref, back_ref, gates_ref, grad_two_ref, gain_three_ref, c_ref, resid_ref, probs_ref, query_ref,
    key_ref, value_ref, mixed_ref, normed_ref, gains_ref, picked_ref, one_ref, two_ref, cos_ref, sin_ref, cos_rows, sin_rows,
    out_ref, grad_one_ref, grad_pack_ref,
    total,
):
    start = start_ref[0]
    planes, _, columns = picked_ref.shape
    gains = gains_ref[...]
    wide = HEAD_COLS + KEY_COLS
    gates = gates_ref[...]
    gate_grad = back_ref[:, D:]
    router_grad = gates * (gate_grad - jnp.sum(gates * gate_grad, axis=1, keepdims=True))
    router_grad = router_grad.astype(bf16)
    grad = back_ref[:, :D] + dot_across(router_grad, one_ref[:, wide:])
    grad_resid, gain_two = norm_back(resid_ref[...], gains[1:2], grad)
    grad_resid = grad_resid + grad_two_ref[...]
    branch = grad_resid.astype(bf16)
    grad_mixed = dot_across(branch, two_ref[:, KEY_COLS : KEY_COLS + D]).astype(bf16)
    query, key, value = query_ref[...], key_ref[...], value_ref[...]
    query_parts, key_parts, value_parts = [], [], []
    for h in range(KEY_VALUE_HEADS):
        lanes = slice(h * HEAD_WIDTH, (h + 1) * HEAD_WIDTH)
        probs = probs_ref[h]
        grad_head = head_rows(grad_mixed, h)
        grad_probs = dot_across(grad_head, value[:, lanes]).astype(bf16).astype(f32)
        inner = jnp.sum(grad_probs * probs, axis=-1, keepdims=True)
        grad_scores = probs * (grad_probs - inner)
        value_parts.append(dot(probs.T.astype(bf16), grad_head))
        query_parts.append(dot(grad_scores.astype(bf16), key[:, lanes]) * ROOT)
        key_parts.append(dot(grad_scores.T.astype(bf16), head_rows(query, h)) * ROOT)
    grad_query = turn(head_lanes(query_parts), cos_rows[...], -sin_rows[...]).astype(bf16)
    grad_key = jnp.concatenate(key_parts, axis=1)
    grad_key = turn(grad_key, cos_ref[...], -sin_ref[...]).astype(bf16)
    grad_value = jnp.concatenate(value_parts, axis=1).astype(bf16)
    grad_normed = dot_across(grad_key, one_ref[:, HEAD_COLS:wide])
    grad_normed += dot_across(grad_value, two_ref[:, :KEY_COLS])
    grad_normed += spread(start, dot_across(grad_query, one_ref[:, :HEAD_COLS]))
    for p in range(planes):
        total[:, p * columns : (p + 1) * columns] = picked_ref[p].astype(f32)
    grad_embedded, gain_one = norm_back(total[...], gains[0:1], grad_normed)
    total[...] = grad_embedded + spread(start, grad_resid)
    for p in range(planes):
        out_ref[p] = total[:, p * columns : (p + 1) * columns].astype(bf16)
    pick_rows = selector(start, (COMP, SEQUENCE_TOKENS), 1).astype(bf16)
    a_rows = dot(pick_rows, normed_ref[...])
    turned = normed_ref[...].astype(f32).T.astype(bf16)
    grad_one_ref[:, HEAD_COLS:wide] = dot(turned, grad_key).astype(bf16)
    grad_pack_ref[:, :KEY_COLS] = dot(turned, grad_value).astype(bf16)
    grad_one_ref[:, :HEAD_COLS] = dot(a_rows.T.astype(bf16), grad_query).astype(bf16)
    grad_pack_ref[:, KEY_COLS : KEY_COLS + D] = dot(
        mixed_ref[...].astype(f32).T.astype(bf16), branch
    ).astype(bf16)
    grad_pack_ref[:, KEY_COLS + D :] = jnp.zeros((D, PACK - KEY_COLS - D), bf16)
    left = jnp.concatenate(
        [c_ref[...].astype(f32), gain_one, gain_two, gain_three_ref[...], jnp.zeros((5, D), f32)],
        axis=0,
    )
    lane = lax.broadcasted_iota(jnp.int32, (8, 128), 0) + EXPERTS
    lane = (lane == lax.broadcasted_iota(jnp.int32, (8, 128), 1)).astype(f32)
    right = jnp.concatenate([router_grad.astype(f32), lane], axis=0).astype(bf16)
    grad_one_ref[:, wide:] = dot(left.T.astype(bf16), right).astype(bf16)


def attend_back(start, *operands):
    vm = pl.BlockSpec(memory_space=pltpu.VMEM)
    picked = operands[13]
    return pl.pallas_call(
        attend_back_kernel,
        in_specs=[pl.BlockSpec(memory_space=pltpu.SMEM)] + [vm] * len(operands),
        out_specs=[vm] * 3,
        out_shape=[
            jax.ShapeDtypeStruct(picked.shape, bf16),
            jax.ShapeDtypeStruct((D, PACK), bf16),
            jax.ShapeDtypeStruct((D, PACK), bf16),
        ],
        scratch_shapes=[pltpu.VMEM((SEQUENCE_TOKENS, D), f32)],
        compiler_params=pltpu.CompilerParams(vmem_limit_bytes=44 << 20),
        name="attend_back",
    )(start, *operands)


def lamb_update(weight, moment_one, moment_two, scale_one, scale_two):
    return (moment_one * scale_one) / (jnp.sqrt(moment_two * scale_two) + EPSILON) + DECAY * weight


def lamb_parts(weight, moment_one, moment_two, gradient, scales):
    moment_one = RATE_ONE * moment_one + (1.0 - RATE_ONE) * gradient
    moment_two = RATE_TWO * moment_two + (1.0 - RATE_TWO) * gradient * gradient
    return (moment_one, moment_two, lamb_update(weight, moment_one, moment_two, *scales))


STEPS = 4
TOGETHER = 4


def row_lists(tokens, base, rows):
    inside = (tokens >= base) & (tokens < base + rows)
    count = jnp.sum(inside.astype(jnp.int32), axis=1)
    place = jnp.arange(SEQUENCE_TOKENS, dtype=jnp.int32)
    before = (place[:, None] < place[None, :]).astype(bf16)
    rank = jnp.dot(inside.astype(bf16), before, preferred_element_type=f32).astype(jnp.int32)
    packed = place[None, :] * 65536 + (tokens - base)
    hit = inside[:, :, None] & (rank[:, :, None] == place[None, None, :])
    entry = jnp.sum(jnp.where(hit, packed[:, :, None], 0), axis=1)
    empty = SEQUENCE_TOKENS * 65536
    return jnp.where(place[None, :] < count[:, None], entry, empty), count


def gather_kernel(list_ref, count_ref, table_ref, out_ref, rows_ref):
    for n in range(TOGETHER):
        b = pl.program_id(0) * TOGETHER + n
        rows_ref[n] = jnp.zeros(rows_ref.shape[1:], f32)

        def step(k, carry, n=n, b=b):
            for j in range(STEPS):
                entry = list_ref[b, k * STEPS + j]
                rows_ref[n, pl.ds(entry >> 16, 1), :] = table_ref[pl.ds(entry & 65535, 1), :]
            return carry

        lax.fori_loop(0, (count_ref[b] + STEPS - 1) // STEPS, step, 0)
        out_ref[n] = rows_ref[n, :SEQUENCE_TOKENS].astype(bf16)


def gather_rows(lists, counts, table):
    blocks = lists.shape[0]
    rows, columns = table.shape
    return pl.pallas_call(
        gather_kernel,
        grid_spec=pltpu.PrefetchScalarGridSpec(
            num_scalar_prefetch=2,
            grid=(blocks // TOGETHER,),
            in_specs=[pl.BlockSpec((rows, columns), lambda b, *_: (0, 0))],
            out_specs=pl.BlockSpec((TOGETHER, SEQUENCE_TOKENS, columns), lambda b, *_: (b, 0, 0)),
            scratch_shapes=[pltpu.VMEM((TOGETHER, SEQUENCE_TOKENS + 8, columns), f32)],
        ),
        out_shape=jax.ShapeDtypeStruct((blocks, SEQUENCE_TOKENS, columns), bf16),
        compiler_params=pltpu.CompilerParams(vmem_limit_bytes=22 << 20),
        name="gather_rows",
    )(lists, counts, table)


TABLE_PARTS = 16


def norm_cells(row, weight_sum, update_sum):
    rows = lax.broadcasted_iota(jnp.int32, (8, 128), 0)
    lanes = lax.broadcasted_iota(jnp.int32, (8, 128), 1)
    block = jnp.where(lanes == 0, weight_sum, jnp.where(lanes == 1, update_sum, 0.0))
    return jnp.where(rows == row, block, 0.0)


def total_of(values):
    return jnp.sum(jnp.sum(values, axis=1, keepdims=True), axis=0, keepdims=True)


def fold(values):
    return jnp.sum(values.reshape(-1, 8, values.shape[1]), axis=0)


def table_kernel(
    list_ref, count_ref, scale_ref, grad_ref, head_ref, w_in, first_in, second_in,
    new_first, new_second, updates, norms,
    rows_ref, acc, w, first, second, sums, sems,
):
    b = pl.program_id(0)
    blocks = pl.num_programs(0) - TABLE_PARTS
    loads = [
        pltpu.make_async_copy(src, dst, sems.at[n])
        for n, (src, dst) in enumerate([(w_in, w), (first_in, first), (second_in, second)])
    ]

    @pl.when(b == 0)
    def _():
        for load in loads:
            load.start()
        acc[...] = head_ref[...].astype(f32)
        sums[...] = jnp.zeros_like(sums)

    @pl.when(b < blocks)
    def _():
        for n in range(TOGETHER):
            rows_ref[n, :SEQUENCE_TOKENS] = grad_ref[n].astype(f32)
            rows_ref[n, SEQUENCE_TOKENS:] = jnp.zeros((8, rows_ref.shape[2]), f32)
            own = b * TOGETHER + n

            def step(k, carry, n=n, own=own):
                entries = [list_ref[own, k * STEPS + j] for j in range(STEPS)]
                spots = [entry & 65535 for entry in entries]
                grads = [rows_ref[n, pl.ds(entry >> 16, 1), :] for entry in entries]
                olds = [acc[pl.ds(spot, 1), :] for spot in spots]
                for j in range(STEPS):
                    total = olds[j] + grads[j]
                    for i in range(j):
                        total += jnp.where(spots[i] == spots[j], grads[i], 0.0)
                    acc[pl.ds(spots[j], 1), :] = total
                return carry

            lax.fori_loop(0, (count_ref[own] + STEPS - 1) // STEPS, step, 0)

    @pl.when(b == blocks)
    def _():
        for load in loads:
            load.wait()

    @pl.when(b >= blocks)
    def _():
        size = new_first.shape[0]
        here = pl.ds(pl.multiple_of((b - blocks) * size, 8), size)
        one, two, update = lamb_parts(
            w[here, :], first[here, :], second[here, :], acc[here, :], (scale_ref[0], scale_ref[1])
        )
        new_first[...] = one
        new_second[...] = two
        updates[...] = update
        sums[0] += fold(w[here, :] * w[here, :])
        sums[1] += fold(update * update)

    @pl.when(b == blocks + TABLE_PARTS - 1)
    def _():
        norms[...] = norm_cells(0, total_of(sums[0]), total_of(sums[1]))


def table_moments(lists, counts, scales, grads, head, weight, first, second):
    blocks = lists.shape[0] // TOGETHER
    rows, columns = weight.shape
    part = rows // TABLE_PARTS
    out = pl.BlockSpec((part, columns), lambda b, *_: (jnp.maximum(b - blocks, 0), 0))
    return pl.pallas_call(
        table_kernel,
        grid_spec=pltpu.PrefetchScalarGridSpec(
            num_scalar_prefetch=3,
            grid=(blocks + TABLE_PARTS,),
            in_specs=[
                pl.BlockSpec(
                    (TOGETHER, SEQUENCE_TOKENS, columns),
                    lambda b, *_: (jnp.minimum(b, blocks - 1), 0, 0),
                ),
                pl.BlockSpec(
                    (rows, columns), lambda b, *_: (0, 0), pipeline_mode=pl.Buffered(1)
                ),
            ]
            + [pl.BlockSpec(memory_space=pl.ANY)] * 3,
            out_specs=[out, out, out, pl.BlockSpec((8, 128), lambda b, *_: (0, 0))],
            scratch_shapes=[pltpu.VMEM((TOGETHER, SEQUENCE_TOKENS + 8, columns), f32)]
            + [pltpu.VMEM((rows, columns), f32)] * 4
            + [pltpu.VMEM((2, 8, columns), f32), pltpu.SemaphoreType.DMA((3,))],
        ),
        out_shape=[jax.ShapeDtypeStruct((rows, columns), f32)] * 3
        + [jax.ShapeDtypeStruct((8, 128), f32)],
        compiler_params=pltpu.CompilerParams(vmem_limit_bytes=52 << 20),
        name="table_moments",
    )(lists, counts, scales, grads, head, weight, first, second)


def small_kernel(
    scale_ref, grad_ref, qkv, qkv_one, qkv_two, out, out_one, out_two, router, router_one, router_two,
    gains, gains_one, gains_two, *results
):
    scales = (scale_ref[0], scale_ref[1])
    planes = grad_ref.shape[0]
    packs = []
    for n in range(2):
        pack = grad_ref[0, n].astype(f32)
        for z in range(1, planes):
            pack += grad_ref[z, n].astype(f32)
        packs.append(pack)
    wide = HEAD_COLS + KEY_COLS
    pick = lax.broadcasted_iota(jnp.int32, (8, 128), 0) + EXPERTS
    pick = (pick == lax.broadcasted_iota(jnp.int32, (8, 128), 1)).astype(f32)
    gains_grad = lax.dot_general(
        pick,
        packs[0][:, wide:],
        ACROSS,
        preferred_element_type=f32,
        precision=lax.Precision.HIGHEST,
    )[:3]
    block = jnp.zeros((8, 128), f32)
    sets = [
        (qkv, qkv_one, qkv_two, jnp.concatenate([packs[0][:, :wide], packs[1][:, :KEY_COLS]], axis=1)),
        (out, out_one, out_two, packs[1][:, KEY_COLS : KEY_COLS + D]),
        (router, router_one, router_two, packs[0][:, wide : wide + EXPERTS]),
        (gains, gains_one, gains_two, gains_grad),
    ]
    for n, (weight, first, second, grad) in enumerate(sets):
        one, two, update = lamb_parts(weight[...], first[...], second[...], grad, scales)
        results[3 * n][...] = one
        results[3 * n + 1][...] = two
        results[3 * n + 2][...] = update
        block += norm_cells(n + 1, total_of(weight[...] * weight[...]), total_of(update * update))
    results[12][...] = block


def small_moments(scales, sums, *state):
    vm = pl.BlockSpec(memory_space=pltpu.VMEM)
    return pl.pallas_call(
        small_kernel,
        in_specs=[pl.BlockSpec(memory_space=pltpu.SMEM)] + [vm] * (1 + len(state)),
        out_specs=[vm] * 13,
        out_shape=[jax.ShapeDtypeStruct(x.shape, f32) for x in state[::3] for _ in range(3)]
        + [jax.ShapeDtypeStruct((8, 128), f32)],
        compiler_params=pltpu.CompilerParams(vmem_limit_bytes=62 << 20),
        name="small_moments",
    )(scales, sums, *state)


FINISH_PARTS = 16


def finish_kernel(norms_ref, *refs):
    norms = jnp.sqrt(jnp.sum(norms_ref[...], axis=0))
    count = len(refs) // 3

    def apply(n, row):
        ratio = norms[row : row + 1, 0:1] / norms[row : row + 1, 1:2]
        refs[2 * count + n][...] = refs[2 * n][...] - (STEP_RATE * ratio) * refs[2 * n + 1][...]

    apply(0, 0)
    apply(1, 5)
    apply(2, 6)

    @pl.when(pl.program_id(0) == 0)
    def _():
        apply(3, 1)
        apply(4, 2)


def finish(norms, *state):
    weights = state[::2]

    def spec(n):
        rows, columns = weights[n].shape
        if n < 3:
            return pl.BlockSpec((rows // FINISH_PARTS, columns), lambda i: (i, 0))
        return pl.BlockSpec((rows, columns), lambda i: (0, 0))

    return pl.pallas_call(
        finish_kernel,
        grid=(FINISH_PARTS,),
        in_specs=[pl.BlockSpec(norms.shape, lambda i: (0, 0, 0))]
        + [spec(n) for n in range(5) for _ in range(2)],
        out_specs=[spec(n) for n in range(5)],
        out_shape=[jax.ShapeDtypeStruct(x.shape, f32) for x in weights],
        compiler_params=pltpu.CompilerParams(vmem_limit_bytes=62 << 20),
        name="finish",
    )(norms, *state)


def on_device(
    token_ids,
    positions,
    pair_index,
    ref_logps,
    routes,
    step_count,
    embed_table,
    embed_first,
    embed_second,
    qkv_weight,
    qkv_first,
    qkv_second,
    out_weight,
    out_first,
    out_second,
    router_weight,
    router_first,
    router_second,
    norm_gains,
    gains_first,
    gains_second,
    in_weight,
    in_first,
    in_second,
    down_weight,
    down_first,
    down_second,
):
    shard_id = lax.axis_index("shard")
    expert_id = lax.axis_index("expert")
    shards = lax.axis_size("shard")
    planes = lax.axis_size("expert")
    devices = shards * planes
    vocab_rows, columns = embed_table.shape
    vocab_base = shard_id * vocab_rows
    own_rows = vocab_rows // planes
    local_experts = in_weight.shape[0]
    hidden_units = in_weight.shape[3]
    head_cols = QUERY_HEADS * HEAD_WIDTH
    key_cols = KEY_VALUE_HEADS * HEAD_WIDTH
    rows_all = devices * COMP

    side = math.isqrt(shards // 2)
    grid = (planes, side, side, 2)
    together = devices <= 32

    def send(parts, ident):
        if together:
            return communicate(parts, ident)
        return [
            out for n, part in enumerate(parts) for out in communicate([part], ident + 20 * n)
        ]

    unit = own_rows // 24

    def swap(x, *turns, back=False, held=None):
        turns = [(start * unit, size * unit, rounds) for start, size, rounds in turns]
        return Swap(x, turns, planes, side, back, held)

    def gather_part(rows):
        return Gather([rows], split(0, COMP, rows.shape[1], 2, 2), planes, side)

    def reduce_part(rows, cuts):
        rows = rows.reshape(grid + (COMP, rows.shape[1]))
        return Reduce([rows], split(0, COMP, rows.shape[-1], 2, cuts), planes, side)

    def chain(rows, extra, extra_out, middle, beside, ident):
        gather = gather_part(jax.ShapeDtypeStruct((COMP, D), bf16))
        part = Chain(reduce_part(rows, 2), extra, extra_out, middle, gather)
        out = communicate([part, beside], ident)
        return (out[0].reshape(rows_all, D), *out[1:])

    def gather_tiny(block, ident):
        return communicate([Tiny(block, planes, side)], ident)[0].reshape((devices,) + block.shape)

    weight_rows = qkv_weight.shape[0]
    weight_cols = PACK
    cuts = 3 if weight_rows % 48 == 0 else 1
    weight_groups = [
        [
            (i, slice(n * (weight_rows // cuts), (n + 1) * (weight_rows // cuts)), slice(0, weight_cols), i == 0)
            for i in range(2)
        ]
        for n in range(cuts)
    ]
    embed_groups = split(0, SEQUENCE_TOKENS, columns, 4, 1)

    own_places = lax.dynamic_index_in_dim(positions, shard_id, 0, keepdims=False)
    start = own_places[0]
    own_tokens = lax.dynamic_slice_in_dim(token_ids, shard_id * SEQUENCE_TOKENS, SEQUENCE_TOKENS, 0)
    own_routes = lax.dynamic_slice_in_dim(routes, start, COMP, 0)
    sheet = jnp.concatenate(
        [
            own_tokens,
            own_routes.reshape(-1),
            own_places,
            jnp.zeros((1024 - SEQUENCE_TOKENS - COMP * TOP - COMP,), jnp.int32),
        ]
    )
    sheets = gather_tiny(sheet.reshape(8, 128), 0).reshape(devices, 1024)
    tokens_all = sheets[:, :SEQUENCE_TOKENS]
    routes_all = sheets[:, SEQUENCE_TOKENS : SEQUENCE_TOKENS + COMP * TOP].reshape(rows_all, TOP)
    places_all = sheets[:, SEQUENCE_TOKENS + COMP * TOP : SEQUENCE_TOKENS + COMP * TOP + COMP]
    spots = jnp.arange(SEQUENCE_TOKENS, dtype=jnp.int32)
    targets = jnp.sum(
        jnp.where(
            places_all[:, :, None] + 1 == spots[None, None, :], tokens_all[:, None, :], 0
        ),
        axis=2,
    ).reshape(-1)

    lists, counts = row_lists(tokens_all, vocab_base, vocab_rows)
    picked = gather_rows(lists, counts, embed_table).reshape(grid + (SEQUENCE_TOKENS, columns))
    packs = [
        jnp.concatenate(
            [
                qkv_weight[:, : head_cols + key_cols],
                router_weight,
                norm_gains.T,
                jnp.zeros((weight_rows, 128 - EXPERTS - 3), f32),
            ],
            axis=1,
        ).astype(bf16),
        jnp.concatenate(
            [
                qkv_weight[:, head_cols + key_cols :],
                out_weight,
                jnp.zeros((weight_rows, 128), f32),
            ],
            axis=1,
        ).astype(bf16),
    ]
    table_b = embed_table.astype(bf16)
    packs = jnp.concatenate(packs, axis=0)
    packs, sheets = lax.optimization_barrier((packs, sheets))
    packs = lax.all_to_all(
        jnp.broadcast_to(packs[None], (planes,) + packs.shape),
        "expert",
        split_axis=0,
        concat_axis=0,
        tiled=True,
    )
    table_b = embed_table.astype(bf16)
    first_pack, second_pack, picked, table_own = send(
        [
            Gather(
                [packs[:, :weight_rows], packs[:, weight_rows:]],
                weight_groups,
                planes,
                side,
                prior=True,
            ),
            Reduce([picked], embed_groups, planes, side, exchange=True),
            swap(table_b, (0, 16, 0)),
        ],
        1,
    )
    first_pack = first_pack.reshape(D, weight_cols)
    second_pack = second_pack.reshape(D, weight_cols)

    start_at = start.reshape(1)
    tables = rotary_tables()
    tables += tuple(lax.dynamic_slice_in_dim(table, start, COMP, 0) for table in tables)
    normed_two_b, resid, probs, query, key, value, attended, normed_b, gains = attend(
        start_at, picked, first_pack, second_pack, *tables
    )

    expert_rows, table_own = communicate(
        [gather_part(normed_two_b), swap(table_b, (16, 2, 2), held=table_own)], 2
    )
    expert_rows = expert_rows.reshape(rows_all, D)
    lanes = shard_id * local_experts + jnp.arange(local_experts, dtype=jnp.int32)
    in_rows = in_weight.reshape(-1, hidden_units)
    produced, mid, gates, in_cat, down_b, gated_hidden = experts_forward(
        lanes, expert_rows, routes_all, first_pack, in_rows, down_weight
    )
    own_index = expert_id * shards + shard_id
    own_gates = lax.dynamic_slice(gates, (own_index * COMP, 0), (COMP, 128))
    row_block = jax.ShapeDtypeStruct((COMP, D), f32)
    head_rows, resid_two, table_own = chain(
        produced,
        [resid, gains],
        [row_block],
        final_norm,
        swap(table_b, (18, 3, 0), (21, 3, 8), held=table_own),
        3,
    )

    logits = jnp.einsum("rd,vd->rv", head_rows, table_own, preferred_element_type=f32) / LOGIT_SCALE
    own_base = vocab_base + expert_id * own_rows
    target_hot = targets[:, None] == own_base + jnp.arange(own_rows, dtype=jnp.int32)[None, :]
    row_top = jnp.max(logits, axis=1)
    row_total = jnp.sum(jnp.exp(logits - row_top[:, None]), axis=1)
    row_hit = jnp.sum(jnp.where(target_hot, logits, 0.0), axis=1)
    stats = jnp.stack([row_top, row_total, row_hit]).reshape(8, 3 * rows_all // 8)
    stats = gather_tiny(stats, 5).reshape(devices, 3, rows_all)
    top_all = jnp.max(stats[:, 0], axis=0)
    total_all = jnp.sum(stats[:, 1] * jnp.exp(stats[:, 0] - top_all[None]), axis=0)
    row_lse = top_all + jnp.log(total_all)
    seq_sums = jnp.sum((jnp.sum(stats[:, 2], axis=0) - row_lse).reshape(-1, COMP), axis=1)

    sequences = jnp.arange(devices, dtype=jnp.int32)[None, :]
    pair_sign = (pair_index[:, :1] == sequences).astype(f32) - (
        pair_index[:, 1:] == sequences
    ).astype(f32)
    scaled = BETA * jnp.sum(pair_sign * (seq_sums - ref_logps)[None, :], axis=1)
    loss_value = -jnp.mean(jax.nn.log_sigmoid(scaled))
    pair_grad = jax.nn.sigmoid(-scaled) * (-BETA / scaled.shape[0])
    seq_grad = jnp.sum(pair_sign * pair_grad[:, None], axis=0)
    row_grad = jnp.repeat(seq_grad, COMP)
    grad_logits = (
        row_grad[:, None] * (target_hot.astype(f32) - jnp.exp(logits - row_lse[:, None]))
    ).astype(bf16)
    grad_logits = lax.optimization_barrier(grad_logits)
    grad_rows = jnp.dot(grad_logits, table_own, preferred_element_type=f32) / LOGIT_SCALE
    head_grad = (
        jnp.einsum("rv,rd->vd", grad_logits, head_rows, preferred_element_type=f32) / LOGIT_SCALE
    ).astype(bf16)
    grad_all, grad_resid_two, grad_gain_three, head_back = chain(
        grad_rows.astype(bf16),
        [resid_two, gains],
        [row_block, jax.ShapeDtypeStruct((1, D), f32)],
        final_norm_back,
        swap(head_grad, (0, 3, 0), (3, 3, 8), back=True),
        6,
    )

    back, mid_grad = experts_backward(lanes, grad_all, mid, gates, in_cat, down_b)
    back, head_back = communicate(
        [reduce_part(back, 1), swap(head_grad, (6, 3, 0), back=True, held=head_back)], 8
    )

    grad_embedded, *grad_packs = attend_back(
        start_at,
        back,
        own_gates,
        grad_resid_two,
        grad_gain_three,
        normed_two_b,
        resid,
        probs,
        query,
        key,
        value,
        attended,
        normed_b,
        gains,
        picked,
        first_pack,
        second_pack,
        *tables,
    )
    grad_packs = [pack.reshape(grid + (weight_rows, weight_cols)) for pack in grad_packs]
    wide = head_cols + key_cols
    first_grad, second_grad, sent, head_back = send(
        [
            Reduce(grad_packs, weight_groups, planes, side, partial=True),
            Gather([grad_embedded], embed_groups, planes, side, exchange=True),
            swap(head_grad, (9, 5, 1), (14, 5, 2), (19, 5, 3), back=True, held=head_back),
        ],
        9,
    )
    plane_sums = lax.all_to_all(
        jnp.concatenate([first_grad, second_grad], axis=1),
        "expert",
        split_axis=0,
        concat_axis=0,
        tiled=True,
    ).reshape(planes, 2, weight_rows, weight_cols)

    step_value = step_count.astype(f32)
    scales = jnp.stack([1.0 / (1.0 - RATE_ONE**step_value), 1.0 / (1.0 - RATE_TWO**step_value)])
    grad_in = jnp.einsum("td,tk->dk", expert_rows, mid_grad, preferred_element_type=f32)
    grad_down = jnp.einsum("tk,td->kd", gated_hidden, grad_all, preferred_element_type=f32)
    down_rows = down_weight.reshape(-1, D)
    table_one, table_two, table_update, table_norms = table_moments(
        lists,
        counts,
        scales,
        sent.reshape(devices, SEQUENCE_TOKENS, columns),
        head_back.reshape(vocab_rows, columns),
        embed_table,
        embed_first,
        embed_second,
    )
    *small, small_norms = small_moments(
        scales,
        plane_sums,
        qkv_weight,
        qkv_first,
        qkv_second,
        out_weight,
        out_first,
        out_second,
        router_weight,
        router_first,
        router_second,
        norm_gains,
        gains_first,
        gains_second,
    )
    in_one, in_two, in_update, down_one, down_two, down_update, expert_norms = expert_moments(
        scales,
        table_norms + small_norms,
        grad_in,
        in_rows,
        in_first.reshape(in_rows.shape),
        in_second.reshape(in_rows.shape),
        grad_down,
        down_rows,
        down_first.reshape(down_rows.shape),
        down_second.reshape(down_rows.shape),
    )
    norm_blocks = gather_tiny(expert_norms, 10)
    norm_values = jnp.sqrt(jnp.sum(norm_blocks, axis=0))[:7, :2]
    trust_ratio = norm_values[:, 0] / norm_values[:, 1]
    new_table, new_in, new_down, new_qkv, new_out = finish(
        norm_blocks,
        embed_table,
        table_update,
        in_rows,
        in_update,
        down_rows,
        down_update,
        qkv_weight,
        small[2],
        out_weight,
        small[5],
    )
    new_router = router_weight - STEP_RATE * trust_ratio[3] * small[8]
    new_gains = norm_gains - STEP_RATE * trust_ratio[4] * small[11]
    stats = jnp.stack([norm_values[:, 0], norm_values[:, 1], trust_ratio], axis=1)
    return (
        loss_value,
        new_table,
        table_one,
        table_two,
        new_qkv,
        small[0],
        small[1],
        new_out,
        small[3],
        small[4],
        new_router,
        small[6],
        small[7],
        new_gains,
        small[9],
        small[10],
        new_in.reshape(in_weight.shape),
        in_one.reshape(in_weight.shape),
        in_two.reshape(in_weight.shape),
        new_down.reshape(down_weight.shape),
        down_one.reshape(down_weight.shape),
        down_two.reshape(down_weight.shape),
        stats,
    )


def solution(mesh):
    rows = P(BOTH, None)
    vocab = P("shard", "expert")
    gains = P(None, BOTH)
    inner = P("shard", None, None, "expert")
    outer = P("shard", "expert", None)
    state = (vocab,) * 3 + (rows,) * 9 + (gains,) * 3 + (inner,) * 3 + (outer,) * 3
    return jax.shard_map(
        on_device,
        mesh=mesh,
        in_specs=(P("expert"), P("expert", None), P(), P(), rows, P()) + state,
        out_specs=(P(),) + state + (P(),),
        check_vma=False,
    )
```

```python
import functools
import math

import jax
import jax.numpy as jnp
from jax import lax
from jax.experimental import pallas as pl
from jax.experimental.pallas import tpu as pltpu
from jax.sharding import PartitionSpec as P

D = 1536
QUERY_HEADS = 24
KEY_VALUE_HEADS = 8
GROUP = QUERY_HEADS // KEY_VALUE_HEADS
HEAD_WIDTH = 64
TOP = 8
EXPERTS = 32
SEQUENCE_TOKENS = 256
COMP = 32
QKV = 2560

BETA = 0.1
LOGIT_SCALE = 6.0
RATE_ONE = 0.9
RATE_TWO = 0.999
EPSILON = 1e-06
DECAY = 0.01
STEP_RATE = 0.3

BOTH = ("expert", "shard")
bf16 = jnp.bfloat16
f32 = jnp.float32


MESH = pl.DeviceIdType.MESH


class Spot:
    def __init__(self, planes, side):
        self.planes, self.side = planes, side
        self.z = lax.axis_index("expert")
        self.shard = lax.axis_index("shard")
        self.core = lax.rem(self.shard, 2)
        self.b = lax.rem(lax.div(self.shard, 2), side)
        self.a = lax.div(self.shard, 2 * side)

    def plane(self, k):
        z = lax.rem(self.z + k, self.planes)
        return z, (z, self.shard)

    def along_a(self, k):
        a = lax.rem(self.a + k, self.side)
        return a, (self.z, (a * self.side + self.b) * 2 + self.core)

    def along_b(self, k):
        b = lax.rem(self.b + k, self.side)
        return b, (self.z, (self.a * self.side + b) * 2 + self.core)

    def along(self, first, k):
        return self.along_a(k) if first else self.along_b(k)

    def mate(self):
        other = 1 - self.core
        return other, (self.z, (self.a * self.side + self.b) * 2 + other)

    def near(self, k):
        return self.z, lax.rem(self.shard + k, 2 * self.side * self.side)

    def greet(self, flat):
        targets = [self.plane(k)[1] for k in range(1, self.planes)]
        if flat:
            targets += [self.near(k) for k in range(1, 2 * self.side * self.side)]
        else:
            targets.append(self.mate()[1])
            for k in range(1, self.side):
                targets += [self.along_a(k)[1], self.along_b(k)[1]]
        barrier = pltpu.get_barrier_semaphore()
        for target in targets:
            pl.semaphore_signal(barrier, inc=1, device_id=target, device_id_type=MESH)
        pl.semaphore_wait(barrier, len(targets))


class Mail:
    def __init__(self, send, recv):
        self.send, self.recv, self.count, self.open = send, recv, 0, []

    def start(self, src, dst, target):
        copy = pltpu.make_async_remote_copy(
            src_ref=src,
            dst_ref=dst,
            send_sem=self.send.at[self.count],
            recv_sem=self.recv.at[self.count],
            device_id=target,
            device_id_type=MESH,
        )
        self.count += 1
        copy.start()
        self.open.append(copy)
        return copy

    def finish(self):
        for copy in self.open:
            copy.wait_send()


def arrive(copies):
    for copy in copies:
        copy.wait_recv()


class Tiny:
    flat = True
    scratch = ()

    def __init__(self, x, planes, side):
        self.planes, self.side, self.inputs = planes, side, [x]
        shape = (planes, 2 * side * side) + x.shape
        self.outputs = [jax.ShapeDtypeStruct(shape, x.dtype)]
        self.copies = planes + 2 * side * side - 2

    def steps(self, spot, mail, x, out):
        out[spot.z, spot.shard] = x[...]
        sent = []
        for k in range(1, self.planes):
            sent.append(mail.start(x, out.at[spot.z, spot.shard], spot.plane(k)[1]))
        yield
        arrive(sent)
        part = out.at[:, spot.shard]
        yield
        arrive([mail.start(part, part, spot.near(k)) for k in range(1, 2 * self.side**2)])


def split(array, rows, columns, row_parts, column_parts):
    r, c = rows // row_parts, columns // column_parts
    cuts = [
        (array, slice(i * r, i * r + r), slice(j * c, j * c + c))
        for j in range(column_parts)
        for i in range(row_parts)
    ]
    cuts = [cut + (n % 2 == 0,) for n, cut in enumerate(cuts)]
    return [cuts[n : n + 2] for n in range(0, len(cuts), 2)]


def pipeline(groups, stage, last):
    sent = [[[] for _ in group] for group in groups]
    for tick in range(len(groups) + last):
        for step in range(last, -1, -1):
            turn = tick - step
            if 0 <= turn < len(groups):
                for n, cut in enumerate(groups[turn]):
                    for copy in sent[turn][n]:
                        copy.wait_recv()
                    sent[turn][n] = stage(step, (turn, n), cut)
        yield


class Gather:
    flat = False
    scratch = ()

    def __init__(self, xs, groups, planes, side, exchange=False, prior=None):
        self.planes, self.side, self.inputs, self.groups = planes, side, xs, groups
        self.exchange, self.prior = exchange, prior
        grid = (planes, side, side, 2)
        shapes = [x.shape[-2:] for x in xs]
        if prior:
            shapes = [xs[0].shape[-2:-1] + (width,) for width in prior]
        self.outputs = [jax.ShapeDtypeStruct(grid + shape, xs[0].dtype) for shape in shapes]
        self.copies = sum(map(len, groups)) * (planes - 1 + 2 * (side - 1) + 1)

    def steps(self, spot, mail, *refs):
        xs, outs = refs[: len(self.inputs)], refs[len(self.inputs) :]
        z, a, b, core = spot.z, spot.a, spot.b, spot.core
        if self.prior:
            low = 0
            for width, out in zip(self.prior, outs):
                out[:, a, b, core] = xs[0][:, :, low : low + width]
                low += width
            xs = [None] * len(outs)
        else:
            for x, out in zip(xs, outs):
                out[z, a, b, core] = x[z] if self.exchange else x[...]

        def stage(step, key, cut):
            i, rows, columns, first = cut
            x, out = xs[i], outs[i]
            if step == 0 and self.prior:
                return []
            if step == 0:
                place = out.at[z, a, b, core, rows, columns]
                sent = []
                for k in range(1, self.planes):
                    peer, target = spot.plane(k)
                    own = x.at[peer, rows, columns] if self.exchange else x.at[rows, columns]
                    sent.append(mail.start(own, place, target))
                return sent
            if step in (1, 2):
                if step == 1:
                    part = out.at[:, a, b, core, rows, columns]
                elif first:
                    part = out.at[:, :, b, core, rows, columns]
                else:
                    part = out.at[:, a, :, core, rows, columns]
                return [
                    mail.start(part, part, spot.along(first == (step == 1), k)[1])
                    for k in range(1, self.side)
                ]
            if step == 3:
                part = out.at[:, :, :, core, rows, columns]
                return [mail.start(part, part, spot.mate()[1])]
            return []

        return pipeline(self.groups, stage, 4)


class Reduce:
    flat = False

    def __init__(self, xs, groups, planes, side, exchange=False, partial=False):
        self.planes, self.side, self.inputs, self.groups = planes, side, xs, groups
        self.exchange, self.partial = exchange or partial, partial
        self.outputs = [
            jax.ShapeDtypeStruct((planes,) + x.shape[-2:], x.dtype)
            if self.exchange
            else jax.ShapeDtypeStruct(x.shape[-2:], f32)
            for x in xs
        ]
        if partial:
            shape = (planes, xs[0].shape[-2], sum(x.shape[-1] for x in xs))
            self.outputs = [jax.ShapeDtypeStruct(shape, xs[0].dtype)]
        self.scratch = []
        for i, rows, columns, _ in [cut for group in groups for cut in group]:
            block = (rows.stop - rows.start, columns.stop - columns.start)
            self.scratch += [
                pltpu.VMEM(shape + block, xs[i].dtype)
                for shape in (
                    (planes, side, side),
                    (side - 1, planes, side),
                    (planes, side),
                    (side - 1, planes),
                    (planes,),
                )
                + (() if self.exchange else ((planes - 1,),))
            ]
        self.copies = sum(map(len, groups)) * (planes - 1 + 2 * (side - 1) + 1)

    def steps(self, spot, mail, *refs):
        planes, side, number = self.planes, self.side, len(self.inputs)
        made = number + len(self.outputs)
        xs, outs, rest = refs[:number], refs[number:made], refs[made:]
        lows = [0] * number
        if self.partial:
            outs = [outs[0]] * number
            lows = [sum(x.shape[-1] for x in self.inputs[:n]) for n in range(number)]
        each = 5 if self.exchange else 6
        order = [(t, n) for t, group in enumerate(self.groups) for n in range(len(group))]
        held = {key: rest[each * p : each * (p + 1)] for p, key in enumerate(order)}
        core, z = spot.core, spot.z
        other, mate = spot.mate()

        def stage(step, key, cut):
            i, rows, columns, first = cut
            x, out = xs[i], outs[i]
            one, hop_two, two, hop_three, three = held[key][:5]
            if step == 0:
                return [mail.start(x.at[:, :, :, other, rows, columns], one, mate)]
            sent = []
            if step == 1:

                def add(n, carry):
                    ia, ib = lax.rem(lax.div(n, side), side), lax.rem(n, side)
                    iz = lax.div(n, side * side)
                    total = x[iz, ia, ib, core, rows, columns].astype(f32)
                    one[iz, ia, ib] = (total + one[iz, ia, ib].astype(f32)).astype(one.dtype)
                    return carry

                lax.fori_loop(0, planes * side * side, add, 0)
                for k in range(1, side):
                    peer, target = spot.along(first, k)
                    part = one.at[:, peer] if first else one.at[:, :, peer]
                    sent.append(mail.start(part, hop_two.at[k - 1], target))
            elif step == 2:

                def add(n, carry):
                    iz, ir = lax.div(n, side), lax.rem(n, side)
                    total = (one[iz, spot.a, ir] if first else one[iz, ir, spot.b]).astype(f32)
                    for k in range(side - 1):
                        total += hop_two[k, iz, ir].astype(f32)
                    two[iz, ir] = total.astype(two.dtype)
                    return carry

                lax.fori_loop(0, planes * side, add, 0)
                for k in range(1, side):
                    peer, target = spot.along(not first, k)
                    sent.append(mail.start(two.at[:, peer], hop_three.at[k - 1], target))
            elif step == 3:
                mine = spot.b if first else spot.a

                def add(iz, carry):
                    total = two[iz, mine].astype(f32)
                    for k in range(side - 1):
                        total += hop_three[k, iz].astype(f32)
                    if self.partial:
                        place = slice(lows[i] + columns.start, lows[i] + columns.stop)
                        out[iz, rows, place] = total.astype(out.dtype)
                    else:
                        three[iz] = total.astype(three.dtype)
                    return carry

                lax.fori_loop(0, planes, add, 0)
                if self.partial:
                    return []
                for k in range(1, planes):
                    peer, target = spot.plane(k)
                    if self.exchange:
                        place = out.at[z, rows, columns]
                    else:
                        place = held[key][5].at[k - 1]
                    sent.append(mail.start(three.at[peer], place, target))
                if self.exchange:
                    out[z, rows, columns] = three[z]
            elif not self.exchange:
                total = three[z].astype(f32)
                for k in range(planes - 1):
                    total += held[key][5][k].astype(f32)
                out[rows, columns] = total
            return sent

        return pipeline(self.groups, stage, 4)


class Swap:
    flat = False
    def __init__(self, x, turns, planes, side, back=False, held=None):
        self.planes, self.side = planes, side
        self.inputs = [x] if held is None else [x, held]
        self.in_spaces, self.out_spaces = (pltpu.HBM,) * len(self.inputs), (pltpu.HBM,)
        self.aliases = {} if held is None else {1: 0}
        self.turns, self.back = turns, back
        self.scratch = [pltpu.SemaphoreType.DMA((len(turns),))]
        self.columns = x.shape[1] // planes if back else x.shape[1]
        self.rows = x.shape[0] if back else x.shape[0] // planes
        shape = (planes, self.rows, self.columns) if back else (self.rows, planes * self.columns)
        self.outputs = [jax.ShapeDtypeStruct(shape, x.dtype)]
        self.copies = len(turns) * (planes - 1)

    def steps(self, spot, mail, *refs):
        x, out, own_sem = refs[0], refs[-2], refs[-1]
        def block(z):
            return pl.ds(pl.multiple_of(z * self.columns, 128), self.columns)

        def source(z, begin, size):
            if self.back:
                return x.at[pl.ds(begin, size), block(z)]
            return x.at[pl.ds(pl.multiple_of(z * self.rows + begin, 16), size), :]

        sent, own, now = [], [], 0
        for n, (begin, size, rounds) in enumerate(self.turns):
            while now < rounds:
                now += 1
                yield
            rows = pl.ds(begin, size)
            place = out.at[spot.z, rows] if self.back else out.at[rows, block(spot.z)]
            for k in range(1, self.planes):
                peer, target = spot.plane(k)
                sent.append(mail.start(source(peer, begin, size), place, target))
            own.append(pltpu.make_async_copy(source(spot.z, begin, size), place, own_sem.at[n]))
            own[-1].start()
        while now < 24:
            now += 1
            yield
        for copy in own:
            copy.wait()
        for copy in sent:
            copy.wait_recv()


class Chain:
    flat = False

    def __init__(self, reduce, extra, extra_out, middle, gather):
        self.planes, self.side = reduce.planes, reduce.side
        self.reduce, self.middle, self.gather = reduce, middle, gather
        self.inputs = reduce.inputs + extra
        self.outputs = gather.outputs + extra_out
        self.scratch = reduce.scratch + [
            pltpu.VMEM(x.shape, x.dtype) for x in reduce.outputs + gather.inputs
        ]
        self.copies = reduce.copies + gather.copies

    def steps(self, spot, mail, *refs):
        n_in, n_out = len(self.inputs), len(self.outputs)
        (x, *extra), (out, *extra_out) = refs[:n_in], refs[n_in : n_in + n_out]
        *held, sums, made = refs[n_in + n_out :]
        yield from self.reduce.steps(spot, mail, x, sums, *held)
        self.middle(sums, made, *extra, *extra_out)
        yield from self.gather.steps(spot, mail, made, out)


def final_norm(sums, made, resid, gains, resid_two):
    values = resid[...] + sums[...]
    resid_two[...] = values
    made[...] = (values * inverse_root(values) * gains[2:3]).astype(bf16)


def final_norm_back(sums, made, resid_two, gains, grad_two, gain_grad):
    grad, gain_grad[...] = norm_back(resid_two[...], gains[2:3], sums[...])
    grad_two[...] = grad
    made[...] = grad.astype(bf16)


def communicate(parts, ident):
    planes, side = parts[0].planes, parts[0].side
    counts = [(len(p.inputs), len(p.outputs), len(p.scratch)) for p in parts]
    n_in, n_out = (sum(c[i] for c in counts) for i in range(2))
    copies = sum(p.copies for p in parts)
    aliases, i, o = {}, 0, 0
    for part, (ci, co, _) in zip(parts, counts):
        aliases.update({i + a: o + b for a, b in getattr(part, "aliases", {}).items()})
        i, o = i + ci, o + co

    def kernel(*refs):
        ins, outs, rest = refs[:n_in], refs[n_in : n_in + n_out], refs[n_in + n_out :]
        send, recv = rest[-2:]
        spot = Spot(planes, side)
        spot.greet(parts[0].flat)
        mail = Mail(send, recv)
        running, i, o, s = [], 0, 0, 0
        for part, (ci, co, cs) in zip(parts, counts):
            running.append(
                part.steps(spot, mail, *ins[i : i + ci], *outs[o : o + co], *rest[s : s + cs])
            )
            i, o, s = i + ci, o + co, s + cs
        while running:
            running = [steps for steps in running if next(steps, True) is None]
        mail.finish()

    size = sum(x.size * x.dtype.itemsize for p in parts for x in p.inputs + p.outputs)
    need = size + sum(
        math.prod(x.shape) * x.dtype.itemsize
        for p in parts
        for x in p.scratch
        if x.memory_space == pltpu.VMEM
    )
    out = pl.pallas_call(
        kernel,
        out_shape=[x for p in parts for x in p.outputs],
        in_specs=[
            pl.BlockSpec(memory_space=space)
            for p in parts
            for space in getattr(p, "in_spaces", (pltpu.VMEM,) * len(p.inputs))
        ],
        out_specs=[
            pl.BlockSpec(memory_space=space)
            for p in parts
            for space in getattr(p, "out_spaces", (pltpu.VMEM,) * len(p.outputs))
        ],
        input_output_aliases=aliases,
        scratch_shapes=[s for p in parts for s in p.scratch]
        + [pltpu.SemaphoreType.DMA((copies,)), pltpu.SemaphoreType.DMA((copies,))],
        compiler_params=pltpu.CompilerParams(
            collective_id=ident,
            has_side_effects=True,
            vmem_limit_bytes=min(62 << 20, need * 9 // 8 + (4 << 20)),
        ),
        cost_estimate=pl.CostEstimate(flops=0, bytes_accessed=20 * size, transcendentals=0),
        name="exchange_" + str(ident),
    )(*[x for p in parts for x in p.inputs])
    return list(out)

def expert_gate(gates, lane):
    lanes = lax.broadcasted_iota(jnp.int32, gates.shape, 1)
    return jnp.sum(jnp.where(lanes == lane, gates, 0.0), axis=1, keepdims=True)


CHUNK = 512
BLOCK = 1024
ACROSS = (((1,), (1,)), ((), ()))


def forward_kernel(
    lane_ref, rows_ref, routes_ref, router_ref, in_ref, down_ref, out_ref, mid_ref, gates_ref, cat_ref, down_out, hidden_ref
):
    e, number = pl.program_id(1), pl.num_programs(1)
    units = in_ref.shape[1]
    for j in range(2):
        cat_ref[:, j * units : (j + 1) * units] = in_ref[pl.ds(j, D, stride=2), :].astype(bf16)
    down_out[pl.ds(pl.multiple_of(e * units, units), units), :] = down_ref[0].astype(bf16)

    def chunk(i, carry):
        here = pl.ds(pl.multiple_of(i * CHUNK, CHUNK), CHUNK)
        rows = rows_ref[here, :]

        @pl.when(e == 0)
        def _():
            logits = jnp.dot(rows, router_ref[...], preferred_element_type=f32)
            lanes = lax.broadcasted_iota(jnp.int32, logits.shape, 1)
            mask = lanes == routes_ref[here, 0:1]
            for j in range(1, TOP):
                mask |= lanes == routes_ref[here, j : j + 1]
            top = jnp.max(jnp.where(mask, logits, -3e38), axis=1, keepdims=True)
            weight = jnp.where(mask, jnp.exp(jnp.where(mask, logits - top, 0.0)), 0.0)
            gates_ref[here, :] = weight / jnp.sum(weight, axis=1, keepdims=True)

        mid = jnp.dot(rows, cat_ref[...], preferred_element_type=f32)
        mid_ref[here, :] = mid
        gate, up = mid[:, :units], mid[:, units:]
        hidden = (gate * jax.nn.sigmoid(gate) * up).astype(bf16).astype(f32)
        hidden = (hidden * expert_gate(gates_ref[here, :], lane_ref[0] + e)).astype(bf16)
        hidden_ref[here, pl.ds(pl.multiple_of(e * units, units), units)] = hidden

        @pl.when(e == number - 1)
        def _():
            out_ref[here, :] = jnp.dot(
                hidden_ref[here, :], down_out[...], preferred_element_type=f32
            ).astype(bf16)

        return carry

    lax.fori_loop(0, rows_ref.shape[0] // CHUNK, chunk, 0)


def experts_forward(lane, rows, routes, router, in_rows, down):
    number, units = down.shape[:2]
    total = rows.shape[0]
    block = min(total, BLOCK)
    row = lambda r, e, *_: (r, 0)
    still = lambda r, e, *_: (0, 0)
    return pl.pallas_call(
        forward_kernel,
        grid_spec=pltpu.PrefetchScalarGridSpec(
            num_scalar_prefetch=1,
            grid=(total // block, number),
            in_specs=[
                pl.BlockSpec((block, D), row),
                pl.BlockSpec((block, TOP), row),
                pl.BlockSpec((D, 128), lambda r, e, *_: (0, PACK // 128 - 1)),
                pl.BlockSpec((2 * D, units), lambda r, e, *_: (e, 0)),
                pl.BlockSpec((1, units, D), lambda r, e, *_: (e, 0, 0)),
            ],
            out_specs=[
                pl.BlockSpec((block, D), row),
                pl.BlockSpec((block, 2 * units), lambda r, e, *_: (r, e)),
                pl.BlockSpec((block, 128), row),
                pl.BlockSpec((D, 2 * units), lambda r, e, *_: (0, e)),
                pl.BlockSpec((number * units, D), still),
                pl.BlockSpec((block, number * units), row),
            ],
        ),
        out_shape=[
            jax.ShapeDtypeStruct((total, D), bf16),
            jax.ShapeDtypeStruct((total, 2 * units * number), f32),
            jax.ShapeDtypeStruct((total, 128), f32),
            jax.ShapeDtypeStruct((D, 2 * units * number), bf16),
            jax.ShapeDtypeStruct((number * units, D), bf16),
            jax.ShapeDtypeStruct((total, number * units), bf16),
        ],
        compiler_params=pltpu.CompilerParams(vmem_limit_bytes=42 << 20),
        name="experts_forward",
    )(lane, rows, routes, router, in_rows, down)


def backward_kernel(
    lane_ref, grad_ref, mid_ref, gates_ref, cat_ref, down_ref, out_ref, mid_grad_ref, pulled_ref
):
    number = lane_ref.shape[0]
    units = pulled_ref.shape[1] // number

    def chunk(i, carry):
        here = pl.ds(pl.multiple_of(i * CHUNK, CHUNK), CHUNK)
        pulled_ref[...] = lax.dot_general(
            grad_ref[here, :], down_ref[...], ACROSS, preferred_element_type=f32
        )
        lanes = lax.broadcasted_iota(jnp.int32, (CHUNK, 128), 1)
        gate_part = jnp.zeros((CHUNK, 128), f32)
        for e in range(number):
            lane = lane_ref[e]
            weight = expert_gate(gates_ref[here, :], lane)
            gate = mid_ref[here, 2 * e * units : (2 * e + 1) * units]
            up = mid_ref[here, (2 * e + 1) * units : (2 * e + 2) * units]
            pulled = pulled_ref[:, e * units : (e + 1) * units]
            soft = jax.nn.sigmoid(gate)
            silu = gate * soft
            hidden = (silu * up).astype(bf16).astype(f32)
            gate_grad = jnp.sum(hidden * pulled, axis=1, keepdims=True)
            gate_part = jnp.where(lanes == lane, gate_grad, gate_part)
            hidden_grad = (pulled * weight).astype(bf16).astype(f32)
            turned = hidden_grad * up * (soft * (1.0 + gate * (1.0 - soft)))
            mid_grad_ref[here, 2 * e * units : (2 * e + 1) * units] = turned.astype(bf16)
            mid_grad_ref[here, (2 * e + 1) * units : (2 * e + 2) * units] = (
                hidden_grad * silu
            ).astype(bf16)
        out_ref[here, D:] = gate_part.astype(bf16)
        out_ref[here, :D] = lax.dot_general(
            mid_grad_ref[here, :], cat_ref[...], ACROSS, preferred_element_type=f32
        ).astype(bf16)
        return carry

    lax.fori_loop(0, grad_ref.shape[0] // CHUNK, chunk, 0)


def experts_backward(lanes, grad, mid, gates, cat, down):
    number = lanes.shape[0]
    total = grad.shape[0]
    block = CHUNK
    row = lambda r, *_: (r, 0)
    still = lambda r, *_: (0, 0)
    return pl.pallas_call(
        backward_kernel,
        grid_spec=pltpu.PrefetchScalarGridSpec(
            num_scalar_prefetch=1,
            grid=(total // block,),
            in_specs=[
                pl.BlockSpec((block, D), row),
                pl.BlockSpec((block, mid.shape[1]), row),
                pl.BlockSpec((block, 128), row),
                pl.BlockSpec(cat.shape, still),
                pl.BlockSpec(down.shape, still),
            ],
            out_specs=[
                pl.BlockSpec((block, D + 128), row),
                pl.BlockSpec((block, mid.shape[1]), row),
            ],
            scratch_shapes=[pltpu.VMEM((CHUNK, down.shape[0]), f32)],
        ),
        out_shape=[
            jax.ShapeDtypeStruct((total, D + 128), bf16),
            jax.ShapeDtypeStruct(mid.shape, bf16),
        ],
        compiler_params=pltpu.CompilerParams(vmem_limit_bytes=36 << 20),
        name="experts_backward",
    )(lanes, grad, mid, gates, cat, down)


def moments_kernel(
    scale_ref, other_norms, grad_ref, w_ref, first_ref, second_ref, down_grad, down_w, down_first, down_second,
    new_first, new_second, updates, new_down_first, new_down_second, down_updates, norms, sums, down_sums, turned,
):
    units = w_ref.shape[1]
    part = w_ref.shape[0] // 2
    scales = (scale_ref[0], scale_ref[1])
    step = pl.program_id(0) * pl.num_programs(1) + pl.program_id(1)

    @pl.when(step == 0)
    def _():
        sums[...] = jnp.zeros_like(sums)
        down_sums[...] = jnp.zeros_like(down_sums)

    for j in range(2):
        turned[pl.ds(j, part, stride=2), :] = grad_ref[:, j * units : (j + 1) * units]
    weight = w_ref[...]
    one, two, update = lamb_parts(weight, first_ref[...], second_ref[...], turned[...], scales)
    new_first[...] = one
    new_second[...] = two
    updates[...] = update
    sums[0] += fold(weight * weight)
    sums[1] += fold(update * update)
    weight = down_w[...]
    one, two, update = lamb_parts(weight, down_first[...], down_second[...], down_grad[...], scales)
    new_down_first[...] = one
    new_down_second[...] = two
    down_updates[...] = update
    down_sums[0] += fold(weight * weight)
    down_sums[1] += fold(update * update)

    @pl.when(step == pl.num_programs(0) * pl.num_programs(1) - 1)
    def _():
        block = norm_cells(5, total_of(sums[0]), total_of(sums[1]))
        block += norm_cells(6, total_of(down_sums[0]), total_of(down_sums[1]))
        norms[...] = other_norms[...] + block


def expert_moments(scales, norms, grad, weight, first, second, *down_state):
    units = weight.shape[1]
    down = down_state[1]
    number = grad.shape[1] // (2 * units)
    parts = 2
    cells = pl.BlockSpec((8, 128), lambda e, p, *_: (0, 0))
    row = pl.BlockSpec((2 * D // parts, units), lambda e, p, *_: (e * parts + p, 0))
    down_row = pl.BlockSpec((units // parts, D), lambda e, p, *_: (e * parts + p, 0))
    return pl.pallas_call(
        moments_kernel,
        grid_spec=pltpu.PrefetchScalarGridSpec(
            num_scalar_prefetch=1,
            grid=(number, parts),
            in_specs=[cells, pl.BlockSpec((D // parts, 2 * units), lambda e, p, *_: (p, e))]
            + [row] * 3
            + [down_row] * 4,
            out_specs=[row] * 3 + [down_row] * 3 + [cells],
            scratch_shapes=[
                pltpu.VMEM((2, 8, units), f32),
                pltpu.VMEM((2, 8, D), f32),
                pltpu.VMEM((2 * D // parts, units), f32),
            ],
        ),
        out_shape=[jax.ShapeDtypeStruct(weight.shape, f32)] * 3
        + [jax.ShapeDtypeStruct(down.shape, f32)] * 3
        + [jax.ShapeDtypeStruct((8, 128), f32)],
        compiler_params=pltpu.CompilerParams(vmem_limit_bytes=62 << 20),
        name="expert_moments",
    )(scales, norms, grad, weight, first, second, *down_state)


HEAD_COLS = QUERY_HEADS * HEAD_WIDTH
KEY_COLS = KEY_VALUE_HEADS * HEAD_WIDTH
PACK = HEAD_COLS + KEY_COLS + 128
PACK_TWO = KEY_COLS + D
ROOT = HEAD_WIDTH ** (-0.5)


def turn(u, cosine, sine):
    width = u.shape[1]
    lanes = lax.broadcasted_iota(jnp.int32, u.shape, 1)
    ahead = pltpu.roll(u, width - HEAD_WIDTH // 2, 1)
    behind = pltpu.roll(u, HEAD_WIDTH // 2, 1)
    other = jnp.where(lax.rem(lanes, HEAD_WIDTH) < HEAD_WIDTH // 2, ahead, behind)
    return u * jnp.tile(cosine, (1, width // 128)) + other * jnp.tile(sine, (1, width // 128))


def rotary_tables():
    half = HEAD_WIDTH // 2
    freqs = jnp.exp(-jnp.log(10000.0) * jnp.arange(half, dtype=f32) / half)
    angles = jnp.arange(SEQUENCE_TOKENS, dtype=f32)[:, None] * freqs[None, :]
    cosine, sine = jnp.cos(angles), jnp.sin(angles)
    return jnp.tile(cosine, (1, 4)), jnp.tile(jnp.concatenate([-sine, sine], axis=1), (1, 2))


def inverse_root(values):
    return lax.rsqrt(jnp.mean(values * values, axis=-1, keepdims=True) + 1e-06)


def norm_back(values, gain, grad):
    root = inverse_root(values)
    scaled = grad * gain
    inner = jnp.mean(scaled * values, axis=-1, keepdims=True)
    return root * scaled - values * (root * root * root * inner), jnp.sum(
        grad * values * root, axis=0, keepdims=True
    )


def dot(a, b):
    return jnp.dot(a, b, preferred_element_type=f32)


def dot_across(a, b):
    return lax.dot_general(a, b, ACROSS, preferred_element_type=f32)


def selector(start, shape, axis):
    row = lax.broadcasted_iota(jnp.int32, shape, 1 - axis) + start
    return (row == lax.broadcasted_iota(jnp.int32, shape, axis)).astype(f32)


def spread(start, rows):
    pick = selector(start, (SEQUENCE_TOKENS, COMP), 0)
    return jnp.dot(pick, rows, preferred_element_type=f32, precision=lax.Precision.HIGHEST)


def head_rows(ref_value, h):
    first = h * GROUP * HEAD_WIDTH
    return jnp.concatenate(
        [
            ref_value[:, first + g * HEAD_WIDTH : first + (g + 1) * HEAD_WIDTH]
            for g in range(GROUP)
        ],
        axis=0,
    )


def head_lanes(parts):
    return jnp.concatenate(
        [part[g * COMP : (g + 1) * COMP] for part in parts for g in range(GROUP)], axis=1
    )


def attend_kernel(
    start_ref, picked_ref, one_ref, two_ref, cos_ref, sin_ref, cos_rows, sin_rows,
    c_ref, resid_ref, probs_ref, query_ref, key_ref, value_ref, mixed_ref, normed_ref, gains_ref,
    embedded,
):
    start = start_ref[0]
    pick_rows = selector(start, (COMP, SEQUENCE_TOKENS), 1).astype(bf16)
    planes, _, columns = picked_ref.shape
    for p in range(planes):
        embedded[:, p * columns : (p + 1) * columns] = picked_ref[p].astype(f32)
    pick = lax.broadcasted_iota(jnp.int32, (8, 128), 0) + EXPERTS
    pick = (pick == lax.broadcasted_iota(jnp.int32, (8, 128), 1)).astype(f32).astype(bf16)
    gains = dot_across(pick, one_ref[:, HEAD_COLS + KEY_COLS :])
    gains_ref[...] = gains
    x = embedded[...]
    a = (x * inverse_root(x) * gains[0:1]).astype(bf16)
    normed_ref[...] = a
    a_rows = dot(pick_rows, a).astype(bf16)
    cosine, sine = cos_ref[...], sin_ref[...]
    query = turn(dot(a_rows, one_ref[:, :HEAD_COLS]), cos_rows[...], sin_rows[...])
    query = query.astype(bf16)
    key = turn(dot(a, one_ref[:, HEAD_COLS : HEAD_COLS + KEY_COLS]), cosine, sine).astype(bf16)
    value = dot(a, two_ref[:, :KEY_COLS]).astype(bf16)
    query_ref[...], key_ref[...], value_ref[...] = query, key, value
    rows = GROUP * COMP
    place = lax.rem(lax.broadcasted_iota(jnp.int32, (rows, SEQUENCE_TOKENS), 0), COMP) + start
    seen = place >= lax.broadcasted_iota(jnp.int32, (rows, SEQUENCE_TOKENS), 1)
    parts = []
    for h in range(KEY_VALUE_HEADS):
        lanes = slice(h * HEAD_WIDTH, (h + 1) * HEAD_WIDTH)
        scores = dot_across(head_rows(query, h), key[:, lanes]) * ROOT
        scores = jnp.where(seen, scores, -1000000000.0)
        expd = jnp.exp(scores - jnp.max(scores, axis=-1, keepdims=True))
        probs = expd / jnp.sum(expd, axis=-1, keepdims=True)
        probs_ref[h] = probs
        parts.append(dot(probs.astype(bf16), value[:, lanes]))
    mixed = head_lanes(parts).astype(bf16)
    mixed_ref[...] = mixed
    resid = dot(pick_rows, embedded[...].astype(bf16)) + dot(mixed, two_ref[:, KEY_COLS : KEY_COLS + D])
    resid_ref[...] = resid
    c_ref[...] = (resid * inverse_root(resid) * gains[1:2]).astype(bf16)


def attend(start, picked, one, two, *tables):
    vm = pl.BlockSpec(memory_space=pltpu.VMEM)
    rows = GROUP * COMP
    return pl.pallas_call(
        attend_kernel,
        in_specs=[pl.BlockSpec(memory_space=pltpu.SMEM)] + [vm] * 7,
        out_specs=[vm] * 9,
        out_shape=[
            jax.ShapeDtypeStruct((COMP, D), bf16),
            jax.ShapeDtypeStruct((COMP, D), f32),
            jax.ShapeDtypeStruct((KEY_VALUE_HEADS, rows, SEQUENCE_TOKENS), f32),
            jax.ShapeDtypeStruct((COMP, HEAD_COLS), bf16),
            jax.ShapeDtypeStruct((SEQUENCE_TOKENS, KEY_COLS), bf16),
            jax.ShapeDtypeStruct((SEQUENCE_TOKENS, KEY_COLS), bf16),
            jax.ShapeDtypeStruct((COMP, HEAD_COLS), bf16),
            jax.ShapeDtypeStruct((SEQUENCE_TOKENS, D), bf16),
            jax.ShapeDtypeStruct((8, D), f32),
        ],
        scratch_shapes=[pltpu.VMEM((SEQUENCE_TOKENS, D), f32)],
        compiler_params=pltpu.CompilerParams(vmem_limit_bytes=28 << 20),
        name="attend",
    )(start, picked, one, two, *tables)


def attend_back_kernel(
    start_ref, back_ref, gates_ref, grad_two_ref, gain_three_ref, c_ref, resid_ref, probs_ref, query_ref,
    key_ref, value_ref, mixed_ref, normed_ref, gains_ref, picked_ref, one_ref, two_ref, cos_ref, sin_ref, cos_rows, sin_rows,
    out_ref, grad_one_ref, grad_pack_ref,
    total,
):
    start = start_ref[0]
    planes, _, columns = picked_ref.shape
    gains = gains_ref[...]
    wide = HEAD_COLS + KEY_COLS
    gates = gates_ref[...]
    gate_grad = back_ref[:, D:]
    router_grad = gates * (gate_grad - jnp.sum(gates * gate_grad, axis=1, keepdims=True))
    router_grad = router_grad.astype(bf16)
    grad = back_ref[:, :D] + dot_across(router_grad, one_ref[:, wide:])
    grad_resid, gain_two = norm_back(resid_ref[...], gains[1:2], grad)
    grad_resid = grad_resid + grad_two_ref[...]
    branch = grad_resid.astype(bf16)
    grad_mixed = dot_across(branch, two_ref[:, KEY_COLS : KEY_COLS + D]).astype(bf16)
    query, key, value = query_ref[...], key_ref[...], value_ref[...]
    query_parts, key_parts, value_parts = [], [], []
    for h in range(KEY_VALUE_HEADS):
        lanes = slice(h * HEAD_WIDTH, (h + 1) * HEAD_WIDTH)
        probs = probs_ref[h]
        grad_head = head_rows(grad_mixed, h)
        grad_probs = dot_across(grad_head, value[:, lanes]).astype(bf16).astype(f32)
        inner = jnp.sum(grad_probs * probs, axis=-1, keepdims=True)
        grad_scores = probs * (grad_probs - inner)
        value_parts.append(dot(probs.T.astype(bf16), grad_head))
        query_parts.append(dot(grad_scores.astype(bf16), key[:, lanes]) * ROOT)
        key_parts.append(dot(grad_scores.T.astype(bf16), head_rows(query, h)) * ROOT)
    grad_query = turn(head_lanes(query_parts), cos_rows[...], -sin_rows[...]).astype(bf16)
    grad_key = jnp.concatenate(key_parts, axis=1)
    grad_key = turn(grad_key, cos_ref[...], -sin_ref[...]).astype(bf16)
    grad_value = jnp.concatenate(value_parts, axis=1).astype(bf16)
    grad_normed = dot_across(grad_key, one_ref[:, HEAD_COLS:wide])
    grad_normed += dot_across(grad_value, two_ref[:, :KEY_COLS])
    grad_normed += spread(start, dot_across(grad_query, one_ref[:, :HEAD_COLS]))
    for p in range(planes):
        total[:, p * columns : (p + 1) * columns] = picked_ref[p].astype(f32)
    grad_embedded, gain_one = norm_back(total[...], gains[0:1], grad_normed)
    total[...] = grad_embedded + spread(start, grad_resid)
    for p in range(planes):
        out_ref[p] = total[:, p * columns : (p + 1) * columns].astype(bf16)
    pick_rows = selector(start, (COMP, SEQUENCE_TOKENS), 1).astype(bf16)
    a_rows = dot(pick_rows, normed_ref[...])
    turned = normed_ref[...].astype(f32).T.astype(bf16)
    grad_one_ref[:, HEAD_COLS:wide] = dot(turned, grad_key).astype(bf16)
    grad_pack_ref[:, :KEY_COLS] = dot(turned, grad_value).astype(bf16)
    grad_one_ref[:, :HEAD_COLS] = dot(a_rows.T.astype(bf16), grad_query).astype(bf16)
    grad_pack_ref[:, KEY_COLS : KEY_COLS + D] = dot(
        mixed_ref[...].astype(f32).T.astype(bf16), branch
    ).astype(bf16)
    left = jnp.concatenate(
        [c_ref[...].astype(f32), gain_one, gain_two, gain_three_ref[...], jnp.zeros((5, D), f32)],
        axis=0,
    )
    lane = lax.broadcasted_iota(jnp.int32, (8, 128), 0) + EXPERTS
    lane = (lane == lax.broadcasted_iota(jnp.int32, (8, 128), 1)).astype(f32)
    right = jnp.concatenate([router_grad.astype(f32), lane], axis=0).astype(bf16)
    grad_one_ref[:, wide:] = dot(left.T.astype(bf16), right).astype(bf16)


def attend_back(start, *operands):
    vm = pl.BlockSpec(memory_space=pltpu.VMEM)
    picked = operands[13]
    return pl.pallas_call(
        attend_back_kernel,
        in_specs=[pl.BlockSpec(memory_space=pltpu.SMEM)] + [vm] * len(operands),
        out_specs=[vm] * 3,
        out_shape=[
            jax.ShapeDtypeStruct(picked.shape, bf16),
            jax.ShapeDtypeStruct((D, PACK), bf16),
            jax.ShapeDtypeStruct((D, PACK_TWO), bf16),
        ],
        scratch_shapes=[pltpu.VMEM((SEQUENCE_TOKENS, D), f32)],
        compiler_params=pltpu.CompilerParams(vmem_limit_bytes=44 << 20),
        name="attend_back",
    )(start, *operands)


def lamb_update(weight, moment_one, moment_two, scale_one, scale_two):
    return (moment_one * scale_one) / (jnp.sqrt(moment_two * scale_two) + EPSILON) + DECAY * weight


def lamb_parts(weight, moment_one, moment_two, gradient, scales):
    moment_one = RATE_ONE * moment_one + (1.0 - RATE_ONE) * gradient
    moment_two = RATE_TWO * moment_two + (1.0 - RATE_TWO) * gradient * gradient
    return (moment_one, moment_two, lamb_update(weight, moment_one, moment_two, *scales))


STEPS = 4
TOGETHER = 4


def row_lists(tokens, base, rows):
    inside = (tokens >= base) & (tokens < base + rows)
    count = jnp.sum(inside.astype(jnp.int32), axis=1)
    place = jnp.arange(SEQUENCE_TOKENS, dtype=jnp.int32)
    before = (place[:, None] < place[None, :]).astype(bf16)
    rank = jnp.dot(inside.astype(bf16), before, preferred_element_type=f32).astype(jnp.int32)
    packed = place[None, :] * 65536 + (tokens - base)
    hit = inside[:, :, None] & (rank[:, :, None] == place[None, None, :])
    entry = jnp.sum(jnp.where(hit, packed[:, :, None], 0), axis=1)
    empty = SEQUENCE_TOKENS * 65536
    return jnp.where(place[None, :] < count[:, None], entry, empty), count


def gather_kernel(list_ref, count_ref, table_ref, out_ref, table_out, rows_ref):
    part = table_out.shape[0]
    here = pl.ds(pl.multiple_of(pl.program_id(0) * part, 16), part)
    table_out[...] = table_ref[here, :].astype(bf16)
    for n in range(TOGETHER):
        b = pl.program_id(0) * TOGETHER + n
        rows_ref[n] = jnp.zeros(rows_ref.shape[1:], f32)

        def step(k, carry, n=n, b=b):
            for j in range(STEPS):
                entry = list_ref[b, k * STEPS + j]
                rows_ref[n, pl.ds(entry >> 16, 1), :] = table_ref[pl.ds(entry & 65535, 1), :]
            return carry

        lax.fori_loop(0, (count_ref[b] + STEPS - 1) // STEPS, step, 0)
        out_ref[n] = rows_ref[n, :SEQUENCE_TOKENS].astype(bf16)


def gather_rows(lists, counts, table):
    blocks = lists.shape[0]
    rows, columns = table.shape
    return pl.pallas_call(
        gather_kernel,
        grid_spec=pltpu.PrefetchScalarGridSpec(
            num_scalar_prefetch=2,
            grid=(blocks // TOGETHER,),
            in_specs=[pl.BlockSpec((rows, columns), lambda b, *_: (0, 0))],
            out_specs=[
                pl.BlockSpec((TOGETHER, SEQUENCE_TOKENS, columns), lambda b, *_: (b, 0, 0)),
                pl.BlockSpec((rows * TOGETHER // blocks, columns), lambda b, *_: (b, 0)),
            ],
            scratch_shapes=[pltpu.VMEM((TOGETHER, SEQUENCE_TOKENS + 8, columns), f32)],
        ),
        out_shape=[
            jax.ShapeDtypeStruct((blocks, SEQUENCE_TOKENS, columns), bf16),
            jax.ShapeDtypeStruct((rows, columns), bf16),
        ],
        compiler_params=pltpu.CompilerParams(vmem_limit_bytes=26 << 20),
        name="gather_rows",
    )(lists, counts, table)


TABLE_PARTS = 8


def norm_cells(row, weight_sum, update_sum):
    rows = lax.broadcasted_iota(jnp.int32, (8, 128), 0)
    lanes = lax.broadcasted_iota(jnp.int32, (8, 128), 1)
    block = jnp.where(lanes == 0, weight_sum, jnp.where(lanes == 1, update_sum, 0.0))
    return jnp.where(rows == row, block, 0.0)


def total_of(values):
    return jnp.sum(jnp.sum(values, axis=1, keepdims=True), axis=0, keepdims=True)


def fold(values):
    return jnp.sum(values.reshape(-1, 8, values.shape[1]), axis=0)


def table_kernel(
    list_ref, count_ref, scale_ref, grad_ref, head_ref, w_in, first_in, second_in,
    new_first, new_second, updates, norms,
    rows_ref, acc, w, first, second, sums, sems,
):
    b = pl.program_id(0)
    blocks = pl.num_programs(0) - TABLE_PARTS
    loads = [
        pltpu.make_async_copy(src, dst, sems.at[n])
        for n, (src, dst) in enumerate([(w_in, w), (first_in, first), (second_in, second)])
    ]

    @pl.when(b == 0)
    def _():
        for load in loads:
            load.start()
        acc[...] = head_ref[...].astype(f32)
        sums[...] = jnp.zeros_like(sums)

    @pl.when(b < blocks)
    def _():
        for n in range(TOGETHER):
            rows_ref[n, :SEQUENCE_TOKENS] = grad_ref[n].astype(f32)
            rows_ref[n, SEQUENCE_TOKENS:] = jnp.zeros((8, rows_ref.shape[2]), f32)
            own = b * TOGETHER + n

            def step(k, carry, n=n, own=own):
                entries = [list_ref[own, k * STEPS + j] for j in range(STEPS)]
                spots = [entry & 65535 for entry in entries]
                grads = [rows_ref[n, pl.ds(entry >> 16, 1), :] for entry in entries]
                olds = [acc[pl.ds(spot, 1), :] for spot in spots]
                for j in range(STEPS):
                    total = olds[j] + grads[j]
                    for i in range(j):
                        total += jnp.where(spots[i] == spots[j], grads[i], 0.0)
                    acc[pl.ds(spots[j], 1), :] = total
                return carry

            lax.fori_loop(0, (count_ref[own] + STEPS - 1) // STEPS, step, 0)

    @pl.when(b == blocks)
    def _():
        for load in loads:
            load.wait()

    @pl.when(b >= blocks)
    def _():
        size = new_first.shape[0]
        here = pl.ds(pl.multiple_of((b - blocks) * size, 8), size)
        one, two, update = lamb_parts(
            w[here, :], first[here, :], second[here, :], acc[here, :], (scale_ref[0], scale_ref[1])
        )
        new_first[...] = one
        new_second[...] = two
        updates[...] = update
        sums[0] += fold(w[here, :] * w[here, :])
        sums[1] += fold(update * update)

    @pl.when(b == blocks + TABLE_PARTS - 1)
    def _():
        norms[...] = norm_cells(0, total_of(sums[0]), total_of(sums[1]))


def table_moments(lists, counts, scales, grads, head, weight, first, second):
    blocks = lists.shape[0] // TOGETHER
    rows, columns = weight.shape
    part = rows // TABLE_PARTS
    out = pl.BlockSpec((part, columns), lambda b, *_: (jnp.maximum(b - blocks, 0), 0))
    return pl.pallas_call(
        table_kernel,
        grid_spec=pltpu.PrefetchScalarGridSpec(
            num_scalar_prefetch=3,
            grid=(blocks + TABLE_PARTS,),
            in_specs=[
                pl.BlockSpec(
                    (TOGETHER, SEQUENCE_TOKENS, columns),
                    lambda b, *_: (jnp.minimum(b, blocks - 1), 0, 0),
                ),
                pl.BlockSpec(
                    (rows, columns), lambda b, *_: (0, 0), pipeline_mode=pl.Buffered(1)
                ),
            ]
            + [pl.BlockSpec(memory_space=pl.ANY)] * 3,
            out_specs=[out, out, out, pl.BlockSpec((8, 128), lambda b, *_: (0, 0))],
            scratch_shapes=[pltpu.VMEM((TOGETHER, SEQUENCE_TOKENS + 8, columns), f32)]
            + [pltpu.VMEM((rows, columns), f32)] * 4
            + [pltpu.VMEM((2, 8, columns), f32), pltpu.SemaphoreType.DMA((3,))],
        ),
        out_shape=[jax.ShapeDtypeStruct((rows, columns), f32)] * 3
        + [jax.ShapeDtypeStruct((8, 128), f32)],
        compiler_params=pltpu.CompilerParams(vmem_limit_bytes=58 << 20),
        name="table_moments",
    )(lists, counts, scales, grads, head, weight, first, second)


def small_kernel(
    scale_ref, grad_ref, qkv, qkv_one, qkv_two, out, out_one, out_two, router, router_one, router_two,
    gains, gains_one, gains_two, *results
):
    scales = (scale_ref[0], scale_ref[1])
    planes = grad_ref.shape[0]
    total = grad_ref[0].astype(f32)
    for z in range(1, planes):
        total += grad_ref[z].astype(f32)
    packs = (total[:, :PACK], total[:, PACK:])
    wide = HEAD_COLS + KEY_COLS
    pick = lax.broadcasted_iota(jnp.int32, (8, 128), 0) + EXPERTS
    pick = (pick == lax.broadcasted_iota(jnp.int32, (8, 128), 1)).astype(f32)
    gains_grad = lax.dot_general(
        pick,
        packs[0][:, wide:],
        ACROSS,
        preferred_element_type=f32,
        precision=lax.Precision.HIGHEST,
    )[:3]
    block = jnp.zeros((8, 128), f32)
    sets = [
        (qkv, qkv_one, qkv_two, jnp.concatenate([packs[0][:, :wide], packs[1][:, :KEY_COLS]], axis=1)),
        (out, out_one, out_two, packs[1][:, KEY_COLS : KEY_COLS + D]),
        (router, router_one, router_two, packs[0][:, wide : wide + EXPERTS]),
        (gains, gains_one, gains_two, gains_grad),
    ]
    for n, (weight, first, second, grad) in enumerate(sets):
        one, two, update = lamb_parts(weight[...], first[...], second[...], grad, scales)
        results[3 * n][...] = one
        results[3 * n + 1][...] = two
        results[3 * n + 2][...] = update
        block += norm_cells(n + 1, total_of(weight[...] * weight[...]), total_of(update * update))
    results[12][...] = block


def small_moments(scales, sums, *state):
    vm = pl.BlockSpec(memory_space=pltpu.VMEM)
    return pl.pallas_call(
        small_kernel,
        in_specs=[pl.BlockSpec(memory_space=pltpu.SMEM)] + [vm] * (1 + len(state)),
        out_specs=[vm] * 13,
        out_shape=[jax.ShapeDtypeStruct(x.shape, f32) for x in state[::3] for _ in range(3)]
        + [jax.ShapeDtypeStruct((8, 128), f32)],
        compiler_params=pltpu.CompilerParams(vmem_limit_bytes=62 << 20),
        name="small_moments",
    )(scales, sums, *state)


FINISH_PARTS = 8


def finish_kernel(norms_ref, *refs):
    norms = jnp.sqrt(jnp.sum(norms_ref[...], axis=0))
    count = len(refs) // 3

    def apply(n, row):
        ratio = norms[row : row + 1, 0:1] / norms[row : row + 1, 1:2]
        refs[2 * count + n][...] = refs[2 * n][...] - (STEP_RATE * ratio) * refs[2 * n + 1][...]

    apply(0, 0)
    apply(1, 5)
    apply(2, 6)

    @pl.when(pl.program_id(0) == 0)
    def _():
        apply(3, 1)
        apply(4, 2)


def finish(norms, *state):
    weights = state[::2]

    def spec(n):
        rows, columns = weights[n].shape
        if n < 3:
            return pl.BlockSpec((rows // FINISH_PARTS, columns), lambda i: (i, 0))
        return pl.BlockSpec((rows, columns), lambda i: (0, 0))

    return pl.pallas_call(
        finish_kernel,
        grid=(FINISH_PARTS,),
        in_specs=[pl.BlockSpec(norms.shape, lambda i: (0, 0, 0))]
        + [spec(n) for n in range(5) for _ in range(2)],
        out_specs=[spec(n) for n in range(5)],
        out_shape=[jax.ShapeDtypeStruct(x.shape, f32) for x in weights],
        compiler_params=pltpu.CompilerParams(vmem_limit_bytes=62 << 20),
        name="finish",
    )(norms, *state)


def on_device(
    token_ids,
    positions,
    pair_index,
    ref_logps,
    routes,
    step_count,
    embed_table,
    embed_first,
    embed_second,
    qkv_weight,
    qkv_first,
    qkv_second,
    out_weight,
    out_first,
    out_second,
    router_weight,
    router_first,
    router_second,
    norm_gains,
    gains_first,
    gains_second,
    in_weight,
    in_first,
    in_second,
    down_weight,
    down_first,
    down_second,
):
    shard_id = lax.axis_index("shard")
    expert_id = lax.axis_index("expert")
    shards = lax.axis_size("shard")
    planes = lax.axis_size("expert")
    devices = shards * planes
    vocab_rows, columns = embed_table.shape
    vocab_base = shard_id * vocab_rows
    own_rows = vocab_rows // planes
    local_experts = in_weight.shape[0]
    hidden_units = in_weight.shape[3]
    head_cols = QUERY_HEADS * HEAD_WIDTH
    key_cols = KEY_VALUE_HEADS * HEAD_WIDTH
    rows_all = devices * COMP

    side = math.isqrt(shards // 2)
    grid = (planes, side, side, 2)
    together = devices <= 32

    def send(parts, ident):
        if together:
            return communicate(parts, ident)
        return [
            out for n, part in enumerate(parts) for out in communicate([part], ident + 20 * n)
        ]

    unit = own_rows // 24

    def swap(x, *turns, back=False, held=None):
        turns = [(start * unit, size * unit, rounds) for start, size, rounds in turns]
        return Swap(x, turns, planes, side, back, held)

    def gather_part(rows):
        return Gather([rows], split(0, COMP, rows.shape[1], 2, 2), planes, side)

    def reduce_part(rows, cuts):
        width = rows.shape[1]
        rows = rows.reshape(grid + (COMP, width))
        edges = [width * n // (128 * cuts) * 128 for n in range(cuts + 1)]
        groups = [
            [
                (0, slice(i * COMP // 2, (i + 1) * COMP // 2), slice(low, high), i == 0)
                for i in range(2)
            ]
            for low, high in zip(edges, edges[1:])
        ]
        return Reduce([rows], groups, planes, side)

    def chain(rows, extra, extra_out, middle, beside, ident):
        gather = gather_part(jax.ShapeDtypeStruct((COMP, D), bf16))
        part = Chain(reduce_part(rows, 2), extra, extra_out, middle, gather)
        out = communicate([part, beside], ident)
        return (out[0].reshape(rows_all, D), *out[1:])

    def gather_tiny(block, ident):
        return communicate([Tiny(block, planes, side)], ident)[0].reshape((devices,) + block.shape)

    weight_rows = qkv_weight.shape[0]
    cuts = 3 if weight_rows % 48 == 0 else 1
    widths = (PACK, PACK_TWO)
    weight_groups = [
        [
            (i, slice(n * (weight_rows // cuts), (n + 1) * (weight_rows // cuts)), slice(0, width), i == 0)
            for i, width in enumerate(widths)
        ]
        for n in range(cuts)
    ]
    embed_groups = split(0, SEQUENCE_TOKENS, columns, 4, 1)

    own_places = lax.dynamic_index_in_dim(positions, shard_id, 0, keepdims=False)
    start = own_places[0]
    own_tokens = lax.dynamic_slice_in_dim(token_ids, shard_id * SEQUENCE_TOKENS, SEQUENCE_TOKENS, 0)
    own_routes = lax.dynamic_slice_in_dim(routes, start, COMP, 0)
    sheet = jnp.concatenate(
        [
            own_tokens,
            own_routes.reshape(-1),
            own_places,
            jnp.zeros((1024 - SEQUENCE_TOKENS - COMP * TOP - COMP,), jnp.int32),
        ]
    )
    sheets = gather_tiny(sheet.reshape(8, 128), 0).reshape(devices, 1024)
    tokens_all = sheets[:, :SEQUENCE_TOKENS]
    routes_all = sheets[:, SEQUENCE_TOKENS : SEQUENCE_TOKENS + COMP * TOP].reshape(rows_all, TOP)
    places_all = sheets[:, SEQUENCE_TOKENS + COMP * TOP : SEQUENCE_TOKENS + COMP * TOP + COMP]
    spots = jnp.arange(SEQUENCE_TOKENS, dtype=jnp.int32)
    targets = jnp.sum(
        jnp.where(
            places_all[:, :, None] + 1 == spots[None, None, :], tokens_all[:, None, :], 0
        ),
        axis=2,
    ).reshape(-1)

    lists, counts = row_lists(tokens_all, vocab_base, vocab_rows)
    picked, table_b = gather_rows(lists, counts, embed_table)
    picked = picked.reshape(grid + (SEQUENCE_TOKENS, columns))
    packs = jnp.concatenate(
        [
            qkv_weight[:, : head_cols + key_cols],
            router_weight,
            norm_gains.T,
            jnp.zeros((weight_rows, 128 - EXPERTS - 3), f32),
            qkv_weight[:, head_cols + key_cols :],
            out_weight,
        ],
        axis=1,
    ).astype(bf16)
    packs, sheets = lax.optimization_barrier((packs, sheets))
    packs = lax.all_to_all(
        jnp.broadcast_to(packs[None], (planes,) + packs.shape),
        "expert",
        split_axis=0,
        concat_axis=0,
        tiled=True,
    )
    first_pack, second_pack, picked, table_own = send(
        [
            Gather([packs], weight_groups, planes, side, prior=widths),
            Reduce([picked], embed_groups, planes, side, exchange=True),
            swap(table_b, (0, 16, 0)),
        ],
        1,
    )
    first_pack = first_pack.reshape(D, PACK)
    second_pack = second_pack.reshape(D, PACK_TWO)

    start_at = start.reshape(1)
    tables = rotary_tables()
    tables += tuple(lax.dynamic_slice_in_dim(table, start, COMP, 0) for table in tables)
    normed_two_b, resid, probs, query, key, value, attended, normed_b, gains = attend(
        start_at, picked, first_pack, second_pack, *tables
    )

    expert_rows, table_own = communicate(
        [gather_part(normed_two_b), swap(table_b, (16, 2, 2), held=table_own)], 2
    )
    expert_rows = expert_rows.reshape(rows_all, D)
    lanes = shard_id * local_experts + jnp.arange(local_experts, dtype=jnp.int32)
    in_rows = in_weight.reshape(-1, hidden_units)
    produced, mid, gates, in_cat, down_b, gated_hidden = experts_forward(
        lanes, expert_rows, routes_all, first_pack, in_rows, down_weight
    )
    own_index = expert_id * shards + shard_id
    own_gates = lax.dynamic_slice(gates, (own_index * COMP, 0), (COMP, 128))
    row_block = jax.ShapeDtypeStruct((COMP, D), f32)
    head_rows, resid_two, table_own = chain(
        produced,
        [resid, gains],
        [row_block],
        final_norm,
        swap(table_b, (18, 3, 0), (21, 3, 8), held=table_own),
        3,
    )

    logits = jnp.einsum("rd,vd->rv", head_rows, table_own, preferred_element_type=f32) / LOGIT_SCALE
    own_base = vocab_base + expert_id * own_rows
    target_hot = targets[:, None] == own_base + jnp.arange(own_rows, dtype=jnp.int32)[None, :]
    row_top = jnp.max(logits, axis=1)
    row_total = jnp.sum(jnp.exp(logits - row_top[:, None]), axis=1)
    row_hit = jnp.sum(jnp.where(target_hot, logits, 0.0), axis=1)
    stats = jnp.stack([row_top, row_total, row_hit]).reshape(8, 3 * rows_all // 8)
    stats = gather_tiny(stats, 5).reshape(devices, 3, rows_all)
    top_all = jnp.max(stats[:, 0], axis=0)
    total_all = jnp.sum(stats[:, 1] * jnp.exp(stats[:, 0] - top_all[None]), axis=0)
    row_lse = top_all + jnp.log(total_all)
    seq_sums = jnp.sum((jnp.sum(stats[:, 2], axis=0) - row_lse).reshape(-1, COMP), axis=1)

    sequences = jnp.arange(devices, dtype=jnp.int32)[None, :]
    pair_sign = (pair_index[:, :1] == sequences).astype(f32) - (
        pair_index[:, 1:] == sequences
    ).astype(f32)
    scaled = BETA * jnp.sum(pair_sign * (seq_sums - ref_logps)[None, :], axis=1)
    loss_value = -jnp.mean(jax.nn.log_sigmoid(scaled))
    pair_grad = jax.nn.sigmoid(-scaled) * (-BETA / scaled.shape[0])
    seq_grad = jnp.sum(pair_sign * pair_grad[:, None], axis=0)
    row_grad = jnp.repeat(seq_grad, COMP)
    grad_logits = (
        row_grad[:, None] * (target_hot.astype(f32) - jnp.exp(logits - row_lse[:, None]))
    ).astype(bf16)
    grad_logits = lax.optimization_barrier(grad_logits)
    grad_rows = jnp.dot(grad_logits, table_own, preferred_element_type=f32) / LOGIT_SCALE
    head_grad = (
        jnp.einsum("rv,rd->vd", grad_logits, head_rows, preferred_element_type=f32) / LOGIT_SCALE
    ).astype(bf16)
    grad_all, grad_resid_two, grad_gain_three, head_back = chain(
        grad_rows.astype(bf16),
        [resid_two, gains],
        [row_block, jax.ShapeDtypeStruct((1, D), f32)],
        final_norm_back,
        swap(head_grad, (0, 3, 0), (3, 3, 8), back=True),
        6,
    )

    back, mid_grad = experts_backward(lanes, grad_all, mid, gates, in_cat, down_b)
    back, head_back = communicate(
        [reduce_part(back, 2), swap(head_grad, (6, 3, 0), back=True, held=head_back)], 8
    )

    grad_embedded, *grad_packs = attend_back(
        start_at,
        back,
        own_gates,
        grad_resid_two,
        grad_gain_three,
        normed_two_b,
        resid,
        probs,
        query,
        key,
        value,
        attended,
        normed_b,
        gains,
        picked,
        first_pack,
        second_pack,
        *tables,
    )
    grad_packs = [pack.reshape(grid + (weight_rows, pack.shape[1])) for pack in grad_packs]
    wide = head_cols + key_cols
    plane_sums, sent, head_back = send(
        [
            Reduce(grad_packs, weight_groups, planes, side, partial=True),
            Gather([grad_embedded], embed_groups, planes, side, exchange=True),
            swap(head_grad, (9, 5, 1), (14, 5, 2), (19, 5, 3), back=True, held=head_back),
        ],
        9,
    )
    plane_sums = lax.all_to_all(
        plane_sums, "expert", split_axis=0, concat_axis=0, tiled=True
    )

    step_value = step_count.astype(f32)
    scales = jnp.stack([1.0 / (1.0 - RATE_ONE**step_value), 1.0 / (1.0 - RATE_TWO**step_value)])
    grad_in = jnp.einsum("td,tk->dk", expert_rows, mid_grad, preferred_element_type=f32)
    grad_down = jnp.einsum("tk,td->kd", gated_hidden, grad_all, preferred_element_type=f32)
    down_rows = down_weight.reshape(-1, D)
    table_one, table_two, table_update, table_norms = table_moments(
        lists,
        counts,
        scales,
        sent.reshape(devices, SEQUENCE_TOKENS, columns),
        head_back.reshape(vocab_rows, columns),
        embed_table,
        embed_first,
        embed_second,
    )
    *small, small_norms = small_moments(
        scales,
        plane_sums,
        qkv_weight,
        qkv_first,
        qkv_second,
        out_weight,
        out_first,
        out_second,
        router_weight,
        router_first,
        router_second,
        norm_gains,
        gains_first,
        gains_second,
    )
    in_one, in_two, in_update, down_one, down_two, down_update, expert_norms = expert_moments(
        scales,
        table_norms + small_norms,
        grad_in,
        in_rows,
        in_first.reshape(in_rows.shape),
        in_second.reshape(in_rows.shape),
        grad_down,
        down_rows,
        down_first.reshape(down_rows.shape),
        down_second.reshape(down_rows.shape),
    )
    norm_blocks = gather_tiny(expert_norms, 10)
    norm_values = jnp.sqrt(jnp.sum(norm_blocks, axis=0))[:7, :2]
    trust_ratio = norm_values[:, 0] / norm_values[:, 1]
    new_table, new_in, new_down, new_qkv, new_out = finish(
        norm_blocks,
        embed_table,
        table_update,
        in_rows,
        in_update,
        down_rows,
        down_update,
        qkv_weight,
        small[2],
        out_weight,
        small[5],
    )
    new_router = router_weight - STEP_RATE * trust_ratio[3] * small[8]
    new_gains = norm_gains - STEP_RATE * trust_ratio[4] * small[11]
    stats = jnp.stack([norm_values[:, 0], norm_values[:, 1], trust_ratio], axis=1)
    return (
        loss_value,
        new_table,
        table_one,
        table_two,
        new_qkv,
        small[0],
        small[1],
        new_out,
        small[3],
        small[4],
        new_router,
        small[6],
        small[7],
        new_gains,
        small[9],
        small[10],
        new_in.reshape(in_weight.shape),
        in_one.reshape(in_weight.shape),
        in_two.reshape(in_weight.shape),
        new_down.reshape(down_weight.shape),
        down_one.reshape(down_weight.shape),
        down_two.reshape(down_weight.shape),
        stats,
    )


def solution(mesh):
    rows = P(BOTH, None)
    vocab = P("shard", "expert")
    gains = P(None, BOTH)
    inner = P("shard", None, None, "expert")
    outer = P("shard", "expert", None)
    state = (vocab,) * 3 + (rows,) * 9 + (gains,) * 3 + (inner,) * 3 + (outer,) * 3
    return jax.shard_map(
        on_device,
        mesh=mesh,
        in_specs=(P("expert"), P("expert", None), P(), P(), rows, P()) + state,
        out_specs=(P(),) + state + (P(),),
        check_vma=False,
    )
```

```python
import functools
import math

import jax
import jax.numpy as jnp
from jax import lax
from jax.experimental import pallas as pl
from jax.experimental.pallas import tpu as pltpu
from jax.sharding import PartitionSpec as P

D = 1536
QUERY_HEADS = 24
KEY_VALUE_HEADS = 8
GROUP = QUERY_HEADS // KEY_VALUE_HEADS
HEAD_WIDTH = 64
TOP = 8
EXPERTS = 32
SEQUENCE_TOKENS = 256
COMP = 32
QKV = 2560

BETA = 0.1
LOGIT_SCALE = 6.0
RATE_ONE = 0.9
RATE_TWO = 0.999
EPSILON = 1e-06
DECAY = 0.01
STEP_RATE = 0.3

BOTH = ("expert", "shard")
bf16 = jnp.bfloat16
f32 = jnp.float32


MESH = pl.DeviceIdType.MESH


class Spot:
    def __init__(self, planes, side):
        self.planes, self.side = planes, side
        self.z = lax.axis_index("expert")
        self.shard = lax.axis_index("shard")
        self.core = lax.rem(self.shard, 2)
        self.b = lax.rem(lax.div(self.shard, 2), side)
        self.a = lax.div(self.shard, 2 * side)

    def plane(self, k):
        z = lax.rem(self.z + k, self.planes)
        return z, (z, self.shard)

    def along_a(self, k):
        a = lax.rem(self.a + k, self.side)
        return a, (self.z, (a * self.side + self.b) * 2 + self.core)

    def along_b(self, k):
        b = lax.rem(self.b + k, self.side)
        return b, (self.z, (self.a * self.side + b) * 2 + self.core)

    def along(self, first, k):
        return self.along_a(k) if first else self.along_b(k)

    def mate(self):
        other = 1 - self.core
        return other, (self.z, (self.a * self.side + self.b) * 2 + other)

    def near(self, k):
        return self.z, lax.rem(self.shard + k, 2 * self.side * self.side)

    def greet(self, flat):
        targets = [self.plane(k)[1] for k in range(1, self.planes)]
        if flat:
            targets += [self.near(k) for k in range(1, 2 * self.side * self.side)]
        else:
            targets.append(self.mate()[1])
            for k in range(1, self.side):
                targets += [self.along_a(k)[1], self.along_b(k)[1]]
        barrier = pltpu.get_barrier_semaphore()
        for target in targets:
            pl.semaphore_signal(barrier, inc=1, device_id=target, device_id_type=MESH)
        pl.semaphore_wait(barrier, len(targets))


class Mail:
    def __init__(self, send, recv):
        self.send, self.recv, self.count, self.open = send, recv, 0, []

    def start(self, src, dst, target):
        copy = pltpu.make_async_remote_copy(
            src_ref=src,
            dst_ref=dst,
            send_sem=self.send.at[self.count],
            recv_sem=self.recv.at[self.count],
            device_id=target,
            device_id_type=MESH,
        )
        self.count += 1
        copy.start()
        self.open.append(copy)
        return copy

    def finish(self):
        for copy in self.open:
            copy.wait_send()


def arrive(copies):
    for copy in copies:
        copy.wait_recv()


class Tiny:
    flat = True
    scratch = ()

    def __init__(self, x, planes, side):
        self.planes, self.side, self.inputs = planes, side, [x]
        shape = (planes, 2 * side * side) + x.shape
        self.outputs = [jax.ShapeDtypeStruct(shape, x.dtype)]
        self.copies = planes + 2 * side * side - 2

    def steps(self, spot, mail, x, out):
        out[spot.z, spot.shard] = x[...]
        sent = []
        for k in range(1, self.planes):
            sent.append(mail.start(x, out.at[spot.z, spot.shard], spot.plane(k)[1]))
        yield
        arrive(sent)
        part = out.at[:, spot.shard]
        yield
        arrive([mail.start(part, part, spot.near(k)) for k in range(1, 2 * self.side**2)])


def split(array, rows, columns, row_parts, column_parts):
    r, c = rows // row_parts, columns // column_parts
    cuts = [
        (array, slice(i * r, i * r + r), slice(j * c, j * c + c))
        for j in range(column_parts)
        for i in range(row_parts)
    ]
    cuts = [cut + (n % 2 == 0,) for n, cut in enumerate(cuts)]
    return [cuts[n : n + 2] for n in range(0, len(cuts), 2)]


def pipeline(groups, stage, last):
    sent = [[[] for _ in group] for group in groups]
    for tick in range(len(groups) + last):
        for step in range(last, -1, -1):
            turn = tick - step
            if 0 <= turn < len(groups):
                for n, cut in enumerate(groups[turn]):
                    for copy in sent[turn][n]:
                        copy.wait_recv()
                    sent[turn][n] = stage(step, (turn, n), cut)
        yield


class Gather:
    flat = False
    scratch = ()

    def __init__(self, xs, groups, planes, side, exchange=False, prior=None):
        self.planes, self.side, self.inputs, self.groups = planes, side, xs, groups
        self.exchange, self.prior = exchange, prior
        grid = (planes, side, side, 2)
        shapes = [x.shape[-2:] for x in xs]
        if prior:
            shapes = [xs[0].shape[-2:-1] + (width,) for width in prior]
        self.outputs = [jax.ShapeDtypeStruct(grid + shape, xs[0].dtype) for shape in shapes]
        self.copies = sum(map(len, groups)) * (planes - 1 + 2 * (side - 1) + 1)

    def steps(self, spot, mail, *refs):
        xs, outs = refs[: len(self.inputs)], refs[len(self.inputs) :]
        z, a, b, core = spot.z, spot.a, spot.b, spot.core
        if self.prior:
            low = 0
            for width, out in zip(self.prior, outs):
                out[:, a, b, core] = xs[0][:, :, low : low + width]
                low += width
            xs = [None] * len(outs)
        else:
            for x, out in zip(xs, outs):
                out[z, a, b, core] = x[z] if self.exchange else x[...]

        def stage(step, key, cut):
            i, rows, columns, first = cut
            x, out = xs[i], outs[i]
            if step == 0 and self.prior:
                return []
            if step == 0:
                place = out.at[z, a, b, core, rows, columns]
                sent = []
                for k in range(1, self.planes):
                    peer, target = spot.plane(k)
                    own = x.at[peer, rows, columns] if self.exchange else x.at[rows, columns]
                    sent.append(mail.start(own, place, target))
                return sent
            if step in (1, 2):
                if step == 1:
                    part = out.at[:, a, b, core, rows, columns]
                elif first:
                    part = out.at[:, :, b, core, rows, columns]
                else:
                    part = out.at[:, a, :, core, rows, columns]
                return [
                    mail.start(part, part, spot.along(first == (step == 1), k)[1])
                    for k in range(1, self.side)
                ]
            if step == 3:
                part = out.at[:, :, :, core, rows, columns]
                return [mail.start(part, part, spot.mate()[1])]
            return []

        return pipeline(self.groups, stage, 4)


class Reduce:
    flat = False

    def __init__(self, xs, groups, planes, side, exchange=False, partial=False):
        self.planes, self.side, self.inputs, self.groups = planes, side, xs, groups
        self.exchange, self.partial = exchange or partial, partial
        self.outputs = [
            jax.ShapeDtypeStruct((planes,) + x.shape[-2:], x.dtype)
            if self.exchange
            else jax.ShapeDtypeStruct(x.shape[-2:], f32)
            for x in xs
        ]
        if partial:
            shape = (planes, xs[0].shape[-2], sum(x.shape[-1] for x in xs))
            self.outputs = [jax.ShapeDtypeStruct(shape, xs[0].dtype)]
        self.scratch = []
        for i, rows, columns, _ in [cut for group in groups for cut in group]:
            block = (rows.stop - rows.start, columns.stop - columns.start)
            self.scratch += [
                pltpu.VMEM(shape + block, xs[i].dtype)
                for shape in (
                    (planes, side, side),
                    (side - 1, planes, side),
                    (planes, side),
                    (side - 1, planes),
                    (planes,),
                )
                + (() if self.exchange else ((planes - 1,),))
            ]
        self.copies = sum(map(len, groups)) * (planes - 1 + 2 * (side - 1) + 1)

    def steps(self, spot, mail, *refs):
        planes, side, number = self.planes, self.side, len(self.inputs)
        made = number + len(self.outputs)
        xs, outs, rest = refs[:number], refs[number:made], refs[made:]
        lows = [0] * number
        if self.partial:
            outs = [outs[0]] * number
            lows = [sum(x.shape[-1] for x in self.inputs[:n]) for n in range(number)]
        each = 5 if self.exchange else 6
        order = [(t, n) for t, group in enumerate(self.groups) for n in range(len(group))]
        held = {key: rest[each * p : each * (p + 1)] for p, key in enumerate(order)}
        core, z = spot.core, spot.z
        other, mate = spot.mate()

        def stage(step, key, cut):
            i, rows, columns, first = cut
            x, out = xs[i], outs[i]
            one, hop_two, two, hop_three, three = held[key][:5]
            if step == 0:
                return [mail.start(x.at[:, :, :, other, rows, columns], one, mate)]
            sent = []
            if step == 1:

                def add(n, carry):
                    ia, ib = lax.rem(lax.div(n, side), side), lax.rem(n, side)
                    iz = lax.div(n, side * side)
                    total = x[iz, ia, ib, core, rows, columns].astype(f32)
                    one[iz, ia, ib] = (total + one[iz, ia, ib].astype(f32)).astype(one.dtype)
                    return carry

                lax.fori_loop(0, planes * side * side, add, 0)
                for k in range(1, side):
                    peer, target = spot.along(first, k)
                    part = one.at[:, peer] if first else one.at[:, :, peer]
                    sent.append(mail.start(part, hop_two.at[k - 1], target))
            elif step == 2:

                def add(n, carry):
                    iz, ir = lax.div(n, side), lax.rem(n, side)
                    total = (one[iz, spot.a, ir] if first else one[iz, ir, spot.b]).astype(f32)
                    for k in range(side - 1):
                        total += hop_two[k, iz, ir].astype(f32)
                    two[iz, ir] = total.astype(two.dtype)
                    return carry

                lax.fori_loop(0, planes * side, add, 0)
                for k in range(1, side):
                    peer, target = spot.along(not first, k)
                    sent.append(mail.start(two.at[:, peer], hop_three.at[k - 1], target))
            elif step == 3:
                mine = spot.b if first else spot.a

                def add(iz, carry):
                    total = two[iz, mine].astype(f32)
                    for k in range(side - 1):
                        total += hop_three[k, iz].astype(f32)
                    if self.partial:
                        place = slice(lows[i] + columns.start, lows[i] + columns.stop)
                        out[iz, rows, place] = total.astype(out.dtype)
                    else:
                        three[iz] = total.astype(three.dtype)
                    return carry

                lax.fori_loop(0, planes, add, 0)
                if self.partial:
                    return []
                for k in range(1, planes):
                    peer, target = spot.plane(k)
                    if self.exchange:
                        place = out.at[z, rows, columns]
                    else:
                        place = held[key][5].at[k - 1]
                    sent.append(mail.start(three.at[peer], place, target))
                if self.exchange:
                    out[z, rows, columns] = three[z]
            elif not self.exchange:
                total = three[z].astype(f32)
                for k in range(planes - 1):
                    total += held[key][5][k].astype(f32)
                out[rows, columns] = total
            return sent

        return pipeline(self.groups, stage, 4)


class Swap:
    flat = False
    def __init__(self, x, turns, planes, side, back=False, held=None):
        self.planes, self.side = planes, side
        self.inputs = [x] if held is None else [x, held]
        self.in_spaces, self.out_spaces = (pltpu.HBM,) * len(self.inputs), (pltpu.HBM,)
        self.aliases = {} if held is None else {1: 0}
        self.turns, self.back = turns, back
        self.scratch = [pltpu.SemaphoreType.DMA((len(turns),))]
        self.columns = x.shape[1] // planes if back else x.shape[1]
        self.rows = x.shape[0] if back else x.shape[0] // planes
        shape = (planes, self.rows, self.columns) if back else (self.rows, planes * self.columns)
        self.outputs = [jax.ShapeDtypeStruct(shape, x.dtype)]
        self.copies = len(turns) * (planes - 1)

    def steps(self, spot, mail, *refs):
        x, out, own_sem = refs[0], refs[-2], refs[-1]
        def block(z):
            return pl.ds(pl.multiple_of(z * self.columns, 128), self.columns)

        def source(z, begin, size):
            if self.back:
                return x.at[pl.ds(begin, size), block(z)]
            return x.at[pl.ds(pl.multiple_of(z * self.rows + begin, 16), size), :]

        sent, own, now = [], [], 0
        for n, (begin, size, rounds) in enumerate(self.turns):
            while now < rounds:
                now += 1
                yield
            rows = pl.ds(begin, size)
            place = out.at[spot.z, rows] if self.back else out.at[rows, block(spot.z)]
            for k in range(1, self.planes):
                peer, target = spot.plane(k)
                sent.append(mail.start(source(peer, begin, size), place, target))
            own.append(pltpu.make_async_copy(source(spot.z, begin, size), place, own_sem.at[n]))
            own[-1].start()
        while now < 24:
            now += 1
            yield
        for copy in own:
            copy.wait()
        for copy in sent:
            copy.wait_recv()


class Chain:
    flat = False

    def __init__(self, reduce, extra, extra_out, middle, gather):
        self.planes, self.side = reduce.planes, reduce.side
        self.reduce, self.middle, self.gather = reduce, middle, gather
        self.inputs = reduce.inputs + extra
        self.outputs = gather.outputs + extra_out
        self.scratch = reduce.scratch + [
            pltpu.VMEM(x.shape, x.dtype) for x in reduce.outputs + gather.inputs
        ]
        self.copies = reduce.copies + gather.copies

    def steps(self, spot, mail, *refs):
        n_in, n_out = len(self.inputs), len(self.outputs)
        (x, *extra), (out, *extra_out) = refs[:n_in], refs[n_in : n_in + n_out]
        *held, sums, made = refs[n_in + n_out :]
        yield from self.reduce.steps(spot, mail, x, sums, *held)
        self.middle(sums, made, *extra, *extra_out)
        yield from self.gather.steps(spot, mail, made, out)


def final_norm(sums, made, resid, gains, resid_two):
    values = resid[...] + sums[...]
    resid_two[...] = values
    made[...] = (values * inverse_root(values) * gains[2:3]).astype(bf16)


def final_norm_back(sums, made, resid_two, gains, grad_two, gain_grad):
    grad, gain_grad[...] = norm_back(resid_two[...], gains[2:3], sums[...])
    grad_two[...] = grad
    made[...] = grad.astype(bf16)


def communicate(parts, ident):
    planes, side = parts[0].planes, parts[0].side
    counts = [(len(p.inputs), len(p.outputs), len(p.scratch)) for p in parts]
    n_in, n_out = (sum(c[i] for c in counts) for i in range(2))
    copies = sum(p.copies for p in parts)
    aliases, i, o = {}, 0, 0
    for part, (ci, co, _) in zip(parts, counts):
        aliases.update({i + a: o + b for a, b in getattr(part, "aliases", {}).items()})
        i, o = i + ci, o + co

    def kernel(*refs):
        ins, outs, rest = refs[:n_in], refs[n_in : n_in + n_out], refs[n_in + n_out :]
        send, recv = rest[-2:]
        spot = Spot(planes, side)
        spot.greet(parts[0].flat)
        mail = Mail(send, recv)
        running, i, o, s = [], 0, 0, 0
        for part, (ci, co, cs) in zip(parts, counts):
            running.append(
                part.steps(spot, mail, *ins[i : i + ci], *outs[o : o + co], *rest[s : s + cs])
            )
            i, o, s = i + ci, o + co, s + cs
        while running:
            running = [steps for steps in running if next(steps, True) is None]
        mail.finish()

    size = sum(x.size * x.dtype.itemsize for p in parts for x in p.inputs + p.outputs)
    need = sum(
        math.prod(x.shape) * x.dtype.itemsize
        for p in parts
        for x in p.scratch
        if x.memory_space == pltpu.VMEM
    )
    need += sum(
        x.size * x.dtype.itemsize
        for p in parts
        if not isinstance(p, Swap)
        for x in p.inputs + p.outputs
    )
    out = pl.pallas_call(
        kernel,
        out_shape=[x for p in parts for x in p.outputs],
        in_specs=[
            pl.BlockSpec(memory_space=space)
            for p in parts
            for space in getattr(p, "in_spaces", (pltpu.VMEM,) * len(p.inputs))
        ],
        out_specs=[
            pl.BlockSpec(memory_space=space)
            for p in parts
            for space in getattr(p, "out_spaces", (pltpu.VMEM,) * len(p.outputs))
        ],
        input_output_aliases=aliases,
        scratch_shapes=[s for p in parts for s in p.scratch]
        + [pltpu.SemaphoreType.DMA((copies,)), pltpu.SemaphoreType.DMA((copies,))],
        compiler_params=pltpu.CompilerParams(
            collective_id=ident,
            has_side_effects=True,
            vmem_limit_bytes=min(62 << 20, need * 9 // 8 + (4 << 20)),
        ),
        cost_estimate=pl.CostEstimate(flops=0, bytes_accessed=20 * size, transcendentals=0),
        name="exchange_" + str(ident),
    )(*[x for p in parts for x in p.inputs])
    return list(out)

def expert_gate(gates, lane):
    lanes = lax.broadcasted_iota(jnp.int32, gates.shape, 1)
    return jnp.sum(jnp.where(lanes == lane, gates, 0.0), axis=1, keepdims=True)


CHUNK = 512
BLOCK = 1024
ACROSS = (((1,), (1,)), ((), ()))


def forward_kernel(
    lane_ref, rows_ref, routes_ref, router_ref, in_ref, down_ref, out_ref, mid_ref, gates_ref, cat_ref, down_out, hidden_ref
):
    e, number = pl.program_id(1), pl.num_programs(1)
    units = in_ref.shape[1]
    for j in range(2):
        cat_ref[:, j * units : (j + 1) * units] = in_ref[pl.ds(j, D, stride=2), :].astype(bf16)
    down_out[pl.ds(pl.multiple_of(e * units, units), units), :] = down_ref[0].astype(bf16)

    def chunk(i, carry):
        here = pl.ds(pl.multiple_of(i * CHUNK, CHUNK), CHUNK)
        rows = rows_ref[here, :]

        @pl.when(e == 0)
        def _():
            logits = jnp.dot(rows, router_ref[...], preferred_element_type=f32)
            lanes = lax.broadcasted_iota(jnp.int32, logits.shape, 1)
            mask = lanes == routes_ref[here, 0:1]
            for j in range(1, TOP):
                mask |= lanes == routes_ref[here, j : j + 1]
            top = jnp.max(jnp.where(mask, logits, -3e38), axis=1, keepdims=True)
            weight = jnp.where(mask, jnp.exp(jnp.where(mask, logits - top, 0.0)), 0.0)
            gates_ref[here, :] = weight / jnp.sum(weight, axis=1, keepdims=True)

        mid = jnp.dot(rows, cat_ref[...], preferred_element_type=f32)
        mid_ref[here, :] = mid
        gate, up = mid[:, :units], mid[:, units:]
        hidden = (gate * jax.nn.sigmoid(gate) * up).astype(bf16).astype(f32)
        hidden = (hidden * expert_gate(gates_ref[here, :], lane_ref[0] + e)).astype(bf16)
        hidden_ref[here, pl.ds(pl.multiple_of(e * units, units), units)] = hidden

        @pl.when(e == number - 1)
        def _():
            out_ref[here, :] = jnp.dot(
                hidden_ref[here, :], down_out[...], preferred_element_type=f32
            ).astype(bf16)

        return carry

    lax.fori_loop(0, rows_ref.shape[0] // CHUNK, chunk, 0)


def experts_forward(lane, rows, routes, router, in_rows, down):
    number, units = down.shape[:2]
    total = rows.shape[0]
    block = min(total, BLOCK)
    row = lambda r, e, *_: (r, 0)
    still = lambda r, e, *_: (0, 0)
    return pl.pallas_call(
        forward_kernel,
        grid_spec=pltpu.PrefetchScalarGridSpec(
            num_scalar_prefetch=1,
            grid=(total // block, number),
            in_specs=[
                pl.BlockSpec((block, D), row),
                pl.BlockSpec((block, TOP), row),
                pl.BlockSpec((D, 128), lambda r, e, *_: (0, PACK // 128 - 1)),
                pl.BlockSpec((2 * D, units), lambda r, e, *_: (e, 0)),
                pl.BlockSpec((1, units, D), lambda r, e, *_: (e, 0, 0)),
            ],
            out_specs=[
                pl.BlockSpec((block, D), row),
                pl.BlockSpec((block, 2 * units), lambda r, e, *_: (r, e)),
                pl.BlockSpec((block, 128), row),
                pl.BlockSpec((D, 2 * units), lambda r, e, *_: (0, e)),
                pl.BlockSpec((number * units, D), still),
                pl.BlockSpec((block, number * units), row),
            ],
        ),
        out_shape=[
            jax.ShapeDtypeStruct((total, D), bf16),
            jax.ShapeDtypeStruct((total, 2 * units * number), f32),
            jax.ShapeDtypeStruct((total, 128), f32),
            jax.ShapeDtypeStruct((D, 2 * units * number), bf16),
            jax.ShapeDtypeStruct((number * units, D), bf16),
            jax.ShapeDtypeStruct((total, number * units), bf16),
        ],
        compiler_params=pltpu.CompilerParams(vmem_limit_bytes=42 << 20),
        name="experts_forward",
    )(lane, rows, routes, router, in_rows, down)


def backward_kernel(
    lane_ref, grad_ref, mid_ref, gates_ref, cat_ref, down_ref, out_ref, mid_grad_ref, pulled_ref
):
    number = lane_ref.shape[0]
    units = pulled_ref.shape[1] // number

    def chunk(i, carry):
        here = pl.ds(pl.multiple_of(i * CHUNK, CHUNK), CHUNK)
        pulled_ref[...] = lax.dot_general(
            grad_ref[here, :], down_ref[...], ACROSS, preferred_element_type=f32
        )
        lanes = lax.broadcasted_iota(jnp.int32, (CHUNK, 128), 1)
        gate_part = jnp.zeros((CHUNK, 128), f32)
        for e in range(number):
            lane = lane_ref[e]
            weight = expert_gate(gates_ref[here, :], lane)
            gate = mid_ref[here, 2 * e * units : (2 * e + 1) * units]
            up = mid_ref[here, (2 * e + 1) * units : (2 * e + 2) * units]
            pulled = pulled_ref[:, e * units : (e + 1) * units]
            soft = jax.nn.sigmoid(gate)
            silu = gate * soft
            hidden = (silu * up).astype(bf16).astype(f32)
            gate_grad = jnp.sum(hidden * pulled, axis=1, keepdims=True)
            gate_part = jnp.where(lanes == lane, gate_grad, gate_part)
            hidden_grad = (pulled * weight).astype(bf16).astype(f32)
            turned = hidden_grad * up * (soft * (1.0 + gate * (1.0 - soft)))
            mid_grad_ref[here, 2 * e * units : (2 * e + 1) * units] = turned.astype(bf16)
            mid_grad_ref[here, (2 * e + 1) * units : (2 * e + 2) * units] = (
                hidden_grad * silu
            ).astype(bf16)
        out_ref[here, D:] = gate_part.astype(bf16)
        out_ref[here, :D] = lax.dot_general(
            mid_grad_ref[here, :], cat_ref[...], ACROSS, preferred_element_type=f32
        ).astype(bf16)
        return carry

    lax.fori_loop(0, grad_ref.shape[0] // CHUNK, chunk, 0)


def experts_backward(lanes, grad, mid, gates, cat, down):
    number = lanes.shape[0]
    total = grad.shape[0]
    block = CHUNK
    row = lambda r, *_: (r, 0)
    still = lambda r, *_: (0, 0)
    return pl.pallas_call(
        backward_kernel,
        grid_spec=pltpu.PrefetchScalarGridSpec(
            num_scalar_prefetch=1,
            grid=(total // block,),
            in_specs=[
                pl.BlockSpec((block, D), row),
                pl.BlockSpec((block, mid.shape[1]), row),
                pl.BlockSpec((block, 128), row),
                pl.BlockSpec(cat.shape, still),
                pl.BlockSpec(down.shape, still),
            ],
            out_specs=[
                pl.BlockSpec((block, D + 128), row),
                pl.BlockSpec((block, mid.shape[1]), row),
            ],
            scratch_shapes=[pltpu.VMEM((CHUNK, down.shape[0]), f32)],
        ),
        out_shape=[
            jax.ShapeDtypeStruct((total, D + 128), bf16),
            jax.ShapeDtypeStruct(mid.shape, bf16),
        ],
        compiler_params=pltpu.CompilerParams(vmem_limit_bytes=36 << 20),
        name="experts_backward",
    )(lanes, grad, mid, gates, cat, down)


def moments_kernel(
    scale_ref, other_norms, grad_ref, w_ref, first_ref, second_ref, down_grad, down_w, down_first, down_second,
    new_first, new_second, updates, new_down_first, new_down_second, down_updates, norms, sums, down_sums, turned,
):
    units = w_ref.shape[1]
    part = w_ref.shape[0] // 2
    scales = (scale_ref[0], scale_ref[1])
    step = pl.program_id(0) * pl.num_programs(1) + pl.program_id(1)

    @pl.when(step == 0)
    def _():
        sums[...] = jnp.zeros_like(sums)
        down_sums[...] = jnp.zeros_like(down_sums)

    for j in range(2):
        turned[pl.ds(j, part, stride=2), :] = grad_ref[:, j * units : (j + 1) * units]
    weight = w_ref[...]
    one, two, update = lamb_parts(weight, first_ref[...], second_ref[...], turned[...], scales)
    new_first[...] = one
    new_second[...] = two
    updates[...] = update
    sums[0] += fold(weight * weight)
    sums[1] += fold(update * update)
    weight = down_w[...]
    one, two, update = lamb_parts(weight, down_first[...], down_second[...], down_grad[...], scales)
    new_down_first[...] = one
    new_down_second[...] = two
    down_updates[...] = update
    down_sums[0] += fold(weight * weight)
    down_sums[1] += fold(update * update)

    @pl.when(step == pl.num_programs(0) * pl.num_programs(1) - 1)
    def _():
        block = norm_cells(5, total_of(sums[0]), total_of(sums[1]))
        block += norm_cells(6, total_of(down_sums[0]), total_of(down_sums[1]))
        norms[...] = other_norms[...] + block


def expert_moments(scales, norms, grad, weight, first, second, *down_state):
    units = weight.shape[1]
    down = down_state[1]
    number = grad.shape[1] // (2 * units)
    parts = 2
    cells = pl.BlockSpec((8, 128), lambda e, p, *_: (0, 0))
    row = pl.BlockSpec((2 * D // parts, units), lambda e, p, *_: (e * parts + p, 0))
    down_row = pl.BlockSpec((units // parts, D), lambda e, p, *_: (e * parts + p, 0))
    return pl.pallas_call(
        moments_kernel,
        grid_spec=pltpu.PrefetchScalarGridSpec(
            num_scalar_prefetch=1,
            grid=(number, parts),
            in_specs=[cells, pl.BlockSpec((D // parts, 2 * units), lambda e, p, *_: (p, e))]
            + [row] * 3
            + [down_row] * 4,
            out_specs=[row] * 3 + [down_row] * 3 + [cells],
            scratch_shapes=[
                pltpu.VMEM((2, 8, units), f32),
                pltpu.VMEM((2, 8, D), f32),
                pltpu.VMEM((2 * D // parts, units), f32),
            ],
        ),
        out_shape=[jax.ShapeDtypeStruct(weight.shape, f32)] * 3
        + [jax.ShapeDtypeStruct(down.shape, f32)] * 3
        + [jax.ShapeDtypeStruct((8, 128), f32)],
        compiler_params=pltpu.CompilerParams(vmem_limit_bytes=62 << 20),
        name="expert_moments",
    )(scales, norms, grad, weight, first, second, *down_state)


HEAD_COLS = QUERY_HEADS * HEAD_WIDTH
KEY_COLS = KEY_VALUE_HEADS * HEAD_WIDTH
PACK = HEAD_COLS + KEY_COLS + 128
PACK_TWO = KEY_COLS + D
ROOT = HEAD_WIDTH ** (-0.5)


def turn(u, cosine, sine):
    width = u.shape[1]
    lanes = lax.broadcasted_iota(jnp.int32, u.shape, 1)
    ahead = pltpu.roll(u, width - HEAD_WIDTH // 2, 1)
    behind = pltpu.roll(u, HEAD_WIDTH // 2, 1)
    other = jnp.where(lax.rem(lanes, HEAD_WIDTH) < HEAD_WIDTH // 2, ahead, behind)
    return u * jnp.tile(cosine, (1, width // 128)) + other * jnp.tile(sine, (1, width // 128))


def rotary_tables():
    half = HEAD_WIDTH // 2
    freqs = jnp.exp(-jnp.log(10000.0) * jnp.arange(half, dtype=f32) / half)
    angles = jnp.arange(SEQUENCE_TOKENS, dtype=f32)[:, None] * freqs[None, :]
    cosine, sine = jnp.cos(angles), jnp.sin(angles)
    return jnp.tile(cosine, (1, 4)), jnp.tile(jnp.concatenate([-sine, sine], axis=1), (1, 2))


def inverse_root(values):
    return lax.rsqrt(jnp.mean(values * values, axis=-1, keepdims=True) + 1e-06)


def norm_back(values, gain, grad):
    root = inverse_root(values)
    scaled = grad * gain
    inner = jnp.mean(scaled * values, axis=-1, keepdims=True)
    return root * scaled - values * (root * root * root * inner), jnp.sum(
        grad * values * root, axis=0, keepdims=True
    )


def dot(a, b):
    return jnp.dot(a, b, preferred_element_type=f32)


def dot_across(a, b):
    return lax.dot_general(a, b, ACROSS, preferred_element_type=f32)


def selector(start, shape, axis):
    row = lax.broadcasted_iota(jnp.int32, shape, 1 - axis) + start
    return (row == lax.broadcasted_iota(jnp.int32, shape, axis)).astype(f32)


def spread(start, rows):
    pick = selector(start, (SEQUENCE_TOKENS, COMP), 0)
    return jnp.dot(pick, rows, preferred_element_type=f32, precision=lax.Precision.HIGHEST)


def dot_down(a, b):
    return lax.dot_general(a, b, (((0,), (0,)), ((), ())), preferred_element_type=f32)


def head_rows(ref_value, h):
    first = h * GROUP * HEAD_WIDTH
    return jnp.concatenate(
        [
            ref_value[:, first + g * HEAD_WIDTH : first + (g + 1) * HEAD_WIDTH]
            for g in range(GROUP)
        ],
        axis=0,
    )


def head_lanes(parts):
    return jnp.concatenate(
        [part[g * COMP : (g + 1) * COMP] for part in parts for g in range(GROUP)], axis=1
    )


def attend_kernel(
    start_ref, picked_ref, one_ref, two_ref, cos_ref, sin_ref, cos_rows, sin_rows,
    c_ref, resid_ref, probs_ref, query_ref, key_ref, value_ref, mixed_ref, normed_ref, gains_ref,
    embedded,
):
    start = start_ref[0]
    pick_rows = selector(start, (COMP, SEQUENCE_TOKENS), 1).astype(bf16)
    planes, _, columns = picked_ref.shape
    for p in range(planes):
        embedded[:, p * columns : (p + 1) * columns] = picked_ref[p].astype(f32)
    pick = lax.broadcasted_iota(jnp.int32, (8, 128), 0) + EXPERTS
    pick = (pick == lax.broadcasted_iota(jnp.int32, (8, 128), 1)).astype(f32).astype(bf16)
    gains = dot_across(pick, one_ref[:, HEAD_COLS + KEY_COLS :])
    gains_ref[...] = gains
    x = embedded[...]
    a = (x * inverse_root(x) * gains[0:1]).astype(bf16)
    normed_ref[...] = a
    a_rows = dot(pick_rows, a).astype(bf16)
    cosine, sine = cos_ref[...], sin_ref[...]
    query = turn(dot(a_rows, one_ref[:, :HEAD_COLS]), cos_rows[...], sin_rows[...])
    query = query.astype(bf16)
    key = turn(dot(a, one_ref[:, HEAD_COLS : HEAD_COLS + KEY_COLS]), cosine, sine).astype(bf16)
    value = dot(a, two_ref[:, :KEY_COLS]).astype(bf16)
    query_ref[...], key_ref[...], value_ref[...] = query, key, value
    rows = GROUP * COMP
    place = lax.rem(lax.broadcasted_iota(jnp.int32, (rows, SEQUENCE_TOKENS), 0), COMP) + start
    seen = place >= lax.broadcasted_iota(jnp.int32, (rows, SEQUENCE_TOKENS), 1)
    parts = []
    for h in range(KEY_VALUE_HEADS):
        lanes = slice(h * HEAD_WIDTH, (h + 1) * HEAD_WIDTH)
        scores = dot_across(head_rows(query, h), key[:, lanes]) * ROOT
        scores = jnp.where(seen, scores, -1000000000.0)
        expd = jnp.exp(scores - jnp.max(scores, axis=-1, keepdims=True))
        probs = expd / jnp.sum(expd, axis=-1, keepdims=True)
        probs_ref[h] = probs
        parts.append(dot(probs.astype(bf16), value[:, lanes]))
    mixed = head_lanes(parts).astype(bf16)
    mixed_ref[...] = mixed
    resid = dot(pick_rows, embedded[...].astype(bf16)) + dot(mixed, two_ref[:, KEY_COLS : KEY_COLS + D])
    resid_ref[...] = resid
    c_ref[...] = (resid * inverse_root(resid) * gains[1:2]).astype(bf16)


def attend(start, picked, one, two, *tables):
    vm = pl.BlockSpec(memory_space=pltpu.VMEM)
    rows = GROUP * COMP
    return pl.pallas_call(
        attend_kernel,
        in_specs=[pl.BlockSpec(memory_space=pltpu.SMEM)] + [vm] * 7,
        out_specs=[vm] * 9,
        out_shape=[
            jax.ShapeDtypeStruct((COMP, D), bf16),
            jax.ShapeDtypeStruct((COMP, D), f32),
            jax.ShapeDtypeStruct((KEY_VALUE_HEADS, rows, SEQUENCE_TOKENS), f32),
            jax.ShapeDtypeStruct((COMP, HEAD_COLS), bf16),
            jax.ShapeDtypeStruct((SEQUENCE_TOKENS, KEY_COLS), bf16),
            jax.ShapeDtypeStruct((SEQUENCE_TOKENS, KEY_COLS), bf16),
            jax.ShapeDtypeStruct((COMP, HEAD_COLS), bf16),
            jax.ShapeDtypeStruct((SEQUENCE_TOKENS, D), bf16),
            jax.ShapeDtypeStruct((8, D), f32),
        ],
        scratch_shapes=[pltpu.VMEM((SEQUENCE_TOKENS, D), f32)],
        compiler_params=pltpu.CompilerParams(vmem_limit_bytes=28 << 20),
        name="attend",
    )(start, picked, one, two, *tables)


def attend_back_kernel(
    start_ref, back_ref, gates_ref, grad_two_ref, gain_three_ref, c_ref, resid_ref, probs_ref, query_ref,
    key_ref, value_ref, mixed_ref, normed_ref, gains_ref, picked_ref, one_ref, two_ref, cos_ref, sin_ref, cos_rows, sin_rows,
    out_ref, grad_one_ref, grad_pack_ref,
    total,
):
    start = start_ref[0]
    planes, _, columns = picked_ref.shape
    gains = gains_ref[...]
    wide = HEAD_COLS + KEY_COLS
    gates = gates_ref[...]
    gate_grad = back_ref[:, D:]
    router_grad = gates * (gate_grad - jnp.sum(gates * gate_grad, axis=1, keepdims=True))
    router_grad = router_grad.astype(bf16)
    grad = back_ref[:, :D] + dot_across(router_grad, one_ref[:, wide:])
    grad_resid, gain_two = norm_back(resid_ref[...], gains[1:2], grad)
    grad_resid = grad_resid + grad_two_ref[...]
    branch = grad_resid.astype(bf16)
    grad_mixed = dot_across(branch, two_ref[:, KEY_COLS : KEY_COLS + D]).astype(bf16)
    query, key, value = query_ref[...], key_ref[...], value_ref[...]
    query_parts, key_parts, value_parts = [], [], []
    for h in range(KEY_VALUE_HEADS):
        lanes = slice(h * HEAD_WIDTH, (h + 1) * HEAD_WIDTH)
        probs = probs_ref[h]
        grad_head = head_rows(grad_mixed, h)
        grad_probs = dot_across(grad_head, value[:, lanes]).astype(bf16).astype(f32)
        inner = jnp.sum(grad_probs * probs, axis=-1, keepdims=True)
        grad_scores = probs * (grad_probs - inner)
        value_parts.append(dot_down(probs.astype(bf16), grad_head))
        query_parts.append(dot(grad_scores.astype(bf16), key[:, lanes]) * ROOT)
        key_parts.append(dot_down(grad_scores.astype(bf16), head_rows(query, h)) * ROOT)
    grad_query = turn(head_lanes(query_parts), cos_rows[...], -sin_rows[...]).astype(bf16)
    grad_key = jnp.concatenate(key_parts, axis=1)
    grad_key = turn(grad_key, cos_ref[...], -sin_ref[...]).astype(bf16)
    grad_value = jnp.concatenate(value_parts, axis=1).astype(bf16)
    grad_normed = dot_across(grad_key, one_ref[:, HEAD_COLS:wide])
    grad_normed += dot_across(grad_value, two_ref[:, :KEY_COLS])
    grad_normed += spread(start, dot_across(grad_query, one_ref[:, :HEAD_COLS]))
    for p in range(planes):
        total[:, p * columns : (p + 1) * columns] = picked_ref[p].astype(f32)
    grad_embedded, gain_one = norm_back(total[...], gains[0:1], grad_normed)
    total[...] = grad_embedded + spread(start, grad_resid)
    for p in range(planes):
        out_ref[p] = total[:, p * columns : (p + 1) * columns].astype(bf16)
    pick_rows = selector(start, (COMP, SEQUENCE_TOKENS), 1).astype(bf16)
    a_rows = dot(pick_rows, normed_ref[...])
    turned = normed_ref[...]
    grad_one_ref[:, HEAD_COLS:wide] = dot_down(turned, grad_key).astype(bf16)
    grad_pack_ref[:, :KEY_COLS] = dot_down(turned, grad_value).astype(bf16)
    grad_one_ref[:, :HEAD_COLS] = dot_down(a_rows.astype(bf16), grad_query).astype(bf16)
    grad_pack_ref[:, KEY_COLS : KEY_COLS + D] = dot_down(mixed_ref[...], branch).astype(bf16)
    left = jnp.concatenate(
        [c_ref[...].astype(f32), gain_one, gain_two, gain_three_ref[...], jnp.zeros((5, D), f32)],
        axis=0,
    )
    lane = lax.broadcasted_iota(jnp.int32, (8, 128), 0) + EXPERTS
    lane = (lane == lax.broadcasted_iota(jnp.int32, (8, 128), 1)).astype(f32)
    right = jnp.concatenate([router_grad.astype(f32), lane], axis=0).astype(bf16)
    grad_one_ref[:, wide:] = dot_down(left.astype(bf16), right).astype(bf16)


def attend_back(start, *operands):
    vm = pl.BlockSpec(memory_space=pltpu.VMEM)
    picked = operands[13]
    return pl.pallas_call(
        attend_back_kernel,
        in_specs=[pl.BlockSpec(memory_space=pltpu.SMEM)] + [vm] * len(operands),
        out_specs=[vm] * 3,
        out_shape=[
            jax.ShapeDtypeStruct(picked.shape, bf16),
            jax.ShapeDtypeStruct((D, PACK), bf16),
            jax.ShapeDtypeStruct((D, PACK_TWO), bf16),
        ],
        scratch_shapes=[pltpu.VMEM((SEQUENCE_TOKENS, D), f32)],
        compiler_params=pltpu.CompilerParams(vmem_limit_bytes=44 << 20),
        name="attend_back",
    )(start, *operands)


def lamb_update(weight, moment_one, moment_two, scale_one, scale_two):
    square = moment_two * scale_two
    return (moment_one * scale_one) / (square * lax.rsqrt(square) + EPSILON) + DECAY * weight


def lamb_parts(weight, moment_one, moment_two, gradient, scales):
    moment_one = RATE_ONE * moment_one + (1.0 - RATE_ONE) * gradient
    moment_two = RATE_TWO * moment_two + (1.0 - RATE_TWO) * gradient * gradient
    return (moment_one, moment_two, lamb_update(weight, moment_one, moment_two, *scales))


STEPS = 4
TOGETHER = 4


def row_lists(tokens, base, rows):
    inside = (tokens >= base) & (tokens < base + rows)
    count = jnp.sum(inside.astype(jnp.int32), axis=1)
    place = jnp.arange(SEQUENCE_TOKENS, dtype=jnp.int32)
    before = (place[:, None] < place[None, :]).astype(bf16)
    rank = jnp.dot(inside.astype(bf16), before, preferred_element_type=f32).astype(jnp.int32)
    packed = place[None, :] * 65536 + (tokens - base)
    hit = inside[:, :, None] & (rank[:, :, None] == place[None, None, :])
    entry = jnp.sum(jnp.where(hit, packed[:, :, None], 0), axis=1)
    empty = SEQUENCE_TOKENS * 65536
    return jnp.where(place[None, :] < count[:, None], entry, empty), count


def gather_kernel(list_ref, count_ref, table_ref, out_ref, table_out, rows_ref):
    part = table_out.shape[0]
    here = pl.ds(pl.multiple_of(pl.program_id(0) * part, 16), part)
    table_out[...] = table_ref[here, :].astype(bf16)
    for n in range(TOGETHER):
        b = pl.program_id(0) * TOGETHER + n
        rows_ref[n] = jnp.zeros(rows_ref.shape[1:], f32)

        def step(k, carry, n=n, b=b):
            for j in range(STEPS):
                entry = list_ref[b, k * STEPS + j]
                rows_ref[n, pl.ds(entry >> 16, 1), :] = table_ref[pl.ds(entry & 65535, 1), :]
            return carry

        lax.fori_loop(0, (count_ref[b] + STEPS - 1) // STEPS, step, 0)
        out_ref[n] = rows_ref[n, :SEQUENCE_TOKENS].astype(bf16)


def gather_rows(lists, counts, table):
    blocks = lists.shape[0]
    rows, columns = table.shape
    return pl.pallas_call(
        gather_kernel,
        grid_spec=pltpu.PrefetchScalarGridSpec(
            num_scalar_prefetch=2,
            grid=(blocks // TOGETHER,),
            in_specs=[pl.BlockSpec((rows, columns), lambda b, *_: (0, 0))],
            out_specs=[
                pl.BlockSpec((TOGETHER, SEQUENCE_TOKENS, columns), lambda b, *_: (b, 0, 0)),
                pl.BlockSpec((rows * TOGETHER // blocks, columns), lambda b, *_: (b, 0)),
            ],
            scratch_shapes=[pltpu.VMEM((TOGETHER, SEQUENCE_TOKENS + 8, columns), f32)],
        ),
        out_shape=[
            jax.ShapeDtypeStruct((blocks, SEQUENCE_TOKENS, columns), bf16),
            jax.ShapeDtypeStruct((rows, columns), bf16),
        ],
        compiler_params=pltpu.CompilerParams(vmem_limit_bytes=26 << 20),
        name="gather_rows",
    )(lists, counts, table)


TABLE_PARTS = 8


def norm_cells(row, weight_sum, update_sum):
    rows = lax.broadcasted_iota(jnp.int32, (8, 128), 0)
    lanes = lax.broadcasted_iota(jnp.int32, (8, 128), 1)
    block = jnp.where(lanes == 0, weight_sum, jnp.where(lanes == 1, update_sum, 0.0))
    return jnp.where(rows == row, block, 0.0)


def total_of(values):
    return jnp.sum(jnp.sum(values, axis=1, keepdims=True), axis=0, keepdims=True)


def fold(values):
    return jnp.sum(values.reshape(-1, 8, values.shape[1]), axis=0)


def table_kernel(
    list_ref, count_ref, scale_ref, grad_ref, head_ref, w_in, first_in, second_in,
    new_first, new_second, updates, norms,
    rows_ref, acc, w, first, second, sums, sems,
):
    b = pl.program_id(0)
    blocks = pl.num_programs(0) - TABLE_PARTS
    loads = [
        pltpu.make_async_copy(src, dst, sems.at[n])
        for n, (src, dst) in enumerate([(w_in, w), (first_in, first), (second_in, second)])
    ]

    @pl.when(b == 0)
    def _():
        for load in loads:
            load.start()
        acc[...] = head_ref[...].astype(f32)
        sums[...] = jnp.zeros_like(sums)

    @pl.when(b < blocks)
    def _():
        for n in range(TOGETHER):
            rows_ref[n, :SEQUENCE_TOKENS] = grad_ref[n].astype(f32)
            rows_ref[n, SEQUENCE_TOKENS:] = jnp.zeros((8, rows_ref.shape[2]), f32)
            own = b * TOGETHER + n

            def step(k, carry, n=n, own=own):
                entries = [list_ref[own, k * STEPS + j] for j in range(STEPS)]
                spots = [entry & 65535 for entry in entries]
                grads = [rows_ref[n, pl.ds(entry >> 16, 1), :] for entry in entries]
                olds = [acc[pl.ds(spot, 1), :] for spot in spots]
                for j in range(STEPS):
                    total = olds[j] + grads[j]
                    for i in range(j):
                        total += jnp.where(spots[i] == spots[j], grads[i], 0.0)
                    acc[pl.ds(spots[j], 1), :] = total
                return carry

            lax.fori_loop(0, (count_ref[own] + STEPS - 1) // STEPS, step, 0)

    @pl.when(b == blocks)
    def _():
        for load in loads:
            load.wait()

    @pl.when(b >= blocks)
    def _():
        size = new_first.shape[0]
        here = pl.ds(pl.multiple_of((b - blocks) * size, 8), size)
        one, two, update = lamb_parts(
            w[here, :], first[here, :], second[here, :], acc[here, :], (scale_ref[0], scale_ref[1])
        )
        new_first[...] = one
        new_second[...] = two
        updates[...] = update
        sums[0] += fold(w[here, :] * w[here, :])
        sums[1] += fold(update * update)

    @pl.when(b == blocks + TABLE_PARTS - 1)
    def _():
        norms[...] = norm_cells(0, total_of(sums[0]), total_of(sums[1]))


def table_moments(lists, counts, scales, grads, head, weight, first, second):
    blocks = lists.shape[0] // TOGETHER
    rows, columns = weight.shape
    part = rows // TABLE_PARTS
    out = pl.BlockSpec((part, columns), lambda b, *_: (jnp.maximum(b - blocks, 0), 0))
    return pl.pallas_call(
        table_kernel,
        grid_spec=pltpu.PrefetchScalarGridSpec(
            num_scalar_prefetch=3,
            grid=(blocks + TABLE_PARTS,),
            in_specs=[
                pl.BlockSpec(
                    (TOGETHER, SEQUENCE_TOKENS, columns),
                    lambda b, *_: (jnp.minimum(b, blocks - 1), 0, 0),
                ),
                pl.BlockSpec(
                    (rows, columns), lambda b, *_: (0, 0), pipeline_mode=pl.Buffered(1)
                ),
            ]
            + [pl.BlockSpec(memory_space=pl.ANY)] * 3,
            out_specs=[out, out, out, pl.BlockSpec((8, 128), lambda b, *_: (0, 0))],
            scratch_shapes=[pltpu.VMEM((TOGETHER, SEQUENCE_TOKENS + 8, columns), f32)]
            + [pltpu.VMEM((rows, columns), f32)] * 4
            + [pltpu.VMEM((2, 8, columns), f32), pltpu.SemaphoreType.DMA((3,))],
        ),
        out_shape=[jax.ShapeDtypeStruct((rows, columns), f32)] * 3
        + [jax.ShapeDtypeStruct((8, 128), f32)],
        compiler_params=pltpu.CompilerParams(vmem_limit_bytes=58 << 20),
        name="table_moments",
    )(lists, counts, scales, grads, head, weight, first, second)


def small_kernel(
    scale_ref, grad_ref, qkv, qkv_one, qkv_two, out, out_one, out_two, router, router_one, router_two,
    gains, gains_one, gains_two, *results
):
    scales = (scale_ref[0], scale_ref[1])
    planes = grad_ref.shape[0]
    total = grad_ref[0].astype(f32)
    for z in range(1, planes):
        total += grad_ref[z].astype(f32)
    packs = (total[:, :PACK], total[:, PACK:])
    wide = HEAD_COLS + KEY_COLS
    pick = lax.broadcasted_iota(jnp.int32, (8, 128), 0) + EXPERTS
    pick = (pick == lax.broadcasted_iota(jnp.int32, (8, 128), 1)).astype(f32)
    gains_grad = lax.dot_general(
        pick,
        packs[0][:, wide:],
        ACROSS,
        preferred_element_type=f32,
        precision=lax.Precision.HIGHEST,
    )[:3]
    block = jnp.zeros((8, 128), f32)
    sets = [
        (qkv, qkv_one, qkv_two, jnp.concatenate([packs[0][:, :wide], packs[1][:, :KEY_COLS]], axis=1)),
        (out, out_one, out_two, packs[1][:, KEY_COLS : KEY_COLS + D]),
        (router, router_one, router_two, packs[0][:, wide : wide + EXPERTS]),
        (gains, gains_one, gains_two, gains_grad),
    ]
    for n, (weight, first, second, grad) in enumerate(sets):
        one, two, update = lamb_parts(weight[...], first[...], second[...], grad, scales)
        results[3 * n][...] = one
        results[3 * n + 1][...] = two
        results[3 * n + 2][...] = update
        block += norm_cells(n + 1, total_of(weight[...] * weight[...]), total_of(update * update))
    results[12][...] = block


def small_moments(scales, sums, *state):
    vm = pl.BlockSpec(memory_space=pltpu.VMEM)
    return pl.pallas_call(
        small_kernel,
        in_specs=[pl.BlockSpec(memory_space=pltpu.SMEM)] + [vm] * (1 + len(state)),
        out_specs=[vm] * 13,
        out_shape=[jax.ShapeDtypeStruct(x.shape, f32) for x in state[::3] for _ in range(3)]
        + [jax.ShapeDtypeStruct((8, 128), f32)],
        compiler_params=pltpu.CompilerParams(vmem_limit_bytes=62 << 20),
        name="small_moments",
    )(scales, sums, *state)


FINISH_PARTS = 8


def finish_kernel(norms_ref, *refs):
    norms = jnp.sqrt(jnp.sum(norms_ref[...], axis=0))
    count = len(refs) // 3

    def apply(n, row):
        ratio = norms[row : row + 1, 0:1] / norms[row : row + 1, 1:2]
        refs[2 * count + n][...] = refs[2 * n][...] - (STEP_RATE * ratio) * refs[2 * n + 1][...]

    apply(0, 0)
    apply(1, 5)
    apply(2, 6)

    @pl.when(pl.program_id(0) == 0)
    def _():
        apply(3, 1)
        apply(4, 2)


def finish(norms, *state):
    weights = state[::2]

    def spec(n):
        rows, columns = weights[n].shape
        if n < 3:
            return pl.BlockSpec((rows // FINISH_PARTS, columns), lambda i: (i, 0))
        return pl.BlockSpec((rows, columns), lambda i: (0, 0))

    return pl.pallas_call(
        finish_kernel,
        grid=(FINISH_PARTS,),
        in_specs=[pl.BlockSpec(norms.shape, lambda i: (0, 0, 0))]
        + [spec(n) for n in range(5) for _ in range(2)],
        out_specs=[spec(n) for n in range(5)],
        out_shape=[jax.ShapeDtypeStruct(x.shape, f32) for x in weights],
        compiler_params=pltpu.CompilerParams(vmem_limit_bytes=62 << 20),
        name="finish",
    )(norms, *state)


def on_device(
    token_ids,
    positions,
    pair_index,
    ref_logps,
    routes,
    step_count,
    embed_table,
    embed_first,
    embed_second,
    qkv_weight,
    qkv_first,
    qkv_second,
    out_weight,
    out_first,
    out_second,
    router_weight,
    router_first,
    router_second,
    norm_gains,
    gains_first,
    gains_second,
    in_weight,
    in_first,
    in_second,
    down_weight,
    down_first,
    down_second,
):
    shard_id = lax.axis_index("shard")
    expert_id = lax.axis_index("expert")
    shards = lax.axis_size("shard")
    planes = lax.axis_size("expert")
    devices = shards * planes
    vocab_rows, columns = embed_table.shape
    vocab_base = shard_id * vocab_rows
    own_rows = vocab_rows // planes
    local_experts = in_weight.shape[0]
    hidden_units = in_weight.shape[3]
    head_cols = QUERY_HEADS * HEAD_WIDTH
    key_cols = KEY_VALUE_HEADS * HEAD_WIDTH
    rows_all = devices * COMP

    side = math.isqrt(shards // 2)
    grid = (planes, side, side, 2)
    together = devices <= 32

    def send(parts, ident):
        if together:
            return communicate(parts, ident)
        return [
            out for n, part in enumerate(parts) for out in communicate([part], ident + 20 * n)
        ]

    unit = own_rows // 24

    def swap(x, *turns, back=False, held=None):
        turns = [(start * unit, size * unit, rounds) for start, size, rounds in turns]
        return Swap(x, turns, planes, side, back, held)

    def gather_part(rows):
        return Gather([rows], split(0, COMP, rows.shape[1], 2, 2), planes, side)

    def reduce_part(rows, cuts):
        width = rows.shape[1]
        rows = rows.reshape(grid + (COMP, width))
        edges = [width * n // (128 * cuts) * 128 for n in range(cuts + 1)]
        groups = [
            [
                (0, slice(i * COMP // 2, (i + 1) * COMP // 2), slice(low, high), i == 0)
                for i in range(2)
            ]
            for low, high in zip(edges, edges[1:])
        ]
        return Reduce([rows], groups, planes, side)

    def chain(rows, extra, extra_out, middle, beside, ident):
        gather = gather_part(jax.ShapeDtypeStruct((COMP, D), bf16))
        part = Chain(reduce_part(rows, 2), extra, extra_out, middle, gather)
        out = communicate([part, beside], ident)
        return (out[0].reshape(rows_all, D), *out[1:])

    def gather_tiny(block, ident):
        return communicate([Tiny(block, planes, side)], ident)[0].reshape((devices,) + block.shape)

    weight_rows = qkv_weight.shape[0]
    cuts = 3 if weight_rows % 48 == 0 else 1
    widths = (PACK, PACK_TWO)
    weight_groups = [
        [
            (i, slice(n * (weight_rows // cuts), (n + 1) * (weight_rows // cuts)), slice(0, width), i == 0)
            for i, width in enumerate(widths)
        ]
        for n in range(cuts)
    ]
    embed_groups = split(0, SEQUENCE_TOKENS, columns, 4, 1)

    own_places = lax.dynamic_index_in_dim(positions, shard_id, 0, keepdims=False)
    start = own_places[0]
    own_tokens = lax.dynamic_slice_in_dim(token_ids, shard_id * SEQUENCE_TOKENS, SEQUENCE_TOKENS, 0)
    own_routes = lax.dynamic_slice_in_dim(routes, start, COMP, 0)
    sheet = jnp.concatenate(
        [
            own_tokens,
            own_routes.reshape(-1),
            own_places,
            jnp.zeros((1024 - SEQUENCE_TOKENS - COMP * TOP - COMP,), jnp.int32),
        ]
    )
    sheets = gather_tiny(sheet.reshape(8, 128), 0).reshape(devices, 1024)
    tokens_all = sheets[:, :SEQUENCE_TOKENS]
    routes_all = sheets[:, SEQUENCE_TOKENS : SEQUENCE_TOKENS + COMP * TOP].reshape(rows_all, TOP)
    places_all = sheets[:, SEQUENCE_TOKENS + COMP * TOP : SEQUENCE_TOKENS + COMP * TOP + COMP]
    spots = jnp.arange(SEQUENCE_TOKENS, dtype=jnp.int32)
    targets = jnp.sum(
        jnp.where(
            places_all[:, :, None] + 1 == spots[None, None, :], tokens_all[:, None, :], 0
        ),
        axis=2,
    ).reshape(-1)

    lists, counts = row_lists(tokens_all, vocab_base, vocab_rows)
    picked, table_b = gather_rows(lists, counts, embed_table)
    picked = picked.reshape(grid + (SEQUENCE_TOKENS, columns))
    packs = jnp.concatenate(
        [
            qkv_weight[:, : head_cols + key_cols],
            router_weight,
            norm_gains.T,
            jnp.zeros((weight_rows, 128 - EXPERTS - 3), f32),
            qkv_weight[:, head_cols + key_cols :],
            out_weight,
        ],
        axis=1,
    ).astype(bf16)
    packs, sheets = lax.optimization_barrier((packs, sheets))
    packs = lax.all_to_all(
        jnp.broadcast_to(packs[None], (planes,) + packs.shape),
        "expert",
        split_axis=0,
        concat_axis=0,
        tiled=True,
    )
    first_pack, second_pack, picked, table_own = send(
        [
            Gather([packs], weight_groups, planes, side, prior=widths),
            Reduce([picked], embed_groups, planes, side, exchange=True),
            swap(table_b, (0, 16, 0)),
        ],
        1,
    )
    first_pack = first_pack.reshape(D, PACK)
    second_pack = second_pack.reshape(D, PACK_TWO)

    start_at = start.reshape(1)
    tables = rotary_tables()
    tables += tuple(lax.dynamic_slice_in_dim(table, start, COMP, 0) for table in tables)
    normed_two_b, resid, probs, query, key, value, attended, normed_b, gains = attend(
        start_at, picked, first_pack, second_pack, *tables
    )

    expert_rows, table_own = communicate(
        [gather_part(normed_two_b), swap(table_b, (16, 2, 2), held=table_own)], 2
    )
    expert_rows = expert_rows.reshape(rows_all, D)
    lanes = shard_id * local_experts + jnp.arange(local_experts, dtype=jnp.int32)
    in_rows = in_weight.reshape(-1, hidden_units)
    produced, mid, gates, in_cat, down_b, gated_hidden = experts_forward(
        lanes, expert_rows, routes_all, first_pack, in_rows, down_weight
    )
    own_index = expert_id * shards + shard_id
    own_gates = lax.dynamic_slice(gates, (own_index * COMP, 0), (COMP, 128))
    row_block = jax.ShapeDtypeStruct((COMP, D), f32)
    head_rows, resid_two, table_own = chain(
        produced,
        [resid, gains],
        [row_block],
        final_norm,
        swap(table_b, (18, 3, 0), (21, 3, 8), held=table_own),
        3,
    )

    logits = jnp.einsum("rd,vd->rv", head_rows, table_own, preferred_element_type=f32) / LOGIT_SCALE
    own_base = vocab_base + expert_id * own_rows
    target_hot = targets[:, None] == own_base + jnp.arange(own_rows, dtype=jnp.int32)[None, :]
    row_top = jnp.max(logits, axis=1)
    row_total = jnp.sum(jnp.exp(logits - row_top[:, None]), axis=1)
    row_hit = jnp.sum(jnp.where(target_hot, logits, 0.0), axis=1)
    stats = jnp.stack([row_top, row_total, row_hit]).reshape(8, 3 * rows_all // 8)
    stats = gather_tiny(stats, 5).reshape(devices, 3, rows_all)
    top_all = jnp.max(stats[:, 0], axis=0)
    total_all = jnp.sum(stats[:, 1] * jnp.exp(stats[:, 0] - top_all[None]), axis=0)
    row_lse = top_all + jnp.log(total_all)
    seq_sums = jnp.sum((jnp.sum(stats[:, 2], axis=0) - row_lse).reshape(-1, COMP), axis=1)

    sequences = jnp.arange(devices, dtype=jnp.int32)[None, :]
    pair_sign = (pair_index[:, :1] == sequences).astype(f32) - (
        pair_index[:, 1:] == sequences
    ).astype(f32)
    scaled = BETA * jnp.sum(pair_sign * (seq_sums - ref_logps)[None, :], axis=1)
    loss_value = -jnp.mean(jax.nn.log_sigmoid(scaled))
    pair_grad = jax.nn.sigmoid(-scaled) * (-BETA / scaled.shape[0])
    seq_grad = jnp.sum(pair_sign * pair_grad[:, None], axis=0)
    row_grad = jnp.repeat(seq_grad, COMP)
    grad_logits = (
        row_grad[:, None] * (target_hot.astype(f32) - jnp.exp(logits - row_lse[:, None]))
    ).astype(bf16)
    grad_logits = lax.optimization_barrier(grad_logits)
    grad_rows = jnp.dot(grad_logits, table_own, preferred_element_type=f32) / LOGIT_SCALE
    head_grad = (
        jnp.einsum("rv,rd->vd", grad_logits, head_rows, preferred_element_type=f32) / LOGIT_SCALE
    ).astype(bf16)
    grad_all, grad_resid_two, grad_gain_three, head_back = chain(
        grad_rows.astype(bf16),
        [resid_two, gains],
        [row_block, jax.ShapeDtypeStruct((1, D), f32)],
        final_norm_back,
        swap(head_grad, (0, 3, 0), (3, 3, 8), back=True),
        6,
    )

    back, mid_grad = experts_backward(lanes, grad_all, mid, gates, in_cat, down_b)
    back, head_back = communicate(
        [reduce_part(back, 2), swap(head_grad, (6, 3, 0), back=True, held=head_back)], 8
    )

    grad_embedded, *grad_packs = attend_back(
        start_at,
        back,
        own_gates,
        grad_resid_two,
        grad_gain_three,
        normed_two_b,
        resid,
        probs,
        query,
        key,
        value,
        attended,
        normed_b,
        gains,
        picked,
        first_pack,
        second_pack,
        *tables,
    )
    grad_packs = [pack.reshape(grid + (weight_rows, pack.shape[1])) for pack in grad_packs]
    wide = head_cols + key_cols
    plane_sums, sent, head_back = send(
        [
            Reduce(grad_packs, weight_groups, planes, side, partial=True),
            Gather([grad_embedded], embed_groups, planes, side, exchange=True),
            swap(head_grad, (9, 5, 1), (14, 5, 2), (19, 5, 3), back=True, held=head_back),
        ],
        9,
    )
    plane_sums = lax.all_to_all(
        plane_sums, "expert", split_axis=0, concat_axis=0, tiled=True
    )

    step_value = step_count.astype(f32)
    scales = jnp.stack([1.0 / (1.0 - RATE_ONE**step_value), 1.0 / (1.0 - RATE_TWO**step_value)])
    grad_in = jnp.einsum("td,tk->dk", expert_rows, mid_grad, preferred_element_type=f32)
    grad_down = jnp.einsum("tk,td->kd", gated_hidden, grad_all, preferred_element_type=f32)
    down_rows = down_weight.reshape(-1, D)
    table_one, table_two, table_update, table_norms = table_moments(
        lists,
        counts,
        scales,
        sent.reshape(devices, SEQUENCE_TOKENS, columns),
        head_back.reshape(vocab_rows, columns),
        embed_table,
        embed_first,
        embed_second,
    )
    *small, small_norms = small_moments(
        scales,
        plane_sums,
        qkv_weight,
        qkv_first,
        qkv_second,
        out_weight,
        out_first,
        out_second,
        router_weight,
        router_first,
        router_second,
        norm_gains,
        gains_first,
        gains_second,
    )
    in_one, in_two, in_update, down_one, down_two, down_update, expert_norms = expert_moments(
        scales,
        table_norms + small_norms,
        grad_in,
        in_rows,
        in_first.reshape(in_rows.shape),
        in_second.reshape(in_rows.shape),
        grad_down,
        down_rows,
        down_first.reshape(down_rows.shape),
        down_second.reshape(down_rows.shape),
    )
    norm_blocks = gather_tiny(expert_norms, 10)
    norm_values = jnp.sqrt(jnp.sum(norm_blocks, axis=0))[:7, :2]
    trust_ratio = norm_values[:, 0] / norm_values[:, 1]
    new_table, new_in, new_down, new_qkv, new_out = finish(
        norm_blocks,
        embed_table,
        table_update,
        in_rows,
        in_update,
        down_rows,
        down_update,
        qkv_weight,
        small[2],
        out_weight,
        small[5],
    )
    new_router = router_weight - STEP_RATE * trust_ratio[3] * small[8]
    new_gains = norm_gains - STEP_RATE * trust_ratio[4] * small[11]
    stats = jnp.stack([norm_values[:, 0], norm_values[:, 1], trust_ratio], axis=1)
    return (
        loss_value,
        new_table,
        table_one,
        table_two,
        new_qkv,
        small[0],
        small[1],
        new_out,
        small[3],
        small[4],
        new_router,
        small[6],
        small[7],
        new_gains,
        small[9],
        small[10],
        new_in.reshape(in_weight.shape),
        in_one.reshape(in_weight.shape),
        in_two.reshape(in_weight.shape),
        new_down.reshape(down_weight.shape),
        down_one.reshape(down_weight.shape),
        down_two.reshape(down_weight.shape),
        stats,
    )


def solution(mesh):
    rows = P(BOTH, None)
    vocab = P("shard", "expert")
    gains = P(None, BOTH)
    inner = P("shard", None, None, "expert")
    outer = P("shard", "expert", None)
    state = (vocab,) * 3 + (rows,) * 9 + (gains,) * 3 + (inner,) * 3 + (outer,) * 3
    return jax.shard_map(
        on_device,
        mesh=mesh,
        in_specs=(P("expert"), P("expert", None), P(), P(), rows, P()) + state,
        out_specs=(P(),) + state + (P(),),
        check_vma=False,
    )
```

```python
import functools
import math

import jax
import jax.numpy as jnp
from jax import lax
from jax.experimental import pallas as pl
from jax.experimental.pallas import tpu as pltpu
from jax.sharding import PartitionSpec as P

D = 1536
QUERY_HEADS = 24
KEY_VALUE_HEADS = 8
GROUP = QUERY_HEADS // KEY_VALUE_HEADS
HEAD_WIDTH = 64
TOP = 8
EXPERTS = 32
SEQUENCE_TOKENS = 256
COMP = 32
QKV = 2560

BETA = 0.1
LOGIT_SCALE = 6.0
RATE_ONE = 0.9
RATE_TWO = 0.999
EPSILON = 1e-06
DECAY = 0.01
STEP_RATE = 0.3

BOTH = ("expert", "shard")
bf16 = jnp.bfloat16
f32 = jnp.float32


MESH = pl.DeviceIdType.MESH


class Spot:
    def __init__(self, planes, side):
        self.planes, self.side = planes, side
        self.z = lax.axis_index("expert")
        self.shard = lax.axis_index("shard")
        self.core = lax.rem(self.shard, 2)
        self.b = lax.rem(lax.div(self.shard, 2), side)
        self.a = lax.div(self.shard, 2 * side)

    def plane(self, k):
        z = lax.rem(self.z + k, self.planes)
        return z, (z, self.shard)

    def along_a(self, k):
        a = lax.rem(self.a + k, self.side)
        return a, (self.z, (a * self.side + self.b) * 2 + self.core)

    def along_b(self, k):
        b = lax.rem(self.b + k, self.side)
        return b, (self.z, (self.a * self.side + b) * 2 + self.core)

    def along(self, first, k):
        return self.along_a(k) if first else self.along_b(k)

    def mate(self):
        other = 1 - self.core
        return other, (self.z, (self.a * self.side + self.b) * 2 + other)

    def near(self, k):
        return self.z, lax.rem(self.shard + k, 2 * self.side * self.side)

    def greet(self, flat):
        targets = [self.plane(k)[1] for k in range(1, self.planes)]
        if flat:
            targets += [self.near(k) for k in range(1, 2 * self.side * self.side)]
        else:
            targets.append(self.mate()[1])
            for k in range(1, self.side):
                targets += [self.along_a(k)[1], self.along_b(k)[1]]
        barrier = pltpu.get_barrier_semaphore()
        for target in targets:
            pl.semaphore_signal(barrier, inc=1, device_id=target, device_id_type=MESH)
        pl.semaphore_wait(barrier, len(targets))


class Mail:
    def __init__(self, send, recv):
        self.send, self.recv, self.count, self.open = send, recv, 0, []

    def start(self, src, dst, target):
        copy = pltpu.make_async_remote_copy(
            src_ref=src,
            dst_ref=dst,
            send_sem=self.send.at[self.count],
            recv_sem=self.recv.at[self.count],
            device_id=target,
            device_id_type=MESH,
        )
        self.count += 1
        copy.start()
        self.open.append(copy)
        return copy

    def finish(self):
        for copy in self.open:
            copy.wait_send()


def arrive(copies):
    for copy in copies:
        copy.wait_recv()


class Tiny:
    flat = True
    scratch = ()

    def __init__(self, x, planes, side):
        self.planes, self.side, self.inputs = planes, side, [x]
        shape = (planes, 2 * side * side) + x.shape
        self.outputs = [jax.ShapeDtypeStruct(shape, x.dtype)]
        self.copies = planes + 2 * side * side - 2

    def steps(self, spot, mail, x, out):
        out[spot.z, spot.shard] = x[...]
        sent = []
        for k in range(1, self.planes):
            sent.append(mail.start(x, out.at[spot.z, spot.shard], spot.plane(k)[1]))
        yield
        arrive(sent)
        part = out.at[:, spot.shard]
        yield
        arrive([mail.start(part, part, spot.near(k)) for k in range(1, 2 * self.side**2)])


def split(array, rows, columns, row_parts, column_parts):
    r, c = rows // row_parts, columns // column_parts
    cuts = [
        (array, slice(i * r, i * r + r), slice(j * c, j * c + c))
        for j in range(column_parts)
        for i in range(row_parts)
    ]
    cuts = [cut + (n % 2 == 0,) for n, cut in enumerate(cuts)]
    return [cuts[n : n + 2] for n in range(0, len(cuts), 2)]


def pipeline(groups, stage, last):
    sent = [[[] for _ in group] for group in groups]
    for tick in range(len(groups) + last):
        for step in range(last, -1, -1):
            turn = tick - step
            if 0 <= turn < len(groups):
                for n, cut in enumerate(groups[turn]):
                    for copy in sent[turn][n]:
                        copy.wait_recv()
                    sent[turn][n] = stage(step, (turn, n), cut)
        yield


class Gather:
    flat = False
    scratch = ()

    def __init__(self, xs, groups, planes, side, exchange=False, prior=None):
        self.planes, self.side, self.inputs, self.groups = planes, side, xs, groups
        self.exchange, self.prior = exchange, prior
        grid = (planes, side, side, 2)
        shapes = [x.shape[-2:] for x in xs]
        if prior:
            shapes = [xs[0].shape[-2:-1] + (width,) for width in prior]
        self.outputs = [jax.ShapeDtypeStruct(grid + shape, xs[0].dtype) for shape in shapes]
        self.copies = sum(map(len, groups)) * (planes - 1 + 2 * (side - 1) + 1)

    def steps(self, spot, mail, *refs):
        xs, outs = refs[: len(self.inputs)], refs[len(self.inputs) :]
        z, a, b, core = spot.z, spot.a, spot.b, spot.core
        if self.prior:
            low = 0
            for width, out in zip(self.prior, outs):
                out[:, a, b, core] = xs[0][:, :, low : low + width]
                low += width
            xs = [None] * len(outs)
        else:
            for x, out in zip(xs, outs):
                out[z, a, b, core] = x[z] if self.exchange else x[...]

        def stage(step, key, cut):
            i, rows, columns, first = cut
            x, out = xs[i], outs[i]
            if step == 0 and self.prior:
                return []
            if step == 0:
                place = out.at[z, a, b, core, rows, columns]
                sent = []
                for k in range(1, self.planes):
                    peer, target = spot.plane(k)
                    own = x.at[peer, rows, columns] if self.exchange else x.at[rows, columns]
                    sent.append(mail.start(own, place, target))
                return sent
            if step in (1, 2):
                if step == 1:
                    part = out.at[:, a, b, core, rows, columns]
                elif first:
                    part = out.at[:, :, b, core, rows, columns]
                else:
                    part = out.at[:, a, :, core, rows, columns]
                return [
                    mail.start(part, part, spot.along(first == (step == 1), k)[1])
                    for k in range(1, self.side)
                ]
            if step == 3:
                part = out.at[:, :, :, core, rows, columns]
                return [mail.start(part, part, spot.mate()[1])]
            return []

        return pipeline(self.groups, stage, 4)


class Reduce:
    flat = False

    def __init__(self, xs, groups, planes, side, exchange=False, partial=False):
        self.planes, self.side, self.inputs, self.groups = planes, side, xs, groups
        self.exchange, self.partial = exchange or partial, partial
        self.outputs = [
            jax.ShapeDtypeStruct((planes,) + x.shape[-2:], x.dtype)
            if self.exchange
            else jax.ShapeDtypeStruct(x.shape[-2:], f32)
            for x in xs
        ]
        if partial:
            shape = (planes, xs[0].shape[-2], sum(x.shape[-1] for x in xs))
            self.outputs = [jax.ShapeDtypeStruct(shape, xs[0].dtype)]
        self.scratch = []
        for i, rows, columns, _ in [cut for group in groups for cut in group]:
            block = (rows.stop - rows.start, columns.stop - columns.start)
            self.scratch += [
                pltpu.VMEM(shape + block, xs[i].dtype)
                for shape in (
                    (planes, side, side),
                    (side - 1, planes, side),
                    (planes, side),
                    (side - 1, planes),
                    (planes,),
                )
                + (() if self.exchange else ((planes - 1,),))
            ]
        self.copies = sum(map(len, groups)) * (planes - 1 + 2 * (side - 1) + 1)

    def steps(self, spot, mail, *refs):
        planes, side, number = self.planes, self.side, len(self.inputs)
        made = number + len(self.outputs)
        xs, outs, rest = refs[:number], refs[number:made], refs[made:]
        lows = [0] * number
        if self.partial:
            outs = [outs[0]] * number
            lows = [sum(x.shape[-1] for x in self.inputs[:n]) for n in range(number)]
        each = 5 if self.exchange else 6
        order = [(t, n) for t, group in enumerate(self.groups) for n in range(len(group))]
        held = {key: rest[each * p : each * (p + 1)] for p, key in enumerate(order)}
        core, z = spot.core, spot.z
        other, mate = spot.mate()

        def stage(step, key, cut):
            i, rows, columns, first = cut
            x, out = xs[i], outs[i]
            one, hop_two, two, hop_three, three = held[key][:5]
            if step == 0:
                return [mail.start(x.at[:, :, :, other, rows, columns], one, mate)]
            sent = []
            if step == 1:

                def add(n, carry):
                    ia, ib = lax.rem(lax.div(n, side), side), lax.rem(n, side)
                    iz = lax.div(n, side * side)
                    total = x[iz, ia, ib, core, rows, columns].astype(f32)
                    one[iz, ia, ib] = (total + one[iz, ia, ib].astype(f32)).astype(one.dtype)
                    return carry

                lax.fori_loop(0, planes * side * side, add, 0)
                for k in range(1, side):
                    peer, target = spot.along(first, k)
                    part = one.at[:, peer] if first else one.at[:, :, peer]
                    sent.append(mail.start(part, hop_two.at[k - 1], target))
            elif step == 2:

                def add(n, carry):
                    iz, ir = lax.div(n, side), lax.rem(n, side)
                    total = (one[iz, spot.a, ir] if first else one[iz, ir, spot.b]).astype(f32)
                    for k in range(side - 1):
                        total += hop_two[k, iz, ir].astype(f32)
                    two[iz, ir] = total.astype(two.dtype)
                    return carry

                lax.fori_loop(0, planes * side, add, 0)
                for k in range(1, side):
                    peer, target = spot.along(not first, k)
                    sent.append(mail.start(two.at[:, peer], hop_three.at[k - 1], target))
            elif step == 3:
                mine = spot.b if first else spot.a

                def add(iz, carry):
                    total = two[iz, mine].astype(f32)
                    for k in range(side - 1):
                        total += hop_three[k, iz].astype(f32)
                    if self.partial:
                        place = slice(lows[i] + columns.start, lows[i] + columns.stop)
                        out[iz, rows, place] = total.astype(out.dtype)
                    else:
                        three[iz] = total.astype(three.dtype)
                    return carry

                lax.fori_loop(0, planes, add, 0)
                if self.partial:
                    return []
                for k in range(1, planes):
                    peer, target = spot.plane(k)
                    if self.exchange:
                        place = out.at[z, rows, columns]
                    else:
                        place = held[key][5].at[k - 1]
                    sent.append(mail.start(three.at[peer], place, target))
                if self.exchange:
                    out[z, rows, columns] = three[z]
            elif not self.exchange:
                total = three[z].astype(f32)
                for k in range(planes - 1):
                    total += held[key][5][k].astype(f32)
                out[rows, columns] = total
            return sent

        return pipeline(self.groups, stage, 4)


class Swap:
    flat = False
    def __init__(self, x, turns, planes, side, back=False, held=None):
        self.planes, self.side = planes, side
        self.inputs = [x] if held is None else [x, held]
        self.in_spaces, self.out_spaces = (pltpu.HBM,) * len(self.inputs), (pltpu.HBM,)
        self.aliases = {} if held is None else {1: 0}
        self.turns, self.back = turns, back
        self.scratch = [pltpu.SemaphoreType.DMA((len(turns),))]
        self.columns = x.shape[1] // planes if back else x.shape[1]
        self.rows = x.shape[0] if back else x.shape[0] // planes
        shape = (planes, self.rows, self.columns) if back else (self.rows, planes * self.columns)
        self.outputs = [jax.ShapeDtypeStruct(shape, x.dtype)]
        self.copies = len(turns) * (planes - 1)

    def steps(self, spot, mail, *refs):
        x, out, own_sem = refs[0], refs[-2], refs[-1]
        def block(z):
            return pl.ds(pl.multiple_of(z * self.columns, 128), self.columns)

        def source(z, begin, size):
            if self.back:
                return x.at[pl.ds(begin, size), block(z)]
            return x.at[pl.ds(pl.multiple_of(z * self.rows + begin, 16), size), :]

        sent, own, now = [], [], 0
        for n, (begin, size, rounds) in enumerate(self.turns):
            while now < rounds:
                now += 1
                yield
            rows = pl.ds(begin, size)
            place = out.at[spot.z, rows] if self.back else out.at[rows, block(spot.z)]
            for k in range(1, self.planes):
                peer, target = spot.plane(k)
                sent.append(mail.start(source(peer, begin, size), place, target))
            own.append(pltpu.make_async_copy(source(spot.z, begin, size), place, own_sem.at[n]))
            own[-1].start()
        while now < 24:
            now += 1
            yield
        for copy in own:
            copy.wait()
        for copy in sent:
            copy.wait_recv()


class Chain:
    flat = False

    def __init__(self, reduce, extra, extra_out, middle, gather):
        self.planes, self.side = reduce.planes, reduce.side
        self.reduce, self.middle, self.gather = reduce, middle, gather
        self.inputs = reduce.inputs + extra
        self.outputs = gather.outputs + extra_out
        self.scratch = reduce.scratch + [
            pltpu.VMEM(x.shape, x.dtype) for x in reduce.outputs + gather.inputs
        ]
        self.copies = reduce.copies + gather.copies

    def steps(self, spot, mail, *refs):
        n_in, n_out = len(self.inputs), len(self.outputs)
        (x, *extra), (out, *extra_out) = refs[:n_in], refs[n_in : n_in + n_out]
        *held, sums, made = refs[n_in + n_out :]
        yield from self.reduce.steps(spot, mail, x, sums, *held)
        self.middle(sums, made, *extra, *extra_out)
        yield from self.gather.steps(spot, mail, made, out)


def final_norm(sums, made, resid, gains, resid_two):
    values = resid[...] + sums[...]
    resid_two[...] = values
    made[...] = (values * inverse_root(values) * gains[2:3]).astype(bf16)


def final_norm_back(sums, made, resid_two, gains, grad_two, gain_grad):
    grad, gain_grad[...] = norm_back(resid_two[...], gains[2:3], sums[...])
    grad_two[...] = grad
    made[...] = grad.astype(bf16)


def communicate(parts, ident):
    planes, side = parts[0].planes, parts[0].side
    counts = [(len(p.inputs), len(p.outputs), len(p.scratch)) for p in parts]
    n_in, n_out = (sum(c[i] for c in counts) for i in range(2))
    copies = sum(p.copies for p in parts)
    aliases, i, o = {}, 0, 0
    for part, (ci, co, _) in zip(parts, counts):
        aliases.update({i + a: o + b for a, b in getattr(part, "aliases", {}).items()})
        i, o = i + ci, o + co

    def kernel(*refs):
        ins, outs, rest = refs[:n_in], refs[n_in : n_in + n_out], refs[n_in + n_out :]
        send, recv = rest[-2:]
        spot = Spot(planes, side)
        spot.greet(parts[0].flat)
        mail = Mail(send, recv)
        running, i, o, s = [], 0, 0, 0
        for part, (ci, co, cs) in zip(parts, counts):
            running.append(
                part.steps(spot, mail, *ins[i : i + ci], *outs[o : o + co], *rest[s : s + cs])
            )
            i, o, s = i + ci, o + co, s + cs
        while running:
            running = [steps for steps in running if next(steps, True) is None]
        mail.finish()

    size = sum(x.size * x.dtype.itemsize for p in parts for x in p.inputs + p.outputs)
    need = sum(
        math.prod(x.shape) * x.dtype.itemsize
        for p in parts
        for x in p.scratch
        if x.memory_space == pltpu.VMEM
    )
    need += sum(
        x.size * x.dtype.itemsize
        for p in parts
        if not isinstance(p, Swap)
        for x in p.inputs + p.outputs
    )
    out = pl.pallas_call(
        kernel,
        out_shape=[x for p in parts for x in p.outputs],
        in_specs=[
            pl.BlockSpec(memory_space=space)
            for p in parts
            for space in getattr(p, "in_spaces", (pltpu.VMEM,) * len(p.inputs))
        ],
        out_specs=[
            pl.BlockSpec(memory_space=space)
            for p in parts
            for space in getattr(p, "out_spaces", (pltpu.VMEM,) * len(p.outputs))
        ],
        input_output_aliases=aliases,
        scratch_shapes=[s for p in parts for s in p.scratch]
        + [pltpu.SemaphoreType.DMA((copies,)), pltpu.SemaphoreType.DMA((copies,))],
        compiler_params=pltpu.CompilerParams(
            collective_id=ident,
            has_side_effects=True,
            vmem_limit_bytes=min(62 << 20, need * 9 // 8 + (4 << 20)),
        ),
        cost_estimate=pl.CostEstimate(flops=0, bytes_accessed=20 * size, transcendentals=0),
        name="exchange_" + str(ident),
    )(*[x for p in parts for x in p.inputs])
    return list(out)

def expert_gate(gates, lane):
    lanes = lax.broadcasted_iota(jnp.int32, gates.shape, 1)
    return jnp.sum(jnp.where(lanes == lane, gates, 0.0), axis=1, keepdims=True)


CHUNK = 512
BLOCK = 1024
ACROSS = (((1,), (1,)), ((), ()))


def forward_kernel(
    lane_ref, rows_ref, routes_ref, router_ref, in_ref, down_ref, out_ref, mid_ref, gates_ref, cat_ref, down_out, hidden_ref
):
    e, number = pl.program_id(1), pl.num_programs(1)
    units = in_ref.shape[1]
    for j in range(2):
        cat_ref[:, j * units : (j + 1) * units] = in_ref[pl.ds(j, D, stride=2), :].astype(bf16)
    down_out[pl.ds(pl.multiple_of(e * units, units), units), :] = down_ref[0].astype(bf16)

    def chunk(i, carry):
        here = pl.ds(pl.multiple_of(i * CHUNK, CHUNK), CHUNK)
        rows = rows_ref[here, :]

        @pl.when(e == 0)
        def _():
            logits = jnp.dot(rows, router_ref[...], preferred_element_type=f32)
            lanes = lax.broadcasted_iota(jnp.int32, logits.shape, 1)
            mask = lanes == routes_ref[here, 0:1]
            for j in range(1, TOP):
                mask |= lanes == routes_ref[here, j : j + 1]
            top = jnp.max(jnp.where(mask, logits, -3e38), axis=1, keepdims=True)
            weight = jnp.where(mask, jnp.exp(jnp.where(mask, logits - top, 0.0)), 0.0)
            gates_ref[here, :] = weight / jnp.sum(weight, axis=1, keepdims=True)

        mid = jnp.dot(rows, cat_ref[...], preferred_element_type=f32)
        mid_ref[here, :] = mid
        gate, up = mid[:, :units], mid[:, units:]
        hidden = (gate * jax.nn.sigmoid(gate) * up).astype(bf16).astype(f32)
        hidden = (hidden * expert_gate(gates_ref[here, :], lane_ref[0] + e)).astype(bf16)
        hidden_ref[here, pl.ds(pl.multiple_of(e * units, units), units)] = hidden

        @pl.when(e == number - 1)
        def _():
            out_ref[here, :] = jnp.dot(
                hidden_ref[here, :], down_out[...], preferred_element_type=f32
            ).astype(bf16)

        return carry

    lax.fori_loop(0, rows_ref.shape[0] // CHUNK, chunk, 0)


def experts_forward(lane, rows, routes, router, in_rows, down):
    number, units = down.shape[:2]
    total = rows.shape[0]
    block = min(total, BLOCK)
    row = lambda r, e, *_: (r, 0)
    still = lambda r, e, *_: (0, 0)
    return pl.pallas_call(
        forward_kernel,
        grid_spec=pltpu.PrefetchScalarGridSpec(
            num_scalar_prefetch=1,
            grid=(total // block, number),
            in_specs=[
                pl.BlockSpec((block, D), row),
                pl.BlockSpec((block, TOP), row),
                pl.BlockSpec((D, 128), lambda r, e, *_: (0, PACK // 128 - 1)),
                pl.BlockSpec((2 * D, units), lambda r, e, *_: (e, 0)),
                pl.BlockSpec((1, units, D), lambda r, e, *_: (e, 0, 0)),
            ],
            out_specs=[
                pl.BlockSpec((block, D), row),
                pl.BlockSpec((block, 2 * units), lambda r, e, *_: (r, e)),
                pl.BlockSpec((block, 128), row),
                pl.BlockSpec((D, 2 * units), lambda r, e, *_: (0, e)),
                pl.BlockSpec((number * units, D), still),
                pl.BlockSpec((block, number * units), row),
            ],
        ),
        out_shape=[
            jax.ShapeDtypeStruct((total, D), bf16),
            jax.ShapeDtypeStruct((total, 2 * units * number), f32),
            jax.ShapeDtypeStruct((total, 128), f32),
            jax.ShapeDtypeStruct((D, 2 * units * number), bf16),
            jax.ShapeDtypeStruct((number * units, D), bf16),
            jax.ShapeDtypeStruct((total, number * units), bf16),
        ],
        compiler_params=pltpu.CompilerParams(vmem_limit_bytes=42 << 20),
        name="experts_forward",
    )(lane, rows, routes, router, in_rows, down)


def backward_kernel(
    lane_ref, grad_ref, mid_ref, gates_ref, cat_ref, down_ref, out_ref, mid_grad_ref, pulled_ref
):
    number = lane_ref.shape[0]
    units = pulled_ref.shape[1] // number

    def chunk(i, carry):
        here = pl.ds(pl.multiple_of(i * CHUNK, CHUNK), CHUNK)
        pulled_ref[...] = lax.dot_general(
            grad_ref[here, :], down_ref[...], ACROSS, preferred_element_type=f32
        )
        lanes = lax.broadcasted_iota(jnp.int32, (CHUNK, 128), 1)
        gate_part = jnp.zeros((CHUNK, 128), f32)
        for e in range(number):
            lane = lane_ref[e]
            weight = expert_gate(gates_ref[here, :], lane)
            gate = mid_ref[here, 2 * e * units : (2 * e + 1) * units]
            up = mid_ref[here, (2 * e + 1) * units : (2 * e + 2) * units]
            pulled = pulled_ref[:, e * units : (e + 1) * units]
            soft = jax.nn.sigmoid(gate)
            silu = gate * soft
            hidden = (silu * up).astype(bf16).astype(f32)
            gate_grad = jnp.sum(hidden * pulled, axis=1, keepdims=True)
            gate_part = jnp.where(lanes == lane, gate_grad, gate_part)
            hidden_grad = (pulled * weight).astype(bf16).astype(f32)
            turned = hidden_grad * up * (soft * (1.0 + gate * (1.0 - soft)))
            mid_grad_ref[here, 2 * e * units : (2 * e + 1) * units] = turned.astype(bf16)
            mid_grad_ref[here, (2 * e + 1) * units : (2 * e + 2) * units] = (
                hidden_grad * silu
            ).astype(bf16)
        out_ref[here, D:] = gate_part.astype(bf16)
        out_ref[here, :D] = lax.dot_general(
            mid_grad_ref[here, :], cat_ref[...], ACROSS, preferred_element_type=f32
        ).astype(bf16)
        return carry

    lax.fori_loop(0, grad_ref.shape[0] // CHUNK, chunk, 0)


def experts_backward(lanes, grad, mid, gates, cat, down):
    number = lanes.shape[0]
    total = grad.shape[0]
    block = CHUNK
    row = lambda r, *_: (r, 0)
    still = lambda r, *_: (0, 0)
    return pl.pallas_call(
        backward_kernel,
        grid_spec=pltpu.PrefetchScalarGridSpec(
            num_scalar_prefetch=1,
            grid=(total // block,),
            in_specs=[
                pl.BlockSpec((block, D), row),
                pl.BlockSpec((block, mid.shape[1]), row),
                pl.BlockSpec((block, 128), row),
                pl.BlockSpec(cat.shape, still),
                pl.BlockSpec(down.shape, still),
            ],
            out_specs=[
                pl.BlockSpec((block, D + 128), row),
                pl.BlockSpec((block, mid.shape[1]), row),
            ],
            scratch_shapes=[pltpu.VMEM((CHUNK, down.shape[0]), f32)],
        ),
        out_shape=[
            jax.ShapeDtypeStruct((total, D + 128), bf16),
            jax.ShapeDtypeStruct(mid.shape, bf16),
        ],
        compiler_params=pltpu.CompilerParams(vmem_limit_bytes=36 << 20),
        name="experts_backward",
    )(lanes, grad, mid, gates, cat, down)


def moments_kernel(
    scale_ref, table_norms, small_norms, grad_ref, w_ref, first_ref, second_ref, down_grad, down_w, down_first, down_second,
    new_first, new_second, updates, new_down_first, new_down_second, down_updates, norms, sums, down_sums, turned,
):
    units = w_ref.shape[1]
    part = w_ref.shape[0] // 2
    scales = (scale_ref[0], scale_ref[1])
    step = pl.program_id(0) * pl.num_programs(1) + pl.program_id(1)

    @pl.when(step == 0)
    def _():
        sums[...] = jnp.zeros_like(sums)
        down_sums[...] = jnp.zeros_like(down_sums)

    for j in range(2):
        turned[pl.ds(j, part, stride=2), :] = grad_ref[:, j * units : (j + 1) * units]
    weight = w_ref[...]
    one, two, update = lamb_parts(weight, first_ref[...], second_ref[...], turned[...], scales)
    new_first[...] = one
    new_second[...] = two
    updates[...] = update
    sums[0] += fold(weight * weight)
    sums[1] += fold(update * update)
    weight = down_w[...]
    one, two, update = lamb_parts(weight, down_first[...], down_second[...], down_grad[...], scales)
    new_down_first[...] = one
    new_down_second[...] = two
    down_updates[...] = update
    down_sums[0] += fold(weight * weight)
    down_sums[1] += fold(update * update)

    @pl.when(step == pl.num_programs(0) * pl.num_programs(1) - 1)
    def _():
        block = norm_cells(5, total_of(sums[0]), total_of(sums[1]))
        block += norm_cells(6, total_of(down_sums[0]), total_of(down_sums[1]))
        norms[...] = table_norms[...] + small_norms[...] + block


def expert_moments(scales, table_norms, small_norms, grad, weight, first, second, *down_state):
    units = weight.shape[1]
    down = down_state[1]
    number = grad.shape[1] // (2 * units)
    parts = 2
    cells = pl.BlockSpec((8, 128), lambda e, p, *_: (0, 0))
    row = pl.BlockSpec((2 * D // parts, units), lambda e, p, *_: (e * parts + p, 0))
    down_row = pl.BlockSpec((units // parts, D), lambda e, p, *_: (e * parts + p, 0))
    return pl.pallas_call(
        moments_kernel,
        grid_spec=pltpu.PrefetchScalarGridSpec(
            num_scalar_prefetch=1,
            grid=(number, parts),
            in_specs=[cells, cells, pl.BlockSpec((D // parts, 2 * units), lambda e, p, *_: (p, e))]
            + [row] * 3
            + [down_row] * 4,
            out_specs=[row] * 3 + [down_row] * 3 + [cells],
            scratch_shapes=[
                pltpu.VMEM((2, 8, units), f32),
                pltpu.VMEM((2, 8, D), f32),
                pltpu.VMEM((2 * D // parts, units), f32),
            ],
        ),
        out_shape=[jax.ShapeDtypeStruct(weight.shape, f32)] * 3
        + [jax.ShapeDtypeStruct(down.shape, f32)] * 3
        + [jax.ShapeDtypeStruct((8, 128), f32)],
        compiler_params=pltpu.CompilerParams(vmem_limit_bytes=62 << 20),
        name="expert_moments",
    )(scales, table_norms, small_norms, grad, weight, first, second, *down_state)


HEAD_COLS = QUERY_HEADS * HEAD_WIDTH
KEY_COLS = KEY_VALUE_HEADS * HEAD_WIDTH
PACK = HEAD_COLS + KEY_COLS + 128
PACK_TWO = KEY_COLS + D
ROOT = HEAD_WIDTH ** (-0.5)


def turn(u, cosine, sine):
    width = u.shape[1]
    lanes = lax.broadcasted_iota(jnp.int32, u.shape, 1)
    ahead = pltpu.roll(u, width - HEAD_WIDTH // 2, 1)
    behind = pltpu.roll(u, HEAD_WIDTH // 2, 1)
    other = jnp.where(lax.rem(lanes, HEAD_WIDTH) < HEAD_WIDTH // 2, ahead, behind)
    return u * jnp.tile(cosine, (1, width // 128)) + other * jnp.tile(sine, (1, width // 128))


def rotary_tables():
    half = HEAD_WIDTH // 2
    freqs = jnp.exp(-jnp.log(10000.0) * jnp.arange(half, dtype=f32) / half)
    angles = jnp.arange(SEQUENCE_TOKENS, dtype=f32)[:, None] * freqs[None, :]
    cosine, sine = jnp.cos(angles), jnp.sin(angles)
    return jnp.tile(cosine, (1, 4)), jnp.tile(jnp.concatenate([-sine, sine], axis=1), (1, 2))


def inverse_root(values):
    return lax.rsqrt(jnp.mean(values * values, axis=-1, keepdims=True) + 1e-06)


def norm_back(values, gain, grad):
    root = inverse_root(values)
    scaled = grad * gain
    inner = jnp.mean(scaled * values, axis=-1, keepdims=True)
    return root * scaled - values * (root * root * root * inner), jnp.sum(
        grad * values * root, axis=0, keepdims=True
    )


def dot(a, b):
    return jnp.dot(a, b, preferred_element_type=f32)


def dot_across(a, b):
    return lax.dot_general(a, b, ACROSS, preferred_element_type=f32)


def selector(start, shape, axis):
    row = lax.broadcasted_iota(jnp.int32, shape, 1 - axis) + start
    return (row == lax.broadcasted_iota(jnp.int32, shape, axis)).astype(f32)


def spread(start, rows):
    pick = selector(start, (SEQUENCE_TOKENS, COMP), 0)
    return jnp.dot(pick, rows, preferred_element_type=f32, precision=lax.Precision.HIGHEST)


def dot_down(a, b):
    return lax.dot_general(a, b, (((0,), (0,)), ((), ())), preferred_element_type=f32)


def head_rows(ref_value, h):
    first = h * GROUP * HEAD_WIDTH
    return jnp.concatenate(
        [
            ref_value[:, first + g * HEAD_WIDTH : first + (g + 1) * HEAD_WIDTH]
            for g in range(GROUP)
        ],
        axis=0,
    )


def head_lanes(parts):
    return jnp.concatenate(
        [part[g * COMP : (g + 1) * COMP] for part in parts for g in range(GROUP)], axis=1
    )


def attend_kernel(
    start_ref, picked_ref, one_ref, two_ref, cos_ref, sin_ref, cos_rows, sin_rows,
    c_ref, resid_ref, probs_ref, query_ref, key_ref, value_ref, mixed_ref, normed_ref, gains_ref,
    embedded,
):
    start = start_ref[0]
    pick_rows = selector(start, (COMP, SEQUENCE_TOKENS), 1).astype(bf16)
    planes, _, columns = picked_ref.shape
    for p in range(planes):
        embedded[:, p * columns : (p + 1) * columns] = picked_ref[p].astype(f32)
    pick = lax.broadcasted_iota(jnp.int32, (8, 128), 0) + EXPERTS
    pick = (pick == lax.broadcasted_iota(jnp.int32, (8, 128), 1)).astype(f32).astype(bf16)
    gains = dot_across(pick, one_ref[:, HEAD_COLS + KEY_COLS :])
    gains_ref[...] = gains
    x = embedded[...]
    a = (x * inverse_root(x) * gains[0:1]).astype(bf16)
    normed_ref[...] = a
    a_rows = dot(pick_rows, a).astype(bf16)
    cosine, sine = cos_ref[...], sin_ref[...]
    query = turn(dot(a_rows, one_ref[:, :HEAD_COLS]), cos_rows[...], sin_rows[...])
    query = query.astype(bf16)
    key = turn(dot(a, one_ref[:, HEAD_COLS : HEAD_COLS + KEY_COLS]), cosine, sine).astype(bf16)
    value = dot(a, two_ref[:, :KEY_COLS]).astype(bf16)
    query_ref[...], key_ref[...], value_ref[...] = query, key, value
    rows = GROUP * COMP
    place = lax.rem(lax.broadcasted_iota(jnp.int32, (rows, SEQUENCE_TOKENS), 0), COMP) + start
    seen = place >= lax.broadcasted_iota(jnp.int32, (rows, SEQUENCE_TOKENS), 1)
    parts = []
    for h in range(KEY_VALUE_HEADS):
        lanes = slice(h * HEAD_WIDTH, (h + 1) * HEAD_WIDTH)
        scores = dot_across(head_rows(query, h), key[:, lanes]) * ROOT
        scores = jnp.where(seen, scores, -1000000000.0)
        expd = jnp.exp(scores - jnp.max(scores, axis=-1, keepdims=True))
        probs = expd / jnp.sum(expd, axis=-1, keepdims=True)
        probs_ref[h] = probs
        parts.append(dot(probs.astype(bf16), value[:, lanes]))
    mixed = head_lanes(parts).astype(bf16)
    mixed_ref[...] = mixed
    resid = dot(pick_rows, embedded[...].astype(bf16)) + dot(mixed, two_ref[:, KEY_COLS : KEY_COLS + D])
    resid_ref[...] = resid
    c_ref[...] = (resid * inverse_root(resid) * gains[1:2]).astype(bf16)


def attend(start, picked, one, two, *tables):
    vm = pl.BlockSpec(memory_space=pltpu.VMEM)
    rows = GROUP * COMP
    return pl.pallas_call(
        attend_kernel,
        in_specs=[pl.BlockSpec(memory_space=pltpu.SMEM)] + [vm] * 7,
        out_specs=[vm] * 9,
        out_shape=[
            jax.ShapeDtypeStruct((COMP, D), bf16),
            jax.ShapeDtypeStruct((COMP, D), f32),
            jax.ShapeDtypeStruct((KEY_VALUE_HEADS, rows, SEQUENCE_TOKENS), f32),
            jax.ShapeDtypeStruct((COMP, HEAD_COLS), bf16),
            jax.ShapeDtypeStruct((SEQUENCE_TOKENS, KEY_COLS), bf16),
            jax.ShapeDtypeStruct((SEQUENCE_TOKENS, KEY_COLS), bf16),
            jax.ShapeDtypeStruct((COMP, HEAD_COLS), bf16),
            jax.ShapeDtypeStruct((SEQUENCE_TOKENS, D), bf16),
            jax.ShapeDtypeStruct((8, D), f32),
        ],
        scratch_shapes=[pltpu.VMEM((SEQUENCE_TOKENS, D), f32)],
        compiler_params=pltpu.CompilerParams(vmem_limit_bytes=28 << 20),
        name="attend",
    )(start, picked, one, two, *tables)


def attend_back_kernel(
    start_ref, back_ref, gates_ref, grad_two_ref, gain_three_ref, c_ref, resid_ref, probs_ref, query_ref,
    key_ref, value_ref, mixed_ref, normed_ref, gains_ref, picked_ref, one_ref, two_ref, cos_ref, sin_ref, cos_rows, sin_rows,
    out_ref, grad_one_ref, grad_pack_ref,
    total,
):
    start = start_ref[0]
    planes, _, columns = picked_ref.shape
    gains = gains_ref[...]
    wide = HEAD_COLS + KEY_COLS
    gates = gates_ref[...]
    gate_grad = back_ref[:, D:]
    router_grad = gates * (gate_grad - jnp.sum(gates * gate_grad, axis=1, keepdims=True))
    router_grad = router_grad.astype(bf16)
    grad = back_ref[:, :D] + dot_across(router_grad, one_ref[:, wide:])
    grad_resid, gain_two = norm_back(resid_ref[...], gains[1:2], grad)
    grad_resid = grad_resid + grad_two_ref[...]
    branch = grad_resid.astype(bf16)
    grad_mixed = dot_across(branch, two_ref[:, KEY_COLS : KEY_COLS + D]).astype(bf16)
    query, key, value = query_ref[...], key_ref[...], value_ref[...]
    query_parts, key_parts, value_parts = [], [], []
    for h in range(KEY_VALUE_HEADS):
        lanes = slice(h * HEAD_WIDTH, (h + 1) * HEAD_WIDTH)
        probs = probs_ref[h]
        grad_head = head_rows(grad_mixed, h)
        grad_probs = dot_across(grad_head, value[:, lanes]).astype(bf16).astype(f32)
        inner = jnp.sum(grad_probs * probs, axis=-1, keepdims=True)
        grad_scores = probs * (grad_probs - inner)
        value_parts.append(dot_down(probs.astype(bf16), grad_head))
        query_parts.append(dot(grad_scores.astype(bf16), key[:, lanes]) * ROOT)
        key_parts.append(dot_down(grad_scores.astype(bf16), head_rows(query, h)) * ROOT)
    grad_query = turn(head_lanes(query_parts), cos_rows[...], -sin_rows[...]).astype(bf16)
    grad_key = jnp.concatenate(key_parts, axis=1)
    grad_key = turn(grad_key, cos_ref[...], -sin_ref[...]).astype(bf16)
    grad_value = jnp.concatenate(value_parts, axis=1).astype(bf16)
    grad_normed = dot_across(grad_key, one_ref[:, HEAD_COLS:wide])
    grad_normed += dot_across(grad_value, two_ref[:, :KEY_COLS])
    grad_normed += spread(start, dot_across(grad_query, one_ref[:, :HEAD_COLS]))
    for p in range(planes):
        total[:, p * columns : (p + 1) * columns] = picked_ref[p].astype(f32)
    grad_embedded, gain_one = norm_back(total[...], gains[0:1], grad_normed)
    total[...] = grad_embedded + spread(start, grad_resid)
    for p in range(planes):
        out_ref[p] = total[:, p * columns : (p + 1) * columns].astype(bf16)
    pick_rows = selector(start, (COMP, SEQUENCE_TOKENS), 1).astype(bf16)
    a_rows = dot(pick_rows, normed_ref[...])
    turned = normed_ref[...]
    grad_one_ref[:, HEAD_COLS:wide] = dot_down(turned, grad_key).astype(bf16)
    grad_pack_ref[:, :KEY_COLS] = dot_down(turned, grad_value).astype(bf16)
    grad_one_ref[:, :HEAD_COLS] = dot_down(a_rows.astype(bf16), grad_query).astype(bf16)
    grad_pack_ref[:, KEY_COLS : KEY_COLS + D] = dot_down(mixed_ref[...], branch).astype(bf16)
    left = jnp.concatenate(
        [c_ref[...].astype(f32), gain_one, gain_two, gain_three_ref[...], jnp.zeros((5, D), f32)],
        axis=0,
    )
    lane = lax.broadcasted_iota(jnp.int32, (8, 128), 0) + EXPERTS
    lane = (lane == lax.broadcasted_iota(jnp.int32, (8, 128), 1)).astype(f32)
    right = jnp.concatenate([router_grad.astype(f32), lane], axis=0).astype(bf16)
    grad_one_ref[:, wide:] = dot_down(left.astype(bf16), right).astype(bf16)


def attend_back(start, *operands):
    vm = pl.BlockSpec(memory_space=pltpu.VMEM)
    picked = operands[13]
    return pl.pallas_call(
        attend_back_kernel,
        in_specs=[pl.BlockSpec(memory_space=pltpu.SMEM)] + [vm] * len(operands),
        out_specs=[vm] * 3,
        out_shape=[
            jax.ShapeDtypeStruct(picked.shape, bf16),
            jax.ShapeDtypeStruct((D, PACK), bf16),
            jax.ShapeDtypeStruct((D, PACK_TWO), bf16),
        ],
        scratch_shapes=[pltpu.VMEM((SEQUENCE_TOKENS, D), f32)],
        compiler_params=pltpu.CompilerParams(vmem_limit_bytes=44 << 20),
        name="attend_back",
    )(start, *operands)


def lamb_update(weight, moment_one, moment_two, scale_one, scale_two):
    square = moment_two * scale_two
    return (moment_one * scale_one) / (square * lax.rsqrt(square) + EPSILON) + DECAY * weight


def lamb_parts(weight, moment_one, moment_two, gradient, scales):
    moment_one = RATE_ONE * moment_one + (1.0 - RATE_ONE) * gradient
    moment_two = RATE_TWO * moment_two + (1.0 - RATE_TWO) * gradient * gradient
    return (moment_one, moment_two, lamb_update(weight, moment_one, moment_two, *scales))


STEPS = 4
TOGETHER = 4


def row_lists(tokens, base, rows):
    inside = (tokens >= base) & (tokens < base + rows)
    count = jnp.sum(inside.astype(jnp.int32), axis=1)
    place = jnp.arange(SEQUENCE_TOKENS, dtype=jnp.int32)
    before = (place[:, None] < place[None, :]).astype(bf16)
    rank = jnp.dot(inside.astype(bf16), before, preferred_element_type=f32).astype(jnp.int32)
    packed = place[None, :] * 65536 + (tokens - base)
    hit = inside[:, :, None] & (rank[:, :, None] == place[None, None, :])
    entry = jnp.sum(jnp.where(hit, packed[:, :, None], 0), axis=1)
    empty = SEQUENCE_TOKENS * 65536
    return jnp.where(place[None, :] < count[:, None], entry, empty), count


def gather_kernel(list_ref, count_ref, table_ref, out_ref, table_out, rows_ref):
    part = table_out.shape[0]
    here = pl.ds(pl.multiple_of(pl.program_id(0) * part, 16), part)
    table_out[...] = table_ref[here, :].astype(bf16)
    for n in range(TOGETHER):
        b = pl.program_id(0) * TOGETHER + n
        rows_ref[n] = jnp.zeros(rows_ref.shape[1:], f32)

        def step(k, carry, n=n, b=b):
            for j in range(STEPS):
                entry = list_ref[b, k * STEPS + j]
                rows_ref[n, pl.ds(entry >> 16, 1), :] = table_ref[pl.ds(entry & 65535, 1), :]
            return carry

        lax.fori_loop(0, (count_ref[b] + STEPS - 1) // STEPS, step, 0)
        out_ref[n] = rows_ref[n, :SEQUENCE_TOKENS].astype(bf16)


def gather_rows(lists, counts, table):
    blocks = lists.shape[0]
    rows, columns = table.shape
    return pl.pallas_call(
        gather_kernel,
        grid_spec=pltpu.PrefetchScalarGridSpec(
            num_scalar_prefetch=2,
            grid=(blocks // TOGETHER,),
            in_specs=[pl.BlockSpec((rows, columns), lambda b, *_: (0, 0))],
            out_specs=[
                pl.BlockSpec((TOGETHER, SEQUENCE_TOKENS, columns), lambda b, *_: (b, 0, 0)),
                pl.BlockSpec((rows * TOGETHER // blocks, columns), lambda b, *_: (b, 0)),
            ],
            scratch_shapes=[pltpu.VMEM((TOGETHER, SEQUENCE_TOKENS + 8, columns), f32)],
        ),
        out_shape=[
            jax.ShapeDtypeStruct((blocks, SEQUENCE_TOKENS, columns), bf16),
            jax.ShapeDtypeStruct((rows, columns), bf16),
        ],
        compiler_params=pltpu.CompilerParams(vmem_limit_bytes=26 << 20),
        name="gather_rows",
    )(lists, counts, table)


TABLE_PARTS = 8


def norm_cells(row, weight_sum, update_sum):
    rows = lax.broadcasted_iota(jnp.int32, (8, 128), 0)
    lanes = lax.broadcasted_iota(jnp.int32, (8, 128), 1)
    block = jnp.where(lanes == 0, weight_sum, jnp.where(lanes == 1, update_sum, 0.0))
    return jnp.where(rows == row, block, 0.0)


def total_of(values):
    return jnp.sum(jnp.sum(values, axis=1, keepdims=True), axis=0, keepdims=True)


def fold(values):
    return jnp.sum(values.reshape(-1, 8, values.shape[1]), axis=0)


def table_kernel(
    list_ref, count_ref, scale_ref, grad_ref, head_ref, w_in, first_in, second_in,
    new_first, new_second, updates, norms,
    rows_ref, acc, w, first, second, sums, sems,
):
    b = pl.program_id(0)
    blocks = pl.num_programs(0) - TABLE_PARTS
    loads = [
        pltpu.make_async_copy(src, dst, sems.at[n])
        for n, (src, dst) in enumerate([(w_in, w), (first_in, first), (second_in, second)])
    ]

    @pl.when(b == 0)
    def _():
        for load in loads:
            load.start()
        acc[...] = head_ref[...].astype(f32)
        sums[...] = jnp.zeros_like(sums)

    @pl.when(b < blocks)
    def _():
        for n in range(TOGETHER):
            rows_ref[n, :SEQUENCE_TOKENS] = grad_ref[n].astype(f32)
            rows_ref[n, SEQUENCE_TOKENS:] = jnp.zeros((8, rows_ref.shape[2]), f32)
            own = b * TOGETHER + n

            def step(k, carry, n=n, own=own):
                entries = [list_ref[own, k * STEPS + j] for j in range(STEPS)]
                spots = [entry & 65535 for entry in entries]
                grads = [rows_ref[n, pl.ds(entry >> 16, 1), :] for entry in entries]
                olds = [acc[pl.ds(spot, 1), :] for spot in spots]
                for j in range(STEPS):
                    total = olds[j] + grads[j]
                    for i in range(j):
                        total += jnp.where(spots[i] == spots[j], grads[i], 0.0)
                    acc[pl.ds(spots[j], 1), :] = total
                return carry

            lax.fori_loop(0, (count_ref[own] + STEPS - 1) // STEPS, step, 0)

    @pl.when(b == blocks)
    def _():
        for load in loads:
            load.wait()

    @pl.when(b >= blocks)
    def _():
        size = new_first.shape[0]
        here = pl.ds(pl.multiple_of((b - blocks) * size, 8), size)
        one, two, update = lamb_parts(
            w[here, :], first[here, :], second[here, :], acc[here, :], (scale_ref[0], scale_ref[1])
        )
        new_first[...] = one
        new_second[...] = two
        updates[...] = update
        sums[0] += fold(w[here, :] * w[here, :])
        sums[1] += fold(update * update)

    @pl.when(b == blocks + TABLE_PARTS - 1)
    def _():
        norms[...] = norm_cells(0, total_of(sums[0]), total_of(sums[1]))


def table_moments(lists, counts, scales, grads, head, weight, first, second):
    blocks = lists.shape[0] // TOGETHER
    rows, columns = weight.shape
    part = rows // TABLE_PARTS
    out = pl.BlockSpec((part, columns), lambda b, *_: (jnp.maximum(b - blocks, 0), 0))
    return pl.pallas_call(
        table_kernel,
        grid_spec=pltpu.PrefetchScalarGridSpec(
            num_scalar_prefetch=3,
            grid=(blocks + TABLE_PARTS,),
            in_specs=[
                pl.BlockSpec(
                    (TOGETHER, SEQUENCE_TOKENS, columns),
                    lambda b, *_: (jnp.minimum(b, blocks - 1), 0, 0),
                ),
                pl.BlockSpec(
                    (rows, columns), lambda b, *_: (0, 0), pipeline_mode=pl.Buffered(1)
                ),
            ]
            + [pl.BlockSpec(memory_space=pl.ANY)] * 3,
            out_specs=[out, out, out, pl.BlockSpec((8, 128), lambda b, *_: (0, 0))],
            scratch_shapes=[pltpu.VMEM((TOGETHER, SEQUENCE_TOKENS + 8, columns), f32)]
            + [pltpu.VMEM((rows, columns), f32)] * 4
            + [pltpu.VMEM((2, 8, columns), f32), pltpu.SemaphoreType.DMA((3,))],
        ),
        out_shape=[jax.ShapeDtypeStruct((rows, columns), f32)] * 3
        + [jax.ShapeDtypeStruct((8, 128), f32)],
        compiler_params=pltpu.CompilerParams(vmem_limit_bytes=58 << 20),
        name="table_moments",
    )(lists, counts, scales, grads, head, weight, first, second)


def small_kernel(
    scale_ref, grad_ref, qkv, qkv_one, qkv_two, out, out_one, out_two, router, router_one, router_two,
    gains, gains_one, gains_two, *results
):
    scales = (scale_ref[0], scale_ref[1])
    planes = grad_ref.shape[0]
    total = grad_ref[0].astype(f32)
    for z in range(1, planes):
        total += grad_ref[z].astype(f32)
    packs = (total[:, :PACK], total[:, PACK:])
    wide = HEAD_COLS + KEY_COLS
    pick = lax.broadcasted_iota(jnp.int32, (EXPERTS + 8, 128), 0)
    pick = (pick == lax.broadcasted_iota(jnp.int32, (EXPERTS + 8, 128), 1)).astype(f32)
    turned = lax.dot_general(
        pick,
        packs[0][:, wide:],
        ACROSS,
        preferred_element_type=f32,
        precision=lax.Precision.HIGHEST,
    )
    block = jnp.zeros((8, 128), f32)
    sets = [
        (qkv, qkv_one, qkv_two, jnp.concatenate([packs[0][:, :wide], packs[1][:, :KEY_COLS]], axis=1)),
        (out, out_one, out_two, packs[1][:, KEY_COLS : KEY_COLS + D]),
        (router, router_one, router_two, turned[:EXPERTS]),
        (gains, gains_one, gains_two, turned[EXPERTS : EXPERTS + 3]),
    ]
    for n, (weight, first, second, grad) in enumerate(sets):
        one, two, update = lamb_parts(weight[...], first[...], second[...], grad, scales)
        results[3 * n][...] = one
        results[3 * n + 1][...] = two
        results[3 * n + 2][...] = update
        block += norm_cells(n + 1, total_of(weight[...] * weight[...]), total_of(update * update))
    results[12][...] = block


def small_moments(scales, sums, *state):
    vm = pl.BlockSpec(memory_space=pltpu.VMEM)
    return pl.pallas_call(
        small_kernel,
        in_specs=[pl.BlockSpec(memory_space=pltpu.SMEM)] + [vm] * (1 + len(state)),
        out_specs=[vm] * 13,
        out_shape=[jax.ShapeDtypeStruct(x.shape, f32) for x in state[::3] for _ in range(3)]
        + [jax.ShapeDtypeStruct((8, 128), f32)],
        compiler_params=pltpu.CompilerParams(vmem_limit_bytes=62 << 20),
        name="small_moments",
    )(scales, sums, *state)


FINISH_PARTS = 8


def finish_kernel(norms_ref, *refs):
    norms = jnp.sqrt(jnp.sum(norms_ref[...], axis=0))
    count = len(refs) // 3

    def apply(n, row):
        ratio = norms[row : row + 1, 0:1] / norms[row : row + 1, 1:2]
        refs[2 * count + n][...] = refs[2 * n][...] - (STEP_RATE * ratio) * refs[2 * n + 1][...]

    apply(0, 0)
    apply(1, 5)
    apply(2, 6)

    @pl.when(pl.program_id(0) == 0)
    def _():
        apply(3, 1)
        apply(4, 2)


def finish(norms, *state):
    weights = state[::2]

    def spec(n):
        rows, columns = weights[n].shape
        if n < 3:
            return pl.BlockSpec((rows // FINISH_PARTS, columns), lambda i: (i, 0))
        return pl.BlockSpec((rows, columns), lambda i: (0, 0))

    return pl.pallas_call(
        finish_kernel,
        grid=(FINISH_PARTS,),
        in_specs=[pl.BlockSpec(norms.shape, lambda i: (0, 0, 0))]
        + [spec(n) for n in range(5) for _ in range(2)],
        out_specs=[spec(n) for n in range(5)],
        out_shape=[jax.ShapeDtypeStruct(x.shape, f32) for x in weights],
        compiler_params=pltpu.CompilerParams(vmem_limit_bytes=62 << 20),
        name="finish",
    )(norms, *state)


def on_device(
    token_ids,
    positions,
    pair_index,
    ref_logps,
    routes,
    step_count,
    embed_table,
    embed_first,
    embed_second,
    qkv_weight,
    qkv_first,
    qkv_second,
    out_weight,
    out_first,
    out_second,
    router_weight,
    router_first,
    router_second,
    norm_gains,
    gains_first,
    gains_second,
    in_weight,
    in_first,
    in_second,
    down_weight,
    down_first,
    down_second,
):
    shard_id = lax.axis_index("shard")
    expert_id = lax.axis_index("expert")
    shards = lax.axis_size("shard")
    planes = lax.axis_size("expert")
    devices = shards * planes
    vocab_rows, columns = embed_table.shape
    vocab_base = shard_id * vocab_rows
    own_rows = vocab_rows // planes
    local_experts = in_weight.shape[0]
    hidden_units = in_weight.shape[3]
    head_cols = QUERY_HEADS * HEAD_WIDTH
    key_cols = KEY_VALUE_HEADS * HEAD_WIDTH
    rows_all = devices * COMP

    side = math.isqrt(shards // 2)
    grid = (planes, side, side, 2)
    together = devices <= 32

    def send(parts, ident):
        if together:
            return communicate(parts, ident)
        return [
            out for n, part in enumerate(parts) for out in communicate([part], ident + 20 * n)
        ]

    unit = own_rows // 24

    def swap(x, *turns, back=False, held=None):
        turns = [(start * unit, size * unit, rounds) for start, size, rounds in turns]
        return Swap(x, turns, planes, side, back, held)

    def gather_part(rows):
        return Gather([rows], split(0, COMP, rows.shape[1], 2, 2), planes, side)

    def reduce_part(rows, cuts):
        width = rows.shape[1]
        rows = rows.reshape(grid + (COMP, width))
        edges = [width * n // (128 * cuts) * 128 for n in range(cuts + 1)]
        groups = [
            [
                (0, slice(i * COMP // 2, (i + 1) * COMP // 2), slice(low, high), i == 0)
                for i in range(2)
            ]
            for low, high in zip(edges, edges[1:])
        ]
        return Reduce([rows], groups, planes, side)

    def chain(rows, extra, extra_out, middle, beside, ident):
        gather = gather_part(jax.ShapeDtypeStruct((COMP, D), bf16))
        part = Chain(reduce_part(rows, 2), extra, extra_out, middle, gather)
        out = communicate([part, beside], ident)
        return (out[0].reshape(rows_all, D), *out[1:])

    def gather_tiny(block, ident):
        return communicate([Tiny(block, planes, side)], ident)[0].reshape((devices,) + block.shape)

    weight_rows = qkv_weight.shape[0]
    cuts = 3 if weight_rows % 48 == 0 else 1
    widths = (PACK, PACK_TWO)
    weight_groups = [
        [
            (i, slice(n * (weight_rows // cuts), (n + 1) * (weight_rows // cuts)), slice(0, width), i == 0)
            for i, width in enumerate(widths)
        ]
        for n in range(cuts)
    ]
    embed_groups = split(0, SEQUENCE_TOKENS, columns, 4, 1)

    own_places = lax.dynamic_index_in_dim(positions, shard_id, 0, keepdims=False)
    start = own_places[0]
    own_tokens = lax.dynamic_slice_in_dim(token_ids, shard_id * SEQUENCE_TOKENS, SEQUENCE_TOKENS, 0)
    own_routes = lax.dynamic_slice_in_dim(routes, start, COMP, 0)
    sheet = jnp.concatenate(
        [
            own_tokens,
            own_routes.reshape(-1),
            own_places,
            jnp.zeros((1024 - SEQUENCE_TOKENS - COMP * TOP - COMP,), jnp.int32),
        ]
    )
    sheets = gather_tiny(sheet.reshape(8, 128), 0).reshape(devices, 1024)
    tokens_all = sheets[:, :SEQUENCE_TOKENS]
    routes_all = sheets[:, SEQUENCE_TOKENS : SEQUENCE_TOKENS + COMP * TOP].reshape(rows_all, TOP)
    places_all = sheets[:, SEQUENCE_TOKENS + COMP * TOP : SEQUENCE_TOKENS + COMP * TOP + COMP]
    spots = jnp.arange(SEQUENCE_TOKENS, dtype=jnp.int32)
    targets = jnp.sum(
        jnp.where(
            places_all[:, :, None] + 1 == spots[None, None, :], tokens_all[:, None, :], 0
        ),
        axis=2,
    ).reshape(-1)

    lists, counts = row_lists(tokens_all, vocab_base, vocab_rows)
    picked, table_b = gather_rows(lists, counts, embed_table)
    picked = picked.reshape(grid + (SEQUENCE_TOKENS, columns))
    packs = jnp.concatenate(
        [
            qkv_weight[:, : head_cols + key_cols],
            router_weight,
            norm_gains.T,
            jnp.zeros((weight_rows, 128 - EXPERTS - 3), f32),
            qkv_weight[:, head_cols + key_cols :],
            out_weight,
        ],
        axis=1,
    ).astype(bf16)
    packs, sheets = lax.optimization_barrier((packs, sheets))
    packs = lax.all_to_all(
        jnp.broadcast_to(packs[None], (planes,) + packs.shape),
        "expert",
        split_axis=0,
        concat_axis=0,
        tiled=True,
    )
    first_pack, second_pack, picked, table_own = send(
        [
            Gather([packs], weight_groups, planes, side, prior=widths),
            Reduce([picked], embed_groups, planes, side, exchange=True),
            swap(table_b, (0, 16, 0)),
        ],
        1,
    )
    first_pack = first_pack.reshape(D, PACK)
    second_pack = second_pack.reshape(D, PACK_TWO)

    start_at = start.reshape(1)
    tables = rotary_tables()
    tables += tuple(lax.dynamic_slice_in_dim(table, start, COMP, 0) for table in tables)
    normed_two_b, resid, probs, query, key, value, attended, normed_b, gains = attend(
        start_at, picked, first_pack, second_pack, *tables
    )

    expert_rows, table_own = communicate(
        [gather_part(normed_two_b), swap(table_b, (16, 2, 2), held=table_own)], 2
    )
    expert_rows = expert_rows.reshape(rows_all, D)
    lanes = shard_id * local_experts + jnp.arange(local_experts, dtype=jnp.int32)
    in_rows = in_weight.reshape(-1, hidden_units)
    produced, mid, gates, in_cat, down_b, gated_hidden = experts_forward(
        lanes, expert_rows, routes_all, first_pack, in_rows, down_weight
    )
    own_index = expert_id * shards + shard_id
    own_gates = lax.dynamic_slice(gates, (own_index * COMP, 0), (COMP, 128))
    row_block = jax.ShapeDtypeStruct((COMP, D), f32)
    head_rows, resid_two, table_own = chain(
        produced,
        [resid, gains],
        [row_block],
        final_norm,
        swap(table_b, (18, 3, 0), (21, 3, 8), held=table_own),
        3,
    )

    logits = jnp.einsum("rd,vd->rv", head_rows, table_own, preferred_element_type=f32) / LOGIT_SCALE
    own_base = vocab_base + expert_id * own_rows
    target_hot = targets[:, None] == own_base + jnp.arange(own_rows, dtype=jnp.int32)[None, :]
    row_top = jnp.max(logits, axis=1)
    row_total = jnp.sum(jnp.exp(logits - row_top[:, None]), axis=1)
    row_hit = jnp.sum(jnp.where(target_hot, logits, 0.0), axis=1)
    stats = jnp.stack([row_top, row_total, row_hit]).reshape(8, 3 * rows_all // 8)
    stats = gather_tiny(stats, 5).reshape(devices, 3, rows_all)
    top_all = jnp.max(stats[:, 0], axis=0)
    total_all = jnp.sum(stats[:, 1] * jnp.exp(stats[:, 0] - top_all[None]), axis=0)
    row_lse = top_all + jnp.log(total_all)
    seq_sums = jnp.sum((jnp.sum(stats[:, 2], axis=0) - row_lse).reshape(-1, COMP), axis=1)

    sequences = jnp.arange(devices, dtype=jnp.int32)[None, :]
    pair_sign = (pair_index[:, :1] == sequences).astype(f32) - (
        pair_index[:, 1:] == sequences
    ).astype(f32)
    scaled = BETA * jnp.sum(pair_sign * (seq_sums - ref_logps)[None, :], axis=1)
    loss_value = -jnp.mean(jax.nn.log_sigmoid(scaled))
    pair_grad = jax.nn.sigmoid(-scaled) * (-BETA / scaled.shape[0])
    seq_grad = jnp.sum(pair_sign * pair_grad[:, None], axis=0)
    row_grad = jnp.repeat(seq_grad, COMP)
    grad_logits = (
        row_grad[:, None] * (target_hot.astype(f32) - jnp.exp(logits - row_lse[:, None]))
    ).astype(bf16)
    grad_logits = lax.optimization_barrier(grad_logits)
    grad_rows = jnp.dot(grad_logits, table_own, preferred_element_type=f32) / LOGIT_SCALE
    head_grad = (
        jnp.einsum("rv,rd->vd", grad_logits, head_rows, preferred_element_type=f32) / LOGIT_SCALE
    ).astype(bf16)
    grad_all, grad_resid_two, grad_gain_three, head_back = chain(
        grad_rows.astype(bf16),
        [resid_two, gains],
        [row_block, jax.ShapeDtypeStruct((1, D), f32)],
        final_norm_back,
        swap(head_grad, (0, 3, 0), (3, 3, 8), back=True),
        6,
    )

    back, mid_grad = experts_backward(lanes, grad_all, mid, gates, in_cat, down_b)
    back, head_back = communicate(
        [reduce_part(back, 2), swap(head_grad, (6, 3, 0), back=True, held=head_back)], 8
    )

    grad_embedded, *grad_packs = attend_back(
        start_at,
        back,
        own_gates,
        grad_resid_two,
        grad_gain_three,
        normed_two_b,
        resid,
        probs,
        query,
        key,
        value,
        attended,
        normed_b,
        gains,
        picked,
        first_pack,
        second_pack,
        *tables,
    )
    grad_packs = [pack.reshape(grid + (weight_rows, pack.shape[1])) for pack in grad_packs]
    wide = head_cols + key_cols
    plane_sums, sent, head_back = send(
        [
            Reduce(grad_packs, weight_groups, planes, side, partial=True),
            Gather([grad_embedded], embed_groups, planes, side, exchange=True),
            swap(head_grad, (9, 5, 1), (14, 5, 2), (19, 5, 3), back=True, held=head_back),
        ],
        9,
    )
    plane_sums = lax.all_to_all(
        plane_sums, "expert", split_axis=0, concat_axis=0, tiled=True
    )

    step_value = step_count.astype(f32)
    scales = jnp.stack([1.0 / (1.0 - RATE_ONE**step_value), 1.0 / (1.0 - RATE_TWO**step_value)])
    grad_in = jnp.einsum("td,tk->dk", expert_rows, mid_grad, preferred_element_type=f32)
    grad_down = jnp.einsum("tk,td->kd", gated_hidden, grad_all, preferred_element_type=f32)
    down_rows = down_weight.reshape(-1, D)
    table_one, table_two, table_update, table_norms = table_moments(
        lists,
        counts,
        scales,
        sent.reshape(devices, SEQUENCE_TOKENS, columns),
        head_back.reshape(vocab_rows, columns),
        embed_table,
        embed_first,
        embed_second,
    )
    *small, small_norms = small_moments(
        scales,
        plane_sums,
        qkv_weight,
        qkv_first,
        qkv_second,
        out_weight,
        out_first,
        out_second,
        router_weight.T,
        router_first.T,
        router_second.T,
        norm_gains,
        gains_first,
        gains_second,
    )
    in_one, in_two, in_update, down_one, down_two, down_update, expert_norms = expert_moments(
        scales,
        table_norms,
        small_norms,
        grad_in,
        in_rows,
        in_first.reshape(in_rows.shape),
        in_second.reshape(in_rows.shape),
        grad_down,
        down_rows,
        down_first.reshape(down_rows.shape),
        down_second.reshape(down_rows.shape),
    )
    norm_blocks = gather_tiny(expert_norms, 10)
    norm_values = jnp.sqrt(jnp.sum(norm_blocks, axis=0))[:7, :2]
    trust_ratio = norm_values[:, 0] / norm_values[:, 1]
    new_table, new_in, new_down, new_qkv, new_out = finish(
        norm_blocks,
        embed_table,
        table_update,
        in_rows,
        in_update,
        down_rows,
        down_update,
        qkv_weight,
        small[2],
        out_weight,
        small[5],
    )
    new_router = (router_weight.T - STEP_RATE * trust_ratio[3] * small[8]).T
    new_gains = norm_gains - STEP_RATE * trust_ratio[4] * small[11]
    stats = jnp.stack([norm_values[:, 0], norm_values[:, 1], trust_ratio], axis=1)
    return (
        loss_value,
        new_table,
        table_one,
        table_two,
        new_qkv,
        small[0],
        small[1],
        new_out,
        small[3],
        small[4],
        new_router,
        small[6].T,
        small[7].T,
        new_gains,
        small[9],
        small[10],
        new_in.reshape(in_weight.shape),
        in_one.reshape(in_weight.shape),
        in_two.reshape(in_weight.shape),
        new_down.reshape(down_weight.shape),
        down_one.reshape(down_weight.shape),
        down_two.reshape(down_weight.shape),
        stats,
    )


def solution(mesh):
    rows = P(BOTH, None)
    vocab = P("shard", "expert")
    gains = P(None, BOTH)
    inner = P("shard", None, None, "expert")
    outer = P("shard", "expert", None)
    state = (vocab,) * 3 + (rows,) * 9 + (gains,) * 3 + (inner,) * 3 + (outer,) * 3
    return jax.shard_map(
        on_device,
        mesh=mesh,
        in_specs=(P("expert"), P("expert", None), P(), P(), rows, P()) + state,
        out_specs=(P(),) + state + (P(),),
        check_vma=False,
    )
```
